32 devices in a mesh: tok: 8 (over z, core), head: 4 (over y, x).
Axes of the slice: x: 2, y: 2, z: 4, core: 2. Of those that a mesh axis runs over, the one named last changes fastest.
Arguments:
- tokens: bfloat16 [16384, 1024], P(('tok', 'head')), may hold values from -6 to 6
- cotangent: bfloat16 [16384, 1024], P(('tok', 'head')), may hold values from -6 to 6
- slot_frame: int32 [128], P('tok'), may hold values from 0 to 23, as said below
- step_count: int32 [1], replicated, may hold values from 2 to 20
- w_qkv: float32 [2, 1024, 3072], P(None, ('tok', 'head')), may hold values from -0.1875 to 0.1875
- w_proj: float32 [2, 1024, 1024], P(None, None, ('tok', 'head')), may hold values from -1.5 to 1.5
- w_fc1: float32 [2, 1024, 4096], P(None, ('tok', 'head')), may hold values from -0.1875 to 0.1875
- w_fc2: float32 [2, 4096, 1024], P(None, None, ('tok', 'head')), may hold values from -0.09375 to 0.09375
- vectors: float32 [2, 15616], P(None, ('tok', 'head')), as said below
- first_qkv: float32 [2, 1024, 3072], P(None, ('tok', 'head')), may hold values from -0.00012207031 to 0.00012207031
- first_proj: float32 [2, 1024, 1024], P(None, None, ('tok', 'head')), may hold values from -0.00012207031 to 0.00012207031
- first_fc1: float32 [2, 1024, 4096], P(None, ('tok', 'head')), may hold values from -0.00012207031 to 0.00012207031
- first_fc2: float32 [2, 4096, 1024], P(None, None, ('tok', 'head')), may hold values from -0.00012207031 to 0.00012207031
- first_vec: float32 [2, 15616], P(None, ('tok', 'head')), may hold values from -0.0004272461 to 0.0004272461
- second_qkv: float32 [2, 1024, 3072], P(None, ('tok', 'head')), may hold values from 1.9843589e-11 to 3.1749742e-10
- second_proj: float32 [2, 1024, 1024], P(None, None, ('tok', 'head')), may hold values from 1.9843589e-11 to 3.1749742e-10
- second_fc1: float32 [2, 1024, 4096], P(None, ('tok', 'head')), may hold values from 1.9843589e-11 to 3.1749742e-10
- second_fc2: float32 [2, 4096, 1024], P(None, None, ('tok', 'head')), may hold values from 1.9843589e-11 to 3.1749742e-10
- second_vec: float32 [2, 15616], P(None, ('tok', 'head')), may hold values from 1.785923e-10 to 2.8574767e-09
- smooth_qkv: float32 [2, 1024, 3072], P(None, ('tok', 'head')), may hold values from -0.1875 to 0.1875
- smooth_proj: float32 [2, 1024, 1024], P(None, None, ('tok', 'head')), may hold values from -1.5 to 1.5
- smooth_fc1: float32 [2, 1024, 4096], P(None, ('tok', 'head')), may hold values from -0.1875 to 0.1875
- smooth_fc2: float32 [2, 4096, 1024], P(None, None, ('tok', 'head')), may hold values from -0.09375 to 0.09375
- smooth_vec: float32 [2, 15616], P(None, ('tok', 'head')), may hold values from 0.2 to 1.2
Outputs:
- output: float32 [16384, 1024], P(('tok', 'head'))
- grad_tokens: float32 [16384, 1024], P(('tok', 'head'))
- grad_norm: float32 [], replicated
- qkv_weight: float32 [2, 1024, 3072], P(None, ('tok', 'head'))
- proj_weight: float32 [2, 1024, 1024], P(None, None, ('tok', 'head'))
- fc1_weight: float32 [2, 1024, 4096], P(None, ('tok', 'head'))
- fc2_weight: float32 [2, 4096, 1024], P(None, None, ('tok', 'head'))
- vec_weight: float32 [2, 15616], P(None, ('tok', 'head'))
- qkv_first: float32 [2, 1024, 3072], P(None, ('tok', 'head'))
- proj_first: float32 [2, 1024, 1024], P(None, None, ('tok', 'head'))
- fc1_first: float32 [2, 1024, 4096], P(None, ('tok', 'head'))
- fc2_first: float32 [2, 4096, 1024], P(None, None, ('tok', 'head'))
- vec_first: float32 [2, 15616], P(None, ('tok', 'head'))
- qkv_second: float32 [2, 1024, 3072], P(None, ('tok', 'head'))
- proj_second: float32 [2, 1024, 1024], P(None, None, ('tok', 'head'))
- fc1_second: float32 [2, 1024, 4096], P(None, ('tok', 'head'))
- fc2_second: float32 [2, 4096, 1024], P(None, None, ('tok', 'head'))
- vec_second: float32 [2, 15616], P(None, ('tok', 'head'))
- qkv_smooth: float32 [2, 1024, 3072], P(None, ('tok', 'head'))
- proj_smooth: float32 [2, 1024, 1024], P(None, None, ('tok', 'head'))
- fc1_smooth: float32 [2, 1024, 4096], P(None, ('tok', 'head'))
- fc2_smooth: float32 [2, 4096, 1024], P(None, None, ('tok', 'head'))
- vec_smooth: float32 [2, 15616], P(None, ('tok', 'head'))
The draws below stay inside these ranges and needn't reach their ends.
Inputs may be any that keep to these rules, and one draw needn't show every extreme that they name: `slot_frame`: frames 0 to 7 are high-resolution frames of 8 blocks each, the others low-resolution frames of 4 blocks; frame f belongs to scene f // 2. The blocks on one index of tok are those of 1 whole high-resolution scenes (on 4 indices) or of 2 whole low-resolution scenes (on the others), in any order. `vectors`: the norms' gains and the layer scales are positive.
All inputs are finite; a program needn't handle non-finite values.
Results may differ from the reference program's by a relative error of at most 0.024.
Values may be sent and summed in bfloat16 or wider, within the bound.
A program may use at most 320 MiB of HBM per device.

```python
import math
import jax
import jax.numpy as jnp
from jax import lax

D = 1024
HEADS = 16
HD = 64
FF = 4096
BLOCK = 128
HI_BLOCKS = 8
LO_BLOCKS = 4
FRAMES = 2
HI_PER = 1
GROUP_BLOCKS = 16
BLOCKS = 128
TOKENS = 16384
LO_PER = 2
HI_FRAMES = 8
HI_TOKENS = 8192
SMALL = 15616
PARAMS = 25197056


def draw_slot_frame(key, part):
    groups = BLOCKS // GROUP_BLOCKS
    hi_groups = groups // 2
    first_key, second_key = jax.random.split(key)
    group_rank = jax.random.permutation(first_key, groups).astype(jnp.int32)
    slot_pos = jnp.arange(GROUP_BLOCKS, dtype=jnp.int32)
    hi_frame = group_rank[:, None] * (HI_PER * FRAMES) + slot_pos[None, :] // HI_BLOCKS
    lo_frame = HI_FRAMES + (group_rank[:, None] - hi_groups) * (LO_PER * FRAMES) + slot_pos[None, :] // LO_BLOCKS
    canonical = jnp.where(group_rank[:, None] < hi_groups, hi_frame, lo_frame)
    scores = jax.random.randint(second_key, (groups, GROUP_BLOCKS), 0, 1 << 20) * GROUP_BLOCKS + slot_pos[None, :]
    shuffle = jnp.argsort(scores, axis=1)
    placed = jnp.take_along_axis(canonical, shuffle, axis=1)
    return placed.reshape(BLOCKS).astype(jnp.int32)


def draw_vectors(key, part):
    shape = (2, SMALL)
    place = jnp.broadcast_to(jnp.arange(SMALL, dtype=jnp.int32)[None, :], shape)
    first_key, second_key = jax.random.split(key)
    rough = jax.random.normal(first_key, shape, jnp.float32)
    ramp_low = 0.6
    ramp_top = 1.2
    even = jax.random.uniform(second_key, shape, jnp.float32)
    width_pos = (place % D).astype(jnp.float32) / D
    gain = (ramp_low + ramp_top * width_pos) * (0.7 + 0.6 * even)
    layer_scale = 0.5 + even
    head_gain = 1.0 + 0.6 * even
    bias = 0.2 * rough
    up_bias = 0.5 * rough

    def inside(start, stop):
        return (place >= start) & (place < stop)
    table = bias
    table = jnp.where(inside(0, D) | inside(7 * D, 8 * D), gain, table)
    table = jnp.where(inside(6 * D, 7 * D) | inside(10 * D + FF, 11 * D + FF), layer_scale, table)
    table = jnp.where(inside(9 * D, 9 * D + FF), up_bias, table)
    base = 11 * D + FF
    table = jnp.where(inside(base, base + HD) | inside(base + 2 * HD, base + 3 * HD), head_gain, table)
    return table.astype(jnp.float32)


def block_levels(rng, shape, shards, low, largest):
    loudness = 1.0
    for position, parts in shards:
        heights = jax.random.uniform(jax.random.fold_in(jax.random.fold_in(rng, 6), position), (parts,), jnp.float32, low / len(shards), largest / len(shards))
        loudness = loudness * jnp.repeat(jnp.exp(heights), shape[position] // parts).reshape((-1,) + (1,) * (len(shape) - 1 - position))
    return loudness


def centred(stream_key, extent, scale, most, shards=(), kind=jnp.bfloat16):
    level = block_levels(stream_key, extent, shards, -0.22, 0.18) if shards else 1.0
    entries = jax.random.normal(stream_key, extent, jnp.float32) * scale * level
    return jnp.minimum(jnp.maximum(entries, -most), most).astype(kind)


def setup_inputs(seed: int = 0) -> dict:
    key_list = jax.random.split(jax.random.key(seed), 25)
    return {
        "tokens": centred(key_list[0], (TOKENS, D), 1.0, 6.0, ((0, 32),)),
        "cotangent": centred(key_list[1], (TOKENS, D), 1.0, 6.0, ((0, 32),)),
        "slot_frame": draw_slot_frame(jax.random.fold_in(key_list[24], 71), 0),
        "step_count": jax.random.randint(key_list[3], (1,), 2, 21).astype(jnp.int32),
        "w_qkv": centred(key_list[4], (2, D, 3 * D), D ** -0.5, 0.1875, ((1, 32),), jnp.float32),
        "w_proj": centred(key_list[5], (2, D, D), (D // 64) ** -0.5, 1.5, ((2, 32),), jnp.float32),
        "w_fc1": centred(key_list[6], (2, D, FF), D ** -0.5, 0.1875, ((1, 32),), jnp.float32),
        "w_fc2": centred(key_list[7], (2, FF, D), FF ** -0.5, 0.09375, ((2, 32),), jnp.float32),
        "vectors": draw_vectors(jax.random.fold_in(key_list[24], 71), 0),
        "first_qkv": centred(key_list[9], (2, D, 3 * D), (0.11 * PARAMS ** -0.5), 0.00012207031, ((1, 32),), jnp.float32),
        "first_proj": centred(key_list[10], (2, D, D), (0.11 * PARAMS ** -0.5), 0.00012207031, ((2, 32),), jnp.float32),
        "first_fc1": centred(key_list[11], (2, D, FF), (0.11 * PARAMS ** -0.5), 0.00012207031, ((1, 32),), jnp.float32),
        "first_fc2": centred(key_list[12], (2, FF, D), (0.11 * PARAMS ** -0.5), 0.00012207031, ((2, 32),), jnp.float32),
        "first_vec": centred(key_list[13], (2, SMALL), (0.33 * PARAMS ** -0.5), 0.0004272461, ((1, 32),), jnp.float32),
        "second_qkv": jnp.clip(jnp.exp(math.log(3.174974172459599e-10) - 2.7725887 * jax.random.uniform(key_list[14], (2, D, 3 * D), jnp.float32) ** block_levels(key_list[14], (2, D, 3 * D), ((1, 32),), -0.2, 0.2)), 1.9843588577872495e-11, 3.174974172459599e-10),
        "second_proj": jnp.clip(jnp.exp(math.log(3.174974172459599e-10) - 2.7725887 * jax.random.uniform(key_list[15], (2, D, D), jnp.float32) ** block_levels(key_list[15], (2, D, D), ((2, 32),), -0.2, 0.2)), 1.9843588577872495e-11, 3.174974172459599e-10),
        "second_fc1": jnp.clip(jnp.exp(math.log(3.174974172459599e-10) - 2.7725887 * jax.random.uniform(key_list[16], (2, D, FF), jnp.float32) ** block_levels(key_list[16], (2, D, FF), ((1, 32),), -0.2, 0.2)), 1.9843588577872495e-11, 3.174974172459599e-10),
        "second_fc2": jnp.clip(jnp.exp(math.log(3.174974172459599e-10) - 2.7725887 * jax.random.uniform(key_list[17], (2, FF, D), jnp.float32) ** block_levels(key_list[17], (2, FF, D), ((2, 32),), -0.2, 0.2)), 1.9843588577872495e-11, 3.174974172459599e-10),
        "second_vec": jnp.clip(jnp.exp(math.log(2.857476699702488e-09) - 2.7725887 * jax.random.uniform(key_list[18], (2, SMALL), jnp.float32) ** block_levels(key_list[18], (2, SMALL), ((1, 32),), -0.2, 0.2)), 1.785922937314055e-10, 2.857476699702488e-09),
        "smooth_qkv": centred(key_list[19], (2, D, 3 * D), D ** -0.5, 0.1875, ((1, 32),), jnp.float32),
        "smooth_proj": centred(key_list[20], (2, D, D), (D // 64) ** -0.5, 1.5, ((2, 32),), jnp.float32),
        "smooth_fc1": centred(key_list[21], (2, D, FF), D ** -0.5, 0.1875, ((1, 32),), jnp.float32),
        "smooth_fc2": centred(key_list[22], (2, FF, D), FF ** -0.5, 0.09375, ((2, 32),), jnp.float32),
        "smooth_vec": jnp.clip(0.2 + 1 * jax.random.uniform(key_list[23], (2, SMALL), jnp.float32) ** block_levels(key_list[23], (2, SMALL), ((1, 32),), -0.2, 0.2), 0.2, 1.2),
    }


@jax.custom_vjp
def low(v):
    return lax.optimization_barrier(v.astype(jnp.bfloat16)).astype(jnp.float32)

@jax.custom_vjp
def low_back(v):
    return v

def low_keep(v):
    return (low(v), None)

def low_pass(kept, grad):
    return (grad,)

def back_keep(v):
    return (v, None)

def back_low(kept, grad):
    return (low(grad),)
low.defvjp(low_keep, low_pass)
low_back.defvjp(back_keep, back_low)
norm_eps = 1e-06
clip_norm = 1.0
beta_one = 0.9
beta_two = 0.999
adam_eps = 1e-08
ema_decay = 0.7
step_rates = (0.05, 0.4, 0.05, 0.025, 0.3)
decays = (0.05, 0.05, 0.05, 0.05, 0.0)
highest = lax.Precision.HIGHEST

def layer_norm(values, gain, shift):
    centered = values - lax.optimization_barrier(jnp.mean(values, axis=-1, keepdims=True))
    spread = lax.optimization_barrier(jnp.mean(centered * centered, axis=-1, keepdims=True))
    return centered * lax.rsqrt(spread + norm_eps) * gain + shift

def head_norm(values, gain, shift):
    return layer_norm(values, gain, shift) * HD ** (-0.5)

def unpack(vector_row):
    lengths = (D, D, 3 * D, D, D, D, D, FF, D, D, HD, HD, HD, HD)
    pieces = []
    offset = 0
    for length in lengths:
        pieces.append(vector_row[offset:offset + length])
        offset = offset + length
    return pieces

def attend_one(triple):
    query_one, key_one, value_one = triple
    scores = low_back(jnp.dot(query_one, key_one.T, precision=highest))
    weights_low = low(jax.nn.softmax(scores, axis=-1))
    return jnp.dot(weights_low, value_one, precision=highest)

def attend(queries, key_rows, values, seg_len):
    seg_count = queries.shape[0] // seg_len

    def arrange(table):
        return table.reshape(seg_count, seg_len, HEADS, HD).transpose(0, 2, 1, 3).reshape(seg_count * HEADS, seg_len, HD)
    result = lax.map(jax.checkpoint(attend_one), (arrange(queries), arrange(key_rows), arrange(values)))
    return result.reshape(seg_count, HEADS, seg_len, HD).transpose(0, 2, 1, 3).reshape(seg_count * seg_len, HEADS * HD)

def mix_heads(queries, key_rows, values, hi_len, lo_len):
    upper = attend(queries[:HI_TOKENS], key_rows[:HI_TOKENS], values[:HI_TOKENS], hi_len)
    lower = attend(queries[HI_TOKENS:], key_rows[HI_TOKENS:], values[HI_TOKENS:], lo_len)
    return jnp.concatenate([upper, lower], axis=0)

def block_forward(hidden, weight_qkv, weight_proj, weight_up, weight_down, vector_row, hi_len, lo_len):
    gain_one, shift_one, qkv_bias, proj_bias, scale_one, gain_two, shift_two, up_bias, down_bias, scale_two, query_gain, query_shift, key_gain, key_shift = unpack(low(vector_row))
    row_count = hidden.shape[0]
    normed = low(layer_norm(hidden, gain_one, shift_one))
    qkv_rows = low_back(jnp.dot(normed, low(weight_qkv), precision=highest) + qkv_bias)
    split_heads = qkv_rows.reshape(row_count, 3, HEADS, HD)
    queries = low(low_back(head_norm(split_heads[:, 0], query_gain, query_shift)))
    key_rows = low(low_back(layer_norm(split_heads[:, 1], key_gain, key_shift)))
    values = low(low_back(split_heads[:, 2]))
    attended = low(low_back(mix_heads(queries, key_rows, values, hi_len, lo_len)))
    branch = low_back(jnp.dot(attended, low(weight_proj), precision=highest) + proj_bias)
    after_attn = hidden + scale_one * branch
    normed_two = low(layer_norm(after_attn, gain_two, shift_two))
    expand = low_back(jnp.dot(normed_two, low(weight_up), precision=highest) + up_bias)
    activated = low(jax.nn.gelu(expand, approximate=False))
    down_out = low_back(jnp.dot(activated, low(weight_down), precision=highest) + down_bias)
    return after_attn + scale_two * down_out

def adam_update(weight, gradient, moment_one, moment_two, average, step_rate, decay_rate, clip_scale, step_float):
    clipped = gradient * clip_scale
    moment_one = beta_one * moment_one + (1.0 - beta_one) * clipped
    moment_two = beta_two * moment_two + (1.0 - beta_two) * clipped * clipped
    first_hat = moment_one / (1.0 - beta_one ** step_float)
    second_hat = moment_two / (1.0 - beta_two ** step_float)
    weight = weight - step_rate * (first_hat / (jnp.sqrt(second_hat) + adam_eps) + decay_rate * weight)
    average = ema_decay * average + (1.0 - ema_decay) * weight
    return (weight, moment_one, moment_two, average)

def reference(tokens, cotangent, slot_frame, step_count, w_qkv, w_proj, w_fc1, w_fc2, vectors, first_qkv, first_proj, first_fc1, first_fc2, first_vec, second_qkv, second_proj, second_fc1, second_fc2, second_vec, smooth_qkv, smooth_proj, smooth_fc1, smooth_fc2, smooth_vec):
    sort_order = jnp.argsort(slot_frame, stable=True).astype(jnp.int32)
    inverse = jnp.argsort(sort_order, stable=True).astype(jnp.int32)

    def arrange(rows, placing):
        return jnp.take(rows.reshape(BLOCKS, BLOCK, D), placing, axis=0).reshape(TOKENS, D)
    start_rows = arrange(tokens.astype(jnp.float32), sort_order)
    back_rows = arrange(cotangent.astype(jnp.float32), sort_order)

    def forward(rows, weight_qkv, weight_proj, weight_up, weight_down, vector_all):
        middle = block_forward(rows, weight_qkv[0], weight_proj[0], weight_up[0], weight_down[0], vector_all[0], HI_BLOCKS * BLOCK, LO_BLOCKS * BLOCK)
        return block_forward(middle, weight_qkv[1], weight_proj[1], weight_up[1], weight_down[1], vector_all[1], FRAMES * HI_BLOCKS * BLOCK, FRAMES * LO_BLOCKS * BLOCK)
    result, pullback = jax.vjp(forward, start_rows, w_qkv, w_proj, w_fc1, w_fc2, vectors)
    grad_rows, grad_qkv, grad_proj, grad_up, grad_down, grad_vec = pullback(back_rows)
    output = arrange(result, inverse)
    grad_tokens = arrange(grad_rows, inverse)
    gradients = (grad_qkv, grad_proj, grad_up, grad_down, grad_vec)
    grad_norm = jnp.sqrt(sum((jnp.sum(gradient * gradient) for gradient in gradients)))
    clip_scale = clip_norm / jnp.maximum(grad_norm, clip_norm)
    step_float = step_count[0].astype(jnp.float32)
    masters = (w_qkv, w_proj, w_fc1, w_fc2, vectors)
    firsts = (first_qkv, first_proj, first_fc1, first_fc2, first_vec)
    seconds = (second_qkv, second_proj, second_fc1, second_fc2, second_vec)
    averages = (smooth_qkv, smooth_proj, smooth_fc1, smooth_fc2, smooth_vec)
    updates = [adam_update(weight, gradient, moment_one, moment_two, average, step_rate, decay_rate, clip_scale, step_float) for weight, gradient, moment_one, moment_two, average, step_rate, decay_rate in zip(masters, gradients, firsts, seconds, averages, step_rates, decays)]
    return (output, grad_tokens, grad_norm, updates[0][0], updates[1][0], updates[2][0], updates[3][0], updates[4][0], updates[0][1], updates[1][1], updates[2][1], updates[3][1], updates[4][1], updates[0][2], updates[1][2], updates[2][2], updates[3][2], updates[4][2], updates[0][3], updates[1][3], updates[2][3], updates[3][3], updates[4][3])
```

```python
import functools
import math

import jax
import jax.numpy as jnp
from jax import lax
from jax.experimental import pallas as pl
from jax.experimental.pallas import tpu as pltpu
from jax.sharding import PartitionSpec as P

D = 1024
HD = 64
FF = 4096
BLOCK = 128
HI_BLOCKS = 8
LO_BLOCKS = 4
FRAMES = 2

norm_eps = 1e-06
clip_norm = 1.0
beta_one = 0.9
beta_two = 0.999
adam_eps = 1e-08
ema_decay = 0.7
step_rates = (0.05, 0.4, 0.05, 0.025, 0.3)
decays = (0.05, 0.05, 0.05, 0.05, 0.0)

LOG2E = math.log2(math.e)
SPAN = 512
MESH_ID = pl.DeviceIdType.MESH
BOTH = ("tok", "head")
bf16 = jnp.bfloat16
f32 = jnp.float32
VMEM_BYTES = 60 << 20


def _peer(step, n_tok, n_head):
    n = n_tok * n_head
    me = lax.axis_index("tok") * n_head + lax.axis_index("head")
    to = lax.rem(me + step, n)
    return me, to, (to // n_head, lax.rem(to, n_head))


def _enter(n_tok, n_head):
    n = n_tok * n_head
    barrier = pltpu.get_barrier_semaphore()

    def greet(step, _):
        _, _, device = _peer(step, n_tok, n_head)
        pl.semaphore_signal(barrier, inc=1, device_id=device, device_id_type=MESH_ID)
        return 0

    lax.fori_loop(1, n, greet, 0)
    pl.semaphore_wait(barrier, n - 1)


def spread_kernel(n_tok, n_head, x_ref, o_ref, send_sem, recv_sem):
    n = n_tok * n_head
    _enter(n_tok, n_head)
    me = lax.axis_index("tok") * n_head + lax.axis_index("head")
    o_ref[me] = x_ref[...]

    def copy(step):
        me, _, device = _peer(step, n_tok, n_head)
        return pltpu.make_async_remote_copy(
            src_ref=x_ref,
            dst_ref=o_ref.at[me],
            send_sem=send_sem.at[step],
            recv_sem=recv_sem.at[step],
            device_id=device,
            device_id_type=MESH_ID,
        )

    def start(step, _):
        copy(step).start()
        return 0

    def finish(step, _):
        copy(step).wait()
        return 0

    lax.fori_loop(1, n, start, 0)
    lax.fori_loop(1, n, finish, 0)


def swap_kernel(n_tok, n_head, x_ref, o_ref, land, send_sem, recv_sem):
    n = n_tok * n_head
    _enter(n_tok, n_head)
    me = lax.axis_index("tok") * n_head + lax.axis_index("head")

    def copy(step):
        me, to, device = _peer(step, n_tok, n_head)
        return pltpu.make_async_remote_copy(
            src_ref=x_ref.at[to],
            dst_ref=land.at[step],
            send_sem=send_sem.at[step],
            recv_sem=recv_sem.at[step],
            device_id=device,
            device_id_type=MESH_ID,
        )

    def start(step, _):
        copy(step).start()
        return 0

    def finish(step, _):
        copy(step).wait()
        return 0

    lax.fori_loop(1, n, start, 0)
    lax.fori_loop(1, n, finish, 0)
    o_ref[...] = x_ref[me] + jnp.sum(land[1:], axis=0)


def spread(tile, n_tok, n_head, collective_id):
    n = n_tok * n_head
    return pl.pallas_call(
        functools.partial(spread_kernel, n_tok, n_head),
        out_shape=jax.ShapeDtypeStruct((n,) + tile.shape, tile.dtype),
        in_specs=[pl.BlockSpec(memory_space=pltpu.VMEM)],
        out_specs=pl.BlockSpec(memory_space=pltpu.VMEM),
        scratch_shapes=[pltpu.SemaphoreType.DMA((n,)), pltpu.SemaphoreType.DMA((n,))],
        compiler_params=pltpu.CompilerParams(collective_id=collective_id, has_side_effects=True),
    )(tile)


def swap(tiles, n_tok, n_head, collective_id):
    n = n_tok * n_head
    return pl.pallas_call(
        functools.partial(swap_kernel, n_tok, n_head),
        out_shape=jax.ShapeDtypeStruct(tiles.shape[1:], tiles.dtype),
        in_specs=[pl.BlockSpec(memory_space=pltpu.VMEM)],
        out_specs=pl.BlockSpec(memory_space=pltpu.VMEM),
        scratch_shapes=[
            pltpu.VMEM(tiles.shape, tiles.dtype),
            pltpu.SemaphoreType.DMA((n,)),
            pltpu.SemaphoreType.DMA((n,)),
        ],
        compiler_params=pltpu.CompilerParams(collective_id=collective_id, has_side_effects=True),
    )(tiles)


def _lane_mean(values, grouping):
    top = values.astype(bf16)
    rest = (values - top.astype(f32)).astype(bf16)
    return jnp.dot(top, grouping, preferred_element_type=f32) + jnp.dot(
        rest, grouping, preferred_element_type=f32
    )


def _grouping(width):
    row = lax.broadcasted_iota(jnp.int32, (width, width), 0) // HD
    col = lax.broadcasted_iota(jnp.int32, (width, width), 1) // HD
    return jnp.where(row == col, 1.0 / HD, 0.0).astype(bf16)


def _unit(values, grouping):
    centered = values - _lane_mean(values, grouping)
    spread_ = _lane_mean(centered * centered, grouping)
    scale = lax.rsqrt(spread_ + norm_eps)
    return centered * scale, scale


def _only(values, head):
    lane = lax.broadcasted_iota(jnp.int32, values.shape, 1)
    return jnp.where(lane // HD == head, values, jnp.zeros_like(values))


NT = (((1,), (1,)), ((), ()))
TN = (((0,), (0,)), ((), ()))


def forward_kernel(
    heads, pieces, spans, tile_rows, order_ref, hi_ref, *refs
):
    x_refs = refs[:pieces]
    w_ref, bias_ref, gains_ref, att_ref, raw_ref, val_ref, lse_ref, q_s, k_s, v_s, acc = refs[pieces:]
    width = heads * HD
    rows = att_ref.shape[0]
    blocks = rows // BLOCK
    piece_rows = rows // pieces
    for at in range(pieces):
        full = jnp.dot(x_refs[at][...], w_ref[...], preferred_element_type=f32) + bias_ref[...]
        here = pl.ds(at * piece_rows, piece_rows)
        raw_ref[here, :] = full[:, : 2 * width]
        val_ref[here, :] = full[:, 2 * width :].astype(bf16)
    grouping = _grouping(width)

    def place(at, _):
        here = pl.ds(pl.multiple_of(order_ref[at] * BLOCK, BLOCK), BLOCK)
        there = pl.ds(pl.multiple_of(at * BLOCK, BLOCK), BLOCK)
        unit_q, _s = _unit(raw_ref[here, :width], grouping)
        unit_k, _s = _unit(raw_ref[here, width:], grouping)
        q_s[there, :] = ((unit_q * gains_ref[0:1, :] + gains_ref[1:2, :]) * HD ** (-0.5)).astype(bf16)
        key = (unit_k * gains_ref[2:3, :] + gains_ref[3:4, :]).astype(bf16)
        value = val_ref[here, :]
        for head in range(heads):
            k_s[head, there, :] = _only(key, head)
            v_s[head, there, :] = _only(value, head)
        return 0

    lax.fori_loop(0, blocks, place, 0)
    per_tile = tile_rows // BLOCK

    def attend(span):
        def tile(at, _):
            here = pl.ds(pl.multiple_of(at * tile_rows, tile_rows), tile_rows)
            first = at * tile_rows // span * span
            there = pl.ds(pl.multiple_of(first, span), span)
            query = q_s[here, :]
            lane = lax.broadcasted_iota(jnp.int32, (tile_rows, 128), 1)
            logs = jnp.zeros((tile_rows, 128), f32)
            for head in range(heads):
                scores = lax.dot_general(query, k_s[head, there, :], NT, preferred_element_type=f32)
                top = jnp.max(scores, axis=1, keepdims=True) * LOG2E
                probs = jnp.exp2(scores * LOG2E - top)
                total = jnp.sum(probs, axis=1, keepdims=True)
                part = jnp.dot(
                    probs.astype(bf16), v_s[head, there, :], preferred_element_type=f32
                ) / total
                if head == 0:
                    acc[...] = part
                else:
                    acc[...] += part
                logs = jnp.where(lane == head, top + jnp.log2(total), logs)
            lse_ref[here, :] = logs
            for sub in range(per_tile):
                out = pl.ds(pl.multiple_of(order_ref[at * per_tile + sub] * BLOCK, BLOCK), BLOCK)
                att_ref[out, :] = acc[sub * BLOCK : (sub + 1) * BLOCK, :].astype(bf16)
            return 0

        lax.fori_loop(0, rows // tile_rows, tile, 0)

    @pl.when(hi_ref[0] == 1)
    def _():
        attend(spans[0])

    @pl.when(hi_ref[0] == 0)
    def _():
        attend(spans[1])


def attention_forward(pieces, weight, bias, gains, order, is_hi, spans):
    heads = weight.shape[1] // (3 * HD)
    width = heads * HD
    rows = sum(piece.shape[0] for piece in pieces)
    tile_rows = 256
    smem = pl.BlockSpec(memory_space=pltpu.SMEM)
    vmem = pl.BlockSpec(memory_space=pltpu.VMEM)
    flops = 2 * rows * (D * 3 * width + 8 * spans[0] * width)
    return pl.pallas_call(
        functools.partial(forward_kernel, heads, len(pieces), spans, tile_rows),
        out_shape=(
            jax.ShapeDtypeStruct((rows, width), bf16),
            jax.ShapeDtypeStruct((rows, 2 * width), f32),
            jax.ShapeDtypeStruct((rows, width), bf16),
            jax.ShapeDtypeStruct((rows, 128), f32),
        ),
        in_specs=[smem, smem] + [vmem] * (len(pieces) + 3),
        out_specs=(vmem,) * 4,
        scratch_shapes=[
            pltpu.VMEM((rows, width), bf16),
            pltpu.VMEM((heads, rows, width), bf16),
            pltpu.VMEM((heads, rows, width), bf16),
            pltpu.VMEM((tile_rows, width), f32),
        ],
        compiler_params=pltpu.CompilerParams(vmem_limit_bytes=VMEM_BYTES),
        cost_estimate=pl.CostEstimate(
            flops=flops, bytes_accessed=rows * (2 * D + 14 * width), transcendentals=rows * spans[0] * heads
        ),
    )(order, is_hi, *pieces, weight, bias, gains)


def backward_kernel(
    heads,
    spans,
    order_ref,
    hi_ref,
    raw_ref,
    val_ref,
    grad_ref,
    att_ref,
    lse_ref,
    gains_ref,
    out_ref,
    sums_ref,
    bias_ref,
    q_s,
    o_s,
    k_m,
    v_m,
    q_m,
    o_m,
    dq_s,
    dk_s,
    dv_s,
    lse_t,
    delta_t,
):
    width = heads * HD
    rows = val_ref.shape[0]
    blocks = rows // BLOCK
    grouping = _grouping(width)
    head_of = lax.broadcasted_iota(jnp.int32, (8, width), 1) // HD
    picks = jnp.where(head_of == lax.broadcasted_iota(jnp.int32, (8, width), 0), 1.0, 0.0).astype(bf16)

    def place(at, _):
        here = pl.ds(pl.multiple_of(order_ref[at] * BLOCK, BLOCK), BLOCK)
        there = pl.ds(pl.multiple_of(at * BLOCK, BLOCK), BLOCK)
        unit_q, _s = _unit(raw_ref[here, :width], grouping)
        unit_k, _s = _unit(raw_ref[here, width:], grouping)
        query = ((unit_q * gains_ref[0:1, :] + gains_ref[1:2, :]) * HD ** (-0.5)).astype(bf16)
        key = (unit_k * gains_ref[2:3, :] + gains_ref[3:4, :]).astype(bf16)
        value = val_ref[here, :]
        grad = grad_ref[here, :]
        q_s[there, :] = query
        o_s[there, :] = grad
        for head in range(heads):
            k_m[head, there, :] = _only(key, head)
            v_m[head, there, :] = _only(value, head)
            q_m[head, there, :] = _only(query, head)
            o_m[head, there, :] = _only(grad, head)
        both = grad.astype(f32) * att_ref[here, :].astype(f32)
        top = both.astype(bf16)
        rest = (both - top.astype(f32)).astype(bf16)
        delta_t[:, there] = lax.dot_general(picks, top, NT, preferred_element_type=f32) + lax.dot_general(
            picks, rest, NT, preferred_element_type=f32
        )
        lse_t[:, there] = jnp.transpose(lse_ref[there, :])[:8, :]
        dq_s[there, :] = jnp.zeros((BLOCK, width), f32)
        dk_s[there, :] = jnp.zeros((BLOCK, width), f32)
        dv_s[there, :] = jnp.zeros((BLOCK, width), f32)
        return 0

    lax.fori_loop(0, blocks, place, 0)
    span = jnp.where(hi_ref[0] == 1, spans[0], spans[1])

    def tile(at, _):
        here = pl.ds(pl.multiple_of(at * SPAN, SPAN), SPAN)
        first = at * SPAN // span * span // SPAN

        def chunk(key_at, _):
            there = pl.ds(pl.multiple_of(key_at * SPAN, SPAN), SPAN)
            for head in range(heads):
                scores = lax.dot_general(k_m[head, there, :], q_s[here, :], NT, preferred_element_type=f32)
                probs = jnp.exp2(scores * LOG2E - lse_t[head : head + 1, here])
                grad_probs = lax.dot_general(
                    v_m[head, there, :], o_s[here, :], NT, preferred_element_type=f32
                )
                grad_scores = (probs * (grad_probs - delta_t[head : head + 1, here])).astype(bf16)
                dv_s[there, :] += jnp.dot(probs.astype(bf16), o_m[head, here, :], preferred_element_type=f32)
                dk_s[there, :] += jnp.dot(grad_scores, q_m[head, here, :], preferred_element_type=f32)
                dq_s[here, :] += lax.dot_general(
                    grad_scores, k_m[head, there, :], TN, preferred_element_type=f32
                )
            return 0

        lax.fori_loop(first, first + span // SPAN, chunk, 0)
        return 0

    lax.fori_loop(0, rows // SPAN, tile, 0)
    sums_ref[...] = jnp.zeros_like(sums_ref)
    bias_ref[...] = jnp.zeros_like(bias_ref)

    def pull(grad, unit, scale, gain):
        grad_unit = grad * gain
        inner = _lane_mean(grad_unit, grouping)
        cross = _lane_mean(grad_unit * unit, grouping)
        return scale * (grad_unit - inner - unit * cross)

    def leave(at, _):
        here = pl.ds(pl.multiple_of(order_ref[at] * BLOCK, BLOCK), BLOCK)
        there = pl.ds(pl.multiple_of(at * BLOCK, BLOCK), BLOCK)
        unit_q, scale_q = _unit(raw_ref[here, :width], grouping)
        unit_k, scale_k = _unit(raw_ref[here, width:], grouping)
        grad_q = dq_s[there, :] * HD ** (-0.5)
        grad_k = dk_s[there, :]
        sums_ref[0:1, :] += jnp.sum(grad_q * unit_q, axis=0, keepdims=True)
        sums_ref[1:2, :] += jnp.sum(grad_q, axis=0, keepdims=True)
        sums_ref[2:3, :] += jnp.sum(grad_k * unit_k, axis=0, keepdims=True)
        sums_ref[3:4, :] += jnp.sum(grad_k, axis=0, keepdims=True)
        low_q = pull(grad_q, unit_q, scale_q, gains_ref[0:1, :]).astype(bf16)
        low_k = pull(grad_k, unit_k, scale_k, gains_ref[2:3, :]).astype(bf16)
        low_v = dv_s[there, :].astype(bf16)
        for part, low in enumerate((low_q, low_k, low_v)):
            lanes = slice(part * width, (part + 1) * width)
            out_ref[here, lanes] = low
            bias_ref[0:1, lanes] += jnp.sum(low.astype(f32), axis=0, keepdims=True)
        return 0

    lax.fori_loop(0, blocks, leave, 0)


def attention_backward(raw, values, grad, attended, lse, gains, order, is_hi, spans):
    rows, width = values.shape
    heads = width // HD
    smem = pl.BlockSpec(memory_space=pltpu.SMEM)
    vmem = pl.BlockSpec(memory_space=pltpu.VMEM)
    flops = 2 * rows * 20 * spans[0] * width
    masked = pltpu.VMEM((heads, rows, width), bf16)
    return pl.pallas_call(
        functools.partial(backward_kernel, heads, spans),
        out_shape=(
            jax.ShapeDtypeStruct((rows, 3 * width), bf16),
            jax.ShapeDtypeStruct((8, width), f32),
            jax.ShapeDtypeStruct((8, 3 * width), f32),
        ),
        in_specs=[smem, smem] + [vmem] * 6,
        out_specs=(vmem,) * 3,
        scratch_shapes=[
            pltpu.VMEM((rows, width), bf16),
            pltpu.VMEM((rows, width), bf16),
            masked,
            masked,
            masked,
            masked,
            pltpu.VMEM((rows, width), f32),
            pltpu.VMEM((rows, width), f32),
            pltpu.VMEM((rows, width), f32),
            pltpu.VMEM((8, rows), f32),
            pltpu.VMEM((8, rows), f32),
        ],
        compiler_params=pltpu.CompilerParams(vmem_limit_bytes=VMEM_BYTES),
        cost_estimate=pl.CostEstimate(
            flops=flops, bytes_accessed=rows * 24 * width, transcendentals=rows * spans[0] * heads
        ),
    )(order, is_hi, raw, values, grad, attended, lse, gains)


class Links:
    def __init__(self, mesh):
        self.n_tok = mesh.shape["tok"]
        self.n_head = mesh.shape["head"]
        self.paired = self.n_tok == 8 and self.n_head == 4

    def head(self, values, step):
        return lax.ppermute(values, "head", [(i, i ^ step) for i in range(self.n_head)])

    def tok(self, values, step):
        return lax.ppermute(values, "tok", [(i, i ^ step) for i in range(self.n_tok)])

    def rows_in(self, rows):
        if not self.paired:
            return [rows] + [self.head(rows, step) for step in range(1, self.n_head)]
        half = rows.shape[0] // 2
        one, two = self.head(rows, 1), self.head(rows, 2)
        far = jnp.concatenate([self.head(one[:half], 2), self.head(two[half:], 1)], axis=0)
        return [rows, one, two, far]

    def rows_out(self, parts):
        if not self.paired:
            moved = [self.head(parts[step], step).astype(f32) for step in range(1, self.n_head)]
            return parts[0].astype(f32) + sum(moved)
        half = parts[0].shape[0] // 2
        upper = [part[:half] for part in parts]
        lower = [part[half:] for part in parts]
        pass_up = (upper[2].astype(f32) + self.head(upper[3], 1).astype(f32)).astype(bf16)
        pass_low = (lower[1].astype(f32) + self.head(lower[3], 2).astype(f32)).astype(bf16)
        up = upper[0].astype(f32) + self.head(upper[1], 1).astype(f32) + self.head(pass_up, 2).astype(f32)
        low = lower[0].astype(f32) + self.head(lower[2], 2).astype(f32) + self.head(pass_low, 1).astype(f32)
        return jnp.concatenate([up, low], axis=0)

    def exchange(self, parts):
        return [parts[0]] + [self.head(parts[step], step) for step in range(1, self.n_head)]

    def by_index(self, pieces, own):
        return [
            lax.select_n((own ^ at).astype(jnp.int32), *pieces) if len(pieces) > 1 else pieces[0]
            for at in range(len(pieces))
        ]

    def gather_full(self, shard):
        return lax.all_gather(shard, BOTH, axis=0, tiled=True)

    def scatter_full(self, grad):
        return lax.psum_scatter(grad, BOTH, scatter_dimension=0, tiled=True).astype(f32)

    def fetch_heads(self, shard, own):
        own_rows = shard.shape[0]
        width = D // self.n_head
        cut = shard.reshape(own_rows, 3, D)
        parts = [
            lax.dynamic_slice_in_dim(cut, (own ^ step) * width, width, 2).reshape(own_rows, 3 * width)
            for step in range(self.n_head)
        ]
        mine = jnp.concatenate(self.by_index(self.exchange(parts), own), axis=0)
        return lax.all_gather(mine, "tok", axis=0, tiled=True)

    def return_heads(self, grad, own):
        width = D // self.n_head
        mine = lax.psum_scatter(grad, "tok", scatter_dimension=0, tiled=True)
        own_rows = mine.shape[0] // self.n_head
        parts = [
            lax.dynamic_slice_in_dim(mine, (own ^ step) * own_rows, own_rows, 0)
            for step in range(self.n_head)
        ]
        back = self.by_index(self.exchange(parts), own)
        back = [part.reshape(own_rows, 3, width) for part in back]
        return jnp.concatenate(back, axis=2).reshape(own_rows, 3 * D).astype(f32)


def layer_norm(values, gain, shift):
    centered = values - jnp.mean(values, axis=-1, keepdims=True)
    spread_ = jnp.mean(centered * centered, axis=-1, keepdims=True)
    return centered * lax.rsqrt(spread_ + norm_eps) * gain + shift


def unpack(vector_row):
    lengths = (D, D, 3 * D, D, D, D, D, FF, D, D, HD, HD, HD, HD)
    pieces = []
    offset = 0
    for length in lengths:
        pieces.append(vector_row[offset : offset + length])
        offset = offset + length
    return pieces


def head_gains(vec, heads):
    rows = [jnp.tile(piece, heads) for piece in vec[10:14]]
    return jnp.concatenate([jnp.stack(rows), jnp.zeros((4, heads * HD), f32)], axis=0)


def gelu_pair(values):
    cdf = 0.5 * (1.0 + lax.erf(values * math.sqrt(0.5)))
    slope = cdf + values * jnp.exp(-0.5 * values * values) * (1.0 / math.sqrt(2.0 * math.pi))
    return values * cdf, slope


def block_forward(hidden, weights, vec, links, own, order, is_hi, spans):
    qkv_cols, proj_t, up, down_t = weights
    width = qkv_cols.shape[1] // 3
    heads = width // HD
    qkv_bias = lax.dynamic_slice_in_dim(vec[2].reshape(3, D), own * width, width, 1).reshape(1, 3 * width)
    gains = head_gains(vec, heads)
    normed = layer_norm(hidden, vec[0], vec[1]).astype(bf16)
    pieces = links.rows_in(normed)
    attended, raw, values, lse = attention_forward(pieces, qkv_cols, qkv_bias, gains, order, is_hi, spans)
    own_rows = hidden.shape[0]
    parts = [attended[step * own_rows : (step + 1) * own_rows] for step in range(links.n_head)]
    attended_own = jnp.concatenate(links.by_index(links.exchange(parts), own), axis=1)
    branch = jnp.einsum("rk,ek->re", attended_own, proj_t, preferred_element_type=f32) + vec[3]
    after = hidden + vec[4] * branch
    normed_two = layer_norm(after, vec[5], vec[6]).astype(bf16)
    expand = jnp.dot(normed_two, up, preferred_element_type=f32) + vec[7]
    activated, slope = gelu_pair(expand)
    activated = activated.astype(bf16)
    slope = slope.astype(bf16)
    down = jnp.einsum("rf,ef->re", activated, down_t, preferred_element_type=f32) + vec[8]
    kept = (hidden, pieces, raw, values, lse, attended, attended_own, branch, after, normed_two, slope, activated, down, gains)
    return after + vec[9] * down, kept


def block_backward(grad_out, kept, weights, vec, links, own, order, is_hi, spans):
    (hidden, pieces, raw, values, lse, attended, attended_own, branch, after, normed_two, slope, activated, down, gains) = kept
    qkv_cols, proj_t, up, down_t = weights
    width = qkv_cols.shape[1] // 3
    own_rows = hidden.shape[0]
    d_down = (vec[9] * grad_out).astype(bf16)
    d_scale_two = jnp.sum(grad_out * down, axis=0)
    d_down_bias = jnp.sum(d_down.astype(f32), axis=0)
    d_act = jnp.einsum("re,ef->rf", d_down, down_t, preferred_element_type=f32)
    d_expand = (slope.astype(f32) * d_act).astype(bf16)
    dw_down = jnp.einsum("re,rf->ef", d_down, activated, preferred_element_type=f32).astype(bf16)
    d_up_bias = jnp.sum(d_expand.astype(f32), axis=0)
    d_normed_two = jnp.einsum("rf,df->rd", d_expand, up, preferred_element_type=f32)
    dw_up = jnp.einsum("rd,rf->df", normed_two, d_expand, preferred_element_type=f32).astype(bf16)
    d_after_norm, d_gain_two, d_shift_two = jax.vjp(layer_norm, after, vec[5], vec[6])[1](d_normed_two)
    d_after = grad_out + d_after_norm
    d_branch = (vec[4] * d_after).astype(bf16)
    d_scale_one = jnp.sum(d_after * branch, axis=0)
    d_proj_bias = jnp.sum(d_branch.astype(f32), axis=0)
    d_attended = jnp.einsum("re,ek->rk", d_branch, proj_t, preferred_element_type=f32).astype(bf16)
    dw_proj = jnp.einsum("re,rk->ek", d_branch, attended_own, preferred_element_type=f32).astype(bf16)
    parts = [
        lax.dynamic_slice_in_dim(d_attended, (own ^ step) * width, width, 1) for step in range(links.n_head)
    ]
    grad_heads = jnp.concatenate(links.exchange(parts), axis=0)
    d_qkv, sums, bias_sums = attention_backward(
        raw, values, grad_heads, attended, lse, gains, order, is_hi, spans
    )
    d_normed = jnp.einsum("rc,dc->rd", d_qkv, qkv_cols, preferred_element_type=f32).astype(bf16)
    back = links.rows_out(
        [d_normed[step * own_rows : (step + 1) * own_rows] for step in range(links.n_head)]
    )
    normed_group = jnp.concatenate(pieces, axis=0)
    dw_qkv = jnp.einsum("rd,rc->dc", normed_group, d_qkv, preferred_element_type=f32).astype(bf16)
    d_hidden_norm, d_gain_one, d_shift_one = jax.vjp(layer_norm, hidden, vec[0], vec[1])[1](back)
    d_qkv_bias = lax.dynamic_update_slice_in_dim(
        jnp.zeros((3, D), f32), bias_sums[0].reshape(3, width), own * width, 1
    ).reshape(3 * D)
    head_sums = jnp.sum(sums[:4].reshape(4, width // HD, HD), axis=1)
    d_vector = jnp.concatenate(
        [
            d_gain_one,
            d_shift_one,
            d_qkv_bias,
            d_proj_bias,
            d_scale_one,
            d_gain_two,
            d_shift_two,
            d_up_bias,
            d_down_bias,
            d_scale_two,
            head_sums.reshape(4 * HD),
        ]
    )
    summed = (
        links.return_heads(dw_qkv, own),
        links.scatter_full(dw_proj),
        links.scatter_full(dw_up),
        links.scatter_full(dw_down),
    )
    return d_after + d_hidden_norm, summed, d_vector


def adam_update(
    weight, gradient, moment_one, moment_two, average, step_rate, decay_rate, clip_scale, fix_one, fix_two
):
    clipped = gradient * clip_scale
    moment_one = beta_one * moment_one + (1.0 - beta_one) * clipped
    moment_two = beta_two * moment_two + (1.0 - beta_two) * clipped * clipped
    first_hat = moment_one / fix_one
    second_hat = moment_two / fix_two
    weight = weight - step_rate * (
        first_hat / (jnp.sqrt(second_hat) + adam_eps) + decay_rate * weight
    )
    average = ema_decay * average + (1.0 - ema_decay) * weight
    return (weight, moment_one, moment_two, average)


def body(
    links,
    tokens,
    cotangent,
    slot_frame,
    step_count,
    *params,
):
    n_tok, n_head = links.n_tok, links.n_head
    devices = n_tok * n_head
    own = lax.axis_index("head")
    flip = lambda leaf: jnp.swapaxes(leaf, 1, 2)
    groups = []
    for at in range(0, 20, 5):
        qkv, proj, fc1, fc2, vec = params[at : at + 5]
        groups.append([qkv, flip(proj), fc1, flip(fc2), vec])
    masters = groups[0]

    slots = slot_frame.shape[0]
    per_head = slots // n_head
    held = slot_frame.reshape(n_head, per_head)
    held = jnp.concatenate(
        [lax.dynamic_slice_in_dim(held, own ^ step, 1, 0)[0] for step in range(n_head)]
    )
    index = jnp.arange(slots, dtype=jnp.int32)
    ahead = (held[None, :] < held[:, None]) | (
        (held[None, :] == held[:, None]) & (index[None, :] < index[:, None])
    )
    rank = jnp.sum(ahead.astype(jnp.int32), axis=1)
    order = jnp.sum(jnp.where(rank[None, :] == index[:, None], index[None, :], 0), axis=1).astype(jnp.int32)
    is_hi = (jnp.sum((held == held[0]).astype(jnp.int32)) == HI_BLOCKS).astype(jnp.int32).reshape(1)
    spans = (
        (HI_BLOCKS * BLOCK, LO_BLOCKS * BLOCK),
        (FRAMES * HI_BLOCKS * BLOCK, FRAMES * LO_BLOCKS * BLOCK),
    )

    vec_here = masters[4].shape[1]
    tile = lax.reduce_precision(masters[4], 8, 7).reshape(-1)
    tile = jnp.pad(tile, (0, 1024 - tile.shape[0])).reshape(8, 128)
    tiles = spread(tile, n_tok, n_head, 0).reshape(devices, 1024)[:, : 2 * vec_here]
    vectors = jnp.swapaxes(tiles.reshape(devices, 2, vec_here), 0, 1).reshape(2, devices * vec_here)
    vecs = [unpack(vectors[block]) for block in range(2)]

    low = [[masters[kind][block].astype(bf16) for kind in range(4)] for block in range(2)]
    weights = []
    for block in range(2):
        weights.append(
            (
                links.fetch_heads(low[block][0], own),
                links.gather_full(low[block][1]),
                links.gather_full(low[block][2]),
                links.gather_full(low[block][3]),
            )
        )
    hidden = tokens.astype(f32)
    kept = []
    for block in range(2):
        hidden, kept_here = block_forward(
            hidden, weights[block], vecs[block], links, own, order, is_hi, spans[block]
        )
        kept.append(kept_here)
    grad_rows = cotangent.astype(f32)
    summed = [None, None]
    d_vectors = [None, None]
    for block in (1, 0):
        grad_rows, summed[block], d_vectors[block] = block_backward(
            grad_rows, kept[block], weights[block], vecs[block], links, own, order, is_hi, spans[block]
        )
    d_tiles = jnp.swapaxes(jnp.stack(d_vectors).reshape(2, devices, vec_here), 0, 1).reshape(devices, -1)
    d_tiles = jnp.pad(d_tiles, ((0, 0), (0, 1024 - d_tiles.shape[1]))).reshape(devices, 8, 128)
    d_vec = swap(d_tiles, n_tok, n_head, 1).reshape(1024)[: 2 * vec_here].reshape(2, vec_here)
    gradients = [jnp.stack([summed[0][kind], summed[1][kind]]) for kind in range(4)] + [d_vec]
    local_square = sum((jnp.sum(gradient * gradient) for gradient in gradients))
    squares = spread(jnp.broadcast_to(local_square, (8, 128)), n_tok, n_head, 2)
    grad_norm = jnp.sqrt(jnp.sum(squares[:, 0, 0]))
    clip_scale = clip_norm / jnp.maximum(grad_norm, clip_norm)
    step_float = step_count[0].astype(f32)
    fix_one = 1.0 - beta_one**step_float
    fix_two = 1.0 - beta_two**step_float
    updates = [
        adam_update(
            groups[0][kind],
            gradients[kind],
            groups[1][kind],
            groups[2][kind],
            groups[3][kind],
            step_rates[kind],
            decays[kind],
            clip_scale,
            fix_one,
            fix_two,
        )
        for kind in range(5)
    ]
    outs = [hidden, grad_rows, grad_norm]
    for part in range(4):
        for kind in range(5):
            leaf = updates[kind][part]
            outs.append(flip(leaf) if kind in (1, 3) else leaf)
    return tuple(outs)


def solution(mesh):
    rows = P(BOTH, None)
    kinds = (
        P(None, BOTH, None),
        P(None, None, BOTH),
        P(None, BOTH, None),
        P(None, None, BOTH),
        P(None, BOTH),
    )
    in_specs = (rows, rows, P("tok"), P()) + kinds * 4
    out_specs = (rows, rows, P()) + kinds * 4
    return jax.shard_map(
        functools.partial(body, Links(mesh)),
        mesh=mesh,
        in_specs=in_specs,
        out_specs=out_specs,
        check_vma=False,
    )
```

```python
import functools
import math

import jax
import jax.numpy as jnp
from jax import lax
from jax.experimental import pallas as pl
from jax.experimental.pallas import tpu as pltpu
from jax.sharding import PartitionSpec as P

D = 1024
HD = 64
FF = 4096
BLOCK = 128
HI_BLOCKS = 8
LO_BLOCKS = 4
FRAMES = 2

norm_eps = 1e-06
clip_norm = 1.0
beta_one = 0.9
beta_two = 0.999
adam_eps = 1e-08
ema_decay = 0.7
step_rates = (0.05, 0.4, 0.05, 0.025, 0.3)
decays = (0.05, 0.05, 0.05, 0.05, 0.0)

LOG2E = math.log2(math.e)
SPAN = 512
MESH_ID = pl.DeviceIdType.MESH
BOTH = ("tok", "head")
bf16 = jnp.bfloat16
f32 = jnp.float32
VMEM_BYTES = 60 << 20


def _peer(step, n_tok, n_head):
    n = n_tok * n_head
    me = lax.axis_index("tok") * n_head + lax.axis_index("head")
    to = lax.rem(me + step, n)
    return me, to, (to // n_head, lax.rem(to, n_head))


def _enter(n_tok, n_head):
    n = n_tok * n_head
    barrier = pltpu.get_barrier_semaphore()

    def greet(step, _):
        _, _, device = _peer(step, n_tok, n_head)
        pl.semaphore_signal(barrier, inc=1, device_id=device, device_id_type=MESH_ID)
        return 0

    lax.fori_loop(1, n, greet, 0)
    pl.semaphore_wait(barrier, n - 1)


def spread_kernel(n_tok, n_head, x_ref, o_ref, send_sem, recv_sem):
    n = n_tok * n_head
    _enter(n_tok, n_head)
    me = lax.axis_index("tok") * n_head + lax.axis_index("head")
    o_ref[me] = x_ref[...]

    def copy(step):
        me, _, device = _peer(step, n_tok, n_head)
        return pltpu.make_async_remote_copy(
            src_ref=x_ref,
            dst_ref=o_ref.at[me],
            send_sem=send_sem.at[step],
            recv_sem=recv_sem.at[step],
            device_id=device,
            device_id_type=MESH_ID,
        )

    def start(step, _):
        copy(step).start()
        return 0

    def finish(step, _):
        copy(step).wait()
        return 0

    lax.fori_loop(1, n, start, 0)
    lax.fori_loop(1, n, finish, 0)


def swap_kernel(n_tok, n_head, x_ref, o_ref, land, send_sem, recv_sem):
    n = n_tok * n_head
    _enter(n_tok, n_head)
    me = lax.axis_index("tok") * n_head + lax.axis_index("head")

    def copy(step):
        me, to, device = _peer(step, n_tok, n_head)
        return pltpu.make_async_remote_copy(
            src_ref=x_ref.at[to],
            dst_ref=land.at[step],
            send_sem=send_sem.at[step],
            recv_sem=recv_sem.at[step],
            device_id=device,
            device_id_type=MESH_ID,
        )

    def start(step, _):
        copy(step).start()
        return 0

    def finish(step, _):
        copy(step).wait()
        return 0

    lax.fori_loop(1, n, start, 0)
    lax.fori_loop(1, n, finish, 0)
    o_ref[...] = x_ref[me] + jnp.sum(land[1:], axis=0)


def spread(tile, n_tok, n_head, collective_id):
    n = n_tok * n_head
    return pl.pallas_call(
        functools.partial(spread_kernel, n_tok, n_head),
        out_shape=jax.ShapeDtypeStruct((n,) + tile.shape, tile.dtype),
        in_specs=[pl.BlockSpec(memory_space=pltpu.VMEM)],
        out_specs=pl.BlockSpec(memory_space=pltpu.VMEM),
        scratch_shapes=[pltpu.SemaphoreType.DMA((n,)), pltpu.SemaphoreType.DMA((n,))],
        compiler_params=pltpu.CompilerParams(collective_id=collective_id, has_side_effects=True),
    )(tile)


def swap(tiles, n_tok, n_head, collective_id):
    n = n_tok * n_head
    return pl.pallas_call(
        functools.partial(swap_kernel, n_tok, n_head),
        out_shape=jax.ShapeDtypeStruct(tiles.shape[1:], tiles.dtype),
        in_specs=[pl.BlockSpec(memory_space=pltpu.VMEM)],
        out_specs=pl.BlockSpec(memory_space=pltpu.VMEM),
        scratch_shapes=[
            pltpu.VMEM(tiles.shape, tiles.dtype),
            pltpu.SemaphoreType.DMA((n,)),
            pltpu.SemaphoreType.DMA((n,)),
        ],
        compiler_params=pltpu.CompilerParams(collective_id=collective_id, has_side_effects=True),
    )(tiles)


def _lane_mean(values, grouping):
    top = values.astype(bf16)
    rest = (values - top.astype(f32)).astype(bf16)
    return jnp.dot(top, grouping, preferred_element_type=f32) + jnp.dot(
        rest, grouping, preferred_element_type=f32
    )


def _grouping(width):
    row = lax.broadcasted_iota(jnp.int32, (width, width), 0) // HD
    col = lax.broadcasted_iota(jnp.int32, (width, width), 1) // HD
    return jnp.where(row == col, 1.0 / HD, 0.0).astype(bf16)


def _unit(values, grouping):
    centered = values - _lane_mean(values, grouping)
    spread_ = _lane_mean(centered * centered, grouping)
    scale = lax.rsqrt(spread_ + norm_eps)
    return centered * scale, scale


def _only(values, head):
    lane = lax.broadcasted_iota(jnp.int32, values.shape, 1)
    return jnp.where(lane // HD == head, values, jnp.zeros_like(values))


NT = (((1,), (1,)), ((), ()))
TN = (((0,), (0,)), ((), ()))


def forward_kernel(
    heads, pieces, spans, tile_rows, order_ref, hi_ref, *refs
):
    x_refs = refs[:pieces]
    w_ref, bias_ref, gains_ref, att_ref, raw_ref, val_ref, lse_ref, q_s, k_s, v_s, acc = refs[pieces:]
    width = heads * HD
    rows = att_ref.shape[0]
    blocks = rows // BLOCK
    piece_rows = rows // pieces
    for at in range(pieces):
        full = jnp.dot(x_refs[at][...], w_ref[...], preferred_element_type=f32) + bias_ref[...]
        here = pl.ds(at * piece_rows, piece_rows)
        raw_ref[here, :] = full[:, : 2 * width]
        val_ref[here, :] = full[:, 2 * width :].astype(bf16)
    grouping = _grouping(width)

    def place(at, _):
        here = pl.ds(pl.multiple_of(order_ref[at] * BLOCK, BLOCK), BLOCK)
        there = pl.ds(pl.multiple_of(at * BLOCK, BLOCK), BLOCK)
        unit_q, _s = _unit(raw_ref[here, :width], grouping)
        unit_k, _s = _unit(raw_ref[here, width:], grouping)
        q_s[there, :] = ((unit_q * gains_ref[0:1, :] + gains_ref[1:2, :]) * HD ** (-0.5)).astype(bf16)
        key = (unit_k * gains_ref[2:3, :] + gains_ref[3:4, :]).astype(bf16)
        value = val_ref[here, :]
        for head in range(heads):
            k_s[head, there, :] = _only(key, head)
            v_s[head, there, :] = _only(value, head)
        return 0

    lax.fori_loop(0, blocks, place, 0)
    per_tile = tile_rows // BLOCK

    def attend(span):
        def tile(at, _):
            here = pl.ds(pl.multiple_of(at * tile_rows, tile_rows), tile_rows)
            first = at * tile_rows // span * span
            there = pl.ds(pl.multiple_of(first, span), span)
            query = q_s[here, :]
            lane = lax.broadcasted_iota(jnp.int32, (tile_rows, 128), 1)
            logs = jnp.zeros((tile_rows, 128), f32)
            for head in range(heads):
                scores = lax.dot_general(query, k_s[head, there, :], NT, preferred_element_type=f32)
                top = jnp.max(scores, axis=1, keepdims=True) * LOG2E
                probs = jnp.exp2(scores * LOG2E - top)
                total = jnp.sum(probs, axis=1, keepdims=True)
                part = jnp.dot(
                    probs.astype(bf16), v_s[head, there, :], preferred_element_type=f32
                ) / total
                if head == 0:
                    acc[...] = part
                else:
                    acc[...] += part
                logs = jnp.where(lane == head, top + jnp.log2(total), logs)
            lse_ref[here, :] = logs
            for sub in range(per_tile):
                out = pl.ds(pl.multiple_of(order_ref[at * per_tile + sub] * BLOCK, BLOCK), BLOCK)
                att_ref[out, :] = acc[sub * BLOCK : (sub + 1) * BLOCK, :].astype(bf16)
            return 0

        lax.fori_loop(0, rows // tile_rows, tile, 0)

    @pl.when(hi_ref[0] == 1)
    def _():
        attend(spans[0])

    @pl.when(hi_ref[0] == 0)
    def _():
        attend(spans[1])


def attention_forward(pieces, weight, bias, gains, order, is_hi, spans):
    heads = weight.shape[1] // (3 * HD)
    width = heads * HD
    rows = sum(piece.shape[0] for piece in pieces)
    tile_rows = 256
    smem = pl.BlockSpec(memory_space=pltpu.SMEM)
    vmem = pl.BlockSpec(memory_space=pltpu.VMEM)
    flops = 2 * rows * (D * 3 * width + 8 * spans[0] * width)
    return pl.pallas_call(
        functools.partial(forward_kernel, heads, len(pieces), spans, tile_rows),
        out_shape=(
            jax.ShapeDtypeStruct((rows, width), bf16),
            jax.ShapeDtypeStruct((rows, 2 * width), f32),
            jax.ShapeDtypeStruct((rows, width), bf16),
            jax.ShapeDtypeStruct((rows, 128), f32),
        ),
        in_specs=[smem, smem] + [vmem] * (len(pieces) + 3),
        out_specs=(vmem,) * 4,
        scratch_shapes=[
            pltpu.VMEM((rows, width), bf16),
            pltpu.VMEM((heads, rows, width), bf16),
            pltpu.VMEM((heads, rows, width), bf16),
            pltpu.VMEM((tile_rows, width), f32),
        ],
        compiler_params=pltpu.CompilerParams(vmem_limit_bytes=VMEM_BYTES),
        cost_estimate=pl.CostEstimate(
            flops=flops, bytes_accessed=rows * (2 * D + 14 * width), transcendentals=rows * spans[0] * heads
        ),
    )(order, is_hi, *pieces, weight, bias, gains)


def backward_kernel(
    heads,
    spans,
    order_ref,
    hi_ref,
    raw_ref,
    val_ref,
    grad_ref,
    att_ref,
    lse_ref,
    gains_ref,
    out_ref,
    sums_ref,
    bias_ref,
    q_s,
    o_s,
    k_m,
    v_m,
    q_m,
    o_m,
    dq_s,
    dk_s,
    dv_s,
    lse_t,
    delta_t,
):
    width = heads * HD
    rows = val_ref.shape[0]
    blocks = rows // BLOCK
    grouping = _grouping(width)
    head_of = lax.broadcasted_iota(jnp.int32, (8, width), 1) // HD
    picks = jnp.where(head_of == lax.broadcasted_iota(jnp.int32, (8, width), 0), 1.0, 0.0).astype(bf16)

    def place(at, _):
        here = pl.ds(pl.multiple_of(order_ref[at] * BLOCK, BLOCK), BLOCK)
        there = pl.ds(pl.multiple_of(at * BLOCK, BLOCK), BLOCK)
        unit_q, _s = _unit(raw_ref[here, :width], grouping)
        unit_k, _s = _unit(raw_ref[here, width:], grouping)
        query = ((unit_q * gains_ref[0:1, :] + gains_ref[1:2, :]) * HD ** (-0.5)).astype(bf16)
        key = (unit_k * gains_ref[2:3, :] + gains_ref[3:4, :]).astype(bf16)
        value = val_ref[here, :]
        grad = grad_ref[here, :]
        q_s[there, :] = query
        o_s[there, :] = grad
        for head in range(heads):
            k_m[head, there, :] = _only(key, head)
            v_m[head, there, :] = _only(value, head)
            q_m[head, there, :] = _only(query, head)
            o_m[head, there, :] = _only(grad, head)
        both = grad.astype(f32) * att_ref[here, :].astype(f32)
        top = both.astype(bf16)
        rest = (both - top.astype(f32)).astype(bf16)
        delta_t[:, there] = lax.dot_general(picks, top, NT, preferred_element_type=f32) + lax.dot_general(
            picks, rest, NT, preferred_element_type=f32
        )
        lse_t[:, there] = jnp.transpose(lse_ref[there, :])[:8, :]
        dq_s[there, :] = jnp.zeros((BLOCK, width), f32)
        dk_s[there, :] = jnp.zeros((BLOCK, width), f32)
        dv_s[there, :] = jnp.zeros((BLOCK, width), f32)
        return 0

    lax.fori_loop(0, blocks, place, 0)
    span = jnp.where(hi_ref[0] == 1, spans[0], spans[1])

    def tile(at, _):
        here = pl.ds(pl.multiple_of(at * SPAN, SPAN), SPAN)
        first = at * SPAN // span * span // SPAN

        def chunk(key_at, _):
            there = pl.ds(pl.multiple_of(key_at * SPAN, SPAN), SPAN)
            for head in range(heads):
                scores = lax.dot_general(k_m[head, there, :], q_s[here, :], NT, preferred_element_type=f32)
                probs = jnp.exp2(scores * LOG2E - lse_t[head : head + 1, here])
                grad_probs = lax.dot_general(
                    v_m[head, there, :], o_s[here, :], NT, preferred_element_type=f32
                )
                grad_scores = (probs * (grad_probs - delta_t[head : head + 1, here])).astype(bf16)
                dv_s[there, :] += jnp.dot(probs.astype(bf16), o_m[head, here, :], preferred_element_type=f32)
                dk_s[there, :] += jnp.dot(grad_scores, q_m[head, here, :], preferred_element_type=f32)
                dq_s[here, :] += lax.dot_general(
                    grad_scores, k_m[head, there, :], TN, preferred_element_type=f32
                )
            return 0

        lax.fori_loop(first, first + span // SPAN, chunk, 0)
        return 0

    lax.fori_loop(0, rows // SPAN, tile, 0)
    sums_ref[...] = jnp.zeros_like(sums_ref)
    bias_ref[...] = jnp.zeros_like(bias_ref)

    def pull(grad, unit, scale, gain):
        grad_unit = grad * gain
        inner = _lane_mean(grad_unit, grouping)
        cross = _lane_mean(grad_unit * unit, grouping)
        return scale * (grad_unit - inner - unit * cross)

    def leave(at, _):
        here = pl.ds(pl.multiple_of(order_ref[at] * BLOCK, BLOCK), BLOCK)
        there = pl.ds(pl.multiple_of(at * BLOCK, BLOCK), BLOCK)
        unit_q, scale_q = _unit(raw_ref[here, :width], grouping)
        unit_k, scale_k = _unit(raw_ref[here, width:], grouping)
        grad_q = dq_s[there, :] * HD ** (-0.5)
        grad_k = dk_s[there, :]
        sums_ref[0:1, :] += jnp.sum(grad_q * unit_q, axis=0, keepdims=True)
        sums_ref[1:2, :] += jnp.sum(grad_q, axis=0, keepdims=True)
        sums_ref[2:3, :] += jnp.sum(grad_k * unit_k, axis=0, keepdims=True)
        sums_ref[3:4, :] += jnp.sum(grad_k, axis=0, keepdims=True)
        low_q = pull(grad_q, unit_q, scale_q, gains_ref[0:1, :]).astype(bf16)
        low_k = pull(grad_k, unit_k, scale_k, gains_ref[2:3, :]).astype(bf16)
        low_v = dv_s[there, :].astype(bf16)
        for part, low in enumerate((low_q, low_k, low_v)):
            lanes = slice(part * width, (part + 1) * width)
            out_ref[here, lanes] = low
            bias_ref[0:1, lanes] += jnp.sum(low.astype(f32), axis=0, keepdims=True)
        return 0

    lax.fori_loop(0, blocks, leave, 0)


def attention_backward(raw, values, grad, attended, lse, gains, order, is_hi, spans):
    rows, width = values.shape
    heads = width // HD
    smem = pl.BlockSpec(memory_space=pltpu.SMEM)
    vmem = pl.BlockSpec(memory_space=pltpu.VMEM)
    flops = 2 * rows * 20 * spans[0] * width
    masked = pltpu.VMEM((heads, rows, width), bf16)
    return pl.pallas_call(
        functools.partial(backward_kernel, heads, spans),
        out_shape=(
            jax.ShapeDtypeStruct((rows, 3 * width), bf16),
            jax.ShapeDtypeStruct((8, width), f32),
            jax.ShapeDtypeStruct((8, 3 * width), f32),
        ),
        in_specs=[smem, smem] + [vmem] * 6,
        out_specs=(vmem,) * 3,
        scratch_shapes=[
            pltpu.VMEM((rows, width), bf16),
            pltpu.VMEM((rows, width), bf16),
            masked,
            masked,
            masked,
            masked,
            pltpu.VMEM((rows, width), f32),
            pltpu.VMEM((rows, width), f32),
            pltpu.VMEM((rows, width), f32),
            pltpu.VMEM((8, rows), f32),
            pltpu.VMEM((8, rows), f32),
        ],
        compiler_params=pltpu.CompilerParams(vmem_limit_bytes=VMEM_BYTES),
        cost_estimate=pl.CostEstimate(
            flops=flops, bytes_accessed=rows * 24 * width, transcendentals=rows * spans[0] * heads
        ),
    )(order, is_hi, raw, values, grad, attended, lse, gains)


class Links:
    def __init__(self, mesh):
        self.n_tok = mesh.shape["tok"]
        self.n_head = mesh.shape["head"]
        self.paired = self.n_tok == 8 and self.n_head == 4

    def head(self, values, step):
        return lax.ppermute(values, "head", [(i, i ^ step) for i in range(self.n_head)])

    def tok(self, values, step):
        return lax.ppermute(values, "tok", [(i, i ^ step) for i in range(self.n_tok)])

    def rows_in(self, rows):
        if not self.paired:
            return [rows] + [self.head(rows, step) for step in range(1, self.n_head)]
        half = rows.shape[0] // 2
        one, two = self.head(rows, 1), self.head(rows, 2)
        far = jnp.concatenate([self.head(one[:half], 2), self.head(two[half:], 1)], axis=0)
        return [rows, one, two, far]

    def rows_out(self, parts):
        if not self.paired:
            moved = [self.head(parts[step], step).astype(f32) for step in range(1, self.n_head)]
            return parts[0].astype(f32) + sum(moved)
        half = parts[0].shape[0] // 2
        upper = [part[:half] for part in parts]
        lower = [part[half:] for part in parts]
        pass_up = (upper[2].astype(f32) + self.head(upper[3], 1).astype(f32)).astype(bf16)
        pass_low = (lower[1].astype(f32) + self.head(lower[3], 2).astype(f32)).astype(bf16)
        up = upper[0].astype(f32) + self.head(upper[1], 1).astype(f32) + self.head(pass_up, 2).astype(f32)
        low = lower[0].astype(f32) + self.head(lower[2], 2).astype(f32) + self.head(pass_low, 1).astype(f32)
        return jnp.concatenate([up, low], axis=0)

    def exchange(self, parts):
        return [parts[0]] + [self.head(parts[step], step) for step in range(1, self.n_head)]

    def by_index(self, pieces, own):
        return [
            lax.select_n((own ^ at).astype(jnp.int32), *pieces) if len(pieces) > 1 else pieces[0]
            for at in range(len(pieces))
        ]

    def zed(self):
        return lax.axis_index("tok") // 2

    def core(self):
        return lax.rem(lax.axis_index("tok"), 2)

    def planes(self, shard):
        pieces = [shard] + [self.tok(shard, 2 * step) for step in range(1, 4)]
        return jnp.stack(self.by_index(pieces, self.zed()))

    def gather_places(self):
        if not self.paired:
            return [None]
        spots = ((0, 4, 0), (0, 4, 1), (0, 4, 2), (0, 2, 3), (2, 2, 3))
        return [(first, count, core, to) for first, count, to in spots for core in range(2)]

    def gather_planes(self, shard):
        if not self.paired:
            whole = lax.all_gather(shard, BOTH, axis=0, tiled=True)
            return [whole.reshape(4, 2, 4, whole.shape[0] // 32, whole.shape[1])]
        return [self.planes(shard)]

    def gather_sides(self, own):
        if not self.paired:
            return own
        return [own[0], self.head(own[0], 1), self.head(own[0], 2)]

    def gather_far(self, near):
        if not self.paired:
            return near
        far = [self.head(near[1][:2], 2), self.head(near[2][2:], 1)]
        pieces = []
        for piece in near + far:
            pieces += [piece, self.tok(piece, 1)]
        return pieces

    def grad_places(self):
        if not self.paired:
            return [None]
        return [(0, 4, step, to) for step in range(2) for to in range(4)]

    def scatter_start(self, pieces):
        if not self.paired:
            return pieces
        return [
            (pieces[to].astype(f32) + self.tok(pieces[4 + to], 1).astype(f32)).astype(bf16)
            for to in range(4)
        ]

    def scatter_first(self, sums):
        if not self.paired:
            return sums
        low = [part[:2] for part in sums]
        top = [part[2:] for part in sums]
        pass_low = (low[2].astype(f32) + self.head(low[3], 1).astype(f32)).astype(bf16)
        pass_top = (top[1].astype(f32) + self.head(top[3], 2).astype(f32)).astype(bf16)
        own_low = low[0].astype(f32) + self.head(low[1], 1).astype(f32)
        own_top = top[0].astype(f32) + self.head(top[2], 2).astype(f32)
        return [own_low.astype(bf16), own_top.astype(bf16), pass_low, pass_top]

    def scatter_second(self, halves):
        if not self.paired:
            return halves
        own_low, own_top, pass_low, pass_top = halves
        low = own_low.astype(f32) + self.head(pass_low, 2).astype(f32)
        top = own_top.astype(f32) + self.head(pass_top, 1).astype(f32)
        return [jnp.concatenate([low, top], axis=0).astype(bf16)]

    def scatter_last(self, planes):
        if not self.paired:
            whole = planes[0].reshape(-1, planes[0].shape[-1])
            return lax.psum_scatter(whole, BOTH, scatter_dimension=0, tiled=True).astype(f32)
        return self.sum_planes(planes[0])

    def sum_planes(self, parts):
        zed = self.zed()
        pick = lambda step: lax.dynamic_slice_in_dim(parts, zed ^ step, 1, 0)[0]
        total = pick(0).astype(f32)
        for step in range(1, 4):
            total = total + self.tok(pick(step).astype(bf16), 2 * step).astype(f32)
        return total

    def fetch_heads(self, shard, own):
        own_rows = shard.shape[0]
        width = D // self.n_head
        cut = shard.reshape(own_rows, 3, D)
        parts = [
            lax.dynamic_slice_in_dim(cut, (own ^ step) * width, width, 2).reshape(own_rows, 3 * width)
            for step in range(self.n_head)
        ]
        mine = jnp.concatenate(self.by_index(self.exchange(parts), own), axis=0)
        if not self.paired:
            return lax.all_gather(mine, "tok", axis=0, tiled=True)
        planes = [mine] + [self.tok(mine, 2 * step) for step in range(1, 4)]
        planes = jnp.stack(self.by_index(planes, self.zed()))
        cores = self.by_index([planes, self.tok(planes, 1)], self.core())
        return jnp.stack(cores, axis=1).reshape(8 * mine.shape[0], mine.shape[1])

    def return_cores(self, grad):
        if not self.paired:
            return grad
        view = grad.reshape((4, 2, grad.shape[0] // 8, grad.shape[1]))
        core = self.core()
        cut = lambda at: lax.dynamic_slice_in_dim(view, at, 1, 1)[:, 0]
        return (cut(core).astype(f32) + self.tok(cut(core ^ 1), 1).astype(f32)).astype(bf16)

    def return_planes(self, grad):
        if not self.paired:
            return lax.psum_scatter(grad, "tok", scatter_dimension=0, tiled=True)
        return self.sum_planes(grad).astype(bf16)

    def return_heads(self, mine, own):
        width = D // self.n_head
        own_rows = mine.shape[0] // self.n_head
        parts = [
            lax.dynamic_slice_in_dim(mine, (own ^ step) * own_rows, own_rows, 0)
            for step in range(self.n_head)
        ]
        back = self.by_index(self.exchange(parts), own)
        back = [part.reshape(own_rows, 3, width) for part in back]
        return jnp.concatenate(back, axis=2).reshape(own_rows, 3 * D).astype(f32)


def together(*values):
    return lax.optimization_barrier(values)


CHUNK = 512


def _slot(ref, place, core, head):
    if place is None:
        return ref
    first, count, core_step, head_step = place
    side = 1 - core if core_step else core
    low, high = lax.rem(head, 2), head // 2
    low = 1 - low if head_step % 2 else low
    high = 1 - high if head_step // 2 else high
    return ref.at[pl.ds(first, count), side, high * 2 + low]


PROJ_AT, UP_AT, DOWN_AT, WIDE = 0, D, D + FF, D + 2 * FF


def _cols(ref, at, size):
    window = pl.ds(pl.multiple_of(at, 128), size)
    return ref.at[(slice(None),) * (len(ref.shape) - 1) + (window,)]


def _copies(pieces, places, whole, at, size, sems, inward):
    core = lax.rem(lax.axis_index("tok"), 2)
    head = lax.axis_index("head")
    moves = []
    for index, (piece, place) in enumerate(zip(pieces, places)):
        outside = _cols(piece, at, size)
        inside = _slot(whole, place, core, head)
        pair = (outside, inside) if inward else (inside, outside)
        moves.append(pltpu.make_async_copy(pair[0], pair[1], sems.at[index]))
    return moves


def _start(moves):
    for move in moves:
        move.start()


def _wait(moves):
    for move in moves:
        move.wait()


def _flat(values):
    return values.reshape(D, values.shape[-1])


def _norm(values):
    centered = values - jnp.mean(values, axis=-1, keepdims=True)
    scale = lax.rsqrt(jnp.mean(centered * centered, axis=-1, keepdims=True) + norm_eps)
    return centered * scale, scale


def _own_column(step, n_head):
    own = lax.axis_index("head")
    at = 0
    for bit in range(n_head.bit_length() - 1):
        one = lax.rem(own // (1 << bit), 2)
        one = 1 - one if (step >> bit) % 2 else one
        at = at + one * (1 << bit)
    return pl.multiple_of(at * (D // n_head), 128)


def post_forward_kernel(n_head, places, last, *refs):
    count = len(places)
    att_refs, refs = refs[:n_head], refs[n_head:]
    hidden_ref, rows_ref, up_bias_ref, refs = refs[0], refs[1], refs[2], refs[3:]
    weight_refs, refs = refs[:count], refs[count:]
    next_ref, normed_ref, down_ref, act_ref, slope_ref, branch_hbm, after_hbm, two_hbm, refs = *refs[:8], refs[8:]
    proj_s, up_s, down_s, att_s, branch_s, after_s, two_s, acc, proj_sem, up_sem, down_sem, out_sem = refs
    at = pl.program_id(0)
    chunks = pl.num_programs(0)

    def fetch(chunk, slot):
        up_at, down_at = UP_AT + chunk * CHUNK, DOWN_AT + chunk * CHUNK
        return _copies(weight_refs, places, up_s.at[slot], up_at, CHUNK, up_sem.at[slot], True) + _copies(
            weight_refs, places, down_s.at[slot], down_at, CHUNK, down_sem.at[slot], True
        )

    leaving = [
        pltpu.make_async_copy(branch_s, branch_hbm, out_sem.at[0]),
        pltpu.make_async_copy(after_s, after_hbm, out_sem.at[1]),
        pltpu.make_async_copy(two_s, two_hbm, out_sem.at[2]),
    ]

    @pl.when(at == 0)
    def _():
        proj = _copies(weight_refs, places, proj_s, PROJ_AT, D, proj_sem, True)
        _start(proj)
        _start(fetch(0, 0))
        width = D // n_head
        for step in range(n_head):
            att_s[:, pl.ds(_own_column(step, n_head), width)] = att_refs[step][...]
        _wait(proj)
        branch = (
            lax.dot_general(att_s[...], _flat(proj_s[...]), NT, preferred_element_type=f32) + rows_ref[0:1, :]
        )
        branch_s[...] = branch
        after = hidden_ref[...] + rows_ref[1:2, :] * branch
        after_s[...] = after
        unit, _s = _norm(after)
        two_s[...] = (unit * rows_ref[2:3, :] + rows_ref[3:4, :]).astype(bf16)
        _start(leaving)

    @pl.when(at + 1 < chunks)
    def _():
        _start(fetch(at + 1, lax.rem(at + 1, 2)))

    slot = lax.rem(at, 2)
    _wait(fetch(at, slot))
    expand = jnp.dot(two_s[...], _flat(up_s[slot]), preferred_element_type=f32) + up_bias_ref[...]
    cdf = 0.5 * (1.0 + lax.erf(expand * math.sqrt(0.5)))
    slope = cdf + expand * jnp.exp(-0.5 * expand * expand) * (1.0 / math.sqrt(2.0 * math.pi))
    act = (expand * cdf).astype(bf16)
    act_ref[...] = act
    slope_ref[...] = slope.astype(bf16)
    part = lax.dot_general(act, _flat(down_s[slot]), NT, preferred_element_type=f32)

    @pl.when(at == 0)
    def _():
        acc[...] = part

    @pl.when(at > 0)
    def _():
        acc[...] += part

    @pl.when(at == chunks - 1)
    def _():
        down = acc[...] + rows_ref[4:5, :]
        down_ref[...] = down
        hidden = after_s[...] + rows_ref[5:6, :] * down
        next_ref[...] = hidden
        if last:
            normed_ref[...] = jnp.zeros_like(normed_ref)
        else:
            unit, _s = _norm(hidden)
            normed_ref[...] = (unit * rows_ref[6:7, :] + rows_ref[7:8, :]).astype(bf16)
        _wait(leaving)


def post_forward(att_parts, hidden, rows, up_bias, gathered, n_head, last):
    own_rows = hidden.shape[0]
    pieces, places = gathered
    count = len(places)
    unit_rows = D // 32
    vmem = pl.BlockSpec(memory_space=pltpu.VMEM)
    hbm = pl.BlockSpec(memory_space=pl.ANY)
    column = pl.BlockSpec((own_rows, CHUNK), lambda at: (0, at))
    fixed = lambda leaf_rows: pl.BlockSpec((leaf_rows, D), lambda at: (0, 0))
    whole = lambda dtype: jax.ShapeDtypeStruct((own_rows, D), dtype)
    wide = jax.ShapeDtypeStruct((own_rows, FF), bf16)
    weight = lambda *lead: pltpu.VMEM(lead + (4, 2, 4, unit_rows), bf16)
    normed_rows = 16 if last else own_rows
    return pl.pallas_call(
        functools.partial(post_forward_kernel, n_head, places, last),
        grid=(FF // CHUNK,),
        out_shape=(
            whole(f32),
            jax.ShapeDtypeStruct((normed_rows, D), bf16),
            whole(f32),
            wide,
            wide,
            whole(f32),
            whole(f32),
            whole(bf16),
        ),
        in_specs=[vmem] * n_head
        + [vmem, vmem, pl.BlockSpec((1, CHUNK), lambda at: (0, at))]
        + [hbm] * count,
        out_specs=(fixed(own_rows), fixed(normed_rows), fixed(own_rows), column, column, hbm, hbm, hbm),
        scratch_shapes=[
            pltpu.VMEM((4, 2, 4, unit_rows, D), bf16),
            pltpu.VMEM((2, 4, 2, 4, unit_rows, CHUNK), bf16),
            pltpu.VMEM((2, 4, 2, 4, unit_rows, CHUNK), bf16),
            pltpu.VMEM((own_rows, D), bf16),
            pltpu.VMEM((own_rows, D), f32),
            pltpu.VMEM((own_rows, D), f32),
            pltpu.VMEM((own_rows, D), bf16),
            pltpu.VMEM((own_rows, D), f32),
            pltpu.SemaphoreType.DMA((count,)),
            pltpu.SemaphoreType.DMA((2, count)),
            pltpu.SemaphoreType.DMA((2, count)),
            pltpu.SemaphoreType.DMA((3,)),
        ],
        compiler_params=pltpu.CompilerParams(
            dimension_semantics=("arbitrary",), vmem_limit_bytes=VMEM_BYTES
        ),
        cost_estimate=pl.CostEstimate(
            flops=2 * own_rows * D * (D + 2 * FF),
            bytes_accessed=2 * D * (D + 2 * FF) + own_rows * (22 * D + 4 * FF),
            transcendentals=2 * own_rows * FF,
        ),
    )(*att_parts, hidden, rows, up_bias, *pieces)


def post_backward_kernel(n_head, places, out_places, *refs):
    count, out_count = len(places), len(out_places)
    att_refs, refs = refs[:n_head], refs[n_head:]
    grad_ref, down_ref, branch_ref, after_ref, two_ref, rows_ref, act_ref, slope_ref, refs = *refs[:8], refs[8:]
    weight_refs, refs = refs[:count], refs[count:]
    d_att_refs, refs = refs[:n_head], refs[n_head:]
    d_after_ref, sums_ref, up_sum_ref, refs = refs[0], refs[1], refs[2], refs[3:]
    grad_refs, refs = refs[:out_count], refs[out_count:]
    proj_s, up_s, down_s, d_proj_s, d_up_s, d_down_s, att_s, low_s, low_t, two_t, acc, refs = *refs[:11], refs[11:]
    proj_sem, up_sem, down_sem, d_proj_sem, d_up_sem, d_down_sem = refs
    at = pl.program_id(0)
    chunks = pl.num_programs(0)
    width = D // n_head

    def fetch(chunk, slot):
        up_at, down_at = UP_AT + chunk * CHUNK, DOWN_AT + chunk * CHUNK
        return _copies(weight_refs, places, up_s.at[slot], up_at, CHUNK, up_sem.at[slot], True) + _copies(
            weight_refs, places, down_s.at[slot], down_at, CHUNK, down_sem.at[slot], True
        )

    def leave(chunk, slot):
        up_at, down_at = UP_AT + chunk * CHUNK, DOWN_AT + chunk * CHUNK
        return _copies(grad_refs, out_places, d_up_s.at[slot], up_at, CHUNK, d_up_sem.at[slot], False) + _copies(
            grad_refs, out_places, d_down_s.at[slot], down_at, CHUNK, d_down_sem.at[slot], False
        )

    proj = lambda: _copies(weight_refs, places, proj_s, PROJ_AT, D, proj_sem, True)

    @pl.when(at == 0)
    def _():
        _start(fetch(0, 0))
        _start(proj())
        grad = grad_ref[...]
        low = (rows_ref[2:3, :] * grad).astype(bf16)
        low_s[...] = low
        low_t[...] = jnp.transpose(low)
        two_t[...] = jnp.transpose(two_ref[...])
        sums_ref[...] = jnp.zeros_like(sums_ref)
        sums_ref[0:1, :] = jnp.sum(grad * down_ref[...], axis=0, keepdims=True)
        sums_ref[1:2, :] = jnp.sum(low.astype(f32), axis=0, keepdims=True)
        acc[...] = jnp.zeros_like(acc)

    @pl.when(at + 1 < chunks)
    def _():
        _start(fetch(at + 1, lax.rem(at + 1, 2)))

    slot = lax.rem(at, 2)
    _wait(fetch(at, slot))

    @pl.when(at >= 2)
    def _():
        _wait(leave(at - 2, slot))

    d_act = jnp.dot(low_s[...], _flat(down_s[slot]), preferred_element_type=f32)
    d_expand = (slope_ref[...].astype(f32) * d_act).astype(bf16)
    up_sum_ref[...] = jnp.sum(d_expand.astype(f32), axis=0, keepdims=True)
    acc[...] += lax.dot_general(d_expand, _flat(up_s[slot]), NT, preferred_element_type=f32)
    shape = d_up_s.shape[1:]
    d_up_s[slot] = jnp.dot(two_t[...], d_expand, preferred_element_type=f32).astype(bf16).reshape(shape)
    d_down_s[slot] = jnp.dot(low_t[...], act_ref[...], preferred_element_type=f32).astype(bf16).reshape(shape)
    _start(leave(at, slot))

    @pl.when(at == chunks - 1)
    def _():
        _wait(leave(at - 1, 1 - slot))
        for step in range(n_head):
            att_s[:, pl.ds(_own_column(step, n_head), width)] = att_refs[step][...]
        d_two = acc[...]
        unit, scale = _norm(after_ref[...])
        sums_ref[2:3, :] = jnp.sum(d_two * unit, axis=0, keepdims=True)
        sums_ref[3:4, :] = jnp.sum(d_two, axis=0, keepdims=True)
        d_unit = d_two * rows_ref[1:2, :]
        inner = jnp.mean(d_unit, axis=-1, keepdims=True)
        cross = jnp.mean(d_unit * unit, axis=-1, keepdims=True)
        d_after = grad_ref[...] + scale * (d_unit - inner - unit * cross)
        d_after_ref[...] = d_after
        sums_ref[4:5, :] = jnp.sum(d_after * branch_ref[...], axis=0, keepdims=True)
        d_branch = (rows_ref[0:1, :] * d_after).astype(bf16)
        sums_ref[5:6, :] = jnp.sum(d_branch.astype(f32), axis=0, keepdims=True)
        d_proj_s[...] = (
            lax.dot_general(d_branch, att_s[...], TN, preferred_element_type=f32)
            .astype(bf16)
            .reshape(d_proj_s.shape)
        )
        gone = _copies(grad_refs, out_places, d_proj_s, PROJ_AT, D, d_proj_sem, False)
        _start(gone)
        _wait(proj())
        att_s[...] = jnp.dot(d_branch, _flat(proj_s[...]), preferred_element_type=f32).astype(bf16)
        for step in range(n_head):
            d_att_refs[step][...] = att_s[:, pl.ds(_own_column(step, n_head), width)]
        _wait(leave(at, slot))
        _wait(gone)


def post_backward(att_parts, grad, down_out, branch, after, two, rows, act, slope, gathered, out_places, n_head):
    own_rows = grad.shape[0]
    pieces, places = gathered
    count, out_count = len(places), len(out_places)
    unit_rows = D // 32
    vmem = pl.BlockSpec(memory_space=pltpu.VMEM)
    hbm = pl.BlockSpec(memory_space=pl.ANY)
    column = pl.BlockSpec((own_rows, CHUNK), lambda at: (0, at))
    fixed = lambda *shape: pl.BlockSpec(shape, lambda at: (0, 0))
    lead = (4, 2, 4, unit_rows) if out_places[0] is None else (4, unit_rows)
    width = D // n_head
    outs = pl.pallas_call(
        functools.partial(post_backward_kernel, n_head, places, out_places),
        grid=(FF // CHUNK,),
        out_shape=tuple(
            [jax.ShapeDtypeStruct((own_rows, width), bf16)] * n_head
            + [
                jax.ShapeDtypeStruct((own_rows, D), f32),
                jax.ShapeDtypeStruct((8, D), f32),
                jax.ShapeDtypeStruct((1, FF), f32),
            ]
            + [jax.ShapeDtypeStruct(lead + (WIDE,), bf16)] * out_count
        ),
        in_specs=[vmem] * n_head + [vmem] * 6 + [column, column] + [hbm] * count,
        out_specs=tuple(
            [fixed(own_rows, width)] * n_head
            + [fixed(own_rows, D), fixed(8, D), pl.BlockSpec((1, CHUNK), lambda at: (0, at))]
            + [hbm] * out_count
        ),
        scratch_shapes=[
            pltpu.VMEM((4, 2, 4, unit_rows, D), bf16),
            pltpu.VMEM((2, 4, 2, 4, unit_rows, CHUNK), bf16),
            pltpu.VMEM((2, 4, 2, 4, unit_rows, CHUNK), bf16),
            pltpu.VMEM((4, 2, 4, unit_rows, D), bf16),
            pltpu.VMEM((2, 4, 2, 4, unit_rows, CHUNK), bf16),
            pltpu.VMEM((2, 4, 2, 4, unit_rows, CHUNK), bf16),
            pltpu.VMEM((own_rows, D), bf16),
            pltpu.VMEM((own_rows, D), bf16),
            pltpu.VMEM((D, own_rows), bf16),
            pltpu.VMEM((D, own_rows), bf16),
            pltpu.VMEM((own_rows, D), f32),
            pltpu.SemaphoreType.DMA((count,)),
            pltpu.SemaphoreType.DMA((2, count)),
            pltpu.SemaphoreType.DMA((2, count)),
            pltpu.SemaphoreType.DMA((out_count,)),
            pltpu.SemaphoreType.DMA((2, out_count)),
            pltpu.SemaphoreType.DMA((2, out_count)),
        ],
        compiler_params=pltpu.CompilerParams(
            dimension_semantics=("arbitrary",), vmem_limit_bytes=VMEM_BYTES
        ),
        cost_estimate=pl.CostEstimate(
            flops=4 * own_rows * D * (D + 2 * FF),
            bytes_accessed=4 * D * (D + 2 * FF) + own_rows * (22 * D + 4 * FF),
            transcendentals=0,
        ),
    )(*att_parts, grad, down_out, branch, after, two, rows, act, slope, *pieces)
    d_att, outs = outs[:n_head], outs[n_head:]
    d_after, sums, up_sum, outs = outs[0], outs[1], outs[2], outs[3:]
    return d_att, d_after, sums, up_sum[0], list(outs)


def layer_norm(values, gain, shift):
    centered = values - jnp.mean(values, axis=-1, keepdims=True)
    spread_ = jnp.mean(centered * centered, axis=-1, keepdims=True)
    return centered * lax.rsqrt(spread_ + norm_eps) * gain + shift


def unpack(vector_row):
    lengths = (D, D, 3 * D, D, D, D, D, FF, D, D, HD, HD, HD, HD)
    pieces = []
    offset = 0
    for length in lengths:
        pieces.append(vector_row[offset : offset + length])
        offset = offset + length
    return pieces


def head_gains(vec, heads):
    rows = [jnp.tile(piece, heads) for piece in vec[10:14]]
    return jnp.concatenate([jnp.stack(rows), jnp.zeros((4, heads * HD), f32)], axis=0)


def adam_update(
    weight, gradient, moment_one, moment_two, average, step_rate, decay_rate, clip_scale, fix_one, fix_two
):
    clipped = gradient * clip_scale
    moment_one = beta_one * moment_one + (1.0 - beta_one) * clipped
    moment_two = beta_two * moment_two + (1.0 - beta_two) * clipped * clipped
    first_hat = moment_one / fix_one
    second_hat = moment_two / fix_two
    weight = weight - step_rate * (
        first_hat / (jnp.sqrt(second_hat) + adam_eps) + decay_rate * weight
    )
    average = ema_decay * average + (1.0 - ema_decay) * weight
    return (weight, moment_one, moment_two, average)


def body(
    links,
    tokens,
    cotangent,
    slot_frame,
    step_count,
    *params,
):
    n_tok, n_head = links.n_tok, links.n_head
    devices = n_tok * n_head
    own = lax.axis_index("head")
    flip = lambda leaf: jnp.swapaxes(leaf, 1, 2)
    groups = []
    for at in range(0, 20, 5):
        qkv, proj, fc1, fc2, vec = params[at : at + 5]
        groups.append([qkv, flip(proj), fc1, flip(fc2), vec])
    masters = groups[0]

    slots = slot_frame.shape[0]
    per_head = slots // n_head
    held = slot_frame.reshape(n_head, per_head)
    held = jnp.concatenate(
        [lax.dynamic_slice_in_dim(held, own ^ step, 1, 0)[0] for step in range(n_head)]
    )
    index = jnp.arange(slots, dtype=jnp.int32)
    ahead = (held[None, :] < held[:, None]) | (
        (held[None, :] == held[:, None]) & (index[None, :] < index[:, None])
    )
    rank = jnp.sum(ahead.astype(jnp.int32), axis=1)
    order = jnp.sum(jnp.where(rank[None, :] == index[:, None], index[None, :], 0), axis=1).astype(jnp.int32)
    is_hi = (jnp.sum((held == held[0]).astype(jnp.int32)) == HI_BLOCKS).astype(jnp.int32).reshape(1)
    spans = (
        (HI_BLOCKS * BLOCK, LO_BLOCKS * BLOCK),
        (FRAMES * HI_BLOCKS * BLOCK, FRAMES * LO_BLOCKS * BLOCK),
    )

    vec_here = masters[4].shape[1]
    tile = lax.reduce_precision(masters[4], 8, 7).reshape(-1)
    tile = jnp.pad(tile, (0, 1024 - tile.shape[0])).reshape(8, 128)
    tiles = spread(tile, n_tok, n_head, 0).reshape(devices, 1024)[:, : 2 * vec_here]
    vectors = jnp.swapaxes(tiles.reshape(devices, 2, vec_here), 0, 1).reshape(2, devices * vec_here)
    vecs = [unpack(vectors[block]) for block in range(2)]

    qkv_low = [masters[0][block].astype(bf16) for block in range(2)]
    low = [
        jnp.concatenate([masters[kind][block].astype(bf16) for kind in (1, 2, 3)], axis=1)
        for block in range(2)
    ]
    places = links.gather_places()
    width = D // n_head
    heads = width // HD
    own_rows = tokens.shape[0]
    cut = lambda rows: [rows[step * own_rows : (step + 1) * own_rows] for step in range(n_head)]
    gains = [head_gains(vec, heads) for vec in vecs]

    def attend(block, pieces, qkv_cols):
        qkv_bias = lax.dynamic_slice_in_dim(vecs[block][2].reshape(3, D), own * width, width, 1)
        return attention_forward(
            pieces, qkv_cols, qkv_bias.reshape(1, 3 * width), gains[block], order, is_hi, spans[block]
        )

    def post(block, att_own, hidden, pieces):
        vec, tail = vecs[block], vecs[1]
        rows = jnp.stack([vec[3], vec[4], vec[5], vec[6], vec[8], vec[9], tail[0], tail[1]])
        return post_forward(att_own, hidden, rows, vec[7].reshape(1, FF), (pieces, places), n_head, block == 1)

    hidden_in = [tokens.astype(f32), None]
    normed = layer_norm(hidden_in[0], vecs[0][0], vecs[0][1]).astype(bf16)
    group, qkv_cols, saved, att_owns, mids, weights = ([None, None] for _ in range(6))

    planes = links.gather_planes(low[0])
    group[0] = links.rows_in(normed)
    qkv_cols[0] = links.fetch_heads(qkv_low[0], own)
    group[0], planes, qkv_cols[0], low[1] = together(group[0], planes, qkv_cols[0], low[1])
    near = links.gather_sides(planes)
    planes = links.gather_planes(low[1])
    saved[0] = attend(0, group[0], qkv_cols[0])
    saved[0], near, planes, qkv_low[1] = together(saved[0], near, planes, qkv_low[1])
    att_owns[0] = links.exchange(cut(saved[0][0]))
    weights[0] = links.gather_far(near)
    qkv_cols[1] = links.fetch_heads(qkv_low[1], own)
    att_owns[0], weights[0], planes, qkv_cols[1] = together(att_owns[0], weights[0], planes, qkv_cols[1])
    near = links.gather_sides(planes)
    hidden_in[1], normed, *mids[0] = post(0, att_owns[0], hidden_in[0], weights[0])

    group[1] = links.rows_in(normed)
    group[1], near = together(group[1], near)
    weights[1] = links.gather_far(near)
    saved[1] = attend(1, group[1], qkv_cols[1])
    saved[1], weights[1] = together(saved[1], weights[1])
    att_owns[1] = links.exchange(cut(saved[1][0]))
    hidden, _normed, *mids[1] = post(1, att_owns[1], hidden_in[1], weights[1])

    def post_back(block, grad):
        vec = vecs[block]
        down, act, slope, branch, after, two = mids[block]
        rows = jnp.stack([vec[4], vec[5], vec[9]] + [vec[9]] * 5)
        return post_backward(
            att_owns[block],
            grad,
            down,
            branch,
            after,
            two,
            rows,
            act,
            slope,
            (weights[block], places),
            links.grad_places(),
            n_head,
        )

    def attend_back(block, grad_parts):
        attended, raw, values, lse = saved[block]
        return attention_backward(
            raw,
            values,
            jnp.concatenate(grad_parts, axis=0),
            attended,
            lse,
            gains[block],
            order,
            is_hi,
            spans[block],
        )

    def rows_back(block, d_qkv):
        d_normed = jnp.einsum("rc,dc->rd", d_qkv, qkv_cols[block], preferred_element_type=f32)
        return links.rows_out(cut(d_normed.astype(bf16)))

    def qkv_grad(block, d_qkv):
        rows = jnp.concatenate(group[block], axis=0)
        return jnp.einsum("rd,rc->dc", rows, d_qkv, preferred_element_type=f32).astype(bf16)

    def norm_back(block, back, d_after):
        d_hidden, d_gain, d_shift = jax.vjp(layer_norm, hidden_in[block], vecs[block][0], vecs[block][1])[1](back)
        return d_after + d_hidden, d_gain, d_shift

    def vector_grad(norm_sums, sums, d_up_bias, head_sums, bias_sums):
        d_qkv_bias = lax.dynamic_update_slice_in_dim(
            jnp.zeros((3, D), f32), bias_sums[0].reshape(3, width), own * width, 1
        ).reshape(3 * D)
        head_sums = jnp.sum(head_sums[:4].reshape(4, heads, HD), axis=1).reshape(4 * HD)
        parts = [*norm_sums, d_qkv_bias, sums[5], sums[4], sums[2], sums[3], d_up_bias, sums[1], sums[0], head_sums]
        return jnp.concatenate(parts)

    d_att, d_after, sums, d_up_bias, grads = post_back(1, cotangent.astype(f32))
    d_att = links.exchange(list(d_att))
    grads = links.scatter_start(grads)
    d_att, grads = together(d_att, grads)
    grads = links.scatter_first(grads)
    d_qkv, head_sums, bias_sums = attend_back(1, d_att)
    d_qkv, head_sums, bias_sums, grads = together(d_qkv, head_sums, bias_sums, grads)
    back = rows_back(1, d_qkv)
    dw_qkv = links.return_cores(qkv_grad(1, d_qkv))
    grad_rows, *norm_sums = norm_back(1, back, d_after)
    d_vec_one = vector_grad(norm_sums, sums, d_up_bias, head_sums, bias_sums)
    grad_rows, grads, dw_qkv = together(grad_rows, grads, dw_qkv)
    grads = links.scatter_second(grads)
    dw_qkv = links.return_planes(dw_qkv)

    d_att, d_after, sums, d_up_bias, grads_zero = post_back(0, grad_rows)
    d_att, grads_zero, grads, dw_qkv = together(d_att, grads_zero, grads, dw_qkv)
    d_att = links.exchange(list(d_att))
    grads_zero = links.scatter_start(grads_zero)
    d_att, grads_zero = together(d_att, grads_zero)
    grads_zero = links.scatter_first(grads_zero)
    sum_one = links.scatter_last(grads)
    qkv_one = links.return_heads(dw_qkv, own)
    d_qkv, head_sums, bias_sums = attend_back(0, d_att)
    d_qkv, head_sums, bias_sums, grads_zero, sum_one, qkv_one = together(
        d_qkv, head_sums, bias_sums, grads_zero, sum_one, qkv_one
    )
    back = rows_back(0, d_qkv)
    dw_qkv = links.return_cores(qkv_grad(0, d_qkv))
    grad_rows, *norm_sums = norm_back(0, back, d_after)
    d_vectors = [vector_grad(norm_sums, sums, d_up_bias, head_sums, bias_sums), d_vec_one]
    sum_zero = links.scatter_last(links.scatter_second(grads_zero))
    qkv_zero = links.return_heads(links.return_planes(dw_qkv), own)
    summed = []
    for qkv_part, rest in ((qkv_zero, sum_zero), (qkv_one, sum_one)):
        summed.append([qkv_part, rest[:, PROJ_AT:UP_AT], rest[:, UP_AT:DOWN_AT], rest[:, DOWN_AT:WIDE]])
    d_tiles = jnp.swapaxes(jnp.stack(d_vectors).reshape(2, devices, vec_here), 0, 1).reshape(devices, -1)
    d_tiles = jnp.pad(d_tiles, ((0, 0), (0, 1024 - d_tiles.shape[1]))).reshape(devices, 8, 128)
    d_vec = swap(d_tiles, n_tok, n_head, 1).reshape(1024)[: 2 * vec_here].reshape(2, vec_here)
    gradients = [jnp.stack([summed[0][kind], summed[1][kind]]) for kind in range(4)] + [d_vec]
    local_square = sum((jnp.sum(gradient * gradient) for gradient in gradients))
    squares = spread(jnp.broadcast_to(local_square, (8, 128)), n_tok, n_head, 2)
    grad_norm = jnp.sqrt(jnp.sum(squares[:, 0, 0]))
    clip_scale = clip_norm / jnp.maximum(grad_norm, clip_norm)
    step_float = step_count[0].astype(f32)
    fix_one = 1.0 - beta_one**step_float
    fix_two = 1.0 - beta_two**step_float
    updates = [
        adam_update(
            groups[0][kind],
            gradients[kind],
            groups[1][kind],
            groups[2][kind],
            groups[3][kind],
            step_rates[kind],
            decays[kind],
            clip_scale,
            fix_one,
            fix_two,
        )
        for kind in range(5)
    ]
    outs = [hidden, grad_rows, grad_norm]
    for part in range(4):
        for kind in range(5):
            leaf = updates[kind][part]
            outs.append(flip(leaf) if kind in (1, 3) else leaf)
    return tuple(outs)


def solution(mesh):
    rows = P(BOTH, None)
    kinds = (
        P(None, BOTH, None),
        P(None, None, BOTH),
        P(None, BOTH, None),
        P(None, None, BOTH),
        P(None, BOTH),
    )
    in_specs = (rows, rows, P("tok"), P()) + kinds * 4
    out_specs = (rows, rows, P()) + kinds * 4
    return jax.shard_map(
        functools.partial(body, Links(mesh)),
        mesh=mesh,
        in_specs=in_specs,
        out_specs=out_specs,
        check_vma=False,
    )
```

```python
import functools
import math

import jax
import jax.numpy as jnp
from jax import lax
from jax.experimental import pallas as pl
from jax.experimental.pallas import tpu as pltpu
from jax.sharding import PartitionSpec as P

D = 1024
HD = 64
FF = 4096
BLOCK = 128
HI_BLOCKS = 8
LO_BLOCKS = 4
FRAMES = 2

norm_eps = 1e-06
clip_norm = 1.0
beta_one = 0.9
beta_two = 0.999
adam_eps = 1e-08
ema_decay = 0.7
step_rates = (0.05, 0.4, 0.05, 0.025, 0.3)
decays = (0.05, 0.05, 0.05, 0.05, 0.0)

LOG2E = math.log2(math.e)
SPAN = 512
MESH_ID = pl.DeviceIdType.MESH
BOTH = ("tok", "head")
bf16 = jnp.bfloat16
f32 = jnp.float32
VMEM_BYTES = 60 << 20


def _peer(step, n_tok, n_head):
    n = n_tok * n_head
    me = lax.axis_index("tok") * n_head + lax.axis_index("head")
    to = lax.rem(me + step, n)
    return me, to, (to // n_head, lax.rem(to, n_head))


def _enter(n_tok, n_head):
    n = n_tok * n_head
    barrier = pltpu.get_barrier_semaphore()

    def greet(step, _):
        _, _, device = _peer(step, n_tok, n_head)
        pl.semaphore_signal(barrier, inc=1, device_id=device, device_id_type=MESH_ID)
        return 0

    lax.fori_loop(1, n, greet, 0)
    pl.semaphore_wait(barrier, n - 1)


def spread_kernel(n_tok, n_head, x_ref, o_ref, send_sem, recv_sem):
    n = n_tok * n_head
    _enter(n_tok, n_head)
    me = lax.axis_index("tok") * n_head + lax.axis_index("head")
    o_ref[me] = x_ref[...]

    def copy(step):
        me, _, device = _peer(step, n_tok, n_head)
        return pltpu.make_async_remote_copy(
            src_ref=x_ref,
            dst_ref=o_ref.at[me],
            send_sem=send_sem.at[step],
            recv_sem=recv_sem.at[step],
            device_id=device,
            device_id_type=MESH_ID,
        )

    def start(step, _):
        copy(step).start()
        return 0

    def finish(step, _):
        copy(step).wait()
        return 0

    lax.fori_loop(1, n, start, 0)
    lax.fori_loop(1, n, finish, 0)


def swap_kernel(n_tok, n_head, x_ref, o_ref, land, send_sem, recv_sem):
    n = n_tok * n_head
    _enter(n_tok, n_head)
    me = lax.axis_index("tok") * n_head + lax.axis_index("head")

    def copy(step):
        me, to, device = _peer(step, n_tok, n_head)
        return pltpu.make_async_remote_copy(
            src_ref=x_ref.at[to],
            dst_ref=land.at[step],
            send_sem=send_sem.at[step],
            recv_sem=recv_sem.at[step],
            device_id=device,
            device_id_type=MESH_ID,
        )

    def start(step, _):
        copy(step).start()
        return 0

    def finish(step, _):
        copy(step).wait()
        return 0

    lax.fori_loop(1, n, start, 0)
    lax.fori_loop(1, n, finish, 0)
    o_ref[...] = x_ref[me] + jnp.sum(land[1:], axis=0)


def spread(tile, n_tok, n_head, collective_id):
    n = n_tok * n_head
    return pl.pallas_call(
        functools.partial(spread_kernel, n_tok, n_head),
        out_shape=jax.ShapeDtypeStruct((n,) + tile.shape, tile.dtype),
        in_specs=[pl.BlockSpec(memory_space=pltpu.VMEM)],
        out_specs=pl.BlockSpec(memory_space=pltpu.VMEM),
        scratch_shapes=[pltpu.SemaphoreType.DMA((n,)), pltpu.SemaphoreType.DMA((n,))],
        compiler_params=pltpu.CompilerParams(collective_id=collective_id, has_side_effects=True),
    )(tile)


def swap(tiles, n_tok, n_head, collective_id):
    n = n_tok * n_head
    return pl.pallas_call(
        functools.partial(swap_kernel, n_tok, n_head),
        out_shape=jax.ShapeDtypeStruct(tiles.shape[1:], tiles.dtype),
        in_specs=[pl.BlockSpec(memory_space=pltpu.VMEM)],
        out_specs=pl.BlockSpec(memory_space=pltpu.VMEM),
        scratch_shapes=[
            pltpu.VMEM(tiles.shape, tiles.dtype),
            pltpu.SemaphoreType.DMA((n,)),
            pltpu.SemaphoreType.DMA((n,)),
        ],
        compiler_params=pltpu.CompilerParams(collective_id=collective_id, has_side_effects=True),
    )(tiles)


def _lane_mean(values, grouping):
    top = values.astype(bf16)
    rest = (values - top.astype(f32)).astype(bf16)
    return jnp.dot(top, grouping, preferred_element_type=f32) + jnp.dot(
        rest, grouping, preferred_element_type=f32
    )


def _grouping(width):
    row = lax.broadcasted_iota(jnp.int32, (width, width), 0) // HD
    col = lax.broadcasted_iota(jnp.int32, (width, width), 1) // HD
    return jnp.where(row == col, 1.0 / HD, 0.0).astype(bf16)


def _unit(values, grouping):
    centered = values - _lane_mean(values, grouping)
    spread_ = _lane_mean(centered * centered, grouping)
    scale = lax.rsqrt(spread_ + norm_eps)
    return centered * scale, scale


def _only(values, head):
    lane = lax.broadcasted_iota(jnp.int32, values.shape, 1)
    return jnp.where(lane // HD == head, values, jnp.zeros_like(values))


NT = (((1,), (1,)), ((), ()))
TN = (((0,), (0,)), ((), ()))


def forward_kernel(
    heads, pieces, spans, tile_rows, order_ref, hi_ref, *refs
):
    x_refs = refs[:pieces]
    w_ref, bias_ref, gains_ref, att_ref, raw_ref, val_ref, lse_ref, q_s, k_s, v_s, acc = refs[pieces:]
    width = heads * HD
    rows = att_ref.shape[0]
    blocks = rows // BLOCK
    piece_rows = rows // pieces
    for at in range(pieces):
        full = jnp.dot(x_refs[at][...], w_ref[...], preferred_element_type=f32) + bias_ref[...]
        here = pl.ds(at * piece_rows, piece_rows)
        raw_ref[here, :] = full[:, : 2 * width]
        val_ref[here, :] = full[:, 2 * width :].astype(bf16)
    grouping = _grouping(width)

    def place(at, _):
        here = pl.ds(pl.multiple_of(order_ref[at] * BLOCK, BLOCK), BLOCK)
        there = pl.ds(pl.multiple_of(at * BLOCK, BLOCK), BLOCK)
        unit_q, _s = _unit(raw_ref[here, :width], grouping)
        unit_k, _s = _unit(raw_ref[here, width:], grouping)
        q_s[there, :] = ((unit_q * gains_ref[0:1, :] + gains_ref[1:2, :]) * HD ** (-0.5)).astype(bf16)
        key = (unit_k * gains_ref[2:3, :] + gains_ref[3:4, :]).astype(bf16)
        value = val_ref[here, :]
        for head in range(heads):
            k_s[head, there, :] = _only(key, head)
            v_s[head, there, :] = _only(value, head)
        return 0

    lax.fori_loop(0, blocks, place, 0)
    per_tile = tile_rows // BLOCK

    def attend(span):
        def tile(at, _):
            here = pl.ds(pl.multiple_of(at * tile_rows, tile_rows), tile_rows)
            first = at * tile_rows // span * span
            there = pl.ds(pl.multiple_of(first, span), span)
            query = q_s[here, :]
            lane = lax.broadcasted_iota(jnp.int32, (tile_rows, 128), 1)
            logs = jnp.zeros((tile_rows, 128), f32)
            for head in range(heads):
                scores = lax.dot_general(query, k_s[head, there, :], NT, preferred_element_type=f32)
                top = jnp.max(scores, axis=1, keepdims=True) * LOG2E
                probs = jnp.exp2(scores * LOG2E - top)
                total = jnp.sum(probs, axis=1, keepdims=True)
                part = jnp.dot(
                    probs.astype(bf16), v_s[head, there, :], preferred_element_type=f32
                ) / total
                if head == 0:
                    acc[...] = part
                else:
                    acc[...] += part
                logs = jnp.where(lane == head, top + jnp.log2(total), logs)
            lse_ref[here, :] = logs
            for sub in range(per_tile):
                out = pl.ds(pl.multiple_of(order_ref[at * per_tile + sub] * BLOCK, BLOCK), BLOCK)
                att_ref[out, :] = acc[sub * BLOCK : (sub + 1) * BLOCK, :].astype(bf16)
            return 0

        lax.fori_loop(0, rows // tile_rows, tile, 0)

    @pl.when(hi_ref[0] == 1)
    def _():
        attend(spans[0])

    @pl.when(hi_ref[0] == 0)
    def _():
        attend(spans[1])


def attention_forward(pieces, weight, bias, gains, order, is_hi, spans):
    heads = weight.shape[1] // (3 * HD)
    width = heads * HD
    rows = sum(piece.shape[0] for piece in pieces)
    tile_rows = 256
    smem = pl.BlockSpec(memory_space=pltpu.SMEM)
    vmem = pl.BlockSpec(memory_space=pltpu.VMEM)
    flops = 2 * rows * (D * 3 * width + 8 * spans[0] * width)
    return pl.pallas_call(
        functools.partial(forward_kernel, heads, len(pieces), spans, tile_rows),
        out_shape=(
            jax.ShapeDtypeStruct((rows, width), bf16),
            jax.ShapeDtypeStruct((rows, 2 * width), f32),
            jax.ShapeDtypeStruct((rows, width), bf16),
            jax.ShapeDtypeStruct((rows, 128), f32),
        ),
        in_specs=[smem, smem] + [vmem] * (len(pieces) + 3),
        out_specs=(vmem,) * 4,
        scratch_shapes=[
            pltpu.VMEM((rows, width), bf16),
            pltpu.VMEM((heads, rows, width), bf16),
            pltpu.VMEM((heads, rows, width), bf16),
            pltpu.VMEM((tile_rows, width), f32),
        ],
        compiler_params=pltpu.CompilerParams(vmem_limit_bytes=VMEM_BYTES),
        cost_estimate=pl.CostEstimate(
            flops=flops, bytes_accessed=rows * (2 * D + 14 * width), transcendentals=rows * spans[0] * heads
        ),
    )(order, is_hi, *pieces, weight, bias, gains)


def backward_kernel(
    heads,
    spans,
    order_ref,
    hi_ref,
    raw_ref,
    val_ref,
    grad_ref,
    att_ref,
    lse_ref,
    gains_ref,
    out_ref,
    sums_ref,
    bias_ref,
    q_s,
    o_s,
    k_m,
    v_m,
    q_m,
    o_m,
    dq_s,
    dk_s,
    dv_s,
    lse_t,
    delta_t,
):
    width = heads * HD
    rows = val_ref.shape[0]
    blocks = rows // BLOCK
    grouping = _grouping(width)
    head_of = lax.broadcasted_iota(jnp.int32, (8, width), 1) // HD
    picks = jnp.where(head_of == lax.broadcasted_iota(jnp.int32, (8, width), 0), 1.0, 0.0).astype(bf16)

    def place(at, _):
        here = pl.ds(pl.multiple_of(order_ref[at] * BLOCK, BLOCK), BLOCK)
        there = pl.ds(pl.multiple_of(at * BLOCK, BLOCK), BLOCK)
        unit_q, _s = _unit(raw_ref[here, :width], grouping)
        unit_k, _s = _unit(raw_ref[here, width:], grouping)
        query = ((unit_q * gains_ref[0:1, :] + gains_ref[1:2, :]) * HD ** (-0.5)).astype(bf16)
        key = (unit_k * gains_ref[2:3, :] + gains_ref[3:4, :]).astype(bf16)
        value = val_ref[here, :]
        grad = grad_ref[here, :]
        q_s[there, :] = query
        o_s[there, :] = grad
        for head in range(heads):
            k_m[head, there, :] = _only(key, head)
            v_m[head, there, :] = _only(value, head)
            q_m[head, there, :] = _only(query, head)
            o_m[head, there, :] = _only(grad, head)
        both = grad.astype(f32) * att_ref[here, :].astype(f32)
        top = both.astype(bf16)
        rest = (both - top.astype(f32)).astype(bf16)
        delta_t[:, there] = lax.dot_general(picks, top, NT, preferred_element_type=f32) + lax.dot_general(
            picks, rest, NT, preferred_element_type=f32
        )
        lse_t[:, there] = jnp.transpose(lse_ref[there, :])[:8, :]
        dq_s[there, :] = jnp.zeros((BLOCK, width), f32)
        dk_s[there, :] = jnp.zeros((BLOCK, width), f32)
        dv_s[there, :] = jnp.zeros((BLOCK, width), f32)
        return 0

    lax.fori_loop(0, blocks, place, 0)
    span = jnp.where(hi_ref[0] == 1, spans[0], spans[1])

    def tile(at, _):
        here = pl.ds(pl.multiple_of(at * SPAN, SPAN), SPAN)
        first = at * SPAN // span * span // SPAN

        def chunk(key_at, _):
            there = pl.ds(pl.multiple_of(key_at * SPAN, SPAN), SPAN)
            for head in range(heads):
                scores = lax.dot_general(k_m[head, there, :], q_s[here, :], NT, preferred_element_type=f32)
                probs = jnp.exp2(scores * LOG2E - lse_t[head : head + 1, here])
                grad_probs = lax.dot_general(
                    v_m[head, there, :], o_s[here, :], NT, preferred_element_type=f32
                )
                grad_scores = (probs * (grad_probs - delta_t[head : head + 1, here])).astype(bf16)
                dv_s[there, :] += jnp.dot(probs.astype(bf16), o_m[head, here, :], preferred_element_type=f32)
                dk_s[there, :] += jnp.dot(grad_scores, q_m[head, here, :], preferred_element_type=f32)
                dq_s[here, :] += lax.dot_general(
                    grad_scores, k_m[head, there, :], TN, preferred_element_type=f32
                )
            return 0

        lax.fori_loop(first, first + span // SPAN, chunk, 0)
        return 0

    lax.fori_loop(0, rows // SPAN, tile, 0)
    sums_ref[...] = jnp.zeros_like(sums_ref)
    bias_ref[...] = jnp.zeros_like(bias_ref)

    def pull(grad, unit, scale, gain):
        grad_unit = grad * gain
        inner = _lane_mean(grad_unit, grouping)
        cross = _lane_mean(grad_unit * unit, grouping)
        return scale * (grad_unit - inner - unit * cross)

    def leave(at, _):
        here = pl.ds(pl.multiple_of(order_ref[at] * BLOCK, BLOCK), BLOCK)
        there = pl.ds(pl.multiple_of(at * BLOCK, BLOCK), BLOCK)
        unit_q, scale_q = _unit(raw_ref[here, :width], grouping)
        unit_k, scale_k = _unit(raw_ref[here, width:], grouping)
        grad_q = dq_s[there, :] * HD ** (-0.5)
        grad_k = dk_s[there, :]
        sums_ref[0:1, :] += jnp.sum(grad_q * unit_q, axis=0, keepdims=True)
        sums_ref[1:2, :] += jnp.sum(grad_q, axis=0, keepdims=True)
        sums_ref[2:3, :] += jnp.sum(grad_k * unit_k, axis=0, keepdims=True)
        sums_ref[3:4, :] += jnp.sum(grad_k, axis=0, keepdims=True)
        low_q = pull(grad_q, unit_q, scale_q, gains_ref[0:1, :]).astype(bf16)
        low_k = pull(grad_k, unit_k, scale_k, gains_ref[2:3, :]).astype(bf16)
        low_v = dv_s[there, :].astype(bf16)
        for part, low in enumerate((low_q, low_k, low_v)):
            lanes = slice(part * width, (part + 1) * width)
            out_ref[here, lanes] = low
            bias_ref[0:1, lanes] += jnp.sum(low.astype(f32), axis=0, keepdims=True)
        return 0

    lax.fori_loop(0, blocks, leave, 0)


def attention_backward(raw, values, grad, attended, lse, gains, order, is_hi, spans):
    rows, width = values.shape
    heads = width // HD
    smem = pl.BlockSpec(memory_space=pltpu.SMEM)
    vmem = pl.BlockSpec(memory_space=pltpu.VMEM)
    flops = 2 * rows * 20 * spans[0] * width
    masked = pltpu.VMEM((heads, rows, width), bf16)
    return pl.pallas_call(
        functools.partial(backward_kernel, heads, spans),
        out_shape=(
            jax.ShapeDtypeStruct((rows, 3 * width), bf16),
            jax.ShapeDtypeStruct((8, width), f32),
            jax.ShapeDtypeStruct((8, 3 * width), f32),
        ),
        in_specs=[smem, smem] + [vmem] * 6,
        out_specs=(vmem,) * 3,
        scratch_shapes=[
            pltpu.VMEM((rows, width), bf16),
            pltpu.VMEM((rows, width), bf16),
            masked,
            masked,
            masked,
            masked,
            pltpu.VMEM((rows, width), f32),
            pltpu.VMEM((rows, width), f32),
            pltpu.VMEM((rows, width), f32),
            pltpu.VMEM((8, rows), f32),
            pltpu.VMEM((8, rows), f32),
        ],
        compiler_params=pltpu.CompilerParams(vmem_limit_bytes=VMEM_BYTES),
        cost_estimate=pl.CostEstimate(
            flops=flops, bytes_accessed=rows * 24 * width, transcendentals=rows * spans[0] * heads
        ),
    )(order, is_hi, raw, values, grad, attended, lse, gains)


class Links:
    def __init__(self, mesh):
        self.n_tok = mesh.shape["tok"]
        self.n_head = mesh.shape["head"]
        self.paired = self.n_tok == 8 and self.n_head == 4

    def head(self, values, step):
        return lax.ppermute(values, "head", [(i, i ^ step) for i in range(self.n_head)])

    def tok(self, values, step):
        return lax.ppermute(values, "tok", [(i, i ^ step) for i in range(self.n_tok)])

    def rows_in(self, rows):
        if not self.paired:
            return [rows] + [self.head(rows, step) for step in range(1, self.n_head)]
        half = rows.shape[0] // 2
        one, two = self.head(rows, 1), self.head(rows, 2)
        far = jnp.concatenate([self.head(one[:half], 2), self.head(two[half:], 1)], axis=0)
        return [rows, one, two, far]

    def rows_out(self, parts):
        if not self.paired:
            moved = [self.head(parts[step], step).astype(f32) for step in range(1, self.n_head)]
            return parts[0].astype(f32) + sum(moved)
        half = parts[0].shape[0] // 2
        upper = [part[:half] for part in parts]
        lower = [part[half:] for part in parts]
        pass_up = (upper[2].astype(f32) + self.head(upper[3], 1).astype(f32)).astype(bf16)
        pass_low = (lower[1].astype(f32) + self.head(lower[3], 2).astype(f32)).astype(bf16)
        up = upper[0].astype(f32) + self.head(upper[1], 1).astype(f32) + self.head(pass_up, 2).astype(f32)
        low = lower[0].astype(f32) + self.head(lower[2], 2).astype(f32) + self.head(pass_low, 1).astype(f32)
        return jnp.concatenate([up, low], axis=0)

    def exchange(self, parts):
        return [parts[0]] + [self.head(parts[step], step) for step in range(1, self.n_head)]

    def by_index(self, pieces, own):
        return [
            lax.select_n((own ^ at).astype(jnp.int32), *pieces) if len(pieces) > 1 else pieces[0]
            for at in range(len(pieces))
        ]

    def zed(self):
        return lax.axis_index("tok") // 2

    def core(self):
        return lax.rem(lax.axis_index("tok"), 2)

    def planes(self, shard):
        pieces = [shard] + [self.tok(shard, 2 * step) for step in range(1, 4)]
        return jnp.stack(self.by_index(pieces, self.zed()))

    def gather_places(self):
        if not self.paired:
            return [None]
        spots = ((0, 4, 0), (0, 4, 1), (0, 4, 2), (0, 2, 3), (2, 2, 3))
        return [("head", first, count, core, to) for first, count, to in spots for core in range(2)]

    def gather_planes(self, shard):
        if not self.paired:
            whole = lax.all_gather(shard, BOTH, axis=0, tiled=True)
            return [whole.reshape(4, 2, 4, whole.shape[0] // 32, whole.shape[1])]
        return [self.planes(shard)]

    def gather_sides(self, own):
        if not self.paired:
            return own
        return [own[0], self.head(own[0], 1), self.head(own[0], 2)]

    def gather_far(self, near):
        if not self.paired:
            return near
        far = [self.head(near[1][:2], 2), self.head(near[2][2:], 1)]
        pieces = []
        for piece in near + far:
            pieces += [piece, self.tok(piece, 1)]
        return pieces

    def scatter_start(self, pieces, got):
        if not self.paired:
            return pieces
        return [(one.astype(f32) + two.astype(f32)).astype(bf16) for one, two in zip(pieces, got)]

    def scatter_first(self, sums):
        if not self.paired:
            return sums
        low = [part[:2] for part in sums]
        top = [part[2:] for part in sums]
        come_low = self.head(jnp.concatenate([low[1], low[3]], axis=0), 1).astype(f32)
        come_top = self.head(jnp.concatenate([top[2], top[3]], axis=0), 2).astype(f32)
        pass_low = (low[2].astype(f32) + come_low[2:]).astype(bf16)
        pass_top = (top[1].astype(f32) + come_top[2:]).astype(bf16)
        own_low = low[0].astype(f32) + come_low[:2]
        own_top = top[0].astype(f32) + come_top[:2]
        return [own_low.astype(bf16), own_top.astype(bf16), pass_low, pass_top]

    def scatter_second(self, halves):
        if not self.paired:
            return halves
        own_low, own_top, pass_low, pass_top = halves
        low = own_low.astype(f32) + self.head(pass_low, 2).astype(f32)
        top = own_top.astype(f32) + self.head(pass_top, 1).astype(f32)
        return [jnp.concatenate([low, top], axis=0).astype(bf16)]

    def scatter_last(self, planes):
        if not self.paired:
            whole = planes[0].reshape(-1, planes[0].shape[-1])
            return lax.psum_scatter(whole, BOTH, scatter_dimension=0, tiled=True).astype(f32)
        return self.sum_planes(planes[0])

    def sum_planes(self, parts):
        zed = self.zed()
        pick = lambda step: lax.dynamic_slice_in_dim(parts, zed ^ step, 1, 0)[0]
        total = pick(0).astype(f32)
        for step in range(1, 4):
            total = total + self.tok(pick(step).astype(bf16), 2 * step).astype(f32)
        return total

    def fetch_heads(self, shards, own):
        own_rows = shards[0].shape[0]
        width = D // self.n_head
        cut = jnp.stack(shards).reshape(len(shards), own_rows, 3, D)
        parts = [
            lax.dynamic_slice_in_dim(cut, (own ^ step) * width, width, 3).reshape(
                len(shards), own_rows, 3 * width
            )
            for step in range(self.n_head)
        ]
        moved = jnp.stack(self.by_index(self.exchange(parts), own), axis=1)
        return [moved[at].reshape(self.n_head * own_rows, 3 * width) for at in range(len(shards))]

    def return_cores(self, grad):
        if not self.paired:
            return grad
        view = grad.reshape((4, 2, grad.shape[0] // 8, grad.shape[1]))
        core = self.core()
        cut = lambda at: lax.dynamic_slice_in_dim(view, at, 1, 1)[:, 0]
        return (cut(core).astype(f32) + self.tok(cut(core ^ 1), 1).astype(f32)).astype(bf16)

    def return_planes(self, grad):
        if not self.paired:
            return lax.psum_scatter(grad, "tok", scatter_dimension=0, tiled=True)
        return self.sum_planes(grad).astype(bf16)

    def return_heads(self, both, own):
        width = D // self.n_head
        stack = jnp.stack(both)
        own_rows = stack.shape[1] // self.n_head
        parts = [
            lax.dynamic_slice_in_dim(stack, (own ^ step) * own_rows, own_rows, 1)
            for step in range(self.n_head)
        ]
        back = jnp.stack(self.by_index(self.exchange(parts), own), axis=2)
        back = back.reshape(len(both), own_rows, self.n_head, 3, width)
        return jnp.swapaxes(back, 2, 3).reshape(len(both), own_rows, 3 * D).astype(f32)


def together(*values):
    return lax.optimization_barrier(values)


CHUNK = 512


def _paired(value, step, bits):
    total = 0
    for bit in range(bits):
        one = lax.rem(value // (1 << bit), 2)
        total = total + (1 - one if (step >> bit) % 2 else one) * (1 << bit)
    return total


def _slot(ref, place):
    if place is None:
        return ref
    tok = lax.axis_index("tok")
    side = _paired(lax.rem(tok, 2), place[-1] if place[0] == "plane" else place[3], 1)
    if place[0] == "plane":
        return ref.at[_paired(tok // 2, place[1], 2), side]
    return ref.at[pl.ds(place[1], place[2]), side, _paired(lax.axis_index("head"), place[4], 2)]


PROJ_AT, UP_AT, DOWN_AT, WIDE = 0, D, D + FF, D + 2 * FF


def _cols(ref, at, size):
    window = pl.ds(pl.multiple_of(at, 128), size)
    return ref.at[(slice(None),) * (len(ref.shape) - 1) + (window,)]


def _copies(pieces, places, whole, at, size, sems, inward):
    moves = []
    for index, (piece, place) in enumerate(zip(pieces, places)):
        outside = _cols(piece, at, size)
        inside = _slot(whole, place)
        pair = (outside, inside) if inward else (inside, outside)
        moves.append(pltpu.make_async_copy(pair[0], pair[1], sems.at[index]))
    return moves


def _start(moves):
    for move in moves:
        move.start()


def _wait(moves):
    for move in moves:
        move.wait()


def _flat(values):
    return values.reshape(D, values.shape[-1])


def _norm(values):
    centered = values - jnp.mean(values, axis=-1, keepdims=True)
    scale = lax.rsqrt(jnp.mean(centered * centered, axis=-1, keepdims=True) + norm_eps)
    return centered * scale, scale


def _own_column(step, n_head):
    at = _paired(lax.axis_index("head"), step, n_head.bit_length() - 1)
    return pl.multiple_of(at * (D // n_head), 128)


def _mate(step):
    return lax.axis_index("tok"), _paired(lax.axis_index("head"), step, 2)


def _sibling():
    return _paired(lax.axis_index("tok"), 1, 3), lax.axis_index("head")


def _greet(devices):
    barrier = pltpu.get_barrier_semaphore()
    for device in devices:
        pl.semaphore_signal(barrier, inc=1, device_id=device, device_id_type=MESH_ID)
    pl.semaphore_wait(barrier, len(devices))


def _send(source, target, send_sem, recv_sem, device):
    return pltpu.make_async_remote_copy(
        src_ref=source,
        dst_ref=target,
        send_sem=send_sem,
        recv_sem=recv_sem,
        device_id=device,
        device_id_type=MESH_ID,
    )


def enter_kernel(wide, *refs):
    x_ref, q_ref, refs = refs[0], refs[1], refs[2:]
    if wide:
        shard_ref, refs = refs[0], refs[1:]
    one_ref, two_ref, far_ref, full_ref, refs = *refs[:4], refs[4:]
    if wide:
        planes_ref, refs = refs[0], refs[1:]
    send_sem, recv_sem, z_send, z_recv, own_sem, core_sem = refs
    tok, head = lax.axis_index("tok"), lax.axis_index("head")
    zed, core = tok // 2, lax.rem(tok, 2)
    one_way, two_way = _mate(1), _mate(2)
    barrier = pltpu.get_barrier_semaphore()
    greet = lambda device: pl.semaphore_signal(barrier, inc=1, device_id=device, device_id_type=MESH_ID)
    for device in (one_way, two_way, _sibling()):
        greet(device)

    @pl.when(zed < 3)
    def _():
        greet((tok + 2, head))

    @pl.when(zed > 0)
    def _():
        greet((tok - 2, head))

    edge = (zed == 0) | (zed == 3)

    @pl.when(edge)
    def _():
        pl.semaphore_wait(barrier, 4)

    @pl.when(jnp.logical_not(edge))
    def _():
        pl.semaphore_wait(barrier, 5)

    rows = x_ref.shape[0]
    parts = 4
    size = rows // parts

    def move(lane, part, source, target, device):
        here = pl.ds(part * size, size)
        return _send(source.at[here], target.at[here], send_sem.at[lane, part], recv_sem.at[lane, part], device)

    to_one = lambda part: move(0, part, x_ref, one_ref, one_way)
    to_two = lambda part: move(1, part, x_ref, two_ref, two_way)
    on_two = lambda part: move(2, part, one_ref, far_ref, two_way)
    on_one = lambda part: move(2, part, two_ref, far_ref, one_way)
    homes = [(q_ref, lambda plane: full_ref.at[plane, core])]
    if wide:
        homes.append((shard_ref, lambda plane: planes_ref.at[plane]))

    def climb(up, step):
        plane = jnp.clip(zed - step if up else zed + step, 0, 3)
        device = (jnp.clip(tok + 2 if up else tok - 2, 0, 7), head)
        return [
            _send(
                home(plane) if step else source,
                home(plane),
                z_send.at[int(up), step, index],
                z_recv.at[int(up), step, index],
                device,
            )
            for index, (source, home) in enumerate(homes)
        ]

    def sends(up, step):
        return (zed >= step) & (zed < 3) if up else (zed <= 3 - step) & (zed > 0)

    def comes(up, step):
        return zed >= step + 1 if up else zed <= 2 - step

    def climb_start(up, step):
        @pl.when(sends(up, step))
        def _():
            _start(climb(up, step))

    def climb_come(up, step):
        @pl.when(comes(up, step))
        def _():
            for copy in climb(up, step):
                copy.wait_recv()

    for turn in range(parts):
        to_one(turn).start()
        to_two(parts - 1 - turn).start()
    for up in (True, False):
        climb_start(up, 0)
    stays = [
        pltpu.make_async_copy(source, home(zed), own_sem.at[index]) for index, (source, home) in enumerate(homes)
    ]
    _start(stays)
    for turn in range(parts // 2):
        to_one(turn).wait_recv()
        on_two(turn).start()
        to_two(parts - 1 - turn).wait_recv()
        on_one(parts - 1 - turn).start()
    for step in range(3):
        for up in (True, False):
            climb_come(up, step)
            if step < 2:
                climb_start(up, step + 1)
    _wait(stays)
    mine = full_ref.at[:, core]
    over = _send(mine, mine, core_sem.at[0], core_sem.at[1], _sibling())
    over.start()
    for turn in range(parts // 2, parts):
        to_one(turn).wait_recv()
        to_two(parts - 1 - turn).wait_recv()
    for turn in range(parts):
        to_one(turn).wait_send()
        to_two(turn).wait_send()
    for turn in range(parts // 2):
        on_two(turn).wait()
        on_one(parts - 1 - turn).wait()
    for step in range(3):
        for up in (True, False):

            @pl.when(sends(up, step))
            def _():
                for copy in climb(up, step):
                    copy.wait_send()

    over.wait()


def enter_rows(rows, mine, shard, collective_id):
    hbm = pl.BlockSpec(memory_space=pl.ANY)
    like = jax.ShapeDtypeStruct(rows.shape, rows.dtype)
    outs = [like, like, like, jax.ShapeDtypeStruct((4, 2) + mine.shape, mine.dtype)]
    given = [rows, mine]
    if shard is not None:
        outs.append(jax.ShapeDtypeStruct((4,) + shard.shape, shard.dtype))
        given.append(shard)
    sems = pltpu.SemaphoreType.DMA
    one, two, far, full, *planes = pl.pallas_call(
        functools.partial(enter_kernel, shard is not None),
        out_shape=tuple(outs),
        in_specs=[hbm] * len(given),
        out_specs=(hbm,) * len(outs),
        scratch_shapes=[sems((3, 4)), sems((3, 4)), sems((2, 3, 2)), sems((2, 3, 2)), sems((2,)), sems((2,))],
        compiler_params=pltpu.CompilerParams(collective_id=collective_id, has_side_effects=True),
        cost_estimate=pl.CostEstimate(flops=0, bytes_accessed=150 << 20, transcendentals=0),
    )(*given)
    return [rows, one, two, far], full.reshape(8 * mine.shape[0], mine.shape[1]), planes


def rows_out_kernel(grad_ref, weight_ref, hidden_ref, after_ref, gain_ref, out_ref, sums_ref, away, come, send_sem, recv_sem):
    one_way, two_way = _mate(1), _mate(2)
    _greet([one_way, two_way])
    rows = hidden_ref.shape[0]
    half = rows // 2

    def term(step, low):
        here = pl.ds(step * rows + (0 if low else half), half)
        return lax.dot_general(grad_ref[here, :], weight_ref[...], NT, preferred_element_type=f32)

    def move(slot, device):
        return _send(away.at[slot], come.at[slot], send_sem.at[slot], recv_sem.at[slot], device)

    ways = (one_way, two_way, one_way, two_way, two_way, one_way)
    for slot, (step, low) in enumerate(((3, True), (3, False), (1, True), (2, False))):
        away[slot] = term(step, low).astype(bf16)
        move(slot, ways[slot]).start()
    pass_low = term(2, True)
    pass_top = term(1, False)
    move(0, ways[0]).wait_recv()
    away[4] = (pass_low + come[0].astype(f32)).astype(bf16)
    move(4, ways[4]).start()
    move(1, ways[1]).wait_recv()
    away[5] = (pass_top + come[1].astype(f32)).astype(bf16)
    move(5, ways[5]).start()
    sums_ref[...] = jnp.zeros_like(sums_ref)
    for low in (True, False):
        here = pl.ds(0 if low else half, half)
        own = term(0, low)
        unit, scale = _norm(hidden_ref[here, :])
        near, far = (2, 4) if low else (3, 5)
        move(near, ways[near]).wait_recv()
        move(far, ways[far]).wait_recv()
        grad = own + come[near].astype(f32) + come[far].astype(f32)
        sums_ref[0:1, :] += jnp.sum(grad * unit, axis=0, keepdims=True)
        sums_ref[1:2, :] += jnp.sum(grad, axis=0, keepdims=True)
        grad_unit = grad * gain_ref[0:1, :]
        inner = jnp.mean(grad_unit, axis=-1, keepdims=True)
        cross = jnp.mean(grad_unit * unit, axis=-1, keepdims=True)
        out_ref[here, :] = after_ref[here, :] + scale * (grad_unit - inner - unit * cross)
    for slot in range(6):
        move(slot, ways[slot]).wait_send()


def rows_out(grad, weight, hidden, after, gain, collective_id):
    rows = hidden.shape[0]
    vmem = pl.BlockSpec(memory_space=pltpu.VMEM)
    buffer = pltpu.VMEM((6, rows // 2, D), bf16)
    sems = pltpu.SemaphoreType.DMA((6,))
    return pl.pallas_call(
        rows_out_kernel,
        out_shape=(jax.ShapeDtypeStruct((rows, D), f32), jax.ShapeDtypeStruct((8, D), f32)),
        in_specs=[vmem] * 5,
        out_specs=(vmem, vmem),
        scratch_shapes=[buffer, buffer, sems, sems],
        compiler_params=pltpu.CompilerParams(
            collective_id=collective_id, has_side_effects=True, vmem_limit_bytes=VMEM_BYTES
        ),
        cost_estimate=pl.CostEstimate(flops=0, bytes_accessed=150 << 20, transcendentals=0),
    )(grad, weight, hidden, after, gain)


def post_forward_kernel(n_head, places, last, remote, *refs):
    count = len(places)
    att_ref, refs = refs[0], refs[1:]
    hidden_ref, rows_ref, up_bias_ref, refs = refs[0], refs[1], refs[2], refs[3:]
    weight_refs, refs = refs[:count], refs[count:]
    next_ref, normed_ref, down_ref, act_ref, slope_ref, branch_hbm, after_hbm, two_hbm, att_hbm, refs = *refs[:9], refs[9:]
    proj_s, up_s, down_s, att_s, branch_s, after_s, two_s, acc, proj_sem, up_sem, down_sem, out_sem, send_sem, recv_sem = refs
    at = pl.program_id(0)
    chunks = pl.num_programs(0)

    def fetch(chunk, slot):
        up_at, down_at = UP_AT + chunk * CHUNK, DOWN_AT + chunk * CHUNK
        return _copies(weight_refs, places, up_s.at[slot], up_at, CHUNK, up_sem.at[slot], True) + _copies(
            weight_refs, places, down_s.at[slot], down_at, CHUNK, down_sem.at[slot], True
        )

    leaving = [
        pltpu.make_async_copy(branch_s, branch_hbm, out_sem.at[0]),
        pltpu.make_async_copy(after_s, after_hbm, out_sem.at[1]),
        pltpu.make_async_copy(two_s, two_hbm, out_sem.at[2]),
        pltpu.make_async_copy(att_s, att_hbm, out_sem.at[3]),
    ]

    @pl.when(at == 0)
    def _():
        proj = _copies(weight_refs, places, proj_s, PROJ_AT, D, proj_sem, True)
        if remote:
            width, rows = D // n_head, hidden_ref.shape[0]
            _greet([_mate(step) for step in range(1, n_head)])
            mine = att_s.at[:, pl.ds(_own_column(0, n_head), width)]
            moves = [
                _send(
                    att_ref.at[pl.ds(step * rows, rows)], mine, send_sem.at[step], recv_sem.at[step], _mate(step)
                )
                for step in range(1, n_head)
            ]
            moves.append(pltpu.make_async_copy(att_ref.at[pl.ds(0, rows)], mine, send_sem.at[0]))
            _start(moves)
        _start(proj)
        _start(fetch(0, 0))
        if remote:
            _wait(moves)
        else:
            att_s[...] = att_ref[...]
        _wait(proj)
        branch = (
            lax.dot_general(att_s[...], _flat(proj_s[...]), NT, preferred_element_type=f32) + rows_ref[0:1, :]
        )
        branch_s[...] = branch
        after = hidden_ref[...] + rows_ref[1:2, :] * branch
        after_s[...] = after
        unit, _s = _norm(after)
        two_s[...] = (unit * rows_ref[2:3, :] + rows_ref[3:4, :]).astype(bf16)
        _start(leaving)

    @pl.when(at + 1 < chunks)
    def _():
        _start(fetch(at + 1, lax.rem(at + 1, 2)))

    slot = lax.rem(at, 2)
    _wait(fetch(at, slot))
    expand = jnp.dot(two_s[...], _flat(up_s[slot]), preferred_element_type=f32) + up_bias_ref[...]
    cdf = 0.5 * (1.0 + lax.erf(expand * math.sqrt(0.5)))
    slope = cdf + expand * jnp.exp(-0.5 * expand * expand) * (1.0 / math.sqrt(2.0 * math.pi))
    act = (expand * cdf).astype(bf16)
    act_ref[...] = act
    slope_ref[...] = slope.astype(bf16)
    part = lax.dot_general(act, _flat(down_s[slot]), NT, preferred_element_type=f32)

    @pl.when(at == 0)
    def _():
        acc[...] = part

    @pl.when(at > 0)
    def _():
        acc[...] += part

    @pl.when(at == chunks - 1)
    def _():
        down = acc[...] + rows_ref[4:5, :]
        down_ref[...] = down
        hidden = after_s[...] + rows_ref[5:6, :] * down
        next_ref[...] = hidden
        if last:
            normed_ref[...] = jnp.zeros_like(normed_ref)
        else:
            unit, _s = _norm(hidden)
            normed_ref[...] = (unit * rows_ref[6:7, :] + rows_ref[7:8, :]).astype(bf16)
        _wait(leaving)


def _params(remote, collective_id):
    if not remote:
        return pltpu.CompilerParams(dimension_semantics=("arbitrary",), vmem_limit_bytes=VMEM_BYTES)
    return pltpu.CompilerParams(
        dimension_semantics=("arbitrary",),
        vmem_limit_bytes=VMEM_BYTES,
        collective_id=collective_id,
        has_side_effects=True,
    )


def post_forward(att, hidden, rows, up_bias, gathered, n_head, last, remote, collective_id):
    own_rows = hidden.shape[0]
    pieces, places = gathered
    count = len(places)
    unit_rows = D // 32
    vmem = pl.BlockSpec(memory_space=pltpu.VMEM)
    hbm = pl.BlockSpec(memory_space=pl.ANY)
    column = pl.BlockSpec((own_rows, CHUNK), lambda at: (0, at))
    fixed = lambda leaf_rows: pl.BlockSpec((leaf_rows, D), lambda at: (0, 0))
    whole = lambda dtype: jax.ShapeDtypeStruct((own_rows, D), dtype)
    wide = jax.ShapeDtypeStruct((own_rows, FF), bf16)
    weight = lambda *lead: pltpu.VMEM(lead + (4, 2, 4, unit_rows), bf16)
    normed_rows = 16 if last else own_rows
    return pl.pallas_call(
        functools.partial(post_forward_kernel, n_head, places, last, remote),
        grid=(FF // CHUNK,),
        out_shape=(
            whole(f32),
            jax.ShapeDtypeStruct((normed_rows, D), bf16),
            whole(f32),
            wide,
            wide,
            whole(f32),
            whole(f32),
            whole(bf16),
            whole(bf16),
        ),
        in_specs=[hbm if remote else vmem, vmem, vmem, pl.BlockSpec((1, CHUNK), lambda at: (0, at))]
        + [hbm] * count,
        out_specs=(fixed(own_rows), fixed(normed_rows), fixed(own_rows), column, column, hbm, hbm, hbm, hbm),
        scratch_shapes=[
            pltpu.VMEM((4, 2, 4, unit_rows, D), bf16),
            pltpu.VMEM((2, 4, 2, 4, unit_rows, CHUNK), bf16),
            pltpu.VMEM((2, 4, 2, 4, unit_rows, CHUNK), bf16),
            pltpu.VMEM((own_rows, D), bf16),
            pltpu.VMEM((own_rows, D), f32),
            pltpu.VMEM((own_rows, D), f32),
            pltpu.VMEM((own_rows, D), bf16),
            pltpu.VMEM((own_rows, D), f32),
            pltpu.SemaphoreType.DMA((count,)),
            pltpu.SemaphoreType.DMA((2, count)),
            pltpu.SemaphoreType.DMA((2, count)),
            pltpu.SemaphoreType.DMA((4,)),
            pltpu.SemaphoreType.DMA((n_head,)),
            pltpu.SemaphoreType.DMA((n_head,)),
        ],
        compiler_params=_params(remote, collective_id),
        cost_estimate=pl.CostEstimate(
            flops=2 * own_rows * D * (D + 2 * FF),
            bytes_accessed=2 * D * (D + 2 * FF) + own_rows * (22 * D + 4 * FF),
            transcendentals=2 * own_rows * FF,
        ),
    )(att, hidden, rows, up_bias, *pieces)


def post_backward_kernel(n_head, places, remote, *refs):
    count = len(places)
    own_places = [("head", 0, 4, 0, to) for to in range(4)] if remote else [None]
    far_places = [("head", 0, 4, 1, to) for to in range(4)] if remote else []
    out_count = len(own_places)
    att_ref, grad_ref, down_ref, branch_ref, after_ref, two_ref, rows_ref, act_ref, slope_ref, refs = *refs[:9], refs[9:]
    weight_refs, refs = refs[:count], refs[count:]
    d_att_ref, d_after_ref, sums_ref, up_sum_ref, refs = *refs[:4], refs[4:]
    own_refs, refs = refs[:out_count], refs[out_count:]
    got_refs, refs = refs[: len(far_places)], refs[len(far_places) :]
    proj_s, up_s, down_s, d_proj_s, d_up_s, d_down_s, att_s, low_s, low_t, two_t, acc, refs = *refs[:11], refs[11:]
    proj_sem, up_sem, down_sem, own_sem, far_sem, got_sem, send_sem, recv_sem = refs
    at = pl.program_id(0)
    chunks = pl.num_programs(0)
    width = D // n_head

    def fetch(chunk, slot):
        up_at, down_at = UP_AT + chunk * CHUNK, DOWN_AT + chunk * CHUNK
        return _copies(weight_refs, places, up_s.at[slot], up_at, CHUNK, up_sem.at[slot], True) + _copies(
            weight_refs, places, down_s.at[slot], down_at, CHUNK, down_sem.at[slot], True
        )

    def stay(whole, column, size, lane):
        return _copies(own_refs, own_places, whole, column, size, own_sem.at[lane], False)

    def away(whole, column, size, lane, mark):
        return [
            _send(
                _slot(whole, place),
                _cols(got_refs[to], column, size),
                far_sem.at[lane, to],
                got_sem.at[mark, to],
                _sibling(),
            )
            for to, place in enumerate(far_places)
        ]

    def over(chunk, slot):
        up_at, down_at = UP_AT + chunk * CHUNK, DOWN_AT + chunk * CHUNK
        return away(d_up_s.at[slot], up_at, CHUNK, slot, chunk) + away(
            d_down_s.at[slot], down_at, CHUNK, 2 + slot, chunks + chunk
        )

    def leave(chunk, slot):
        up_at, down_at = UP_AT + chunk * CHUNK, DOWN_AT + chunk * CHUNK
        local = stay(d_up_s.at[slot], up_at, CHUNK, slot) + stay(d_down_s.at[slot], down_at, CHUNK, 2 + slot)
        return local, over(chunk, slot)

    def left(pair):
        _wait(pair[0])
        for move in pair[1]:
            move.wait_send()

    proj = lambda: _copies(weight_refs, places, proj_s, PROJ_AT, D, proj_sem, True)

    @pl.when(at == 0)
    def _():
        if remote:
            _greet([_mate(step) for step in range(1, n_head)] + [_sibling()])
        _start(fetch(0, 0))
        _start(proj())
        grad = grad_ref[...]
        low = (rows_ref[2:3, :] * grad).astype(bf16)
        low_s[...] = low
        low_t[...] = jnp.transpose(low)
        two_t[...] = jnp.transpose(two_ref[...])
        sums_ref[...] = jnp.zeros_like(sums_ref)
        sums_ref[0:1, :] = jnp.sum(grad * down_ref[...], axis=0, keepdims=True)
        sums_ref[1:2, :] = jnp.sum(low.astype(f32), axis=0, keepdims=True)
        acc[...] = jnp.zeros_like(acc)

    @pl.when(at + 1 < chunks)
    def _():
        _start(fetch(at + 1, lax.rem(at + 1, 2)))

    slot = lax.rem(at, 2)
    _wait(fetch(at, slot))

    @pl.when(at >= 2)
    def _():
        left(leave(at - 2, slot))

    d_act = jnp.dot(low_s[...], _flat(down_s[slot]), preferred_element_type=f32)
    d_expand = (slope_ref[...].astype(f32) * d_act).astype(bf16)
    up_sum_ref[...] = jnp.sum(d_expand.astype(f32), axis=0, keepdims=True)
    acc[...] += lax.dot_general(d_expand, _flat(up_s[slot]), NT, preferred_element_type=f32)
    shape = d_up_s.shape[1:]
    d_up_s[slot] = jnp.dot(two_t[...], d_expand, preferred_element_type=f32).astype(bf16).reshape(shape)
    d_down_s[slot] = jnp.dot(low_t[...], act_ref[...], preferred_element_type=f32).astype(bf16).reshape(shape)
    for moves in leave(at, slot):
        _start(moves)

    @pl.when(at == chunks - 1)
    def _():
        d_two = acc[...]
        unit, scale = _norm(after_ref[...])
        sums_ref[2:3, :] = jnp.sum(d_two * unit, axis=0, keepdims=True)
        sums_ref[3:4, :] = jnp.sum(d_two, axis=0, keepdims=True)
        d_unit = d_two * rows_ref[1:2, :]
        inner = jnp.mean(d_unit, axis=-1, keepdims=True)
        cross = jnp.mean(d_unit * unit, axis=-1, keepdims=True)
        d_after = grad_ref[...] + scale * (d_unit - inner - unit * cross)
        d_after_ref[...] = d_after
        sums_ref[4:5, :] = jnp.sum(d_after * branch_ref[...], axis=0, keepdims=True)
        d_branch = (rows_ref[0:1, :] * d_after).astype(bf16)
        sums_ref[5:6, :] = jnp.sum(d_branch.astype(f32), axis=0, keepdims=True)
        d_proj_s[...] = (
            lax.dot_general(d_branch, att_ref[...], TN, preferred_element_type=f32)
            .astype(bf16)
            .reshape(d_proj_s.shape)
        )
        gone = stay(d_proj_s, PROJ_AT, D, 4), away(d_proj_s, PROJ_AT, D, 4, 2 * chunks)
        for moves in gone:
            _start(moves)
        _wait(proj())
        d_att = jnp.dot(d_branch, _flat(proj_s[...]), preferred_element_type=f32).astype(bf16)
        if remote:
            rows = d_att.shape[0]
            att_s[...] = d_att
            moves = [
                _send(
                    att_s.at[:, pl.ds(_own_column(step, n_head), width)],
                    d_att_ref.at[pl.ds(step * rows, rows)],
                    send_sem.at[step],
                    recv_sem.at[step],
                    _mate(step),
                )
                for step in range(1, n_head)
            ]
            own = att_s.at[:, pl.ds(_own_column(0, n_head), width)]
            moves.append(pltpu.make_async_copy(own, d_att_ref.at[pl.ds(0, rows)], send_sem.at[0]))
            _start(moves)
            _wait(moves)
        else:
            d_att_ref[...] = d_att
        left(leave(at - 1, 1 - slot))
        left(leave(at, slot))
        left(gone)
        if remote:

            def arrive(chunk, _):
                for move in over(chunk, 0):
                    move.wait_recv()
                return 0

            lax.fori_loop(0, chunks, arrive, 0)
            for move in gone[1]:
                move.wait_recv()


def post_backward(att, grad, down_out, branch, after, two, rows, act, slope, gathered, n_head, remote, collective_id):
    own_rows = grad.shape[0]
    pieces, places = gathered
    count = len(places)
    unit_rows = D // 32
    vmem = pl.BlockSpec(memory_space=pltpu.VMEM)
    hbm = pl.BlockSpec(memory_space=pl.ANY)
    column = pl.BlockSpec((own_rows, CHUNK), lambda at: (0, at))
    fixed = lambda *shape: pl.BlockSpec(shape, lambda at: (0, 0))
    width = D // n_head
    chunks = FF // CHUNK
    if remote:
        d_att_shape, d_att_spec = (n_head * own_rows, width), hbm
        grads = [jax.ShapeDtypeStruct((4, unit_rows, WIDE), bf16)] * 8
    else:
        d_att_shape, d_att_spec = (own_rows, D), fixed(own_rows, D)
        grads = [jax.ShapeDtypeStruct((4, 2, 4, unit_rows, WIDE), bf16)]
    sems = pltpu.SemaphoreType.DMA
    outs = pl.pallas_call(
        functools.partial(post_backward_kernel, n_head, places, remote),
        grid=(chunks,),
        out_shape=tuple(
            [
                jax.ShapeDtypeStruct(d_att_shape, bf16),
                jax.ShapeDtypeStruct((own_rows, D), f32),
                jax.ShapeDtypeStruct((8, D), f32),
                jax.ShapeDtypeStruct((1, FF), f32),
            ]
            + grads
        ),
        in_specs=[vmem] * 7 + [column, column] + [hbm] * count,
        out_specs=tuple(
            [d_att_spec, fixed(own_rows, D), fixed(8, D), pl.BlockSpec((1, CHUNK), lambda at: (0, at))]
            + [hbm] * len(grads)
        ),
        scratch_shapes=[
            pltpu.VMEM((4, 2, 4, unit_rows, D), bf16),
            pltpu.VMEM((2, 4, 2, 4, unit_rows, CHUNK), bf16),
            pltpu.VMEM((2, 4, 2, 4, unit_rows, CHUNK), bf16),
            pltpu.VMEM((4, 2, 4, unit_rows, D), bf16),
            pltpu.VMEM((2, 4, 2, 4, unit_rows, CHUNK), bf16),
            pltpu.VMEM((2, 4, 2, 4, unit_rows, CHUNK), bf16),
            pltpu.VMEM((own_rows, D), bf16),
            pltpu.VMEM((own_rows, D), bf16),
            pltpu.VMEM((D, own_rows), bf16),
            pltpu.VMEM((D, own_rows), bf16),
            pltpu.VMEM((own_rows, D), f32),
            sems((count,)),
            sems((2, count)),
            sems((2, count)),
            sems((5, 4)),
            sems((5, 4)),
            sems((2 * chunks + 1, 4)),
            sems((n_head,)),
            sems((n_head,)),
        ],
        compiler_params=_params(remote, collective_id),
        cost_estimate=pl.CostEstimate(
            flops=4 * own_rows * D * (D + 2 * FF),
            bytes_accessed=4 * D * (D + 2 * FF) + own_rows * (22 * D + 4 * FF),
            transcendentals=0,
        ),
    )(att, grad, down_out, branch, after, two, rows, act, slope, *pieces)
    d_att, d_after, sums, up_sum, grads = *outs[:4], list(outs[4:])
    return d_att, d_after, sums, up_sum[0], (grads[:4], grads[4:]) if remote else (grads, grads)


def layer_norm(values, gain, shift):
    centered = values - jnp.mean(values, axis=-1, keepdims=True)
    spread_ = jnp.mean(centered * centered, axis=-1, keepdims=True)
    return centered * lax.rsqrt(spread_ + norm_eps) * gain + shift


def unpack(vector_row):
    lengths = (D, D, 3 * D, D, D, D, D, FF, D, D, HD, HD, HD, HD)
    pieces = []
    offset = 0
    for length in lengths:
        pieces.append(vector_row[offset : offset + length])
        offset = offset + length
    return pieces


def head_gains(vec, heads):
    rows = [jnp.tile(piece, heads) for piece in vec[10:14]]
    return jnp.concatenate([jnp.stack(rows), jnp.zeros((4, heads * HD), f32)], axis=0)


def adam_update(
    weight, gradient, moment_one, moment_two, average, step_rate, decay_rate, clip_scale, fix_one, fix_two
):
    clipped = gradient * clip_scale
    moment_one = beta_one * moment_one + (1.0 - beta_one) * clipped
    moment_two = beta_two * moment_two + (1.0 - beta_two) * clipped * clipped
    first_hat = moment_one / fix_one
    second_hat = moment_two / fix_two
    weight = weight - step_rate * (
        first_hat / (jnp.sqrt(second_hat) + adam_eps) + decay_rate * weight
    )
    average = ema_decay * average + (1.0 - ema_decay) * weight
    return (weight, moment_one, moment_two, average)


def body(
    links,
    tokens,
    cotangent,
    slot_frame,
    step_count,
    *params,
):
    n_tok, n_head = links.n_tok, links.n_head
    devices = n_tok * n_head
    own = lax.axis_index("head")
    flip = lambda leaf: jnp.swapaxes(leaf, 1, 2)
    groups = []
    for at in range(0, 20, 5):
        qkv, proj, fc1, fc2, vec = params[at : at + 5]
        groups.append([qkv, flip(proj), fc1, flip(fc2), vec])
    masters = groups[0]

    slots = slot_frame.shape[0]
    per_head = slots // n_head
    held = slot_frame.reshape(n_head, per_head)
    held = jnp.concatenate(
        [lax.dynamic_slice_in_dim(held, own ^ step, 1, 0)[0] for step in range(n_head)]
    )
    index = jnp.arange(slots, dtype=jnp.int32)
    ahead = (held[None, :] < held[:, None]) | (
        (held[None, :] == held[:, None]) & (index[None, :] < index[:, None])
    )
    rank = jnp.sum(ahead.astype(jnp.int32), axis=1)
    order = jnp.sum(jnp.where(rank[None, :] == index[:, None], index[None, :], 0), axis=1).astype(jnp.int32)
    is_hi = (jnp.sum((held == held[0]).astype(jnp.int32)) == HI_BLOCKS).astype(jnp.int32).reshape(1)
    spans = (
        (HI_BLOCKS * BLOCK, LO_BLOCKS * BLOCK),
        (FRAMES * HI_BLOCKS * BLOCK, FRAMES * LO_BLOCKS * BLOCK),
    )

    vec_here = masters[4].shape[1]
    tile = lax.reduce_precision(masters[4], 8, 7).reshape(-1)
    tile = jnp.pad(tile, (0, 1024 - tile.shape[0])).reshape(8, 128)
    tiles = spread(tile, n_tok, n_head, 0).reshape(devices, 1024)[:, : 2 * vec_here]
    vectors = jnp.swapaxes(tiles.reshape(devices, 2, vec_here), 0, 1).reshape(2, devices * vec_here)
    vecs = [unpack(vectors[block]) for block in range(2)]

    qkv_low = [masters[0][block].astype(bf16) for block in range(2)]
    low = [
        jnp.concatenate([masters[kind][block].astype(bf16) for kind in (1, 2, 3)], axis=1)
        for block in range(2)
    ]
    places = links.gather_places()
    paired = links.paired
    width = D // n_head
    heads = width // HD
    own_rows = tokens.shape[0]
    cut = lambda rows: [rows[step * own_rows : (step + 1) * own_rows] for step in range(n_head)]
    gains = [head_gains(vec, heads) for vec in vecs]

    def attend(block, pieces, qkv_cols):
        qkv_bias = lax.dynamic_slice_in_dim(vecs[block][2].reshape(3, D), own * width, width, 1)
        return attention_forward(
            pieces, qkv_cols, qkv_bias.reshape(1, 3 * width), gains[block], order, is_hi, spans[block]
        )

    def enter(rows, mine, shard, collective_id):
        if paired:
            return enter_rows(rows, mine, shard, collective_id)
        planes = None if shard is None else links.gather_planes(shard)
        return links.rows_in(rows), lax.all_gather(mine, "tok", axis=0, tiled=True), planes

    def post(block, attended, hidden, pieces):
        vec, tail = vecs[block], vecs[1]
        rows = jnp.stack([vec[3], vec[4], vec[5], vec[6], vec[8], vec[9], tail[0], tail[1]])
        if not paired:
            attended = jnp.concatenate(links.by_index(links.exchange(cut(attended)), own), axis=1)
        return post_forward(
            attended,
            hidden,
            rows,
            vec[7].reshape(1, FF),
            (pieces, places),
            n_head,
            block == 1,
            paired,
            3 + block,
        )

    hidden_in = [tokens.astype(f32), None]
    normed = layer_norm(hidden_in[0], vecs[0][0], vecs[0][1]).astype(bf16)
    group, qkv_cols, saved, att_owns, mids, weights = ([None, None] for _ in range(6))

    mine = links.fetch_heads(qkv_low, own)
    normed, mine, low[0] = together(normed, mine, low[0])
    group[0], qkv_cols[0], planes = enter(normed, mine[0], low[0], 5)
    group[0], planes, qkv_cols[0], low[1] = together(group[0], planes, qkv_cols[0], low[1])
    near = links.gather_sides(planes)
    planes = links.gather_planes(low[1])
    saved[0] = attend(0, group[0], qkv_cols[0])
    saved[0], near, planes = together(saved[0], near, planes)
    weights[0] = links.gather_far(near)
    hidden_in[1], normed, *mids[0] = post(0, saved[0][0], hidden_in[0], weights[0])

    group[1], qkv_cols[1], _planes = enter(normed, mine[1], None, 6)
    group[1], planes = together(group[1], planes)
    near = links.gather_sides(planes)
    saved[1] = attend(1, group[1], qkv_cols[1])
    saved[1], near = together(saved[1], near)
    weights[1] = links.gather_far(near)
    hidden, _normed, *mids[1] = post(1, saved[1][0], hidden_in[1], weights[1])

    def post_back(block, grad):
        vec = vecs[block]
        down, act, slope, branch, after, two, att_own = mids[block]
        rows = jnp.stack([vec[4], vec[5], vec[9]] + [vec[9]] * 5)
        d_att, *rest = post_backward(
            att_own,
            grad,
            down,
            branch,
            after,
            two,
            rows,
            act,
            slope,
            (weights[block], places),
            n_head,
            paired,
            7 + block,
        )
        if not paired:
            parts = [
                lax.dynamic_slice_in_dim(d_att, (own ^ step) * width, width, 1) for step in range(n_head)
            ]
            d_att = jnp.concatenate(links.exchange(parts), axis=0)
        return d_att, *rest

    def attend_back(block, grad_heads):
        attended, raw, values, lse = saved[block]
        return attention_backward(
            raw, values, grad_heads, attended, lse, gains[block], order, is_hi, spans[block]
        )

    def rows_back(block, d_qkv, d_after):
        gain, shift = vecs[block][0], vecs[block][1]
        if paired:
            grad, sums = rows_out(
                d_qkv, qkv_cols[block], hidden_in[block], d_after, gain.reshape(1, D), 9 + block
            )
            return grad, sums[0], sums[1]
        d_normed = jnp.einsum("rc,dc->rd", d_qkv, qkv_cols[block], preferred_element_type=f32)
        back = links.rows_out(cut(d_normed.astype(bf16)))
        d_hidden, d_gain, d_shift = jax.vjp(layer_norm, hidden_in[block], gain, shift)[1](back)
        return d_after + d_hidden, d_gain, d_shift

    def qkv_grad(block, d_qkv):
        rows = jnp.concatenate(group[block], axis=0)
        return jnp.einsum("rd,rc->dc", rows, d_qkv, preferred_element_type=f32).astype(bf16)

    def vector_grad(norm_sums, sums, d_up_bias, head_sums, bias_sums):
        d_qkv_bias = lax.dynamic_update_slice_in_dim(
            jnp.zeros((3, D), f32), bias_sums[0].reshape(3, width), own * width, 1
        ).reshape(3 * D)
        head_sums = jnp.sum(head_sums[:4].reshape(4, heads, HD), axis=1).reshape(4 * HD)
        parts = [*norm_sums, d_qkv_bias, sums[5], sums[4], sums[2], sums[3], d_up_bias, sums[1], sums[0], head_sums]
        return jnp.concatenate(parts)

    d_att, d_after, sums, d_up_bias, grads = post_back(1, cotangent.astype(f32))
    grads = links.scatter_start(*grads)
    d_att, grads = together(d_att, grads)
    grads = links.scatter_first(grads)
    d_qkv, head_sums, bias_sums = attend_back(1, d_att)
    d_qkv, head_sums, bias_sums, grads = together(d_qkv, head_sums, bias_sums, grads)
    grad_rows, *norm_sums = rows_back(1, d_qkv, d_after)
    dw_qkv = qkv_grad(1, d_qkv)
    d_vec_one = vector_grad(norm_sums, sums, d_up_bias, head_sums, bias_sums)
    grad_rows, grads, dw_qkv = together(grad_rows, grads, dw_qkv)
    grads_one = links.scatter_second(grads)
    mine_one = links.return_planes(links.return_cores(dw_qkv))

    d_att, d_after, sums, d_up_bias, grads = post_back(0, grad_rows)
    d_att, grads_one, mine_one, grads = together(d_att, grads_one, mine_one, grads)
    grads = links.scatter_start(*grads)
    d_att, grads, grads_one = together(d_att, grads, grads_one)
    sum_one = links.scatter_last(grads_one)
    grads = links.scatter_first(grads)
    d_qkv, head_sums, bias_sums = attend_back(0, d_att)
    d_qkv, head_sums, bias_sums, grads, sum_one = together(d_qkv, head_sums, bias_sums, grads, sum_one)
    grad_rows, *norm_sums = rows_back(0, d_qkv, d_after)
    dw_qkv = links.return_cores(qkv_grad(0, d_qkv))
    d_vectors = [vector_grad(norm_sums, sums, d_up_bias, head_sums, bias_sums), d_vec_one]
    sum_zero = links.scatter_last(links.scatter_second(grads))
    qkv_zero, qkv_one = links.return_heads([links.return_planes(dw_qkv), mine_one], own)
    summed = []
    for qkv_part, rest in ((qkv_zero, sum_zero), (qkv_one, sum_one)):
        summed.append([qkv_part, rest[:, PROJ_AT:UP_AT], rest[:, UP_AT:DOWN_AT], rest[:, DOWN_AT:WIDE]])
    d_tiles = jnp.swapaxes(jnp.stack(d_vectors).reshape(2, devices, vec_here), 0, 1).reshape(devices, -1)
    d_tiles = jnp.pad(d_tiles, ((0, 0), (0, 1024 - d_tiles.shape[1]))).reshape(devices, 8, 128)
    d_vec = swap(d_tiles, n_tok, n_head, 1).reshape(1024)[: 2 * vec_here].reshape(2, vec_here)
    gradients = [jnp.stack([summed[0][kind], summed[1][kind]]) for kind in range(4)] + [d_vec]
    local_square = sum((jnp.sum(gradient * gradient) for gradient in gradients))
    squares = spread(jnp.broadcast_to(local_square, (8, 128)), n_tok, n_head, 2)
    grad_norm = jnp.sqrt(jnp.sum(squares[:, 0, 0]))
    clip_scale = clip_norm / jnp.maximum(grad_norm, clip_norm)
    step_float = step_count[0].astype(f32)
    fix_one = 1.0 - beta_one**step_float
    fix_two = 1.0 - beta_two**step_float
    updates = [
        adam_update(
            groups[0][kind],
            gradients[kind],
            groups[1][kind],
            groups[2][kind],
            groups[3][kind],
            step_rates[kind],
            decays[kind],
            clip_scale,
            fix_one,
            fix_two,
        )
        for kind in range(5)
    ]
    outs = [hidden, grad_rows, grad_norm]
    for part in range(4):
        for kind in range(5):
            leaf = updates[kind][part]
            outs.append(flip(leaf) if kind in (1, 3) else leaf)
    return tuple(outs)


def solution(mesh):
    rows = P(BOTH, None)
    kinds = (
        P(None, BOTH, None),
        P(None, None, BOTH),
        P(None, BOTH, None),
        P(None, None, BOTH),
        P(None, BOTH),
    )
    in_specs = (rows, rows, P("tok"), P()) + kinds * 4
    out_specs = (rows, rows, P()) + kinds * 4
    return jax.shard_map(
        functools.partial(body, Links(mesh)),
        mesh=mesh,
        in_specs=in_specs,
        out_specs=out_specs,
        check_vma=False,
    )
```

```python
import functools
import math

import jax
import jax.numpy as jnp
from jax import lax
from jax.experimental import pallas as pl
from jax.experimental.pallas import tpu as pltpu
from jax.sharding import PartitionSpec as P

D = 1024
HD = 64
FF = 4096
BLOCK = 128
HI_BLOCKS = 8
LO_BLOCKS = 4
FRAMES = 2

norm_eps = 1e-06
clip_norm = 1.0
beta_one = 0.9
beta_two = 0.999
adam_eps = 1e-08
ema_decay = 0.7
step_rates = (0.05, 0.4, 0.05, 0.025, 0.3)
decays = (0.05, 0.05, 0.05, 0.05, 0.0)

LOG2E = math.log2(math.e)
SPAN = 512
MESH_ID = pl.DeviceIdType.MESH
BOTH = ("tok", "head")
bf16 = jnp.bfloat16
f32 = jnp.float32
VMEM_BYTES = 60 << 20


def _peer(step, n_tok, n_head):
    n = n_tok * n_head
    me = lax.axis_index("tok") * n_head + lax.axis_index("head")
    to = lax.rem(me + step, n)
    return me, to, (to // n_head, lax.rem(to, n_head))


def _enter(n_tok, n_head):
    n = n_tok * n_head
    barrier = pltpu.get_barrier_semaphore()

    def greet(step, _):
        _, _, device = _peer(step, n_tok, n_head)
        pl.semaphore_signal(barrier, inc=1, device_id=device, device_id_type=MESH_ID)
        return 0

    lax.fori_loop(1, n, greet, 0)
    pl.semaphore_wait(barrier, n - 1)


def spread_kernel(n_tok, n_head, x_ref, o_ref, send_sem, recv_sem):
    n = n_tok * n_head
    _enter(n_tok, n_head)
    me = lax.axis_index("tok") * n_head + lax.axis_index("head")
    o_ref[me] = x_ref[...]

    def copy(step):
        me, _, device = _peer(step, n_tok, n_head)
        return pltpu.make_async_remote_copy(
            src_ref=x_ref,
            dst_ref=o_ref.at[me],
            send_sem=send_sem.at[step],
            recv_sem=recv_sem.at[step],
            device_id=device,
            device_id_type=MESH_ID,
        )

    def start(step, _):
        copy(step).start()
        return 0

    def finish(step, _):
        copy(step).wait()
        return 0

    lax.fori_loop(1, n, start, 0)
    lax.fori_loop(1, n, finish, 0)


def swap_kernel(n_tok, n_head, x_ref, o_ref, land, send_sem, recv_sem):
    n = n_tok * n_head
    _enter(n_tok, n_head)
    me = lax.axis_index("tok") * n_head + lax.axis_index("head")

    def copy(step):
        me, to, device = _peer(step, n_tok, n_head)
        return pltpu.make_async_remote_copy(
            src_ref=x_ref.at[to],
            dst_ref=land.at[step],
            send_sem=send_sem.at[step],
            recv_sem=recv_sem.at[step],
            device_id=device,
            device_id_type=MESH_ID,
        )

    def start(step, _):
        copy(step).start()
        return 0

    def finish(step, _):
        copy(step).wait()
        return 0

    lax.fori_loop(1, n, start, 0)
    lax.fori_loop(1, n, finish, 0)
    o_ref[...] = x_ref[me] + jnp.sum(land[1:], axis=0)


def spread(tile, n_tok, n_head, collective_id):
    n = n_tok * n_head
    return pl.pallas_call(
        functools.partial(spread_kernel, n_tok, n_head),
        out_shape=jax.ShapeDtypeStruct((n,) + tile.shape, tile.dtype),
        in_specs=[pl.BlockSpec(memory_space=pltpu.VMEM)],
        out_specs=pl.BlockSpec(memory_space=pltpu.VMEM),
        scratch_shapes=[pltpu.SemaphoreType.DMA((n,)), pltpu.SemaphoreType.DMA((n,))],
        compiler_params=pltpu.CompilerParams(collective_id=collective_id, has_side_effects=True),
    )(tile)


def swap(tiles, n_tok, n_head, collective_id):
    n = n_tok * n_head
    return pl.pallas_call(
        functools.partial(swap_kernel, n_tok, n_head),
        out_shape=jax.ShapeDtypeStruct(tiles.shape[1:], tiles.dtype),
        in_specs=[pl.BlockSpec(memory_space=pltpu.VMEM)],
        out_specs=pl.BlockSpec(memory_space=pltpu.VMEM),
        scratch_shapes=[
            pltpu.VMEM(tiles.shape, tiles.dtype),
            pltpu.SemaphoreType.DMA((n,)),
            pltpu.SemaphoreType.DMA((n,)),
        ],
        compiler_params=pltpu.CompilerParams(collective_id=collective_id, has_side_effects=True),
    )(tiles)


def _lane_mean(values, grouping):
    top = values.astype(bf16)
    rest = (values - top.astype(f32)).astype(bf16)
    return jnp.dot(top, grouping, preferred_element_type=f32) + jnp.dot(
        rest, grouping, preferred_element_type=f32
    )


def _grouping(width):
    row = lax.broadcasted_iota(jnp.int32, (width, width), 0) // HD
    col = lax.broadcasted_iota(jnp.int32, (width, width), 1) // HD
    return jnp.where(row == col, 1.0 / HD, 0.0).astype(bf16)


def _unit(values, grouping):
    centered = values - _lane_mean(values, grouping)
    spread_ = _lane_mean(centered * centered, grouping)
    scale = lax.rsqrt(spread_ + norm_eps)
    return centered * scale, scale


def _only(values, head):
    lane = lax.broadcasted_iota(jnp.int32, values.shape, 1)
    return jnp.where(lane // HD == head, values, jnp.zeros_like(values))


NT = (((1,), (1,)), ((), ()))
TN = (((0,), (0,)), ((), ()))


def forward_kernel(
    heads, pieces, spans, tile_rows, order_ref, hi_ref, *refs
):
    x_refs = refs[:pieces]
    w_ref, bias_ref, gains_ref, att_ref, raw_ref, val_ref, lse_ref, q_s, k_s, v_s, acc = refs[pieces:]
    width = heads * HD
    rows = att_ref.shape[0]
    blocks = rows // BLOCK
    piece_rows = rows // pieces
    for at in range(pieces):
        full = jnp.dot(x_refs[at][...], w_ref[...], preferred_element_type=f32) + bias_ref[...]
        here = pl.ds(at * piece_rows, piece_rows)
        raw_ref[here, :] = full[:, : 2 * width]
        val_ref[here, :] = full[:, 2 * width :].astype(bf16)
    grouping = _grouping(width)

    def place(at, _):
        here = pl.ds(pl.multiple_of(order_ref[at] * BLOCK, BLOCK), BLOCK)
        there = pl.ds(pl.multiple_of(at * BLOCK, BLOCK), BLOCK)
        unit_q, _s = _unit(raw_ref[here, :width], grouping)
        unit_k, _s = _unit(raw_ref[here, width:], grouping)
        q_s[there, :] = ((unit_q * gains_ref[0:1, :] + gains_ref[1:2, :]) * HD ** (-0.5)).astype(bf16)
        key = (unit_k * gains_ref[2:3, :] + gains_ref[3:4, :]).astype(bf16)
        value = val_ref[here, :]
        for head in range(heads):
            k_s[head, there, :] = _only(key, head)
            v_s[head, there, :] = _only(value, head)
        return 0

    lax.fori_loop(0, blocks, place, 0)
    per_tile = tile_rows // BLOCK

    def attend(span):
        def tile(at, _):
            here = pl.ds(pl.multiple_of(at * tile_rows, tile_rows), tile_rows)
            first = at * tile_rows // span * span
            there = pl.ds(pl.multiple_of(first, span), span)
            query = q_s[here, :]
            lane = lax.broadcasted_iota(jnp.int32, (tile_rows, 128), 1)
            logs = jnp.zeros((tile_rows, 128), f32)
            for head in range(heads):
                scores = lax.dot_general(query, k_s[head, there, :], NT, preferred_element_type=f32)
                top = jnp.max(scores, axis=1, keepdims=True) * LOG2E
                probs = jnp.exp2(scores * LOG2E - top)
                total = jnp.sum(probs, axis=1, keepdims=True)
                part = jnp.dot(
                    probs.astype(bf16), v_s[head, there, :], preferred_element_type=f32
                ) / total
                if head == 0:
                    acc[...] = part
                else:
                    acc[...] += part
                logs = jnp.where(lane == head, top + jnp.log2(total), logs)
            lse_ref[here, :] = logs
            for sub in range(per_tile):
                out = pl.ds(pl.multiple_of(order_ref[at * per_tile + sub] * BLOCK, BLOCK), BLOCK)
                att_ref[out, :] = acc[sub * BLOCK : (sub + 1) * BLOCK, :].astype(bf16)
            return 0

        lax.fori_loop(0, rows // tile_rows, tile, 0)

    @pl.when(hi_ref[0] == 1)
    def _():
        attend(spans[0])

    @pl.when(hi_ref[0] == 0)
    def _():
        attend(spans[1])


def attention_forward(pieces, weight, bias, gains, order, is_hi, spans):
    heads = weight.shape[1] // (3 * HD)
    width = heads * HD
    rows = sum(piece.shape[0] for piece in pieces)
    tile_rows = 256
    smem = pl.BlockSpec(memory_space=pltpu.SMEM)
    vmem = pl.BlockSpec(memory_space=pltpu.VMEM)
    flops = 2 * rows * (D * 3 * width + 8 * spans[0] * width)
    return pl.pallas_call(
        functools.partial(forward_kernel, heads, len(pieces), spans, tile_rows),
        out_shape=(
            jax.ShapeDtypeStruct((rows, width), bf16),
            jax.ShapeDtypeStruct((rows, 2 * width), f32),
            jax.ShapeDtypeStruct((rows, width), bf16),
            jax.ShapeDtypeStruct((rows, 128), f32),
        ),
        in_specs=[smem, smem] + [vmem] * (len(pieces) + 3),
        out_specs=(vmem,) * 4,
        scratch_shapes=[
            pltpu.VMEM((rows, width), bf16),
            pltpu.VMEM((heads, rows, width), bf16),
            pltpu.VMEM((heads, rows, width), bf16),
            pltpu.VMEM((tile_rows, width), f32),
        ],
        compiler_params=pltpu.CompilerParams(vmem_limit_bytes=VMEM_BYTES),
        cost_estimate=pl.CostEstimate(
            flops=flops, bytes_accessed=rows * (2 * D + 14 * width), transcendentals=rows * spans[0] * heads
        ),
    )(order, is_hi, *pieces, weight, bias, gains)


def backward_kernel(
    heads,
    spans,
    order_ref,
    hi_ref,
    raw_ref,
    val_ref,
    grad_ref,
    att_ref,
    lse_ref,
    gains_ref,
    out_ref,
    sums_ref,
    bias_ref,
    q_s,
    o_s,
    k_m,
    v_m,
    q_m,
    o_m,
    dq_s,
    dk_s,
    dv_s,
    lse_t,
    delta_t,
):
    width = heads * HD
    rows = val_ref.shape[0]
    blocks = rows // BLOCK
    grouping = _grouping(width)
    head_of = lax.broadcasted_iota(jnp.int32, (8, width), 1) // HD
    picks = jnp.where(head_of == lax.broadcasted_iota(jnp.int32, (8, width), 0), 1.0, 0.0).astype(bf16)

    def place(at, _):
        here = pl.ds(pl.multiple_of(order_ref[at] * BLOCK, BLOCK), BLOCK)
        there = pl.ds(pl.multiple_of(at * BLOCK, BLOCK), BLOCK)
        unit_q, _s = _unit(raw_ref[here, :width], grouping)
        unit_k, _s = _unit(raw_ref[here, width:], grouping)
        query = ((unit_q * gains_ref[0:1, :] + gains_ref[1:2, :]) * HD ** (-0.5)).astype(bf16)
        key = (unit_k * gains_ref[2:3, :] + gains_ref[3:4, :]).astype(bf16)
        value = val_ref[here, :]
        grad = grad_ref[here, :]
        q_s[there, :] = query
        o_s[there, :] = grad
        for head in range(heads):
            k_m[head, there, :] = _only(key, head)
            v_m[head, there, :] = _only(value, head)
            q_m[head, there, :] = _only(query, head)
            o_m[head, there, :] = _only(grad, head)
        both = grad.astype(f32) * att_ref[here, :].astype(f32)
        top = both.astype(bf16)
        rest = (both - top.astype(f32)).astype(bf16)
        delta_t[:, there] = lax.dot_general(picks, top, NT, preferred_element_type=f32) + lax.dot_general(
            picks, rest, NT, preferred_element_type=f32
        )
        lse_t[:, there] = jnp.transpose(lse_ref[there, :])[:8, :]
        dq_s[there, :] = jnp.zeros((BLOCK, width), f32)
        dk_s[there, :] = jnp.zeros((BLOCK, width), f32)
        dv_s[there, :] = jnp.zeros((BLOCK, width), f32)
        return 0

    lax.fori_loop(0, blocks, place, 0)
    span = jnp.where(hi_ref[0] == 1, spans[0], spans[1])

    def tile(at, _):
        here = pl.ds(pl.multiple_of(at * SPAN, SPAN), SPAN)
        first = at * SPAN // span * span // SPAN

        def chunk(key_at, _):
            there = pl.ds(pl.multiple_of(key_at * SPAN, SPAN), SPAN)
            for head in range(heads):
                scores = lax.dot_general(k_m[head, there, :], q_s[here, :], NT, preferred_element_type=f32)
                probs = jnp.exp2(scores * LOG2E - lse_t[head : head + 1, here])
                grad_probs = lax.dot_general(
                    v_m[head, there, :], o_s[here, :], NT, preferred_element_type=f32
                )
                grad_scores = (probs * (grad_probs - delta_t[head : head + 1, here])).astype(bf16)
                dv_s[there, :] += jnp.dot(probs.astype(bf16), o_m[head, here, :], preferred_element_type=f32)
                dk_s[there, :] += jnp.dot(grad_scores, q_m[head, here, :], preferred_element_type=f32)
                dq_s[here, :] += lax.dot_general(
                    grad_scores, k_m[head, there, :], TN, preferred_element_type=f32
                )
            return 0

        lax.fori_loop(first, first + span // SPAN, chunk, 0)
        return 0

    lax.fori_loop(0, rows // SPAN, tile, 0)
    sums_ref[...] = jnp.zeros_like(sums_ref)
    bias_ref[...] = jnp.zeros_like(bias_ref)

    def pull(grad, unit, scale, gain):
        grad_unit = grad * gain
        inner = _lane_mean(grad_unit, grouping)
        cross = _lane_mean(grad_unit * unit, grouping)
        return scale * (grad_unit - inner - unit * cross)

    def leave(at, _):
        here = pl.ds(pl.multiple_of(order_ref[at] * BLOCK, BLOCK), BLOCK)
        there = pl.ds(pl.multiple_of(at * BLOCK, BLOCK), BLOCK)
        unit_q, scale_q = _unit(raw_ref[here, :width], grouping)
        unit_k, scale_k = _unit(raw_ref[here, width:], grouping)
        grad_q = dq_s[there, :] * HD ** (-0.5)
        grad_k = dk_s[there, :]
        sums_ref[0:1, :] += jnp.sum(grad_q * unit_q, axis=0, keepdims=True)
        sums_ref[1:2, :] += jnp.sum(grad_q, axis=0, keepdims=True)
        sums_ref[2:3, :] += jnp.sum(grad_k * unit_k, axis=0, keepdims=True)
        sums_ref[3:4, :] += jnp.sum(grad_k, axis=0, keepdims=True)
        low_q = pull(grad_q, unit_q, scale_q, gains_ref[0:1, :]).astype(bf16)
        low_k = pull(grad_k, unit_k, scale_k, gains_ref[2:3, :]).astype(bf16)
        low_v = dv_s[there, :].astype(bf16)
        for part, low in enumerate((low_q, low_k, low_v)):
            lanes = slice(part * width, (part + 1) * width)
            out_ref[here, lanes] = low
            bias_ref[0:1, lanes] += jnp.sum(low.astype(f32), axis=0, keepdims=True)
        return 0

    lax.fori_loop(0, blocks, leave, 0)


def attention_backward(raw, values, grad, attended, lse, gains, order, is_hi, spans):
    rows, width = values.shape
    heads = width // HD
    smem = pl.BlockSpec(memory_space=pltpu.SMEM)
    vmem = pl.BlockSpec(memory_space=pltpu.VMEM)
    flops = 2 * rows * 20 * spans[0] * width
    masked = pltpu.VMEM((heads, rows, width), bf16)
    return pl.pallas_call(
        functools.partial(backward_kernel, heads, spans),
        out_shape=(
            jax.ShapeDtypeStruct((rows, 3 * width), bf16),
            jax.ShapeDtypeStruct((8, width), f32),
            jax.ShapeDtypeStruct((8, 3 * width), f32),
        ),
        in_specs=[smem, smem] + [vmem] * 6,
        out_specs=(vmem,) * 3,
        scratch_shapes=[
            pltpu.VMEM((rows, width), bf16),
            pltpu.VMEM((rows, width), bf16),
            masked,
            masked,
            masked,
            masked,
            pltpu.VMEM((rows, width), f32),
            pltpu.VMEM((rows, width), f32),
            pltpu.VMEM((rows, width), f32),
            pltpu.VMEM((8, rows), f32),
            pltpu.VMEM((8, rows), f32),
        ],
        compiler_params=pltpu.CompilerParams(vmem_limit_bytes=VMEM_BYTES),
        cost_estimate=pl.CostEstimate(
            flops=flops, bytes_accessed=rows * 24 * width, transcendentals=rows * spans[0] * heads
        ),
    )(order, is_hi, raw, values, grad, attended, lse, gains)


class Links:
    def __init__(self, mesh):
        self.n_tok = mesh.shape["tok"]
        self.n_head = mesh.shape["head"]
        self.paired = self.n_tok == 8 and self.n_head == 4

    def head(self, values, step):
        return lax.ppermute(values, "head", [(i, i ^ step) for i in range(self.n_head)])

    def tok(self, values, step):
        return lax.ppermute(values, "tok", [(i, i ^ step) for i in range(self.n_tok)])

    def rows_in(self, rows):
        if not self.paired:
            return [rows] + [self.head(rows, step) for step in range(1, self.n_head)]
        half = rows.shape[0] // 2
        one, two = self.head(rows, 1), self.head(rows, 2)
        far = jnp.concatenate([self.head(one[:half], 2), self.head(two[half:], 1)], axis=0)
        return [rows, one, two, far]

    def rows_out(self, parts):
        if not self.paired:
            moved = [self.head(parts[step], step).astype(f32) for step in range(1, self.n_head)]
            return parts[0].astype(f32) + sum(moved)
        half = parts[0].shape[0] // 2
        upper = [part[:half] for part in parts]
        lower = [part[half:] for part in parts]
        pass_up = (upper[2].astype(f32) + self.head(upper[3], 1).astype(f32)).astype(bf16)
        pass_low = (lower[1].astype(f32) + self.head(lower[3], 2).astype(f32)).astype(bf16)
        up = upper[0].astype(f32) + self.head(upper[1], 1).astype(f32) + self.head(pass_up, 2).astype(f32)
        low = lower[0].astype(f32) + self.head(lower[2], 2).astype(f32) + self.head(pass_low, 1).astype(f32)
        return jnp.concatenate([up, low], axis=0)

    def exchange(self, parts):
        return [parts[0]] + [self.head(parts[step], step) for step in range(1, self.n_head)]

    def by_index(self, pieces, own):
        return [
            lax.select_n((own ^ at).astype(jnp.int32), *pieces) if len(pieces) > 1 else pieces[0]
            for at in range(len(pieces))
        ]

    def zed(self):
        return lax.axis_index("tok") // 2

    def core(self):
        return lax.rem(lax.axis_index("tok"), 2)

    def planes(self, shard):
        pieces = [shard] + [self.tok(shard, 2 * step) for step in range(1, 4)]
        return jnp.stack(self.by_index(pieces, self.zed()))

    def gather_places(self):
        if not self.paired:
            return [None]
        spots = ((0, 4, 0), (0, 4, 1), (0, 4, 2), (0, 2, 3), (2, 2, 3))
        return [("head", first, count, core, to) for first, count, to in spots for core in range(2)]

    def gather_planes(self, shard):
        if not self.paired:
            whole = lax.all_gather(shard, BOTH, axis=0, tiled=True)
            return [whole.reshape(4, 2, 4, whole.shape[0] // 32, whole.shape[1])]
        return [self.planes(shard)]

    def gather_sides(self, own):
        if not self.paired:
            return own
        return [own[0], self.head(own[0], 1), self.head(own[0], 2)]

    def gather_far(self, near):
        if not self.paired:
            return near
        far = [self.head(near[1][:2], 2), self.head(near[2][2:], 1)]
        pieces = []
        for piece in near + far:
            pieces += [piece, self.tok(piece, 1)]
        return pieces

    def scatter_start(self, pieces, got):
        if not self.paired:
            return pieces
        return [(one.astype(f32) + two.astype(f32)).astype(bf16) for one, two in zip(pieces, got)]

    def scatter_first(self, sums):
        if not self.paired:
            return sums
        low = [part[:2] for part in sums]
        top = [part[2:] for part in sums]
        come_low = self.head(jnp.concatenate([low[1], low[3]], axis=0), 1).astype(f32)
        come_top = self.head(jnp.concatenate([top[2], top[3]], axis=0), 2).astype(f32)
        pass_low = (low[2].astype(f32) + come_low[2:]).astype(bf16)
        pass_top = (top[1].astype(f32) + come_top[2:]).astype(bf16)
        own_low = low[0].astype(f32) + come_low[:2]
        own_top = top[0].astype(f32) + come_top[:2]
        own = jnp.concatenate([own_low.astype(bf16), own_top.astype(bf16)], axis=0)
        return [own, jnp.concatenate([pass_low, pass_top], axis=0)]

    def scatter_second(self, halves):
        if not self.paired:
            return halves
        own, passed = halves
        low = own[:2].astype(f32) + self.head(passed[:2], 2).astype(f32)
        top = own[2:].astype(f32) + self.head(passed[2:], 1).astype(f32)
        return [jnp.concatenate([low, top], axis=0).astype(bf16)]

    def scatter_last(self, planes):
        if not self.paired:
            whole = planes[0].reshape(-1, planes[0].shape[-1])
            return lax.psum_scatter(whole, BOTH, scatter_dimension=0, tiled=True).astype(f32)
        return self.sum_planes(planes[0])

    def sum_planes(self, parts):
        zed = self.zed()
        pick = lambda step: lax.dynamic_slice_in_dim(parts, zed ^ step, 1, 0)[0]
        total = pick(0).astype(f32)
        for step in range(1, 4):
            total = total + self.tok(pick(step).astype(bf16), 2 * step).astype(f32)
        return total

    def fetch_heads(self, shards, own):
        own_rows = shards[0].shape[0]
        width = D // self.n_head
        cut = jnp.stack(shards).reshape(len(shards), own_rows, 3, D)
        parts = [
            lax.dynamic_slice_in_dim(cut, (own ^ step) * width, width, 3).reshape(
                len(shards), own_rows, 3 * width
            )
            for step in range(self.n_head)
        ]
        moved = jnp.stack(self.by_index(self.exchange(parts), own), axis=1)
        return [moved[at].reshape(self.n_head * own_rows, 3 * width) for at in range(len(shards))]

    def return_cores(self, grad):
        if not self.paired:
            return grad
        view = grad.reshape((4, 2, grad.shape[0] // 8, grad.shape[1]))
        core = self.core()
        cut = lambda at: lax.dynamic_slice_in_dim(view, at, 1, 1)[:, 0]
        return (cut(core).astype(f32) + self.tok(cut(core ^ 1), 1).astype(f32)).astype(bf16)

    def return_planes(self, grad):
        if not self.paired:
            return lax.psum_scatter(grad, "tok", scatter_dimension=0, tiled=True)
        return self.sum_planes(grad).astype(bf16)

    def return_heads(self, both, own):
        width = D // self.n_head
        stack = jnp.stack(both)
        own_rows = stack.shape[1] // self.n_head
        parts = [
            lax.dynamic_slice_in_dim(stack, (own ^ step) * own_rows, own_rows, 1)
            for step in range(self.n_head)
        ]
        back = jnp.stack(self.by_index(self.exchange(parts), own), axis=2)
        back = back.reshape(len(both), own_rows, self.n_head, 3, width)
        return jnp.swapaxes(back, 2, 3).reshape(len(both), own_rows, 3 * D).astype(f32)


def together(*values):
    return lax.optimization_barrier(values)


CHUNK = 512


def _paired(value, step, bits):
    total = 0
    for bit in range(bits):
        one = lax.rem(value // (1 << bit), 2)
        total = total + (1 - one if (step >> bit) % 2 else one) * (1 << bit)
    return total


def _slot(ref, place):
    if place is None:
        return ref
    tok = lax.axis_index("tok")
    side = _paired(lax.rem(tok, 2), place[-1] if place[0] == "plane" else place[3], 1)
    if place[0] == "plane":
        return ref.at[_paired(tok // 2, place[1], 2), side]
    return ref.at[pl.ds(place[1], place[2]), side, _paired(lax.axis_index("head"), place[4], 2)]


PROJ_AT, UP_AT, DOWN_AT, WIDE = 0, D, D + FF, D + 2 * FF


def _cols(ref, at, size):
    window = pl.ds(pl.multiple_of(at, 128), size)
    return ref.at[(slice(None),) * (len(ref.shape) - 1) + (window,)]


def _copies(pieces, places, whole, at, size, sems, inward):
    moves = []
    for index, (piece, place) in enumerate(zip(pieces, places)):
        outside = _cols(piece, at, size)
        inside = _slot(whole, place)
        pair = (outside, inside) if inward else (inside, outside)
        moves.append(pltpu.make_async_copy(pair[0], pair[1], sems.at[index]))
    return moves


def _start(moves):
    for move in moves:
        move.start()


def _wait(moves):
    for move in moves:
        move.wait()


def _flat(values):
    return values.reshape(D, values.shape[-1])


def _norm(values):
    centered = values - jnp.mean(values, axis=-1, keepdims=True)
    scale = lax.rsqrt(jnp.mean(centered * centered, axis=-1, keepdims=True) + norm_eps)
    return centered * scale, scale


def _own_column(step, n_head):
    at = _paired(lax.axis_index("head"), step, n_head.bit_length() - 1)
    return pl.multiple_of(at * (D // n_head), 128)


def _mate(step):
    return lax.axis_index("tok"), _paired(lax.axis_index("head"), step, 2)


def _sibling():
    return _paired(lax.axis_index("tok"), 1, 3), lax.axis_index("head")


def _greet(devices):
    barrier = pltpu.get_barrier_semaphore()
    for device in devices:
        pl.semaphore_signal(barrier, inc=1, device_id=device, device_id_type=MESH_ID)
    pl.semaphore_wait(barrier, len(devices))


def _send(source, target, send_sem, recv_sem, device):
    return pltpu.make_async_remote_copy(
        src_ref=source,
        dst_ref=target,
        send_sem=send_sem,
        recv_sem=recv_sem,
        device_id=device,
        device_id_type=MESH_ID,
    )


def enter_kernel(wide, *refs):
    x_ref, q_ref, refs = refs[0], refs[1], refs[2:]
    if wide:
        shard_ref, refs = refs[0], refs[1:]
    one_ref, two_ref, far_ref, full_ref, refs = *refs[:4], refs[4:]
    if wide:
        planes_ref, refs = refs[0], refs[1:]
    send_sem, recv_sem, z_send, z_recv, own_sem, core_sem = refs
    tok, head = lax.axis_index("tok"), lax.axis_index("head")
    zed, core = tok // 2, lax.rem(tok, 2)
    one_way, two_way = _mate(1), _mate(2)
    barrier = pltpu.get_barrier_semaphore()
    greet = lambda device: pl.semaphore_signal(barrier, inc=1, device_id=device, device_id_type=MESH_ID)
    for device in (one_way, two_way, _sibling()):
        greet(device)

    @pl.when(zed < 3)
    def _():
        greet((tok + 2, head))

    @pl.when(zed > 0)
    def _():
        greet((tok - 2, head))

    edge = (zed == 0) | (zed == 3)

    @pl.when(edge)
    def _():
        pl.semaphore_wait(barrier, 4)

    @pl.when(jnp.logical_not(edge))
    def _():
        pl.semaphore_wait(barrier, 5)

    rows = x_ref.shape[0]
    parts = 4
    size = rows // parts

    def move(lane, part, source, target, device):
        here = pl.ds(part * size, size)
        return _send(source.at[here], target.at[here], send_sem.at[lane, part], recv_sem.at[lane, part], device)

    to_one = lambda part: move(0, part, x_ref, one_ref, one_way)
    to_two = lambda part: move(1, part, x_ref, two_ref, two_way)
    on_two = lambda part: move(2, part, one_ref, far_ref, two_way)
    on_one = lambda part: move(2, part, two_ref, far_ref, one_way)
    homes = [(q_ref, lambda plane: full_ref.at[plane, core])]
    if wide:
        homes.append((shard_ref, lambda plane: planes_ref.at[plane]))

    def climb(up, step):
        plane = jnp.clip(zed - step if up else zed + step, 0, 3)
        device = (jnp.clip(tok + 2 if up else tok - 2, 0, 7), head)
        return [
            _send(
                home(plane) if step else source,
                home(plane),
                z_send.at[int(up), step, index],
                z_recv.at[int(up), step, index],
                device,
            )
            for index, (source, home) in enumerate(homes)
        ]

    def sends(up, step):
        return (zed >= step) & (zed < 3) if up else (zed <= 3 - step) & (zed > 0)

    def comes(up, step):
        return zed >= step + 1 if up else zed <= 2 - step

    def climb_start(up, step):
        @pl.when(sends(up, step))
        def _():
            _start(climb(up, step))

    def climb_come(up, step):
        @pl.when(comes(up, step))
        def _():
            for copy in climb(up, step):
                copy.wait_recv()

    for turn in range(parts):
        to_one(turn).start()
        to_two(parts - 1 - turn).start()
    for up in (True, False):
        climb_start(up, 0)
    stays = [
        pltpu.make_async_copy(source, home(zed), own_sem.at[index]) for index, (source, home) in enumerate(homes)
    ]
    _start(stays)
    for turn in range(parts // 2):
        to_one(turn).wait_recv()
        on_two(turn).start()
        to_two(parts - 1 - turn).wait_recv()
        on_one(parts - 1 - turn).start()
    for step in range(3):
        for up in (True, False):
            climb_come(up, step)
            if step < 2:
                climb_start(up, step + 1)
    _wait(stays)
    mine = full_ref.at[:, core]
    over = _send(mine, mine, core_sem.at[0], core_sem.at[1], _sibling())
    over.start()
    for turn in range(parts // 2, parts):
        to_one(turn).wait_recv()
        to_two(parts - 1 - turn).wait_recv()
    for turn in range(parts):
        to_one(turn).wait_send()
        to_two(turn).wait_send()
    for turn in range(parts // 2):
        on_two(turn).wait()
        on_one(parts - 1 - turn).wait()
    for step in range(3):
        for up in (True, False):

            @pl.when(sends(up, step))
            def _():
                for copy in climb(up, step):
                    copy.wait_send()

    over.wait()


def enter_rows(rows, mine, shard, collective_id):
    hbm = pl.BlockSpec(memory_space=pl.ANY)
    like = jax.ShapeDtypeStruct(rows.shape, rows.dtype)
    outs = [like, like, like, jax.ShapeDtypeStruct((4, 2) + mine.shape, mine.dtype)]
    given = [rows, mine]
    if shard is not None:
        outs.append(jax.ShapeDtypeStruct((4,) + shard.shape, shard.dtype))
        given.append(shard)
    sems = pltpu.SemaphoreType.DMA
    one, two, far, full, *planes = pl.pallas_call(
        functools.partial(enter_kernel, shard is not None),
        out_shape=tuple(outs),
        in_specs=[hbm] * len(given),
        out_specs=(hbm,) * len(outs),
        scratch_shapes=[sems((3, 4)), sems((3, 4)), sems((2, 3, 2)), sems((2, 3, 2)), sems((2,)), sems((2,))],
        compiler_params=pltpu.CompilerParams(collective_id=collective_id, has_side_effects=True),
        cost_estimate=pl.CostEstimate(flops=0, bytes_accessed=150 << 20, transcendentals=0),
    )(*given)
    return [rows, one, two, far], full.reshape(8 * mine.shape[0], mine.shape[1]), planes


def _norm_pull(grad_unit, unit, scale):
    inner = jnp.mean(grad_unit, axis=-1, keepdims=True)
    cross = jnp.mean(grad_unit * unit, axis=-1, keepdims=True)
    return scale * (grad_unit - inner - unit * cross)


def rows_out_kernel(grad_ref, weight_ref, hidden_ref, after_ref, gain_ref, out_ref, sums_ref, away, come, send_sem, recv_sem):
    one_way, two_way = _mate(1), _mate(2)
    _greet([one_way, two_way])
    rows = hidden_ref.shape[0]
    half = rows // 2

    def term(step, low):
        here = pl.ds(step * rows + (0 if low else half), half)
        return lax.dot_general(grad_ref[here, :], weight_ref[...], NT, preferred_element_type=f32)

    def move(slot, device):
        return _send(away.at[slot], come.at[slot], send_sem.at[slot], recv_sem.at[slot], device)

    ways = (one_way, two_way, one_way, two_way, two_way, one_way)
    for slot, (step, low) in enumerate(((3, True), (3, False), (1, True), (2, False))):
        away[slot] = term(step, low).astype(bf16)
        move(slot, ways[slot]).start()
    pass_low = term(2, True)
    pass_top = term(1, False)
    move(0, ways[0]).wait_recv()
    away[4] = (pass_low + come[0].astype(f32)).astype(bf16)
    move(4, ways[4]).start()
    move(1, ways[1]).wait_recv()
    away[5] = (pass_top + come[1].astype(f32)).astype(bf16)
    move(5, ways[5]).start()
    sums_ref[...] = jnp.zeros_like(sums_ref)
    for low in (True, False):
        here = pl.ds(0 if low else half, half)
        own = term(0, low)
        unit, scale = _norm(hidden_ref[here, :])
        near, far = (2, 4) if low else (3, 5)
        move(near, ways[near]).wait_recv()
        move(far, ways[far]).wait_recv()
        grad = own + come[near].astype(f32) + come[far].astype(f32)
        sums_ref[0:1, :] += jnp.sum(grad * unit, axis=0, keepdims=True)
        sums_ref[1:2, :] += jnp.sum(grad, axis=0, keepdims=True)
        out_ref[here, :] = after_ref[here, :] + _norm_pull(grad * gain_ref[0:1, :], unit, scale)
    for slot in range(6):
        move(slot, ways[slot]).wait_send()


def rows_out(grad, weight, hidden, after, gain, collective_id):
    rows = hidden.shape[0]
    vmem = pl.BlockSpec(memory_space=pltpu.VMEM)
    buffer = pltpu.VMEM((6, rows // 2, D), bf16)
    sems = pltpu.SemaphoreType.DMA((6,))
    return pl.pallas_call(
        rows_out_kernel,
        out_shape=(jax.ShapeDtypeStruct((rows, D), f32), jax.ShapeDtypeStruct((8, D), f32)),
        in_specs=[vmem] * 5,
        out_specs=(vmem, vmem),
        scratch_shapes=[buffer, buffer, sems, sems],
        compiler_params=pltpu.CompilerParams(
            collective_id=collective_id, has_side_effects=True, vmem_limit_bytes=VMEM_BYTES
        ),
        cost_estimate=pl.CostEstimate(flops=0, bytes_accessed=150 << 20, transcendentals=0),
    )(grad, weight, hidden, after, gain)


def post_forward_kernel(n_head, places, last, remote, *refs):
    count = len(places)
    att_ref, refs = refs[0], refs[1:]
    hidden_ref, rows_ref, up_bias_ref, refs = refs[0], refs[1], refs[2], refs[3:]
    weight_refs, refs = refs[:count], refs[count:]
    next_ref, normed_ref, down_ref, act_ref, slope_ref, branch_hbm, after_hbm, two_hbm, att_hbm, refs = *refs[:9], refs[9:]
    proj_s, up_s, down_s, att_s, branch_s, after_s, two_s, acc, proj_sem, up_sem, down_sem, out_sem, send_sem, recv_sem = refs
    at = pl.program_id(0)
    chunks = pl.num_programs(0)

    def fetch(chunk, slot):
        up_at, down_at = UP_AT + chunk * CHUNK, DOWN_AT + chunk * CHUNK
        return _copies(weight_refs, places, up_s.at[slot], up_at, CHUNK, up_sem.at[slot], True) + _copies(
            weight_refs, places, down_s.at[slot], down_at, CHUNK, down_sem.at[slot], True
        )

    leaving = [
        pltpu.make_async_copy(branch_s, branch_hbm, out_sem.at[0]),
        pltpu.make_async_copy(after_s, after_hbm, out_sem.at[1]),
        pltpu.make_async_copy(two_s, two_hbm, out_sem.at[2]),
        pltpu.make_async_copy(att_s, att_hbm, out_sem.at[3]),
    ]

    @pl.when(at == 0)
    def _():
        proj = _copies(weight_refs, places, proj_s, PROJ_AT, D, proj_sem, True)
        if remote:
            width, rows = D // n_head, hidden_ref.shape[0]
            _greet([_mate(step) for step in range(1, n_head)])
            mine = att_s.at[:, pl.ds(_own_column(0, n_head), width)]
            moves = [
                _send(
                    att_ref.at[pl.ds(step * rows, rows)], mine, send_sem.at[step], recv_sem.at[step], _mate(step)
                )
                for step in range(1, n_head)
            ]
            moves.append(pltpu.make_async_copy(att_ref.at[pl.ds(0, rows)], mine, send_sem.at[0]))
            _start(moves)
        _start(proj)
        _start(fetch(0, 0))
        if remote:
            _wait(moves)
        else:
            att_s[...] = att_ref[...]
        _wait(proj)
        branch = (
            lax.dot_general(att_s[...], _flat(proj_s[...]), NT, preferred_element_type=f32) + rows_ref[0:1, :]
        )
        branch_s[...] = branch
        after = hidden_ref[...] + rows_ref[1:2, :] * branch
        after_s[...] = after
        unit, _s = _norm(after)
        two_s[...] = (unit * rows_ref[2:3, :] + rows_ref[3:4, :]).astype(bf16)
        _start(leaving)

    @pl.when(at + 1 < chunks)
    def _():
        _start(fetch(at + 1, lax.rem(at + 1, 2)))

    slot = lax.rem(at, 2)
    _wait(fetch(at, slot))
    expand = jnp.dot(two_s[...], _flat(up_s[slot]), preferred_element_type=f32) + up_bias_ref[...]
    cdf = 0.5 * (1.0 + lax.erf(expand * math.sqrt(0.5)))
    slope = cdf + expand * jnp.exp(-0.5 * expand * expand) * (1.0 / math.sqrt(2.0 * math.pi))
    act = (expand * cdf).astype(bf16)
    act_ref[...] = act
    slope_ref[...] = slope.astype(bf16)
    part = lax.dot_general(act, _flat(down_s[slot]), NT, preferred_element_type=f32)

    @pl.when(at == 0)
    def _():
        acc[...] = part

    @pl.when(at > 0)
    def _():
        acc[...] += part

    @pl.when(at == chunks - 1)
    def _():
        down = acc[...] + rows_ref[4:5, :]
        down_ref[...] = down
        hidden = after_s[...] + rows_ref[5:6, :] * down
        next_ref[...] = hidden
        if last:
            normed_ref[...] = jnp.zeros_like(normed_ref)
        else:
            unit, _s = _norm(hidden)
            normed_ref[...] = (unit * rows_ref[6:7, :] + rows_ref[7:8, :]).astype(bf16)
        _wait(leaving)


def _params(remote, collective_id):
    if not remote:
        return pltpu.CompilerParams(dimension_semantics=("arbitrary",), vmem_limit_bytes=VMEM_BYTES)
    return pltpu.CompilerParams(
        dimension_semantics=("arbitrary",),
        vmem_limit_bytes=VMEM_BYTES,
        collective_id=collective_id,
        has_side_effects=True,
    )


def post_forward(att, hidden, rows, up_bias, gathered, n_head, last, remote, collective_id):
    own_rows = hidden.shape[0]
    pieces, places = gathered
    count = len(places)
    unit_rows = D // 32
    vmem = pl.BlockSpec(memory_space=pltpu.VMEM)
    hbm = pl.BlockSpec(memory_space=pl.ANY)
    column = pl.BlockSpec((own_rows, CHUNK), lambda at: (0, at))
    fixed = lambda leaf_rows: pl.BlockSpec((leaf_rows, D), lambda at: (0, 0))
    whole = lambda dtype: jax.ShapeDtypeStruct((own_rows, D), dtype)
    wide = jax.ShapeDtypeStruct((own_rows, FF), bf16)
    weight = lambda *lead: pltpu.VMEM(lead + (4, 2, 4, unit_rows), bf16)
    normed_rows = 16 if last else own_rows
    return pl.pallas_call(
        functools.partial(post_forward_kernel, n_head, places, last, remote),
        grid=(FF // CHUNK,),
        out_shape=(
            whole(f32),
            jax.ShapeDtypeStruct((normed_rows, D), bf16),
            whole(f32),
            wide,
            wide,
            whole(f32),
            whole(f32),
            whole(bf16),
            whole(bf16),
        ),
        in_specs=[hbm if remote else vmem, vmem, vmem, pl.BlockSpec((1, CHUNK), lambda at: (0, at))]
        + [hbm] * count,
        out_specs=(fixed(own_rows), fixed(normed_rows), fixed(own_rows), column, column, hbm, hbm, hbm, hbm),
        scratch_shapes=[
            pltpu.VMEM((4, 2, 4, unit_rows, D), bf16),
            pltpu.VMEM((2, 4, 2, 4, unit_rows, CHUNK), bf16),
            pltpu.VMEM((2, 4, 2, 4, unit_rows, CHUNK), bf16),
            pltpu.VMEM((own_rows, D), bf16),
            pltpu.VMEM((own_rows, D), f32),
            pltpu.VMEM((own_rows, D), f32),
            pltpu.VMEM((own_rows, D), bf16),
            pltpu.VMEM((own_rows, D), f32),
            pltpu.SemaphoreType.DMA((count,)),
            pltpu.SemaphoreType.DMA((2, count)),
            pltpu.SemaphoreType.DMA((2, count)),
            pltpu.SemaphoreType.DMA((4,)),
            pltpu.SemaphoreType.DMA((n_head,)),
            pltpu.SemaphoreType.DMA((n_head,)),
        ],
        compiler_params=_params(remote, collective_id),
        cost_estimate=pl.CostEstimate(
            flops=2 * own_rows * D * (D + 2 * FF),
            bytes_accessed=2 * D * (D + 2 * FF) + own_rows * (22 * D + 4 * FF),
            transcendentals=2 * own_rows * FF,
        ),
    )(att, hidden, rows, up_bias, *pieces)


def post_backward_kernel(n_head, places, remote, *refs):
    count = len(places)
    own_places = [("head", 0, 4, 0, to) for to in range(4)] if remote else [None]
    far_places = [("head", 0, 4, 1, to) for to in range(4)] if remote else []
    out_count = len(own_places)
    att_ref, grad_ref, down_ref, branch_ref, after_ref, two_ref, rows_ref, act_ref, slope_ref, refs = *refs[:9], refs[9:]
    weight_refs, refs = refs[:count], refs[count:]
    d_att_ref, d_after_ref, sums_ref, up_sum_ref, refs = *refs[:4], refs[4:]
    own_refs, refs = refs[:out_count], refs[out_count:]
    got_refs, refs = refs[: len(far_places)], refs[len(far_places) :]
    proj_s, up_s, down_s, d_proj_s, d_up_s, d_down_s, att_s, low_s, low_t, two_t, acc, refs = *refs[:11], refs[11:]
    proj_sem, up_sem, down_sem, own_sem, far_sem, got_sem, send_sem, recv_sem = refs
    at = pl.program_id(0)
    chunks = pl.num_programs(0)
    width = D // n_head

    def fetch(chunk, slot):
        up_at, down_at = UP_AT + chunk * CHUNK, DOWN_AT + chunk * CHUNK
        return _copies(weight_refs, places, up_s.at[slot], up_at, CHUNK, up_sem.at[slot], True) + _copies(
            weight_refs, places, down_s.at[slot], down_at, CHUNK, down_sem.at[slot], True
        )

    def stay(whole, column, size, lane):
        return _copies(own_refs, own_places, whole, column, size, own_sem.at[lane], False)

    def away(whole, column, size, lane, mark):
        return [
            _send(
                _slot(whole, place),
                _cols(got_refs[to], column, size),
                far_sem.at[lane, to],
                got_sem.at[mark, to],
                _sibling(),
            )
            for to, place in enumerate(far_places)
        ]

    def over(chunk, slot):
        up_at, down_at = UP_AT + chunk * CHUNK, DOWN_AT + chunk * CHUNK
        return away(d_up_s.at[slot], up_at, CHUNK, slot, chunk) + away(
            d_down_s.at[slot], down_at, CHUNK, 2 + slot, chunks + chunk
        )

    def leave(chunk, slot):
        up_at, down_at = UP_AT + chunk * CHUNK, DOWN_AT + chunk * CHUNK
        local = stay(d_up_s.at[slot], up_at, CHUNK, slot) + stay(d_down_s.at[slot], down_at, CHUNK, 2 + slot)
        return local, over(chunk, slot)

    def left(pair):
        _wait(pair[0])
        for move in pair[1]:
            move.wait_send()

    proj = lambda: _copies(weight_refs, places, proj_s, PROJ_AT, D, proj_sem, True)

    @pl.when(at == 0)
    def _():
        if remote:
            _greet([_mate(step) for step in range(1, n_head)] + [_sibling()])
        _start(fetch(0, 0))
        _start(proj())
        grad = grad_ref[...]
        low = (rows_ref[2:3, :] * grad).astype(bf16)
        low_s[...] = low
        low_t[...] = jnp.transpose(low)
        two_t[...] = jnp.transpose(two_ref[...])
        sums_ref[...] = jnp.zeros_like(sums_ref)
        sums_ref[0:1, :] = jnp.sum(grad * down_ref[...], axis=0, keepdims=True)
        sums_ref[1:2, :] = jnp.sum(low.astype(f32), axis=0, keepdims=True)
        acc[...] = jnp.zeros_like(acc)

    @pl.when(at + 1 < chunks)
    def _():
        _start(fetch(at + 1, lax.rem(at + 1, 2)))

    slot = lax.rem(at, 2)
    _wait(fetch(at, slot))

    @pl.when(at >= 2)
    def _():
        left(leave(at - 2, slot))

    d_act = jnp.dot(low_s[...], _flat(down_s[slot]), preferred_element_type=f32)
    d_expand = (slope_ref[...].astype(f32) * d_act).astype(bf16)
    up_sum_ref[...] = jnp.sum(d_expand.astype(f32), axis=0, keepdims=True)
    acc[...] += lax.dot_general(d_expand, _flat(up_s[slot]), NT, preferred_element_type=f32)
    shape = d_up_s.shape[1:]
    d_up_s[slot] = jnp.dot(two_t[...], d_expand, preferred_element_type=f32).astype(bf16).reshape(shape)
    d_down_s[slot] = jnp.dot(low_t[...], act_ref[...], preferred_element_type=f32).astype(bf16).reshape(shape)
    for moves in leave(at, slot):
        _start(moves)

    @pl.when(at == chunks - 1)
    def _():
        d_two = acc[...]
        unit, scale = _norm(after_ref[...])
        sums_ref[2:3, :] = jnp.sum(d_two * unit, axis=0, keepdims=True)
        sums_ref[3:4, :] = jnp.sum(d_two, axis=0, keepdims=True)
        d_unit = d_two * rows_ref[1:2, :]
        inner = jnp.mean(d_unit, axis=-1, keepdims=True)
        cross = jnp.mean(d_unit * unit, axis=-1, keepdims=True)
        d_after = grad_ref[...] + scale * (d_unit - inner - unit * cross)
        d_after_ref[...] = d_after
        sums_ref[4:5, :] = jnp.sum(d_after * branch_ref[...], axis=0, keepdims=True)
        d_branch = (rows_ref[0:1, :] * d_after).astype(bf16)
        sums_ref[5:6, :] = jnp.sum(d_branch.astype(f32), axis=0, keepdims=True)
        d_proj_s[...] = (
            lax.dot_general(d_branch, att_ref[...], TN, preferred_element_type=f32)
            .astype(bf16)
            .reshape(d_proj_s.shape)
        )
        gone = stay(d_proj_s, PROJ_AT, D, 4), away(d_proj_s, PROJ_AT, D, 4, 2 * chunks)
        for moves in gone:
            _start(moves)
        _wait(proj())
        d_att = jnp.dot(d_branch, _flat(proj_s[...]), preferred_element_type=f32).astype(bf16)
        if remote:
            rows = d_att.shape[0]
            att_s[...] = d_att
            moves = [
                _send(
                    att_s.at[:, pl.ds(_own_column(step, n_head), width)],
                    d_att_ref.at[pl.ds(step * rows, rows)],
                    send_sem.at[step],
                    recv_sem.at[step],
                    _mate(step),
                )
                for step in range(1, n_head)
            ]
            own = att_s.at[:, pl.ds(_own_column(0, n_head), width)]
            moves.append(pltpu.make_async_copy(own, d_att_ref.at[pl.ds(0, rows)], send_sem.at[0]))
            _start(moves)
            _wait(moves)
        else:
            d_att_ref[...] = d_att
        left(leave(at - 1, 1 - slot))
        left(leave(at, slot))
        left(gone)
        if remote:

            def arrive(chunk, _):
                for move in over(chunk, 0):
                    move.wait_recv()
                return 0

            lax.fori_loop(0, chunks, arrive, 0)
            for move in gone[1]:
                move.wait_recv()


def post_backward(att, grad, down_out, branch, after, two, rows, act, slope, gathered, n_head, remote, collective_id):
    own_rows = grad.shape[0]
    pieces, places = gathered
    count = len(places)
    unit_rows = D // 32
    vmem = pl.BlockSpec(memory_space=pltpu.VMEM)
    hbm = pl.BlockSpec(memory_space=pl.ANY)
    column = pl.BlockSpec((own_rows, CHUNK), lambda at: (0, at))
    fixed = lambda *shape: pl.BlockSpec(shape, lambda at: (0, 0))
    width = D // n_head
    chunks = FF // CHUNK
    if remote:
        d_att_shape, d_att_spec = (n_head * own_rows, width), hbm
        grads = [jax.ShapeDtypeStruct((4, unit_rows, WIDE), bf16)] * 8
    else:
        d_att_shape, d_att_spec = (own_rows, D), fixed(own_rows, D)
        grads = [jax.ShapeDtypeStruct((4, 2, 4, unit_rows, WIDE), bf16)]
    sems = pltpu.SemaphoreType.DMA
    outs = pl.pallas_call(
        functools.partial(post_backward_kernel, n_head, places, remote),
        grid=(chunks,),
        out_shape=tuple(
            [
                jax.ShapeDtypeStruct(d_att_shape, bf16),
                jax.ShapeDtypeStruct((own_rows, D), f32),
                jax.ShapeDtypeStruct((8, D), f32),
                jax.ShapeDtypeStruct((1, FF), f32),
            ]
            + grads
        ),
        in_specs=[vmem] * 7 + [column, column] + [hbm] * count,
        out_specs=tuple(
            [d_att_spec, fixed(own_rows, D), fixed(8, D), pl.BlockSpec((1, CHUNK), lambda at: (0, at))]
            + [hbm] * len(grads)
        ),
        scratch_shapes=[
            pltpu.VMEM((4, 2, 4, unit_rows, D), bf16),
            pltpu.VMEM((2, 4, 2, 4, unit_rows, CHUNK), bf16),
            pltpu.VMEM((2, 4, 2, 4, unit_rows, CHUNK), bf16),
            pltpu.VMEM((4, 2, 4, unit_rows, D), bf16),
            pltpu.VMEM((2, 4, 2, 4, unit_rows, CHUNK), bf16),
            pltpu.VMEM((2, 4, 2, 4, unit_rows, CHUNK), bf16),
            pltpu.VMEM((own_rows, D), bf16),
            pltpu.VMEM((own_rows, D), bf16),
            pltpu.VMEM((D, own_rows), bf16),
            pltpu.VMEM((D, own_rows), bf16),
            pltpu.VMEM((own_rows, D), f32),
            sems((count,)),
            sems((2, count)),
            sems((2, count)),
            sems((5, 4)),
            sems((5, 4)),
            sems((2 * chunks + 1, 4)),
            sems((n_head,)),
            sems((n_head,)),
        ],
        compiler_params=_params(remote, collective_id),
        cost_estimate=pl.CostEstimate(
            flops=4 * own_rows * D * (D + 2 * FF),
            bytes_accessed=4 * D * (D + 2 * FF) + own_rows * (22 * D + 4 * FF),
            transcendentals=0,
        ),
    )(att, grad, down_out, branch, after, two, rows, act, slope, *pieces)
    d_att, d_after, sums, up_sum, grads = *outs[:4], list(outs[4:])
    return d_att, d_after, sums, up_sum[0], (grads[:4], grads[4:]) if remote else (grads, grads)


FINISH_CUTS = 3


def finish_kernel(
    n_tok,
    n_head,
    grad_ref,
    weight_ref,
    hidden_ref,
    after_ref,
    gain_ref,
    x0_ref,
    x1_ref,
    x2_ref,
    x3_ref,
    own_ref,
    pass_ref,
    tiles_ref,
    one_ref,
    out_ref,
    sums_ref,
    rest_ref,
    qkv_ref,
    qkv_one_ref,
    vec_ref,
    away,
    come,
    come_rest,
    away_z,
    come_z,
    q_acc,
    q_all,
    q_come,
    q_mine,
    q_z,
    q_sum,
    q_land,
    one_land,
    land,
    send_sem,
    recv_sem,
    rest_send,
    rest_recv,
    z_send,
    z_recv,
    q_send,
    q_recv,
    v_send,
    v_recv,
):
    n = n_tok * n_head
    _enter(n_tok, n_head)
    tok = lax.axis_index("tok")
    head = lax.axis_index("head")
    me = tok * n_head + head
    zed, core = tok // 2, lax.rem(tok, 2)
    one_way, two_way = _mate(1), _mate(2)
    plane = lambda step: _paired(zed, step, 2)
    over = lambda step: (plane(step) * 2 + core, head)

    def tile(step):
        _, to, device = _peer(step, n_tok, n_head)
        return _send(tiles_ref.at[to], land.at[step], v_send.at[step], v_recv.at[step], device)

    def tile_start(step, _):
        tile(step).start()
        return 0

    def tile_wait(step, _):
        tile(step).wait()
        return 0

    lax.fori_loop(1, n, tile_start, 0)
    mate_at = lambda step: _paired(head, step, 2)

    def go_home(source, target, first):
        return [
            _send(
                source.at[mate_at(step)],
                target.at[head],
                q_send.at[first + step],
                q_recv.at[first + step],
                _mate(step),
            )
            for step in range(1, 4)
        ]

    one_home = go_home(one_ref, one_land, 6)
    _start(one_home)
    wide = own_ref.shape[2] // FINISH_CUTS

    def rest(low, at):
        part = pl.ds(0 if low else 2, 2)
        lanes = pl.ds(at * wide, wide)
        side = 0 if low else 1
        return _send(
            pass_ref.at[part, :, lanes],
            come_rest.at[part, :, lanes],
            rest_send.at[side, at],
            rest_recv.at[side, at],
            two_way if low else one_way,
        )

    for at in range(FINISH_CUTS):
        rest(True, at).start()
        rest(False, at).start()
    rows = hidden_ref.shape[0]
    half = rows // 2

    def term(step, low):
        here = pl.ds(step * rows + (0 if low else half), half)
        return lax.dot_general(grad_ref[here, :], weight_ref[...], NT, preferred_element_type=f32)

    def move(slot):
        return _send(away.at[slot], come.at[slot], send_sem.at[slot], recv_sem.at[slot], ways[slot])

    ways = (one_way, two_way, one_way, two_way, two_way, one_way)
    for slot, (step, low) in enumerate(((3, True), (3, False), (1, True), (2, False))):
        away[slot] = term(step, low).astype(bf16)
        move(slot).start()

    def cross(step, at):
        lanes = pl.ds(at * wide, wide)
        return _send(
            away_z.at[step - 1, :, lanes],
            come_z.at[step - 1, :, lanes],
            z_send.at[step - 1, at],
            z_recv.at[step - 1, at],
            over(step),
        )

    def rest_on(at):
        rest(True, at).wait_recv()
        rest(False, at).wait_recv()
        lanes = pl.ds(at * wide, wide)
        for step in range(4):
            total = own_ref[plane(step), :, lanes].astype(f32) + come_rest[plane(step), :, lanes].astype(f32)
            if step:
                away_z[step - 1, :, lanes] = total.astype(bf16)
                cross(step, at).start()
            else:
                rest_ref[:, lanes] = total

    rest_on(0)
    q_acc[...] = lax.dot_general(x0_ref[...], grad_ref[0:rows, :], TN, preferred_element_type=f32)
    for step, x_ref in ((1, x1_ref), (2, x2_ref), (3, x3_ref)):
        here = slice(step * rows, (step + 1) * rows)
        q_acc[...] += lax.dot_general(x_ref[...], grad_ref[here, :], TN, preferred_element_type=f32)
    q_all[...] = q_acc[...].astype(bf16).reshape(q_all.shape)
    swap_core = _send(q_all.at[:, 1 - core], q_come, q_send.at[0], q_recv.at[0], _sibling())
    swap_core.start()
    rest_on(1)
    swap_core.wait_recv()
    q_mine[...] = (q_all[:, core].astype(f32) + q_come[...].astype(f32)).astype(bf16)
    q_cross = [
        _send(q_mine.at[plane(step)], q_z.at[step - 1], q_send.at[step], q_recv.at[step], over(step))
        for step in range(1, 4)
    ]
    _start(q_cross)
    rest_on(2)
    pass_low = term(2, True)
    pass_top = term(1, False)
    move(0).wait_recv()
    away[4] = (pass_low + come[0].astype(f32)).astype(bf16)
    move(4).start()
    move(1).wait_recv()
    away[5] = (pass_top + come[1].astype(f32)).astype(bf16)
    move(5).start()
    sums_ref[...] = jnp.zeros_like(sums_ref)
    for low in (True, False):
        here = pl.ds(0 if low else half, half)
        own = term(0, low)
        unit, scale = _norm(hidden_ref[here, :])
        near, far = (2, 4) if low else (3, 5)
        move(near).wait_recv()
        move(far).wait_recv()
        grad = own + come[near].astype(f32) + come[far].astype(f32)
        sums_ref[0:1, :] += jnp.sum(grad * unit, axis=0, keepdims=True)
        sums_ref[1:2, :] += jnp.sum(grad, axis=0, keepdims=True)
        out_ref[here, :] = after_ref[here, :] + _norm_pull(grad * gain_ref[0:1, :], unit, scale)
    for copy in q_cross:
        copy.wait_recv()
    total = q_mine[zed].astype(f32)
    for step in range(3):
        total = total + q_z[step].astype(f32)
    q_sum[...] = total.astype(bf16).reshape(q_sum.shape)
    q_home = go_home(q_sum, q_land, 3)
    _start(q_home)
    qkv_ref[head] = q_sum[head].astype(f32)
    qkv_one_ref[head] = one_ref[head].astype(f32)
    for step, copy in enumerate(one_home):
        copy.wait_recv()
        qkv_one_ref[mate_at(step + 1)] = one_land[mate_at(step + 1)].astype(f32)
    for at in range(FINISH_CUTS):
        lanes = pl.ds(at * wide, wide)
        for step in range(1, 4):
            cross(step, at).wait_recv()
            rest_ref[:, lanes] += come_z[step - 1, :, lanes].astype(f32)
    for step, copy in enumerate(q_home):
        copy.wait_recv()
        qkv_ref[mate_at(step + 1)] = q_land[mate_at(step + 1)].astype(f32)
    lax.fori_loop(1, n, tile_wait, 0)
    vec_ref[...] = tiles_ref[me] + jnp.sum(land[1:], axis=0)
    for copy in [swap_core] + q_cross + q_home + one_home:
        copy.wait_send()
    for slot in range(6):
        move(slot).wait_send()
    for at in range(FINISH_CUTS):
        rest(True, at).wait_send()
        rest(False, at).wait_send()
        for step in range(1, 4):
            cross(step, at).wait_send()


def finish(grad, weight, hidden, after, gain, pieces, own, passed, tiles, mine_one, n_tok, n_head, collective_id):
    rows = hidden.shape[0]
    n = n_tok * n_head
    unit_rows, width = D // n, grad.shape[1]
    vmem = pl.BlockSpec(memory_space=pltpu.VMEM)
    hbm = pl.BlockSpec(memory_space=pl.ANY)
    sems = pltpu.SemaphoreType.DMA
    buffer = pltpu.VMEM((6, rows // 2, D), bf16)
    tok_rows = unit_rows * n_head
    low = lambda *shape: pltpu.VMEM(shape, bf16)
    return pl.pallas_call(
        functools.partial(finish_kernel, n_tok, n_head),
        out_shape=(
            jax.ShapeDtypeStruct((rows, D), f32),
            jax.ShapeDtypeStruct((8, D), f32),
            jax.ShapeDtypeStruct((unit_rows, WIDE), f32),
            jax.ShapeDtypeStruct((n_head, unit_rows, width), f32),
            jax.ShapeDtypeStruct((n_head, unit_rows, width), f32),
            jax.ShapeDtypeStruct(tiles.shape[1:], f32),
        ),
        in_specs=[vmem] * 10 + [hbm, vmem, vmem],
        out_specs=(vmem,) * 6,
        scratch_shapes=[
            buffer,
            buffer,
            low(4, unit_rows, WIDE),
            low(3, unit_rows, WIDE),
            low(3, unit_rows, WIDE),
            pltpu.VMEM((D, width), f32),
            low(4, 2, tok_rows, width),
            low(4, tok_rows, width),
            low(4, tok_rows, width),
            low(3, tok_rows, width),
            low(n_head, unit_rows, width),
            low(n_head, unit_rows, width),
            low(n_head, unit_rows, width),
            pltpu.VMEM(tiles.shape, f32),
            sems((6,)),
            sems((6,)),
            sems((2, FINISH_CUTS)),
            sems((2, FINISH_CUTS)),
            sems((3, FINISH_CUTS)),
            sems((3, FINISH_CUTS)),
            sems((10,)),
            sems((10,)),
            sems((n,)),
            sems((n,)),
        ],
        compiler_params=pltpu.CompilerParams(
            collective_id=collective_id, has_side_effects=True, vmem_limit_bytes=VMEM_BYTES
        ),
        cost_estimate=pl.CostEstimate(flops=0, bytes_accessed=250 << 20, transcendentals=0),
    )(grad, weight, hidden, after, gain, *pieces, own, passed, tiles, mine_one.reshape(n_head, unit_rows, width))


def layer_norm(values, gain, shift):
    centered = values - jnp.mean(values, axis=-1, keepdims=True)
    spread_ = jnp.mean(centered * centered, axis=-1, keepdims=True)
    return centered * lax.rsqrt(spread_ + norm_eps) * gain + shift


def unpack(vector_row):
    lengths = (D, D, 3 * D, D, D, D, D, FF, D, D, HD, HD, HD, HD)
    pieces = []
    offset = 0
    for length in lengths:
        pieces.append(vector_row[offset : offset + length])
        offset = offset + length
    return pieces


def head_gains(vec, heads):
    rows = [jnp.tile(piece, heads) for piece in vec[10:14]]
    return jnp.concatenate([jnp.stack(rows), jnp.zeros((4, heads * HD), f32)], axis=0)


def adam_update(
    weight, gradient, moment_one, moment_two, average, step_rate, decay_rate, clip_scale, fix_one, fix_two
):
    clipped = gradient * clip_scale
    moment_one = beta_one * moment_one + (1.0 - beta_one) * clipped
    moment_two = beta_two * moment_two + (1.0 - beta_two) * clipped * clipped
    first_hat = moment_one / fix_one
    second_hat = moment_two / fix_two
    weight = weight - step_rate * (
        first_hat / (jnp.sqrt(second_hat) + adam_eps) + decay_rate * weight
    )
    average = ema_decay * average + (1.0 - ema_decay) * weight
    return (weight, moment_one, moment_two, average)


def body(
    links,
    tokens,
    cotangent,
    slot_frame,
    step_count,
    *params,
):
    n_tok, n_head = links.n_tok, links.n_head
    devices = n_tok * n_head
    own = lax.axis_index("head")
    flip = lambda leaf: jnp.swapaxes(leaf, 1, 2)
    groups = []
    for at in range(0, 20, 5):
        qkv, proj, fc1, fc2, vec = params[at : at + 5]
        groups.append([qkv, flip(proj), fc1, flip(fc2), vec])
    masters = groups[0]

    slots = slot_frame.shape[0]
    per_head = slots // n_head
    held = slot_frame.reshape(n_head, per_head)
    held = jnp.concatenate(
        [lax.dynamic_slice_in_dim(held, own ^ step, 1, 0)[0] for step in range(n_head)]
    )
    index = jnp.arange(slots, dtype=jnp.int32)
    ahead = (held[None, :] < held[:, None]) | (
        (held[None, :] == held[:, None]) & (index[None, :] < index[:, None])
    )
    rank = jnp.sum(ahead.astype(jnp.int32), axis=1)
    order = jnp.sum(jnp.where(rank[None, :] == index[:, None], index[None, :], 0), axis=1).astype(jnp.int32)
    is_hi = (jnp.sum((held == held[0]).astype(jnp.int32)) == HI_BLOCKS).astype(jnp.int32).reshape(1)
    spans = (
        (HI_BLOCKS * BLOCK, LO_BLOCKS * BLOCK),
        (FRAMES * HI_BLOCKS * BLOCK, FRAMES * LO_BLOCKS * BLOCK),
    )

    vec_here = masters[4].shape[1]
    tile = lax.reduce_precision(masters[4], 8, 7).reshape(-1)
    tile = jnp.pad(tile, (0, 1024 - tile.shape[0])).reshape(8, 128)
    tiles = spread(tile, n_tok, n_head, 0).reshape(devices, 1024)[:, : 2 * vec_here]
    vectors = jnp.swapaxes(tiles.reshape(devices, 2, vec_here), 0, 1).reshape(2, devices * vec_here)
    vecs = [unpack(vectors[block]) for block in range(2)]

    qkv_low = [masters[0][block].astype(bf16) for block in range(2)]
    low = [
        jnp.concatenate([masters[kind][block].astype(bf16) for kind in (1, 2, 3)], axis=1)
        for block in range(2)
    ]
    places = links.gather_places()
    paired = links.paired
    width = D // n_head
    heads = width // HD
    own_rows = tokens.shape[0]
    cut = lambda rows: [rows[step * own_rows : (step + 1) * own_rows] for step in range(n_head)]
    gains = [head_gains(vec, heads) for vec in vecs]

    def attend(block, pieces, qkv_cols):
        qkv_bias = lax.dynamic_slice_in_dim(vecs[block][2].reshape(3, D), own * width, width, 1)
        return attention_forward(
            pieces, qkv_cols, qkv_bias.reshape(1, 3 * width), gains[block], order, is_hi, spans[block]
        )

    def enter(rows, mine, shard, collective_id):
        if paired:
            return enter_rows(rows, mine, shard, collective_id)
        planes = None if shard is None else links.gather_planes(shard)
        return links.rows_in(rows), lax.all_gather(mine, "tok", axis=0, tiled=True), planes

    def post(block, attended, hidden, pieces):
        vec, tail = vecs[block], vecs[1]
        rows = jnp.stack([vec[3], vec[4], vec[5], vec[6], vec[8], vec[9], tail[0], tail[1]])
        if not paired:
            attended = jnp.concatenate(links.by_index(links.exchange(cut(attended)), own), axis=1)
        return post_forward(
            attended,
            hidden,
            rows,
            vec[7].reshape(1, FF),
            (pieces, places),
            n_head,
            block == 1,
            paired,
            3 + block,
        )

    hidden_in = [tokens.astype(f32), None]
    normed = layer_norm(hidden_in[0], vecs[0][0], vecs[0][1]).astype(bf16)
    group, qkv_cols, saved, att_owns, mids, weights = ([None, None] for _ in range(6))

    mine = links.fetch_heads(qkv_low, own)
    normed, mine, low[0] = together(normed, mine, low[0])
    group[0], qkv_cols[0], planes = enter(normed, mine[0], low[0], 5)
    group[0], planes, qkv_cols[0], low[1] = together(group[0], planes, qkv_cols[0], low[1])
    near = links.gather_sides(planes)
    planes = links.gather_planes(low[1])
    saved[0] = attend(0, group[0], qkv_cols[0])
    saved[0], near, planes = together(saved[0], near, planes)
    weights[0] = links.gather_far(near)
    hidden_in[1], normed, *mids[0] = post(0, saved[0][0], hidden_in[0], weights[0])

    group[1], qkv_cols[1], _planes = enter(normed, mine[1], None, 6)
    group[1], planes = together(group[1], planes)
    near = links.gather_sides(planes)
    saved[1] = attend(1, group[1], qkv_cols[1])
    saved[1], near = together(saved[1], near)
    weights[1] = links.gather_far(near)
    hidden, _normed, *mids[1] = post(1, saved[1][0], hidden_in[1], weights[1])

    def post_back(block, grad):
        vec = vecs[block]
        down, act, slope, branch, after, two, att_own = mids[block]
        rows = jnp.stack([vec[4], vec[5], vec[9]] + [vec[9]] * 5)
        d_att, *rest = post_backward(
            att_own,
            grad,
            down,
            branch,
            after,
            two,
            rows,
            act,
            slope,
            (weights[block], places),
            n_head,
            paired,
            7 + block,
        )
        if not paired:
            parts = [
                lax.dynamic_slice_in_dim(d_att, (own ^ step) * width, width, 1) for step in range(n_head)
            ]
            d_att = jnp.concatenate(links.exchange(parts), axis=0)
        return d_att, *rest

    def attend_back(block, grad_heads):
        attended, raw, values, lse = saved[block]
        return attention_backward(
            raw, values, grad_heads, attended, lse, gains[block], order, is_hi, spans[block]
        )

    def rows_back(block, d_qkv, d_after):
        gain, shift = vecs[block][0], vecs[block][1]
        if paired:
            grad, sums = rows_out(
                d_qkv, qkv_cols[block], hidden_in[block], d_after, gain.reshape(1, D), 9 + block
            )
            return grad, sums[0], sums[1]
        d_normed = jnp.einsum("rc,dc->rd", d_qkv, qkv_cols[block], preferred_element_type=f32)
        back = links.rows_out(cut(d_normed.astype(bf16)))
        d_hidden, d_gain, d_shift = jax.vjp(layer_norm, hidden_in[block], gain, shift)[1](back)
        return d_after + d_hidden, d_gain, d_shift

    def qkv_grad(block, d_qkv):
        rows = jnp.concatenate(group[block], axis=0)
        return jnp.einsum("rd,rc->dc", rows, d_qkv, preferred_element_type=f32).astype(bf16)

    def vector_grad(norm_sums, sums, d_up_bias, head_sums, bias_sums):
        d_qkv_bias = lax.dynamic_update_slice_in_dim(
            jnp.zeros((3, D), f32), bias_sums[0].reshape(3, width), own * width, 1
        ).reshape(3 * D)
        head_sums = jnp.sum(head_sums[:4].reshape(4, heads, HD), axis=1).reshape(4 * HD)
        parts = [*norm_sums, d_qkv_bias, sums[5], sums[4], sums[2], sums[3], d_up_bias, sums[1], sums[0], head_sums]
        return jnp.concatenate(parts)

    d_att, d_after, sums, d_up_bias, grads = post_back(1, cotangent.astype(f32))
    grads = links.scatter_start(*grads)
    d_att, grads = together(d_att, grads)
    grads = links.scatter_first(grads)
    d_qkv, head_sums, bias_sums = attend_back(1, d_att)
    d_qkv, head_sums, bias_sums, grads = together(d_qkv, head_sums, bias_sums, grads)
    dw_qkv = links.return_cores(qkv_grad(1, d_qkv))
    grad_rows, *norm_sums = rows_back(1, d_qkv, d_after)
    d_vec_one = vector_grad(norm_sums, sums, d_up_bias, head_sums, bias_sums)
    grad_rows, grads, dw_qkv = together(grad_rows, grads, dw_qkv)
    grads_one = links.scatter_second(grads)
    mine_one = links.return_planes(dw_qkv)

    d_att, d_after, sums, d_up_bias, grads = post_back(0, grad_rows)
    d_att, grads_one, mine_one, grads = together(d_att, grads_one, mine_one, grads)
    grads = links.scatter_start(*grads)
    d_att, grads, grads_one = together(d_att, grads, grads_one)
    sum_one = links.scatter_last(grads_one)
    grads = links.scatter_first(grads)
    d_qkv, head_sums, bias_sums = attend_back(0, d_att)
    d_qkv, head_sums, bias_sums, grads, sum_one = together(d_qkv, head_sums, bias_sums, grads, sum_one)
    vec_shape = (devices, 2 * vec_here)

    def tiles_of(row_zero, row_one):
        both = jnp.stack([row_zero, row_one]).reshape(2, devices, vec_here)
        flat = jnp.swapaxes(both, 0, 1).reshape(vec_shape)
        return jnp.pad(flat, ((0, 0), (0, 1024 - vec_shape[1]))).reshape(devices, 8, 128)

    if paired:
        none = jnp.zeros((D,), f32)
        tiles = tiles_of(vector_grad((none, none), sums, d_up_bias, head_sums, bias_sums), d_vec_one)
        gain = vecs[0][0].reshape(1, D)
        grad_rows, norm_sums, sum_zero, *qkv_grads, d_vec = finish(
            d_qkv, qkv_cols[0], hidden_in[0], d_after, gain, group[0], *grads, tiles, mine_one, n_tok, n_head, 11
        )
        qkv_zero, qkv_one = [
            jnp.transpose(part.reshape(n_head, -1, 3, width), (1, 2, 0, 3)).reshape(-1, 3 * D) for part in qkv_grads
        ]
        late = jnp.concatenate([norm_sums[0], norm_sums[1]]).reshape(16, 128)
    else:
        grad_rows, *norm_sums = rows_back(0, d_qkv, d_after)
        dw_qkv = links.return_cores(qkv_grad(0, d_qkv))
        tiles = tiles_of(vector_grad(norm_sums, sums, d_up_bias, head_sums, bias_sums), d_vec_one)
        d_vec = swap(tiles, n_tok, n_head, 1)
        sum_zero = links.scatter_last(links.scatter_second(grads))
        qkv_zero, qkv_one = links.return_heads([links.return_planes(dw_qkv), mine_one], own)
        late = jnp.zeros((16, 128), f32)
    summed = []
    for qkv_part, rest in ((qkv_zero, sum_zero), (qkv_one, sum_one)):
        summed.append([qkv_part, rest[:, PROJ_AT:UP_AT], rest[:, UP_AT:DOWN_AT], rest[:, DOWN_AT:WIDE]])
    d_vec = d_vec.reshape(1024)[: 2 * vec_here].reshape(2, vec_here)
    gradients = [jnp.stack([summed[0][kind], summed[1][kind]]) for kind in range(4)]
    local_square = sum((jnp.sum(gradient * gradient) for gradient in gradients)) + jnp.sum(d_vec * d_vec)
    tile = jnp.concatenate([jnp.broadcast_to(local_square, (8, 128)), late], axis=0)
    squares = spread(tile, n_tok, n_head, 2)
    late = jnp.sum(squares[:, 8:], axis=0).reshape(2 * D)
    grad_norm = jnp.sqrt(jnp.sum(squares[:, 0, 0]) + jnp.sum(late * late))
    if paired:
        flat = jnp.concatenate([late, jnp.zeros((devices * vec_here - 2 * D,), f32)]).reshape(devices, vec_here)
        mine_late = lax.dynamic_slice_in_dim(flat, lax.axis_index("tok") * n_head + own, 1, 0)
        d_vec = d_vec + jnp.concatenate([mine_late, jnp.zeros((1, vec_here), f32)], axis=0)
    gradients.append(d_vec)
    clip_scale = clip_norm / jnp.maximum(grad_norm, clip_norm)
    step_float = step_count[0].astype(f32)
    fix_one = 1.0 - beta_one**step_float
    fix_two = 1.0 - beta_two**step_float
    updates = [
        adam_update(
            groups[0][kind],
            gradients[kind],
            groups[1][kind],
            groups[2][kind],
            groups[3][kind],
            step_rates[kind],
            decays[kind],
            clip_scale,
            fix_one,
            fix_two,
        )
        for kind in range(5)
    ]
    outs = [hidden, grad_rows, grad_norm]
    for part in range(4):
        for kind in range(5):
            leaf = updates[kind][part]
            outs.append(flip(leaf) if kind in (1, 3) else leaf)
    return tuple(outs)


def solution(mesh):
    rows = P(BOTH, None)
    kinds = (
        P(None, BOTH, None),
        P(None, None, BOTH),
        P(None, BOTH, None),
        P(None, None, BOTH),
        P(None, BOTH),
    )
    in_specs = (rows, rows, P("tok"), P()) + kinds * 4
    out_specs = (rows, rows, P()) + kinds * 4
    return jax.shard_map(
        functools.partial(body, Links(mesh)),
        mesh=mesh,
        in_specs=in_specs,
        out_specs=out_specs,
        check_vma=False,
    )
```

```python
import functools
import math

import jax
import jax.numpy as jnp
from jax import lax
from jax.experimental import pallas as pl
from jax.experimental.pallas import tpu as pltpu
from jax.sharding import PartitionSpec as P

D = 1024
HD = 64
FF = 4096
BLOCK = 128
HI_BLOCKS = 8
LO_BLOCKS = 4
FRAMES = 2

norm_eps = 1e-06
clip_norm = 1.0
beta_one = 0.9
beta_two = 0.999
adam_eps = 1e-08
ema_decay = 0.7
step_rates = (0.05, 0.4, 0.05, 0.025, 0.3)
decays = (0.05, 0.05, 0.05, 0.05, 0.0)

LOG2E = math.log2(math.e)
SPAN = 512
MESH_ID = pl.DeviceIdType.MESH
BOTH = ("tok", "head")
bf16 = jnp.bfloat16
f32 = jnp.float32
VMEM_BYTES = 60 << 20


def _peer(step, n_tok, n_head):
    n = n_tok * n_head
    me = lax.axis_index("tok") * n_head + lax.axis_index("head")
    to = lax.rem(me + step, n)
    return me, to, (to // n_head, lax.rem(to, n_head))


def _enter(n_tok, n_head):
    n = n_tok * n_head
    barrier = pltpu.get_barrier_semaphore()

    def greet(step, _):
        _, _, device = _peer(step, n_tok, n_head)
        pl.semaphore_signal(barrier, inc=1, device_id=device, device_id_type=MESH_ID)
        return 0

    lax.fori_loop(1, n, greet, 0)
    pl.semaphore_wait(barrier, n - 1)


def spread_kernel(n_tok, n_head, x_ref, o_ref, send_sem, recv_sem):
    n = n_tok * n_head
    _enter(n_tok, n_head)
    me = lax.axis_index("tok") * n_head + lax.axis_index("head")
    o_ref[me] = x_ref[...]

    def copy(step):
        me, _, device = _peer(step, n_tok, n_head)
        return pltpu.make_async_remote_copy(
            src_ref=x_ref,
            dst_ref=o_ref.at[me],
            send_sem=send_sem.at[step],
            recv_sem=recv_sem.at[step],
            device_id=device,
            device_id_type=MESH_ID,
        )

    def start(step, _):
        copy(step).start()
        return 0

    def finish(step, _):
        copy(step).wait()
        return 0

    lax.fori_loop(1, n, start, 0)
    lax.fori_loop(1, n, finish, 0)


def swap_kernel(n_tok, n_head, x_ref, o_ref, land, send_sem, recv_sem):
    n = n_tok * n_head
    _enter(n_tok, n_head)
    me = lax.axis_index("tok") * n_head + lax.axis_index("head")

    def copy(step):
        me, to, device = _peer(step, n_tok, n_head)
        return pltpu.make_async_remote_copy(
            src_ref=x_ref.at[to],
            dst_ref=land.at[step],
            send_sem=send_sem.at[step],
            recv_sem=recv_sem.at[step],
            device_id=device,
            device_id_type=MESH_ID,
        )

    def start(step, _):
        copy(step).start()
        return 0

    def finish(step, _):
        copy(step).wait()
        return 0

    lax.fori_loop(1, n, start, 0)
    lax.fori_loop(1, n, finish, 0)
    o_ref[...] = x_ref[me] + jnp.sum(land[1:], axis=0)


def spread(tile, n_tok, n_head, collective_id):
    n = n_tok * n_head
    return pl.pallas_call(
        functools.partial(spread_kernel, n_tok, n_head),
        out_shape=jax.ShapeDtypeStruct((n,) + tile.shape, tile.dtype),
        in_specs=[pl.BlockSpec(memory_space=pltpu.VMEM)],
        out_specs=pl.BlockSpec(memory_space=pltpu.VMEM),
        scratch_shapes=[pltpu.SemaphoreType.DMA((n,)), pltpu.SemaphoreType.DMA((n,))],
        compiler_params=pltpu.CompilerParams(collective_id=collective_id, has_side_effects=True),
    )(tile)


def swap(tiles, n_tok, n_head, collective_id):
    n = n_tok * n_head
    return pl.pallas_call(
        functools.partial(swap_kernel, n_tok, n_head),
        out_shape=jax.ShapeDtypeStruct(tiles.shape[1:], tiles.dtype),
        in_specs=[pl.BlockSpec(memory_space=pltpu.VMEM)],
        out_specs=pl.BlockSpec(memory_space=pltpu.VMEM),
        scratch_shapes=[
            pltpu.VMEM(tiles.shape, tiles.dtype),
            pltpu.SemaphoreType.DMA((n,)),
            pltpu.SemaphoreType.DMA((n,)),
        ],
        compiler_params=pltpu.CompilerParams(collective_id=collective_id, has_side_effects=True),
    )(tiles)


def _lane_mean(values, grouping):
    top = values.astype(bf16)
    rest = (values - top.astype(f32)).astype(bf16)
    return jnp.dot(top, grouping, preferred_element_type=f32) + jnp.dot(
        rest, grouping, preferred_element_type=f32
    )


def _grouping(width):
    row = lax.broadcasted_iota(jnp.int32, (width, width), 0) // HD
    col = lax.broadcasted_iota(jnp.int32, (width, width), 1) // HD
    return jnp.where(row == col, 1.0 / HD, 0.0).astype(bf16)


def _unit(values, grouping):
    centered = values - _lane_mean(values, grouping)
    spread_ = _lane_mean(centered * centered, grouping)
    scale = lax.rsqrt(spread_ + norm_eps)
    return centered * scale, scale


def _only(values, head):
    lane = lax.broadcasted_iota(jnp.int32, values.shape, 1)
    return jnp.where(lane // HD == head, values, jnp.zeros_like(values))


NT = (((1,), (1,)), ((), ()))
TN = (((0,), (0,)), ((), ()))


def forward_kernel(
    heads, pieces, spans, tile_rows, order_ref, hi_ref, *refs
):
    x_refs = refs[:pieces]
    w_ref, bias_ref, gains_ref, att_ref, raw_ref, val_ref, lse_ref, q_s, k_s, v_s, acc = refs[pieces:]
    width = heads * HD
    rows = att_ref.shape[0]
    blocks = rows // BLOCK
    piece_rows = rows // pieces
    for at in range(pieces):
        full = jnp.dot(x_refs[at][...], w_ref[...], preferred_element_type=f32) + bias_ref[...]
        here = pl.ds(at * piece_rows, piece_rows)
        raw_ref[here, :] = full[:, : 2 * width]
        val_ref[here, :] = full[:, 2 * width :].astype(bf16)
    grouping = _grouping(width)

    def place(at, _):
        here = pl.ds(pl.multiple_of(order_ref[at] * BLOCK, BLOCK), BLOCK)
        there = pl.ds(pl.multiple_of(at * BLOCK, BLOCK), BLOCK)
        unit_q, _s = _unit(raw_ref[here, :width], grouping)
        unit_k, _s = _unit(raw_ref[here, width:], grouping)
        q_s[there, :] = ((unit_q * gains_ref[0:1, :] + gains_ref[1:2, :]) * HD ** (-0.5)).astype(bf16)
        key = (unit_k * gains_ref[2:3, :] + gains_ref[3:4, :]).astype(bf16)
        value = val_ref[here, :]
        for head in range(heads):
            k_s[head, there, :] = _only(key, head)
            v_s[head, there, :] = _only(value, head)
        return 0

    lax.fori_loop(0, blocks, place, 0)
    per_tile = tile_rows // BLOCK

    def attend(span):
        def tile(at, _):
            here = pl.ds(pl.multiple_of(at * tile_rows, tile_rows), tile_rows)
            first = at * tile_rows // span * span
            there = pl.ds(pl.multiple_of(first, span), span)
            query = q_s[here, :]
            lane = lax.broadcasted_iota(jnp.int32, (tile_rows, 128), 1)
            logs = jnp.zeros((tile_rows, 128), f32)
            for head in range(heads):
                scores = lax.dot_general(query, k_s[head, there, :], NT, preferred_element_type=f32)
                top = jnp.max(scores, axis=1, keepdims=True) * LOG2E
                probs = jnp.exp2(scores * LOG2E - top)
                total = jnp.sum(probs, axis=1, keepdims=True)
                part = jnp.dot(
                    probs.astype(bf16), v_s[head, there, :], preferred_element_type=f32
                ) / total
                if head == 0:
                    acc[...] = part
                else:
                    acc[...] += part
                logs = jnp.where(lane == head, top + jnp.log2(total), logs)
            lse_ref[here, :] = logs
            for sub in range(per_tile):
                out = pl.ds(pl.multiple_of(order_ref[at * per_tile + sub] * BLOCK, BLOCK), BLOCK)
                att_ref[out, :] = acc[sub * BLOCK : (sub + 1) * BLOCK, :].astype(bf16)
            return 0

        lax.fori_loop(0, rows // tile_rows, tile, 0)

    @pl.when(hi_ref[0] == 1)
    def _():
        attend(spans[0])

    @pl.when(hi_ref[0] == 0)
    def _():
        attend(spans[1])


def attention_forward(pieces, weight, bias, gains, order, is_hi, spans):
    heads = weight.shape[1] // (3 * HD)
    width = heads * HD
    rows = sum(piece.shape[0] for piece in pieces)
    tile_rows = 256
    smem = pl.BlockSpec(memory_space=pltpu.SMEM)
    vmem = pl.BlockSpec(memory_space=pltpu.VMEM)
    flops = 2 * rows * (D * 3 * width + 8 * spans[0] * width)
    return pl.pallas_call(
        functools.partial(forward_kernel, heads, len(pieces), spans, tile_rows),
        out_shape=(
            jax.ShapeDtypeStruct((rows, width), bf16),
            jax.ShapeDtypeStruct((rows, 2 * width), f32),
            jax.ShapeDtypeStruct((rows, width), bf16),
            jax.ShapeDtypeStruct((rows, 128), f32),
        ),
        in_specs=[smem, smem] + [vmem] * (len(pieces) + 3),
        out_specs=(vmem,) * 4,
        scratch_shapes=[
            pltpu.VMEM((rows, width), bf16),
            pltpu.VMEM((heads, rows, width), bf16),
            pltpu.VMEM((heads, rows, width), bf16),
            pltpu.VMEM((tile_rows, width), f32),
        ],
        compiler_params=pltpu.CompilerParams(vmem_limit_bytes=VMEM_BYTES),
        cost_estimate=pl.CostEstimate(
            flops=flops, bytes_accessed=rows * (2 * D + 14 * width), transcendentals=rows * spans[0] * heads
        ),
    )(order, is_hi, *pieces, weight, bias, gains)


def backward_kernel(
    heads,
    spans,
    order_ref,
    hi_ref,
    raw_ref,
    val_ref,
    grad_ref,
    att_ref,
    lse_ref,
    gains_ref,
    out_ref,
    sums_ref,
    bias_ref,
    q_s,
    o_s,
    k_m,
    v_m,
    q_m,
    o_m,
    dq_s,
    dk_s,
    dv_s,
    lse_t,
    delta_t,
):
    width = heads * HD
    rows = val_ref.shape[0]
    blocks = rows // BLOCK
    grouping = _grouping(width)
    head_of = lax.broadcasted_iota(jnp.int32, (8, width), 1) // HD
    picks = jnp.where(head_of == lax.broadcasted_iota(jnp.int32, (8, width), 0), 1.0, 0.0).astype(bf16)

    def place(at, _):
        here = pl.ds(pl.multiple_of(order_ref[at] * BLOCK, BLOCK), BLOCK)
        there = pl.ds(pl.multiple_of(at * BLOCK, BLOCK), BLOCK)
        unit_q, _s = _unit(raw_ref[here, :width], grouping)
        unit_k, _s = _unit(raw_ref[here, width:], grouping)
        query = ((unit_q * gains_ref[0:1, :] + gains_ref[1:2, :]) * HD ** (-0.5)).astype(bf16)
        key = (unit_k * gains_ref[2:3, :] + gains_ref[3:4, :]).astype(bf16)
        value = val_ref[here, :]
        grad = grad_ref[here, :]
        q_s[there, :] = query
        o_s[there, :] = grad
        for head in range(heads):
            k_m[head, there, :] = _only(key, head)
            v_m[head, there, :] = _only(value, head)
            q_m[head, there, :] = _only(query, head)
            o_m[head, there, :] = _only(grad, head)
        both = grad.astype(f32) * att_ref[here, :].astype(f32)
        top = both.astype(bf16)
        rest = (both - top.astype(f32)).astype(bf16)
        delta_t[:, there] = lax.dot_general(picks, top, NT, preferred_element_type=f32) + lax.dot_general(
            picks, rest, NT, preferred_element_type=f32
        )
        lse_t[:, there] = jnp.transpose(lse_ref[there, :])[:8, :]
        dq_s[there, :] = jnp.zeros((BLOCK, width), f32)
        dk_s[there, :] = jnp.zeros((BLOCK, width), f32)
        dv_s[there, :] = jnp.zeros((BLOCK, width), f32)
        return 0

    lax.fori_loop(0, blocks, place, 0)
    span = jnp.where(hi_ref[0] == 1, spans[0], spans[1])

    def tile(at, _):
        here = pl.ds(pl.multiple_of(at * SPAN, SPAN), SPAN)
        first = at * SPAN // span * span // SPAN

        def chunk(key_at, _):
            there = pl.ds(pl.multiple_of(key_at * SPAN, SPAN), SPAN)
            for head in range(heads):
                scores = lax.dot_general(k_m[head, there, :], q_s[here, :], NT, preferred_element_type=f32)
                probs = jnp.exp2(scores * LOG2E - lse_t[head : head + 1, here])
                grad_probs = lax.dot_general(
                    v_m[head, there, :], o_s[here, :], NT, preferred_element_type=f32
                )
                grad_scores = (probs * (grad_probs - delta_t[head : head + 1, here])).astype(bf16)
                dv_s[there, :] += jnp.dot(probs.astype(bf16), o_m[head, here, :], preferred_element_type=f32)
                dk_s[there, :] += jnp.dot(grad_scores, q_m[head, here, :], preferred_element_type=f32)
                dq_s[here, :] += lax.dot_general(
                    grad_scores, k_m[head, there, :], TN, preferred_element_type=f32
                )
            return 0

        lax.fori_loop(first, first + span // SPAN, chunk, 0)
        return 0

    lax.fori_loop(0, rows // SPAN, tile, 0)
    sums_ref[...] = jnp.zeros_like(sums_ref)
    bias_ref[...] = jnp.zeros_like(bias_ref)

    def pull(grad, unit, scale, gain):
        grad_unit = grad * gain
        inner = _lane_mean(grad_unit, grouping)
        cross = _lane_mean(grad_unit * unit, grouping)
        return scale * (grad_unit - inner - unit * cross)

    def leave(at, _):
        here = pl.ds(pl.multiple_of(order_ref[at] * BLOCK, BLOCK), BLOCK)
        there = pl.ds(pl.multiple_of(at * BLOCK, BLOCK), BLOCK)
        unit_q, scale_q = _unit(raw_ref[here, :width], grouping)
        unit_k, scale_k = _unit(raw_ref[here, width:], grouping)
        grad_q = dq_s[there, :] * HD ** (-0.5)
        grad_k = dk_s[there, :]
        sums_ref[0:1, :] += jnp.sum(grad_q * unit_q, axis=0, keepdims=True)
        sums_ref[1:2, :] += jnp.sum(grad_q, axis=0, keepdims=True)
        sums_ref[2:3, :] += jnp.sum(grad_k * unit_k, axis=0, keepdims=True)
        sums_ref[3:4, :] += jnp.sum(grad_k, axis=0, keepdims=True)
        low_q = pull(grad_q, unit_q, scale_q, gains_ref[0:1, :]).astype(bf16)
        low_k = pull(grad_k, unit_k, scale_k, gains_ref[2:3, :]).astype(bf16)
        low_v = dv_s[there, :].astype(bf16)
        for part, low in enumerate((low_q, low_k, low_v)):
            lanes = slice(part * width, (part + 1) * width)
            out_ref[here, lanes] = low
            bias_ref[0:1, lanes] += jnp.sum(low.astype(f32), axis=0, keepdims=True)
        return 0

    lax.fori_loop(0, blocks, leave, 0)


def attention_backward(raw, values, grad, attended, lse, gains, order, is_hi, spans):
    rows, width = values.shape
    heads = width // HD
    smem = pl.BlockSpec(memory_space=pltpu.SMEM)
    vmem = pl.BlockSpec(memory_space=pltpu.VMEM)
    flops = 2 * rows * 20 * spans[0] * width
    masked = pltpu.VMEM((heads, rows, width), bf16)
    return pl.pallas_call(
        functools.partial(backward_kernel, heads, spans),
        out_shape=(
            jax.ShapeDtypeStruct((rows, 3 * width), bf16),
            jax.ShapeDtypeStruct((8, width), f32),
            jax.ShapeDtypeStruct((8, 3 * width), f32),
        ),
        in_specs=[smem, smem] + [vmem] * 6,
        out_specs=(vmem,) * 3,
        scratch_shapes=[
            pltpu.VMEM((rows, width), bf16),
            pltpu.VMEM((rows, width), bf16),
            masked,
            masked,
            masked,
            masked,
            pltpu.VMEM((rows, width), f32),
            pltpu.VMEM((rows, width), f32),
            pltpu.VMEM((rows, width), f32),
            pltpu.VMEM((8, rows), f32),
            pltpu.VMEM((8, rows), f32),
        ],
        compiler_params=pltpu.CompilerParams(vmem_limit_bytes=VMEM_BYTES),
        cost_estimate=pl.CostEstimate(
            flops=flops, bytes_accessed=rows * 24 * width, transcendentals=rows * spans[0] * heads
        ),
    )(order, is_hi, raw, values, grad, attended, lse, gains)


class Links:
    def __init__(self, mesh):
        self.n_tok = mesh.shape["tok"]
        self.n_head = mesh.shape["head"]
        self.paired = self.n_tok == 8 and self.n_head == 4

    def head(self, values, step):
        return lax.ppermute(values, "head", [(i, i ^ step) for i in range(self.n_head)])

    def tok(self, values, step):
        return lax.ppermute(values, "tok", [(i, i ^ step) for i in range(self.n_tok)])

    def rows_in(self, rows):
        if not self.paired:
            return [rows] + [self.head(rows, step) for step in range(1, self.n_head)]
        half = rows.shape[0] // 2
        one, two = self.head(rows, 1), self.head(rows, 2)
        far = jnp.concatenate([self.head(one[:half], 2), self.head(two[half:], 1)], axis=0)
        return [rows, one, two, far]

    def rows_out(self, parts):
        if not self.paired:
            moved = [self.head(parts[step], step).astype(f32) for step in range(1, self.n_head)]
            return parts[0].astype(f32) + sum(moved)
        half = parts[0].shape[0] // 2
        upper = [part[:half] for part in parts]
        lower = [part[half:] for part in parts]
        pass_up = (upper[2].astype(f32) + self.head(upper[3], 1).astype(f32)).astype(bf16)
        pass_low = (lower[1].astype(f32) + self.head(lower[3], 2).astype(f32)).astype(bf16)
        up = upper[0].astype(f32) + self.head(upper[1], 1).astype(f32) + self.head(pass_up, 2).astype(f32)
        low = lower[0].astype(f32) + self.head(lower[2], 2).astype(f32) + self.head(pass_low, 1).astype(f32)
        return jnp.concatenate([up, low], axis=0)

    def exchange(self, parts):
        return [parts[0]] + [self.head(parts[step], step) for step in range(1, self.n_head)]

    def by_index(self, pieces, own):
        return [
            lax.select_n((own ^ at).astype(jnp.int32), *pieces) if len(pieces) > 1 else pieces[0]
            for at in range(len(pieces))
        ]

    def zed(self):
        return lax.axis_index("tok") // 2

    def core(self):
        return lax.rem(lax.axis_index("tok"), 2)

    def planes(self, shard):
        pieces = [shard] + [self.tok(shard, 2 * step) for step in range(1, 4)]
        return jnp.stack(self.by_index(pieces, self.zed()))

    def gather_places(self):
        if not self.paired:
            return [None]
        spots = ((0, 4, 0), (0, 4, 1), (0, 4, 2), (0, 2, 3), (2, 2, 3))
        return [("head", first, count, core, to) for first, count, to in spots for core in range(2)]

    def gather_planes(self, shard):
        if not self.paired:
            whole = lax.all_gather(shard, BOTH, axis=0, tiled=True)
            return [whole.reshape(4, 2, 4, whole.shape[0] // 32, whole.shape[1])]
        return [self.planes(shard)]

    def gather_sides(self, own):
        if not self.paired:
            return own
        return [own[0], self.head(own[0], 1), self.head(own[0], 2)]

    def scatter_start(self, pieces, got):
        if not self.paired:
            return pieces
        return [(one.astype(f32) + two.astype(f32)).astype(bf16) for one, two in zip(pieces, got)]

    def scatter_first(self, sums):
        if not self.paired:
            return sums
        low = [part[:2] for part in sums]
        top = [part[2:] for part in sums]
        come_low = self.head(jnp.concatenate([low[1], low[3]], axis=0), 1).astype(f32)
        come_top = self.head(jnp.concatenate([top[2], top[3]], axis=0), 2).astype(f32)
        pass_low = (low[2].astype(f32) + come_low[2:]).astype(bf16)
        pass_top = (top[1].astype(f32) + come_top[2:]).astype(bf16)
        own_low = low[0].astype(f32) + come_low[:2]
        own_top = top[0].astype(f32) + come_top[:2]
        own = jnp.concatenate([own_low.astype(bf16), own_top.astype(bf16)], axis=0)
        return [own, jnp.concatenate([pass_low, pass_top], axis=0)]

    def scatter_second(self, halves):
        if not self.paired:
            return halves
        own, passed = halves
        low = own[:2].astype(f32) + self.head(passed[:2], 2).astype(f32)
        top = own[2:].astype(f32) + self.head(passed[2:], 1).astype(f32)
        return [jnp.concatenate([low, top], axis=0).astype(bf16)]

    def scatter_last(self, planes):
        if not self.paired:
            whole = planes[0].reshape(-1, planes[0].shape[-1])
            return lax.psum_scatter(whole, BOTH, scatter_dimension=0, tiled=True).astype(f32)
        return self.sum_planes(planes[0])

    def sum_planes(self, parts):
        zed = self.zed()
        pick = lambda step: lax.dynamic_slice_in_dim(parts, zed ^ step, 1, 0)[0]
        total = pick(0).astype(f32)
        for step in range(1, 4):
            total = total + self.tok(pick(step).astype(bf16), 2 * step).astype(f32)
        return total

    def fetch_heads(self, shards, own):
        own_rows = shards[0].shape[0]
        width = D // self.n_head
        cut = jnp.stack(shards).reshape(len(shards), own_rows, 3, D)
        parts = [
            lax.dynamic_slice_in_dim(cut, (own ^ step) * width, width, 3).reshape(
                len(shards), own_rows, 3 * width
            )
            for step in range(self.n_head)
        ]
        moved = jnp.stack(self.by_index(self.exchange(parts), own), axis=1)
        return [moved[at].reshape(self.n_head * own_rows, 3 * width) for at in range(len(shards))]

    def return_cores(self, grad):
        if not self.paired:
            return grad
        view = grad.reshape((4, 2, grad.shape[0] // 8, grad.shape[1]))
        core = self.core()
        cut = lambda at: lax.dynamic_slice_in_dim(view, at, 1, 1)[:, 0]
        return (cut(core).astype(f32) + self.tok(cut(core ^ 1), 1).astype(f32)).astype(bf16)

    def return_planes(self, grad):
        if not self.paired:
            return lax.psum_scatter(grad, "tok", scatter_dimension=0, tiled=True)
        return self.sum_planes(grad).astype(bf16)

    def return_heads(self, both, own):
        width = D // self.n_head
        stack = jnp.stack(both)
        own_rows = stack.shape[1] // self.n_head
        parts = [
            lax.dynamic_slice_in_dim(stack, (own ^ step) * own_rows, own_rows, 1)
            for step in range(self.n_head)
        ]
        back = jnp.stack(self.by_index(self.exchange(parts), own), axis=2)
        back = back.reshape(len(both), own_rows, self.n_head, 3, width)
        return jnp.swapaxes(back, 2, 3).reshape(len(both), own_rows, 3 * D).astype(f32)


def together(*values):
    return lax.optimization_barrier(values)


CHUNK = 512


def _paired(value, step, bits):
    total = 0
    for bit in range(bits):
        one = lax.rem(value // (1 << bit), 2)
        total = total + (1 - one if (step >> bit) % 2 else one) * (1 << bit)
    return total


def _slot(ref, place):
    if place is None:
        return ref
    tok = lax.axis_index("tok")
    side = _paired(lax.rem(tok, 2), place[-1] if place[0] == "plane" else place[3], 1)
    if place[0] == "plane":
        return ref.at[_paired(tok // 2, place[1], 2), side]
    return ref.at[pl.ds(place[1], place[2]), side, _paired(lax.axis_index("head"), place[4], 2)]


PROJ_AT, UP_AT, DOWN_AT, WIDE = 0, D, D + FF, D + 2 * FF


def _cols(ref, at, size):
    window = pl.ds(pl.multiple_of(at, 128), size)
    return ref.at[(slice(None),) * (len(ref.shape) - 1) + (window,)]


def _copies(pieces, places, whole, at, size, sems, inward):
    moves = []
    for index, (piece, place) in enumerate(zip(pieces, places)):
        outside = _cols(piece, at, size)
        inside = _slot(whole, place)
        pair = (outside, inside) if inward else (inside, outside)
        moves.append(pltpu.make_async_copy(pair[0], pair[1], sems.at[index]))
    return moves


def _start(moves):
    for move in moves:
        move.start()


def _wait(moves):
    for move in moves:
        move.wait()


def _flat(values):
    return values.reshape(D, values.shape[-1])


def _norm(values):
    centered = values - jnp.mean(values, axis=-1, keepdims=True)
    scale = lax.rsqrt(jnp.mean(centered * centered, axis=-1, keepdims=True) + norm_eps)
    return centered * scale, scale


def _own_column(step, n_head):
    at = _paired(lax.axis_index("head"), step, n_head.bit_length() - 1)
    return pl.multiple_of(at * (D // n_head), 128)


def _mate(step):
    return lax.axis_index("tok"), _paired(lax.axis_index("head"), step, 2)


def _sibling():
    return _paired(lax.axis_index("tok"), 1, 3), lax.axis_index("head")


def _greet(devices):
    barrier = pltpu.get_barrier_semaphore()
    for device in devices:
        pl.semaphore_signal(barrier, inc=1, device_id=device, device_id_type=MESH_ID)
    pl.semaphore_wait(barrier, len(devices))


def _send(source, target, send_sem, recv_sem, device):
    return pltpu.make_async_remote_copy(
        src_ref=source,
        dst_ref=target,
        send_sem=send_sem,
        recv_sem=recv_sem,
        device_id=device,
        device_id_type=MESH_ID,
    )


def enter_kernel(wide, *refs):
    x_ref, q_ref, refs = refs[0], refs[1], refs[2:]
    if wide:
        shard_ref, refs = refs[0], refs[1:]
    one_ref, two_ref, far_ref, full_ref, refs = *refs[:4], refs[4:]
    if wide:
        planes_ref, refs = refs[0], refs[1:]
    send_sem, recv_sem, z_send, z_recv, own_sem, core_sem = refs
    tok, head = lax.axis_index("tok"), lax.axis_index("head")
    zed, core = tok // 2, lax.rem(tok, 2)
    one_way, two_way = _mate(1), _mate(2)
    barrier = pltpu.get_barrier_semaphore()
    greet = lambda device: pl.semaphore_signal(barrier, inc=1, device_id=device, device_id_type=MESH_ID)
    for device in (one_way, two_way, _sibling()):
        greet(device)

    @pl.when(zed < 3)
    def _():
        greet((tok + 2, head))

    @pl.when(zed > 0)
    def _():
        greet((tok - 2, head))

    edge = (zed == 0) | (zed == 3)

    @pl.when(edge)
    def _():
        pl.semaphore_wait(barrier, 4)

    @pl.when(jnp.logical_not(edge))
    def _():
        pl.semaphore_wait(barrier, 5)

    rows = x_ref.shape[0]
    parts = 4
    size = rows // parts

    def move(lane, part, source, target, device):
        here = pl.ds(part * size, size)
        return _send(source.at[here], target.at[here], send_sem.at[lane, part], recv_sem.at[lane, part], device)

    to_one = lambda part: move(0, part, x_ref, one_ref, one_way)
    to_two = lambda part: move(1, part, x_ref, two_ref, two_way)
    on_two = lambda part: move(2, part, one_ref, far_ref, two_way)
    on_one = lambda part: move(2, part, two_ref, far_ref, one_way)
    homes = [(q_ref, lambda plane: full_ref.at[plane, core])]
    if wide:
        homes.append((shard_ref, lambda plane: planes_ref.at[plane]))

    def climb(up, step):
        plane = jnp.clip(zed - step if up else zed + step, 0, 3)
        device = (jnp.clip(tok + 2 if up else tok - 2, 0, 7), head)
        return [
            _send(
                home(plane) if step else source,
                home(plane),
                z_send.at[int(up), step, index],
                z_recv.at[int(up), step, index],
                device,
            )
            for index, (source, home) in enumerate(homes)
        ]

    def sends(up, step):
        return (zed >= step) & (zed < 3) if up else (zed <= 3 - step) & (zed > 0)

    def comes(up, step):
        return zed >= step + 1 if up else zed <= 2 - step

    def climb_start(up, step):
        @pl.when(sends(up, step))
        def _():
            _start(climb(up, step))

    def climb_come(up, step):
        @pl.when(comes(up, step))
        def _():
            for copy in climb(up, step):
                copy.wait_recv()

    for turn in range(parts):
        to_one(turn).start()
        to_two(parts - 1 - turn).start()
    for up in (True, False):
        climb_start(up, 0)
    stays = [
        pltpu.make_async_copy(source, home(zed), own_sem.at[index]) for index, (source, home) in enumerate(homes)
    ]
    _start(stays)
    for turn in range(parts // 2):
        to_one(turn).wait_recv()
        on_two(turn).start()
        to_two(parts - 1 - turn).wait_recv()
        on_one(parts - 1 - turn).start()
    for step in range(3):
        for up in (True, False):
            climb_come(up, step)
            if step < 2:
                climb_start(up, step + 1)
    _wait(stays)
    mine = full_ref.at[:, core]
    over = _send(mine, mine, core_sem.at[0], core_sem.at[1], _sibling())
    over.start()
    for turn in range(parts // 2, parts):
        to_one(turn).wait_recv()
        to_two(parts - 1 - turn).wait_recv()
    for turn in range(parts):
        to_one(turn).wait_send()
        to_two(turn).wait_send()
    for turn in range(parts // 2):
        on_two(turn).wait()
        on_one(parts - 1 - turn).wait()
    for step in range(3):
        for up in (True, False):

            @pl.when(sends(up, step))
            def _():
                for copy in climb(up, step):
                    copy.wait_send()

    over.wait()


def enter_rows(rows, mine, shard, collective_id):
    hbm = pl.BlockSpec(memory_space=pl.ANY)
    like = jax.ShapeDtypeStruct(rows.shape, rows.dtype)
    outs = [like, like, like, jax.ShapeDtypeStruct((4, 2) + mine.shape, mine.dtype)]
    given = [rows, mine]
    if shard is not None:
        outs.append(jax.ShapeDtypeStruct((4,) + shard.shape, shard.dtype))
        given.append(shard)
    sems = pltpu.SemaphoreType.DMA
    one, two, far, full, *planes = pl.pallas_call(
        functools.partial(enter_kernel, shard is not None),
        out_shape=tuple(outs),
        in_specs=[hbm] * len(given),
        out_specs=(hbm,) * len(outs),
        scratch_shapes=[sems((3, 4)), sems((3, 4)), sems((2, 3, 2)), sems((2, 3, 2)), sems((2,)), sems((2,))],
        compiler_params=pltpu.CompilerParams(collective_id=collective_id, has_side_effects=True),
        cost_estimate=pl.CostEstimate(flops=0, bytes_accessed=150 << 20, transcendentals=0),
    )(*given)
    return [rows, one, two, far], full.reshape(8 * mine.shape[0], mine.shape[1]), planes


def _norm_pull(grad_unit, unit, scale):
    inner = jnp.mean(grad_unit, axis=-1, keepdims=True)
    cross = jnp.mean(grad_unit * unit, axis=-1, keepdims=True)
    return scale * (grad_unit - inner - unit * cross)


def rows_out_kernel(grad_ref, weight_ref, hidden_ref, after_ref, gain_ref, out_ref, sums_ref, away, come, send_sem, recv_sem):
    one_way, two_way = _mate(1), _mate(2)
    _greet([one_way, two_way])
    rows = hidden_ref.shape[0]
    half = rows // 2

    def term(step, low):
        here = pl.ds(step * rows + (0 if low else half), half)
        return lax.dot_general(grad_ref[here, :], weight_ref[...], NT, preferred_element_type=f32)

    def move(slot, device):
        return _send(away.at[slot], come.at[slot], send_sem.at[slot], recv_sem.at[slot], device)

    ways = (one_way, two_way, one_way, two_way, two_way, one_way)
    for slot, (step, low) in enumerate(((3, True), (3, False), (1, True), (2, False))):
        away[slot] = term(step, low).astype(bf16)
        move(slot, ways[slot]).start()
    pass_low = term(2, True)
    pass_top = term(1, False)
    move(0, ways[0]).wait_recv()
    away[4] = (pass_low + come[0].astype(f32)).astype(bf16)
    move(4, ways[4]).start()
    move(1, ways[1]).wait_recv()
    away[5] = (pass_top + come[1].astype(f32)).astype(bf16)
    move(5, ways[5]).start()
    sums_ref[...] = jnp.zeros_like(sums_ref)
    for low in (True, False):
        here = pl.ds(0 if low else half, half)
        own = term(0, low)
        unit, scale = _norm(hidden_ref[here, :])
        near, far = (2, 4) if low else (3, 5)
        move(near, ways[near]).wait_recv()
        move(far, ways[far]).wait_recv()
        grad = own + come[near].astype(f32) + come[far].astype(f32)
        sums_ref[0:1, :] += jnp.sum(grad * unit, axis=0, keepdims=True)
        sums_ref[1:2, :] += jnp.sum(grad, axis=0, keepdims=True)
        out_ref[here, :] = after_ref[here, :] + _norm_pull(grad * gain_ref[0:1, :], unit, scale)
    for slot in range(6):
        move(slot, ways[slot]).wait_send()


def rows_out(grad, weight, hidden, after, gain, collective_id):
    rows = hidden.shape[0]
    vmem = pl.BlockSpec(memory_space=pltpu.VMEM)
    buffer = pltpu.VMEM((6, rows // 2, D), bf16)
    sems = pltpu.SemaphoreType.DMA((6,))
    return pl.pallas_call(
        rows_out_kernel,
        out_shape=(jax.ShapeDtypeStruct((rows, D), f32), jax.ShapeDtypeStruct((8, D), f32)),
        in_specs=[vmem] * 5,
        out_specs=(vmem, vmem),
        scratch_shapes=[buffer, buffer, sems, sems],
        compiler_params=pltpu.CompilerParams(
            collective_id=collective_id, has_side_effects=True, vmem_limit_bytes=VMEM_BYTES
        ),
        cost_estimate=pl.CostEstimate(flops=0, bytes_accessed=150 << 20, transcendentals=0),
    )(grad, weight, hidden, after, gain)


def post_forward_kernel(n_head, places, last, remote, *refs):
    count = len(places)
    att_ref, refs = refs[0], refs[1:]
    hidden_ref, rows_ref, up_bias_ref, refs = refs[0], refs[1], refs[2], refs[3:]
    given = 3 if remote else count
    weight_refs, refs = refs[:given], refs[given:]
    next_ref, normed_ref, down_ref, act_ref, slope_ref, branch_hbm, after_hbm, two_hbm, att_hbm, refs = *refs[:9], refs[9:]
    if remote:
        (own, one, two), (far_low, far_top), refs = weight_refs, refs[:2], refs[2:]
        side_own, side_one, side_two, side_low, side_top, refs = *refs[:5], refs[5:]
        weight_refs = (own, side_own, one, side_one, two, side_two, far_low, side_low, far_top, side_top)
    proj_s, up_s, down_s, att_s, branch_s, after_s, two_s, acc, proj_sem, up_sem, down_sem, out_sem, send_sem, recv_sem, refs = (
        *refs[:14],
        refs[14:],
    )
    at = pl.program_id(0)
    chunks = pl.num_programs(0)
    if remote:
        relay_send, relay_recv, side_send, side_recv = refs
        groups = WIDE // D
        order = [0] + [first for pair in zip(range(1, 1 + groups // 2), range(1 + groups // 2, groups)) for first in pair]

        def relay(group):
            part = lambda ref: _cols(ref, group * D, D)
            return [
                _send(
                    part(one.at[pl.ds(0, 2)]),
                    part(far_low),
                    relay_send.at[0, group],
                    relay_recv.at[0, group],
                    _mate(2),
                ),
                _send(
                    part(two.at[pl.ds(2, 2)]),
                    part(far_top),
                    relay_send.at[1, group],
                    relay_recv.at[1, group],
                    _mate(1),
                ),
            ]

        def across(group, pairs, first):
            return [
                _send(
                    _cols(source, group * D, D),
                    _cols(target, group * D, D),
                    side_send.at[first + index, group],
                    side_recv.at[first + index, group],
                    _sibling(),
                )
                for index, (source, target) in enumerate(pairs)
            ]

        near = lambda group: across(group, ((own, side_own), (one, side_one), (two, side_two)), 0)
        far = lambda group: across(group, ((far_low, side_low), (far_top, side_top)), 3)

        def advance(group):
            for copy in relay(group):
                copy.wait_recv()
            _start(far(group))

        def complete(group):
            for copy in near(group) + far(group):
                copy.wait_recv()

    def fetch(chunk, slot):
        up_at, down_at = UP_AT + chunk * CHUNK, DOWN_AT + chunk * CHUNK
        return _copies(weight_refs, places, up_s.at[slot], up_at, CHUNK, up_sem.at[slot], True) + _copies(
            weight_refs, places, down_s.at[slot], down_at, CHUNK, down_sem.at[slot], True
        )

    leaving = [
        pltpu.make_async_copy(branch_s, branch_hbm, out_sem.at[0]),
        pltpu.make_async_copy(after_s, after_hbm, out_sem.at[1]),
        pltpu.make_async_copy(two_s, two_hbm, out_sem.at[2]),
        pltpu.make_async_copy(att_s, att_hbm, out_sem.at[3]),
    ]

    @pl.when(at == 0)
    def _():
        proj = _copies(weight_refs, places, proj_s, PROJ_AT, D, proj_sem, True)
        if remote:
            width, rows = D // n_head, hidden_ref.shape[0]
            _greet([_mate(step) for step in range(1, n_head)] + [_sibling()])
            mine = att_s.at[:, pl.ds(_own_column(0, n_head), width)]
            moves = [
                _send(
                    att_ref.at[pl.ds(step * rows, rows)], mine, send_sem.at[step], recv_sem.at[step], _mate(step)
                )
                for step in range(1, n_head)
            ]
            moves.append(pltpu.make_async_copy(att_ref.at[pl.ds(0, rows)], mine, send_sem.at[0]))
            _start(moves)
            for group in order:
                _start(relay(group))
                _start(near(group))
            advance(order[0])
            _wait(moves)
            complete(order[0])
            _start(proj)
            for group in order[1:3]:
                advance(group)
        else:
            _start(proj)
            _start(fetch(0, 0))
            att_s[...] = att_ref[...]
        _wait(proj)
        branch = (
            lax.dot_general(att_s[...], _flat(proj_s[...]), NT, preferred_element_type=f32) + rows_ref[0:1, :]
        )
        branch_s[...] = branch
        after = hidden_ref[...] + rows_ref[1:2, :] * branch
        after_s[...] = after
        unit, _s = _norm(after)
        two_s[...] = (unit * rows_ref[2:3, :] + rows_ref[3:4, :]).astype(bf16)
        _start(leaving)
        if remote:
            for group in order[1:3]:
                complete(group)
            _start(fetch(0, 0))

    if remote:
        later = at // 2 + 2
        halves = groups // 2

        @pl.when((lax.rem(at, 2) == 0) & (later <= halves))
        def _():
            advance(later)
            advance(later + halves)

        @pl.when((lax.rem(at, 2) == 1) & (later <= halves))
        def _():
            complete(later)
            complete(later + halves)

    @pl.when(at + 1 < chunks)
    def _():
        _start(fetch(at + 1, lax.rem(at + 1, 2)))

    slot = lax.rem(at, 2)
    _wait(fetch(at, slot))
    expand = jnp.dot(two_s[...], _flat(up_s[slot]), preferred_element_type=f32) + up_bias_ref[...]
    cdf = 0.5 * (1.0 + lax.erf(expand * math.sqrt(0.5)))
    slope = cdf + expand * jnp.exp(-0.5 * expand * expand) * (1.0 / math.sqrt(2.0 * math.pi))
    act = (expand * cdf).astype(bf16)
    act_ref[...] = act
    slope_ref[...] = slope.astype(bf16)
    part = lax.dot_general(act, _flat(down_s[slot]), NT, preferred_element_type=f32)

    @pl.when(at == 0)
    def _():
        acc[...] = part

    @pl.when(at > 0)
    def _():
        acc[...] += part

    @pl.when(at == chunks - 1)
    def _():
        down = acc[...] + rows_ref[4:5, :]
        down_ref[...] = down
        hidden = after_s[...] + rows_ref[5:6, :] * down
        next_ref[...] = hidden
        if last:
            normed_ref[...] = jnp.zeros_like(normed_ref)
        else:
            unit, _s = _norm(hidden)
            normed_ref[...] = (unit * rows_ref[6:7, :] + rows_ref[7:8, :]).astype(bf16)
        _wait(leaving)
        if remote:
            for group in range(groups):
                for copy in relay(group) + near(group) + far(group):
                    copy.wait_send()


def _params(remote, collective_id):
    if not remote:
        return pltpu.CompilerParams(dimension_semantics=("arbitrary",), vmem_limit_bytes=VMEM_BYTES)
    return pltpu.CompilerParams(
        dimension_semantics=("arbitrary",),
        vmem_limit_bytes=VMEM_BYTES,
        collective_id=collective_id,
        has_side_effects=True,
    )


def post_forward(att, hidden, rows, up_bias, gathered, n_head, last, remote, collective_id):
    own_rows = hidden.shape[0]
    pieces, places = gathered
    count = len(places)
    unit_rows = D // 32
    vmem = pl.BlockSpec(memory_space=pltpu.VMEM)
    hbm = pl.BlockSpec(memory_space=pl.ANY)
    column = pl.BlockSpec((own_rows, CHUNK), lambda at: (0, at))
    fixed = lambda leaf_rows: pl.BlockSpec((leaf_rows, D), lambda at: (0, 0))
    whole = lambda dtype: jax.ShapeDtypeStruct((own_rows, D), dtype)
    wide = jax.ShapeDtypeStruct((own_rows, FF), bf16)
    weight = lambda *lead: pltpu.VMEM(lead + (4, 2, 4, unit_rows), bf16)
    normed_rows = 16 if last else own_rows
    landed, sems = [], []
    if remote:
        half, full = [
            jax.ShapeDtypeStruct((planes,) + pieces[0].shape[1:], bf16) for planes in (2, 4)
        ]
        landed = [half, half, full, full, full, half, half]
        for kinds in (2, 2, 5, 5):
            sems.append(pltpu.SemaphoreType.DMA((kinds, WIDE // D)))
    outs = pl.pallas_call(
        functools.partial(post_forward_kernel, n_head, places, last, remote),
        grid=(FF // CHUNK,),
        out_shape=(
            whole(f32),
            jax.ShapeDtypeStruct((normed_rows, D), bf16),
            whole(f32),
            wide,
            wide,
            whole(f32),
            whole(f32),
            whole(bf16),
            whole(bf16),
            *landed,
        ),
        in_specs=[hbm if remote else vmem, vmem, vmem, pl.BlockSpec((1, CHUNK), lambda at: (0, at))]
        + [hbm] * len(pieces),
        out_specs=(fixed(own_rows), fixed(normed_rows), fixed(own_rows), column, column)
        + (hbm,) * (4 + len(landed)),
        scratch_shapes=[
            pltpu.VMEM((4, 2, 4, unit_rows, D), bf16),
            pltpu.VMEM((2, 4, 2, 4, unit_rows, CHUNK), bf16),
            pltpu.VMEM((2, 4, 2, 4, unit_rows, CHUNK), bf16),
            pltpu.VMEM((own_rows, D), bf16),
            pltpu.VMEM((own_rows, D), f32),
            pltpu.VMEM((own_rows, D), f32),
            pltpu.VMEM((own_rows, D), bf16),
            pltpu.VMEM((own_rows, D), f32),
            pltpu.SemaphoreType.DMA((count,)),
            pltpu.SemaphoreType.DMA((2, count)),
            pltpu.SemaphoreType.DMA((2, count)),
            pltpu.SemaphoreType.DMA((4,)),
            pltpu.SemaphoreType.DMA((n_head,)),
            pltpu.SemaphoreType.DMA((n_head,)),
            *sems,
        ],
        compiler_params=_params(remote, collective_id),
        cost_estimate=pl.CostEstimate(
            flops=2 * own_rows * D * (D + 2 * FF),
            bytes_accessed=2 * D * (D + 2 * FF) + own_rows * (22 * D + 4 * FF),
            transcendentals=2 * own_rows * FF,
        ),
    )(att, hidden, rows, up_bias, *pieces)
    if remote:
        far_low, far_top, *sides = outs[9:]
        near = [*pieces, far_low, far_top]
        pieces = [piece for pair in zip(near, sides) for piece in pair]
    return list(outs[:9]), pieces


def post_backward_kernel(n_head, places, remote, *refs):
    count = len(places)
    own_places = [("head", 0, 4, 0, to) for to in range(4)] if remote else [None]
    far_places = [("head", 0, 4, 1, to) for to in range(4)] if remote else []
    out_count = len(own_places)
    att_ref, grad_ref, down_ref, branch_ref, after_ref, two_ref, rows_ref, act_ref, slope_ref, refs = *refs[:9], refs[9:]
    weight_refs, refs = refs[:count], refs[count:]
    d_att_ref, d_after_ref, sums_ref, up_sum_ref, refs = *refs[:4], refs[4:]
    own_refs, refs = refs[:out_count], refs[out_count:]
    got_refs, refs = refs[: len(far_places)], refs[len(far_places) :]
    proj_s, up_s, down_s, d_proj_s, d_up_s, d_down_s, att_s, low_s, low_t, two_t, acc, refs = *refs[:11], refs[11:]
    proj_sem, up_sem, down_sem, own_sem, far_sem, got_sem, send_sem, recv_sem = refs
    at = pl.program_id(0)
    chunks = pl.num_programs(0)
    width = D // n_head

    def fetch(chunk, slot):
        up_at, down_at = UP_AT + chunk * CHUNK, DOWN_AT + chunk * CHUNK
        return _copies(weight_refs, places, up_s.at[slot], up_at, CHUNK, up_sem.at[slot], True) + _copies(
            weight_refs, places, down_s.at[slot], down_at, CHUNK, down_sem.at[slot], True
        )

    def stay(whole, column, size, lane):
        return _copies(own_refs, own_places, whole, column, size, own_sem.at[lane], False)

    def away(whole, column, size, lane, mark):
        return [
            _send(
                _slot(whole, place),
                _cols(got_refs[to], column, size),
                far_sem.at[lane, to],
                got_sem.at[mark, to],
                _sibling(),
            )
            for to, place in enumerate(far_places)
        ]

    def over(chunk, slot):
        up_at, down_at = UP_AT + chunk * CHUNK, DOWN_AT + chunk * CHUNK
        return away(d_up_s.at[slot], up_at, CHUNK, slot, chunk) + away(
            d_down_s.at[slot], down_at, CHUNK, 2 + slot, chunks + chunk
        )

    def leave(chunk, slot):
        up_at, down_at = UP_AT + chunk * CHUNK, DOWN_AT + chunk * CHUNK
        local = stay(d_up_s.at[slot], up_at, CHUNK, slot) + stay(d_down_s.at[slot], down_at, CHUNK, 2 + slot)
        return local, over(chunk, slot)

    def left(pair):
        _wait(pair[0])
        for move in pair[1]:
            move.wait_send()

    proj = lambda: _copies(weight_refs, places, proj_s, PROJ_AT, D, proj_sem, True)

    @pl.when(at == 0)
    def _():
        if remote:
            _greet([_mate(step) for step in range(1, n_head)] + [_sibling()])
        _start(fetch(0, 0))
        _start(proj())
        grad = grad_ref[...]
        low = (rows_ref[2:3, :] * grad).astype(bf16)
        low_s[...] = low
        low_t[...] = jnp.transpose(low)
        two_t[...] = jnp.transpose(two_ref[...])
        sums_ref[...] = jnp.zeros_like(sums_ref)
        sums_ref[0:1, :] = jnp.sum(grad * down_ref[...], axis=0, keepdims=True)
        sums_ref[1:2, :] = jnp.sum(low.astype(f32), axis=0, keepdims=True)
        acc[...] = jnp.zeros_like(acc)

    @pl.when(at + 1 < chunks)
    def _():
        _start(fetch(at + 1, lax.rem(at + 1, 2)))

    slot = lax.rem(at, 2)
    _wait(fetch(at, slot))

    @pl.when(at >= 2)
    def _():
        left(leave(at - 2, slot))

    d_act = jnp.dot(low_s[...], _flat(down_s[slot]), preferred_element_type=f32)
    d_expand = (slope_ref[...].astype(f32) * d_act).astype(bf16)
    up_sum_ref[...] = jnp.sum(d_expand.astype(f32), axis=0, keepdims=True)
    acc[...] += lax.dot_general(d_expand, _flat(up_s[slot]), NT, preferred_element_type=f32)
    shape = d_up_s.shape[1:]
    d_up_s[slot] = jnp.dot(two_t[...], d_expand, preferred_element_type=f32).astype(bf16).reshape(shape)
    d_down_s[slot] = jnp.dot(low_t[...], act_ref[...], preferred_element_type=f32).astype(bf16).reshape(shape)
    for moves in leave(at, slot):
        _start(moves)

    @pl.when(at == chunks - 1)
    def _():
        d_two = acc[...]
        unit, scale = _norm(after_ref[...])
        sums_ref[2:3, :] = jnp.sum(d_two * unit, axis=0, keepdims=True)
        sums_ref[3:4, :] = jnp.sum(d_two, axis=0, keepdims=True)
        d_unit = d_two * rows_ref[1:2, :]
        inner = jnp.mean(d_unit, axis=-1, keepdims=True)
        cross = jnp.mean(d_unit * unit, axis=-1, keepdims=True)
        d_after = grad_ref[...] + scale * (d_unit - inner - unit * cross)
        d_after_ref[...] = d_after
        sums_ref[4:5, :] = jnp.sum(d_after * branch_ref[...], axis=0, keepdims=True)
        d_branch = (rows_ref[0:1, :] * d_after).astype(bf16)
        sums_ref[5:6, :] = jnp.sum(d_branch.astype(f32), axis=0, keepdims=True)
        d_proj_s[...] = (
            lax.dot_general(d_branch, att_ref[...], TN, preferred_element_type=f32)
            .astype(bf16)
            .reshape(d_proj_s.shape)
        )
        gone = stay(d_proj_s, PROJ_AT, D, 4), away(d_proj_s, PROJ_AT, D, 4, 2 * chunks)
        for moves in gone:
            _start(moves)
        _wait(proj())
        d_att = jnp.dot(d_branch, _flat(proj_s[...]), preferred_element_type=f32).astype(bf16)
        if remote:
            rows = d_att.shape[0]
            att_s[...] = d_att
            moves = [
                _send(
                    att_s.at[:, pl.ds(_own_column(step, n_head), width)],
                    d_att_ref.at[pl.ds(step * rows, rows)],
                    send_sem.at[step],
                    recv_sem.at[step],
                    _mate(step),
                )
                for step in range(1, n_head)
            ]
            own = att_s.at[:, pl.ds(_own_column(0, n_head), width)]
            moves.append(pltpu.make_async_copy(own, d_att_ref.at[pl.ds(0, rows)], send_sem.at[0]))
            _start(moves)
            _wait(moves)
        else:
            d_att_ref[...] = d_att
        left(leave(at - 1, 1 - slot))
        left(leave(at, slot))
        left(gone)
        if remote:

            def arrive(chunk, _):
                for move in over(chunk, 0):
                    move.wait_recv()
                return 0

            lax.fori_loop(0, chunks, arrive, 0)
            for move in gone[1]:
                move.wait_recv()


def post_backward(att, grad, down_out, branch, after, two, rows, act, slope, gathered, n_head, remote, collective_id):
    own_rows = grad.shape[0]
    pieces, places = gathered
    count = len(places)
    unit_rows = D // 32
    vmem = pl.BlockSpec(memory_space=pltpu.VMEM)
    hbm = pl.BlockSpec(memory_space=pl.ANY)
    column = pl.BlockSpec((own_rows, CHUNK), lambda at: (0, at))
    fixed = lambda *shape: pl.BlockSpec(shape, lambda at: (0, 0))
    width = D // n_head
    chunks = FF // CHUNK
    if remote:
        d_att_shape, d_att_spec = (n_head * own_rows, width), hbm
        grads = [jax.ShapeDtypeStruct((4, unit_rows, WIDE), bf16)] * 8
    else:
        d_att_shape, d_att_spec = (own_rows, D), fixed(own_rows, D)
        grads = [jax.ShapeDtypeStruct((4, 2, 4, unit_rows, WIDE), bf16)]
    sems = pltpu.SemaphoreType.DMA
    outs = pl.pallas_call(
        functools.partial(post_backward_kernel, n_head, places, remote),
        grid=(chunks,),
        out_shape=tuple(
            [
                jax.ShapeDtypeStruct(d_att_shape, bf16),
                jax.ShapeDtypeStruct((own_rows, D), f32),
                jax.ShapeDtypeStruct((8, D), f32),
                jax.ShapeDtypeStruct((1, FF), f32),
            ]
            + grads
        ),
        in_specs=[vmem] * 7 + [column, column] + [hbm] * count,
        out_specs=tuple(
            [d_att_spec, fixed(own_rows, D), fixed(8, D), pl.BlockSpec((1, CHUNK), lambda at: (0, at))]
            + [hbm] * len(grads)
        ),
        scratch_shapes=[
            pltpu.VMEM((4, 2, 4, unit_rows, D), bf16),
            pltpu.VMEM((2, 4, 2, 4, unit_rows, CHUNK), bf16),
            pltpu.VMEM((2, 4, 2, 4, unit_rows, CHUNK), bf16),
            pltpu.VMEM((4, 2, 4, unit_rows, D), bf16),
            pltpu.VMEM((2, 4, 2, 4, unit_rows, CHUNK), bf16),
            pltpu.VMEM((2, 4, 2, 4, unit_rows, CHUNK), bf16),
            pltpu.VMEM((own_rows, D), bf16),
            pltpu.VMEM((own_rows, D), bf16),
            pltpu.VMEM((D, own_rows), bf16),
            pltpu.VMEM((D, own_rows), bf16),
            pltpu.VMEM((own_rows, D), f32),
            sems((count,)),
            sems((2, count)),
            sems((2, count)),
            sems((5, 4)),
            sems((5, 4)),
            sems((2 * chunks + 1, 4)),
            sems((n_head,)),
            sems((n_head,)),
        ],
        compiler_params=_params(remote, collective_id),
        cost_estimate=pl.CostEstimate(
            flops=4 * own_rows * D * (D + 2 * FF),
            bytes_accessed=4 * D * (D + 2 * FF) + own_rows * (22 * D + 4 * FF),
            transcendentals=0,
        ),
    )(att, grad, down_out, branch, after, two, rows, act, slope, *pieces)
    d_att, d_after, sums, up_sum, grads = *outs[:4], list(outs[4:])
    return d_att, d_after, sums, up_sum[0], (grads[:4], grads[4:]) if remote else (grads, grads)


FINISH_CUTS = 3


def finish_kernel(
    n_tok,
    n_head,
    grad_ref,
    weight_ref,
    hidden_ref,
    after_ref,
    gain_ref,
    x0_ref,
    x1_ref,
    x2_ref,
    x3_ref,
    own_ref,
    pass_ref,
    tiles_ref,
    one_ref,
    out_ref,
    sums_ref,
    rest_ref,
    qkv_ref,
    qkv_one_ref,
    vec_ref,
    away,
    come,
    come_rest,
    away_z,
    come_z,
    q_acc,
    q_all,
    q_come,
    q_mine,
    q_z,
    q_sum,
    q_land,
    one_land,
    land,
    send_sem,
    recv_sem,
    rest_send,
    rest_recv,
    z_send,
    z_recv,
    q_send,
    q_recv,
    v_send,
    v_recv,
):
    n = n_tok * n_head
    _enter(n_tok, n_head)
    tok = lax.axis_index("tok")
    head = lax.axis_index("head")
    me = tok * n_head + head
    zed, core = tok // 2, lax.rem(tok, 2)
    one_way, two_way = _mate(1), _mate(2)
    plane = lambda step: _paired(zed, step, 2)
    over = lambda step: (plane(step) * 2 + core, head)

    def tile(step):
        _, to, device = _peer(step, n_tok, n_head)
        return _send(tiles_ref.at[to], land.at[step], v_send.at[step], v_recv.at[step], device)

    def tile_start(step, _):
        tile(step).start()
        return 0

    def tile_wait(step, _):
        tile(step).wait()
        return 0

    lax.fori_loop(1, n, tile_start, 0)
    mate_at = lambda step: _paired(head, step, 2)

    def go_home(source, target, first):
        return [
            _send(
                source.at[mate_at(step)],
                target.at[head],
                q_send.at[first + step],
                q_recv.at[first + step],
                _mate(step),
            )
            for step in range(1, 4)
        ]

    one_home = go_home(one_ref, one_land, 6)
    _start(one_home)
    wide = own_ref.shape[2] // FINISH_CUTS

    def rest(low, at):
        part = pl.ds(0 if low else 2, 2)
        lanes = pl.ds(at * wide, wide)
        side = 0 if low else 1
        return _send(
            pass_ref.at[part, :, lanes],
            come_rest.at[part, :, lanes],
            rest_send.at[side, at],
            rest_recv.at[side, at],
            two_way if low else one_way,
        )

    for at in range(FINISH_CUTS):
        rest(True, at).start()
        rest(False, at).start()
    rows = hidden_ref.shape[0]
    half = rows // 2

    def term(step, low):
        here = pl.ds(step * rows + (0 if low else half), half)
        return lax.dot_general(grad_ref[here, :], weight_ref[...], NT, preferred_element_type=f32)

    def move(slot):
        return _send(away.at[slot], come.at[slot], send_sem.at[slot], recv_sem.at[slot], ways[slot])

    ways = (one_way, two_way, one_way, two_way, two_way, one_way)
    for slot, (step, low) in enumerate(((3, True), (3, False), (1, True), (2, False))):
        away[slot] = term(step, low).astype(bf16)
        move(slot).start()

    def cross(step, at):
        lanes = pl.ds(at * wide, wide)
        return _send(
            away_z.at[step - 1, :, lanes],
            come_z.at[step - 1, :, lanes],
            z_send.at[step - 1, at],
            z_recv.at[step - 1, at],
            over(step),
        )

    def rest_on(at):
        rest(True, at).wait_recv()
        rest(False, at).wait_recv()
        lanes = pl.ds(at * wide, wide)
        for step in range(4):
            total = own_ref[plane(step), :, lanes].astype(f32) + come_rest[plane(step), :, lanes].astype(f32)
            if step:
                away_z[step - 1, :, lanes] = total.astype(bf16)
                cross(step, at).start()
            else:
                rest_ref[:, lanes] = total

    rest_on(0)
    q_acc[...] = lax.dot_general(x0_ref[...], grad_ref[0:rows, :], TN, preferred_element_type=f32)
    for step, x_ref in ((1, x1_ref), (2, x2_ref), (3, x3_ref)):
        here = slice(step * rows, (step + 1) * rows)
        q_acc[...] += lax.dot_general(x_ref[...], grad_ref[here, :], TN, preferred_element_type=f32)
    q_all[...] = q_acc[...].astype(bf16).reshape(q_all.shape)
    swap_core = _send(q_all.at[:, 1 - core], q_come, q_send.at[0], q_recv.at[0], _sibling())
    swap_core.start()
    rest_on(1)
    swap_core.wait_recv()
    q_mine[...] = (q_all[:, core].astype(f32) + q_come[...].astype(f32)).astype(bf16)
    q_cross = [
        _send(q_mine.at[plane(step)], q_z.at[step - 1], q_send.at[step], q_recv.at[step], over(step))
        for step in range(1, 4)
    ]
    _start(q_cross)
    rest_on(2)
    pass_low = term(2, True)
    pass_top = term(1, False)
    move(0).wait_recv()
    away[4] = (pass_low + come[0].astype(f32)).astype(bf16)
    move(4).start()
    move(1).wait_recv()
    away[5] = (pass_top + come[1].astype(f32)).astype(bf16)
    move(5).start()
    sums_ref[...] = jnp.zeros_like(sums_ref)
    for low in (True, False):
        here = pl.ds(0 if low else half, half)
        own = term(0, low)
        unit, scale = _norm(hidden_ref[here, :])
        near, far = (2, 4) if low else (3, 5)
        move(near).wait_recv()
        move(far).wait_recv()
        grad = own + come[near].astype(f32) + come[far].astype(f32)
        sums_ref[0:1, :] += jnp.sum(grad * unit, axis=0, keepdims=True)
        sums_ref[1:2, :] += jnp.sum(grad, axis=0, keepdims=True)
        out_ref[here, :] = after_ref[here, :] + _norm_pull(grad * gain_ref[0:1, :], unit, scale)
    for copy in q_cross:
        copy.wait_recv()
    total = q_mine[zed].astype(f32)
    for step in range(3):
        total = total + q_z[step].astype(f32)
    q_sum[...] = total.astype(bf16).reshape(q_sum.shape)
    q_home = go_home(q_sum, q_land, 3)
    _start(q_home)
    qkv_ref[head] = q_sum[head].astype(f32)
    qkv_one_ref[head] = one_ref[head].astype(f32)
    for step, copy in enumerate(one_home):
        copy.wait_recv()
        qkv_one_ref[mate_at(step + 1)] = one_land[mate_at(step + 1)].astype(f32)
    for at in range(FINISH_CUTS):
        lanes = pl.ds(at * wide, wide)
        for step in range(1, 4):
            cross(step, at).wait_recv()
            rest_ref[:, lanes] += come_z[step - 1, :, lanes].astype(f32)
    for step, copy in enumerate(q_home):
        copy.wait_recv()
        qkv_ref[mate_at(step + 1)] = q_land[mate_at(step + 1)].astype(f32)
    lax.fori_loop(1, n, tile_wait, 0)
    vec_ref[...] = tiles_ref[me] + jnp.sum(land[1:], axis=0)
    for copy in [swap_core] + q_cross + q_home + one_home:
        copy.wait_send()
    for slot in range(6):
        move(slot).wait_send()
    for at in range(FINISH_CUTS):
        rest(True, at).wait_send()
        rest(False, at).wait_send()
        for step in range(1, 4):
            cross(step, at).wait_send()


def finish(grad, weight, hidden, after, gain, pieces, own, passed, tiles, mine_one, n_tok, n_head, collective_id):
    rows = hidden.shape[0]
    n = n_tok * n_head
    unit_rows, width = D // n, grad.shape[1]
    vmem = pl.BlockSpec(memory_space=pltpu.VMEM)
    hbm = pl.BlockSpec(memory_space=pl.ANY)
    sems = pltpu.SemaphoreType.DMA
    buffer = pltpu.VMEM((6, rows // 2, D), bf16)
    tok_rows = unit_rows * n_head
    low = lambda *shape: pltpu.VMEM(shape, bf16)
    return pl.pallas_call(
        functools.partial(finish_kernel, n_tok, n_head),
        out_shape=(
            jax.ShapeDtypeStruct((rows, D), f32),
            jax.ShapeDtypeStruct((8, D), f32),
            jax.ShapeDtypeStruct((unit_rows, WIDE), f32),
            jax.ShapeDtypeStruct((n_head, unit_rows, width), f32),
            jax.ShapeDtypeStruct((n_head, unit_rows, width), f32),
            jax.ShapeDtypeStruct(tiles.shape[1:], f32),
        ),
        in_specs=[vmem] * 10 + [hbm, vmem, vmem],
        out_specs=(vmem,) * 6,
        scratch_shapes=[
            buffer,
            buffer,
            low(4, unit_rows, WIDE),
            low(3, unit_rows, WIDE),
            low(3, unit_rows, WIDE),
            pltpu.VMEM((D, width), f32),
            low(4, 2, tok_rows, width),
            low(4, tok_rows, width),
            low(4, tok_rows, width),
            low(3, tok_rows, width),
            low(n_head, unit_rows, width),
            low(n_head, unit_rows, width),
            low(n_head, unit_rows, width),
            pltpu.VMEM(tiles.shape, f32),
            sems((6,)),
            sems((6,)),
            sems((2, FINISH_CUTS)),
            sems((2, FINISH_CUTS)),
            sems((3, FINISH_CUTS)),
            sems((3, FINISH_CUTS)),
            sems((10,)),
            sems((10,)),
            sems((n,)),
            sems((n,)),
        ],
        compiler_params=pltpu.CompilerParams(
            collective_id=collective_id, has_side_effects=True, vmem_limit_bytes=VMEM_BYTES
        ),
        cost_estimate=pl.CostEstimate(flops=0, bytes_accessed=250 << 20, transcendentals=0),
    )(grad, weight, hidden, after, gain, *pieces, own, passed, tiles, mine_one.reshape(n_head, unit_rows, width))


def layer_norm(values, gain, shift):
    centered = values - jnp.mean(values, axis=-1, keepdims=True)
    spread_ = jnp.mean(centered * centered, axis=-1, keepdims=True)
    return centered * lax.rsqrt(spread_ + norm_eps) * gain + shift


def unpack(vector_row):
    lengths = (D, D, 3 * D, D, D, D, D, FF, D, D, HD, HD, HD, HD)
    pieces = []
    offset = 0
    for length in lengths:
        pieces.append(vector_row[offset : offset + length])
        offset = offset + length
    return pieces


def head_gains(vec, heads):
    rows = [jnp.tile(piece, heads) for piece in vec[10:14]]
    return jnp.concatenate([jnp.stack(rows), jnp.zeros((4, heads * HD), f32)], axis=0)


def adam_update(
    weight, gradient, moment_one, moment_two, average, step_rate, decay_rate, clip_scale, fix_one, fix_two
):
    clipped = gradient * clip_scale
    moment_one = beta_one * moment_one + (1.0 - beta_one) * clipped
    moment_two = beta_two * moment_two + (1.0 - beta_two) * clipped * clipped
    first_hat = moment_one / fix_one
    second_hat = moment_two / fix_two
    weight = weight - step_rate * (
        first_hat / (jnp.sqrt(second_hat) + adam_eps) + decay_rate * weight
    )
    average = ema_decay * average + (1.0 - ema_decay) * weight
    return (weight, moment_one, moment_two, average)


def body(
    links,
    tokens,
    cotangent,
    slot_frame,
    step_count,
    *params,
):
    n_tok, n_head = links.n_tok, links.n_head
    devices = n_tok * n_head
    own = lax.axis_index("head")
    flip = lambda leaf: jnp.swapaxes(leaf, 1, 2)
    groups = []
    for at in range(0, 20, 5):
        qkv, proj, fc1, fc2, vec = params[at : at + 5]
        groups.append([qkv, flip(proj), fc1, flip(fc2), vec])
    masters = groups[0]

    slots = slot_frame.shape[0]
    per_head = slots // n_head
    held = slot_frame.reshape(n_head, per_head)
    held = jnp.concatenate(
        [lax.dynamic_slice_in_dim(held, own ^ step, 1, 0)[0] for step in range(n_head)]
    )
    index = jnp.arange(slots, dtype=jnp.int32)
    ahead = (held[None, :] < held[:, None]) | (
        (held[None, :] == held[:, None]) & (index[None, :] < index[:, None])
    )
    rank = jnp.sum(ahead.astype(jnp.int32), axis=1)
    order = jnp.sum(jnp.where(rank[None, :] == index[:, None], index[None, :], 0), axis=1).astype(jnp.int32)
    is_hi = (jnp.sum((held == held[0]).astype(jnp.int32)) == HI_BLOCKS).astype(jnp.int32).reshape(1)
    spans = (
        (HI_BLOCKS * BLOCK, LO_BLOCKS * BLOCK),
        (FRAMES * HI_BLOCKS * BLOCK, FRAMES * LO_BLOCKS * BLOCK),
    )

    vec_here = masters[4].shape[1]
    tile = lax.reduce_precision(masters[4], 8, 7).reshape(-1)
    tile = jnp.pad(tile, (0, 1024 - tile.shape[0])).reshape(8, 128)
    tiles = spread(tile, n_tok, n_head, 0).reshape(devices, 1024)[:, : 2 * vec_here]
    vectors = jnp.swapaxes(tiles.reshape(devices, 2, vec_here), 0, 1).reshape(2, devices * vec_here)
    vecs = [unpack(vectors[block]) for block in range(2)]

    qkv_low = [masters[0][block].astype(bf16) for block in range(2)]
    low = [
        jnp.concatenate([masters[kind][block].astype(bf16) for kind in (1, 2, 3)], axis=1)
        for block in range(2)
    ]
    places = links.gather_places()
    paired = links.paired
    width = D // n_head
    heads = width // HD
    own_rows = tokens.shape[0]
    cut = lambda rows: [rows[step * own_rows : (step + 1) * own_rows] for step in range(n_head)]
    gains = [head_gains(vec, heads) for vec in vecs]

    def attend(block, pieces, qkv_cols):
        qkv_bias = lax.dynamic_slice_in_dim(vecs[block][2].reshape(3, D), own * width, width, 1)
        return attention_forward(
            pieces, qkv_cols, qkv_bias.reshape(1, 3 * width), gains[block], order, is_hi, spans[block]
        )

    def enter(rows, mine, shard, collective_id):
        if paired:
            return enter_rows(rows, mine, shard, collective_id)
        planes = None if shard is None else links.gather_planes(shard)
        return links.rows_in(rows), lax.all_gather(mine, "tok", axis=0, tiled=True), planes

    def post(block, attended, hidden, pieces):
        vec, tail = vecs[block], vecs[1]
        rows = jnp.stack([vec[3], vec[4], vec[5], vec[6], vec[8], vec[9], tail[0], tail[1]])
        if not paired:
            attended = jnp.concatenate(links.by_index(links.exchange(cut(attended)), own), axis=1)
        return post_forward(
            attended,
            hidden,
            rows,
            vec[7].reshape(1, FF),
            (pieces, places),
            n_head,
            block == 1,
            paired,
            3 + block,
        )

    hidden_in = [tokens.astype(f32), None]
    normed = layer_norm(hidden_in[0], vecs[0][0], vecs[0][1]).astype(bf16)
    group, qkv_cols, saved, att_owns, mids, weights = ([None, None] for _ in range(6))

    mine = links.fetch_heads(qkv_low, own)
    normed, mine, low[0] = together(normed, mine, low[0])
    group[0], qkv_cols[0], planes = enter(normed, mine[0], low[0], 5)
    group[0], planes, qkv_cols[0], low[1] = together(group[0], planes, qkv_cols[0], low[1])
    near = links.gather_sides(planes)
    planes = links.gather_planes(low[1])
    saved[0] = attend(0, group[0], qkv_cols[0])
    saved[0], near, planes = together(saved[0], near, planes)
    (hidden_in[1], normed, *mids[0]), weights[0] = post(0, saved[0][0], hidden_in[0], near)

    group[1], qkv_cols[1], _planes = enter(normed, mine[1], None, 6)
    group[1], planes = together(group[1], planes)
    near = links.gather_sides(planes)
    saved[1] = attend(1, group[1], qkv_cols[1])
    saved[1], near = together(saved[1], near)
    (hidden, _normed, *mids[1]), weights[1] = post(1, saved[1][0], hidden_in[1], near)

    def post_back(block, grad):
        vec = vecs[block]
        down, act, slope, branch, after, two, att_own = mids[block]
        rows = jnp.stack([vec[4], vec[5], vec[9]] + [vec[9]] * 5)
        d_att, *rest = post_backward(
            att_own,
            grad,
            down,
            branch,
            after,
            two,
            rows,
            act,
            slope,
            (weights[block], places),
            n_head,
            paired,
            7 + block,
        )
        if not paired:
            parts = [
                lax.dynamic_slice_in_dim(d_att, (own ^ step) * width, width, 1) for step in range(n_head)
            ]
            d_att = jnp.concatenate(links.exchange(parts), axis=0)
        return d_att, *rest

    def attend_back(block, grad_heads):
        attended, raw, values, lse = saved[block]
        return attention_backward(
            raw, values, grad_heads, attended, lse, gains[block], order, is_hi, spans[block]
        )

    def rows_back(block, d_qkv, d_after):
        gain, shift = vecs[block][0], vecs[block][1]
        if paired:
            grad, sums = rows_out(
                d_qkv, qkv_cols[block], hidden_in[block], d_after, gain.reshape(1, D), 9 + block
            )
            return grad, sums[0], sums[1]
        d_normed = jnp.einsum("rc,dc->rd", d_qkv, qkv_cols[block], preferred_element_type=f32)
        back = links.rows_out(cut(d_normed.astype(bf16)))
        d_hidden, d_gain, d_shift = jax.vjp(layer_norm, hidden_in[block], gain, shift)[1](back)
        return d_after + d_hidden, d_gain, d_shift

    def qkv_grad(block, d_qkv):
        rows = jnp.concatenate(group[block], axis=0)
        return jnp.einsum("rd,rc->dc", rows, d_qkv, preferred_element_type=f32).astype(bf16)

    def vector_grad(norm_sums, sums, d_up_bias, head_sums, bias_sums):
        d_qkv_bias = lax.dynamic_update_slice_in_dim(
            jnp.zeros((3, D), f32), bias_sums[0].reshape(3, width), own * width, 1
        ).reshape(3 * D)
        head_sums = jnp.sum(head_sums[:4].reshape(4, heads, HD), axis=1).reshape(4 * HD)
        parts = [*norm_sums, d_qkv_bias, sums[5], sums[4], sums[2], sums[3], d_up_bias, sums[1], sums[0], head_sums]
        return jnp.concatenate(parts)

    d_att, d_after, sums, d_up_bias, grads = post_back(1, cotangent.astype(f32))
    grads = links.scatter_start(*grads)
    d_att, grads = together(d_att, grads)
    grads = links.scatter_first(grads)
    d_qkv, head_sums, bias_sums = attend_back(1, d_att)
    d_qkv, head_sums, bias_sums, grads = together(d_qkv, head_sums, bias_sums, grads)
    dw_qkv = links.return_cores(qkv_grad(1, d_qkv))
    grad_rows, *norm_sums = rows_back(1, d_qkv, d_after)
    d_vec_one = vector_grad(norm_sums, sums, d_up_bias, head_sums, bias_sums)
    grad_rows, grads, dw_qkv = together(grad_rows, grads, dw_qkv)
    grads_one = links.scatter_second(grads)
    mine_one = links.return_planes(dw_qkv)

    d_att, d_after, sums, d_up_bias, grads = post_back(0, grad_rows)
    d_att, grads_one, mine_one, grads = together(d_att, grads_one, mine_one, grads)
    grads = links.scatter_start(*grads)
    d_att, grads, grads_one = together(d_att, grads, grads_one)
    sum_one = links.scatter_last(grads_one)
    grads = links.scatter_first(grads)
    d_qkv, head_sums, bias_sums = attend_back(0, d_att)
    d_qkv, head_sums, bias_sums, grads, sum_one = together(d_qkv, head_sums, bias_sums, grads, sum_one)
    vec_shape = (devices, 2 * vec_here)

    def tiles_of(row_zero, row_one):
        both = jnp.stack([row_zero, row_one]).reshape(2, devices, vec_here)
        flat = jnp.swapaxes(both, 0, 1).reshape(vec_shape)
        return jnp.pad(flat, ((0, 0), (0, 1024 - vec_shape[1]))).reshape(devices, 8, 128)

    if paired:
        none = jnp.zeros((D,), f32)
        tiles = tiles_of(vector_grad((none, none), sums, d_up_bias, head_sums, bias_sums), d_vec_one)
        gain = vecs[0][0].reshape(1, D)
        grad_rows, norm_sums, sum_zero, *qkv_grads, d_vec = finish(
            d_qkv, qkv_cols[0], hidden_in[0], d_after, gain, group[0], *grads, tiles, mine_one, n_tok, n_head, 11
        )
        qkv_zero, qkv_one = [
            jnp.transpose(part.reshape(n_head, -1, 3, width), (1, 2, 0, 3)).reshape(-1, 3 * D) for part in qkv_grads
        ]
        late = jnp.concatenate([norm_sums[0], norm_sums[1]]).reshape(16, 128)
    else:
        grad_rows, *norm_sums = rows_back(0, d_qkv, d_after)
        dw_qkv = links.return_cores(qkv_grad(0, d_qkv))
        tiles = tiles_of(vector_grad(norm_sums, sums, d_up_bias, head_sums, bias_sums), d_vec_one)
        d_vec = swap(tiles, n_tok, n_head, 1)
        sum_zero = links.scatter_last(links.scatter_second(grads))
        qkv_zero, qkv_one = links.return_heads([links.return_planes(dw_qkv), mine_one], own)
        late = jnp.zeros((16, 128), f32)
    summed = []
    for qkv_part, rest in ((qkv_zero, sum_zero), (qkv_one, sum_one)):
        summed.append([qkv_part, rest[:, PROJ_AT:UP_AT], rest[:, UP_AT:DOWN_AT], rest[:, DOWN_AT:WIDE]])
    d_vec = d_vec.reshape(1024)[: 2 * vec_here].reshape(2, vec_here)
    gradients = [jnp.stack([summed[0][kind], summed[1][kind]]) for kind in range(4)]
    local_square = sum((jnp.sum(gradient * gradient) for gradient in gradients)) + jnp.sum(d_vec * d_vec)
    tile = jnp.concatenate([jnp.broadcast_to(local_square, (8, 128)), late], axis=0)
    squares = spread(tile, n_tok, n_head, 2)
    late = jnp.sum(squares[:, 8:], axis=0).reshape(2 * D)
    grad_norm = jnp.sqrt(jnp.sum(squares[:, 0, 0]) + jnp.sum(late * late))
    if paired:
        flat = jnp.concatenate([late, jnp.zeros((devices * vec_here - 2 * D,), f32)]).reshape(devices, vec_here)
        mine_late = lax.dynamic_slice_in_dim(flat, lax.axis_index("tok") * n_head + own, 1, 0)
        d_vec = d_vec + jnp.concatenate([mine_late, jnp.zeros((1, vec_here), f32)], axis=0)
    gradients.append(d_vec)
    clip_scale = clip_norm / jnp.maximum(grad_norm, clip_norm)
    step_float = step_count[0].astype(f32)
    fix_one = 1.0 - beta_one**step_float
    fix_two = 1.0 - beta_two**step_float
    updates = [
        adam_update(
            groups[0][kind],
            gradients[kind],
            groups[1][kind],
            groups[2][kind],
            groups[3][kind],
            step_rates[kind],
            decays[kind],
            clip_scale,
            fix_one,
            fix_two,
        )
        for kind in range(5)
    ]
    outs = [hidden, grad_rows, grad_norm]
    for part in range(4):
        for kind in range(5):
            leaf = updates[kind][part]
            outs.append(flip(leaf) if kind in (1, 3) else leaf)
    return tuple(outs)


def solution(mesh):
    rows = P(BOTH, None)
    kinds = (
        P(None, BOTH, None),
        P(None, None, BOTH),
        P(None, BOTH, None),
        P(None, None, BOTH),
        P(None, BOTH),
    )
    in_specs = (rows, rows, P("tok"), P()) + kinds * 4
    out_specs = (rows, rows, P()) + kinds * 4
    return jax.shard_map(
        functools.partial(body, Links(mesh)),
        mesh=mesh,
        in_specs=in_specs,
        out_specs=out_specs,
        check_vma=False,
    )
```

```python
import functools
import math

import jax
import jax.numpy as jnp
from jax import lax
from jax.experimental import pallas as pl
from jax.experimental.pallas import tpu as pltpu
from jax.sharding import PartitionSpec as P

D = 1024
HD = 64
FF = 4096
BLOCK = 128
HI_BLOCKS = 8
LO_BLOCKS = 4
FRAMES = 2

norm_eps = 1e-06
clip_norm = 1.0
beta_one = 0.9
beta_two = 0.999
adam_eps = 1e-08
ema_decay = 0.7
step_rates = (0.05, 0.4, 0.05, 0.025, 0.3)
decays = (0.05, 0.05, 0.05, 0.05, 0.0)

LOG2E = math.log2(math.e)
SPAN = 512
MESH_ID = pl.DeviceIdType.MESH
BOTH = ("tok", "head")
bf16 = jnp.bfloat16
f32 = jnp.float32
VMEM_BYTES = 60 << 20


def _peer(step, n_tok, n_head):
    n = n_tok * n_head
    me = lax.axis_index("tok") * n_head + lax.axis_index("head")
    to = lax.rem(me + step, n)
    return me, to, (to // n_head, lax.rem(to, n_head))


def _enter(n_tok, n_head):
    n = n_tok * n_head
    barrier = pltpu.get_barrier_semaphore()

    def greet(step, _):
        _, _, device = _peer(step, n_tok, n_head)
        pl.semaphore_signal(barrier, inc=1, device_id=device, device_id_type=MESH_ID)
        return 0

    lax.fori_loop(1, n, greet, 0)
    pl.semaphore_wait(barrier, n - 1)


def spread_kernel(n_tok, n_head, x_ref, o_ref, send_sem, recv_sem):
    n = n_tok * n_head
    _enter(n_tok, n_head)
    me = lax.axis_index("tok") * n_head + lax.axis_index("head")
    o_ref[me] = x_ref[...]

    def copy(step):
        me, _, device = _peer(step, n_tok, n_head)
        return pltpu.make_async_remote_copy(
            src_ref=x_ref,
            dst_ref=o_ref.at[me],
            send_sem=send_sem.at[step],
            recv_sem=recv_sem.at[step],
            device_id=device,
            device_id_type=MESH_ID,
        )

    def start(step, _):
        copy(step).start()
        return 0

    def finish(step, _):
        copy(step).wait()
        return 0

    lax.fori_loop(1, n, start, 0)
    lax.fori_loop(1, n, finish, 0)


def swap_kernel(n_tok, n_head, x_ref, o_ref, land, send_sem, recv_sem):
    n = n_tok * n_head
    _enter(n_tok, n_head)
    me = lax.axis_index("tok") * n_head + lax.axis_index("head")

    def copy(step):
        me, to, device = _peer(step, n_tok, n_head)
        return pltpu.make_async_remote_copy(
            src_ref=x_ref.at[to],
            dst_ref=land.at[step],
            send_sem=send_sem.at[step],
            recv_sem=recv_sem.at[step],
            device_id=device,
            device_id_type=MESH_ID,
        )

    def start(step, _):
        copy(step).start()
        return 0

    def finish(step, _):
        copy(step).wait()
        return 0

    lax.fori_loop(1, n, start, 0)
    lax.fori_loop(1, n, finish, 0)
    o_ref[...] = x_ref[me] + jnp.sum(land[1:], axis=0)


def spread(tile, n_tok, n_head, collective_id):
    n = n_tok * n_head
    return pl.pallas_call(
        functools.partial(spread_kernel, n_tok, n_head),
        out_shape=jax.ShapeDtypeStruct((n,) + tile.shape, tile.dtype),
        in_specs=[pl.BlockSpec(memory_space=pltpu.VMEM)],
        out_specs=pl.BlockSpec(memory_space=pltpu.VMEM),
        scratch_shapes=[pltpu.SemaphoreType.DMA((n,)), pltpu.SemaphoreType.DMA((n,))],
        compiler_params=pltpu.CompilerParams(collective_id=collective_id, has_side_effects=True),
    )(tile)


def swap(tiles, n_tok, n_head, collective_id):
    n = n_tok * n_head
    return pl.pallas_call(
        functools.partial(swap_kernel, n_tok, n_head),
        out_shape=jax.ShapeDtypeStruct(tiles.shape[1:], tiles.dtype),
        in_specs=[pl.BlockSpec(memory_space=pltpu.VMEM)],
        out_specs=pl.BlockSpec(memory_space=pltpu.VMEM),
        scratch_shapes=[
            pltpu.VMEM(tiles.shape, tiles.dtype),
            pltpu.SemaphoreType.DMA((n,)),
            pltpu.SemaphoreType.DMA((n,)),
        ],
        compiler_params=pltpu.CompilerParams(collective_id=collective_id, has_side_effects=True),
    )(tiles)


def _lane_mean(values, grouping):
    top = values.astype(bf16)
    rest = (values - top.astype(f32)).astype(bf16)
    return jnp.dot(top, grouping, preferred_element_type=f32) + jnp.dot(
        rest, grouping, preferred_element_type=f32
    )


def _grouping(width):
    row = lax.broadcasted_iota(jnp.int32, (width, width), 0) // HD
    col = lax.broadcasted_iota(jnp.int32, (width, width), 1) // HD
    return jnp.where(row == col, 1.0 / HD, 0.0).astype(bf16)


def _unit(values, grouping):
    centered = values - _lane_mean(values, grouping)
    spread_ = _lane_mean(centered * centered, grouping)
    scale = lax.rsqrt(spread_ + norm_eps)
    return centered * scale, scale


def _only(values, head):
    lane = lax.broadcasted_iota(jnp.int32, values.shape, 1)
    return jnp.where(lane // HD == head, values, jnp.zeros_like(values))


NT = (((1,), (1,)), ((), ()))
TN = (((0,), (0,)), ((), ()))


def forward_kernel(
    heads, pieces, spans, tile_rows, order_ref, hi_ref, *refs
):
    x_refs = refs[:pieces]
    w_ref, bias_ref, gains_ref, att_ref, raw_ref, val_ref, lse_ref, q_s, k_s, v_s, acc = refs[pieces:]
    width = heads * HD
    rows = att_ref.shape[0]
    blocks = rows // BLOCK
    piece_rows = rows // pieces
    for at in range(pieces):
        full = jnp.dot(x_refs[at][...], w_ref[...], preferred_element_type=f32) + bias_ref[...]
        here = pl.ds(at * piece_rows, piece_rows)
        raw_ref[here, :] = full[:, : 2 * width]
        val_ref[here, :] = full[:, 2 * width :].astype(bf16)
    grouping = _grouping(width)

    def place(at, _):
        here = pl.ds(pl.multiple_of(order_ref[at] * BLOCK, BLOCK), BLOCK)
        there = pl.ds(pl.multiple_of(at * BLOCK, BLOCK), BLOCK)
        unit_q, _s = _unit(raw_ref[here, :width], grouping)
        unit_k, _s = _unit(raw_ref[here, width:], grouping)
        q_s[there, :] = ((unit_q * gains_ref[0:1, :] + gains_ref[1:2, :]) * HD ** (-0.5)).astype(bf16)
        key = (unit_k * gains_ref[2:3, :] + gains_ref[3:4, :]).astype(bf16)
        value = val_ref[here, :]
        for head in range(heads):
            k_s[head, there, :] = _only(key, head)
            v_s[head, there, :] = _only(value, head)
        return 0

    lax.fori_loop(0, blocks, place, 0)
    per_tile = tile_rows // BLOCK

    def attend(span):
        def tile(at, _):
            here = pl.ds(pl.multiple_of(at * tile_rows, tile_rows), tile_rows)
            first = at * tile_rows // span * span
            there = pl.ds(pl.multiple_of(first, span), span)
            query = q_s[here, :]
            lane = lax.broadcasted_iota(jnp.int32, (tile_rows, 128), 1)
            logs = jnp.zeros((tile_rows, 128), f32)
            for head in range(heads):
                scores = lax.dot_general(query, k_s[head, there, :], NT, preferred_element_type=f32)
                top = jnp.max(scores, axis=1, keepdims=True) * LOG2E
                probs = jnp.exp2(scores * LOG2E - top)
                total = jnp.sum(probs, axis=1, keepdims=True)
                part = jnp.dot(
                    probs.astype(bf16), v_s[head, there, :], preferred_element_type=f32
                ) / total
                if head == 0:
                    acc[...] = part
                else:
                    acc[...] += part
                logs = jnp.where(lane == head, top + jnp.log2(total), logs)
            lse_ref[here, :] = logs
            for sub in range(per_tile):
                out = pl.ds(pl.multiple_of(order_ref[at * per_tile + sub] * BLOCK, BLOCK), BLOCK)
                att_ref[out, :] = acc[sub * BLOCK : (sub + 1) * BLOCK, :].astype(bf16)
            return 0

        lax.fori_loop(0, rows // tile_rows, tile, 0)

    @pl.when(hi_ref[0] == 1)
    def _():
        attend(spans[0])

    @pl.when(hi_ref[0] == 0)
    def _():
        attend(spans[1])


def attention_forward(pieces, weight, bias, gains, order, is_hi, spans):
    heads = weight.shape[1] // (3 * HD)
    width = heads * HD
    rows = sum(piece.shape[0] for piece in pieces)
    tile_rows = 256
    smem = pl.BlockSpec(memory_space=pltpu.SMEM)
    vmem = pl.BlockSpec(memory_space=pltpu.VMEM)
    flops = 2 * rows * (D * 3 * width + 8 * spans[0] * width)
    return pl.pallas_call(
        functools.partial(forward_kernel, heads, len(pieces), spans, tile_rows),
        out_shape=(
            jax.ShapeDtypeStruct((rows, width), bf16),
            jax.ShapeDtypeStruct((rows, 2 * width), f32),
            jax.ShapeDtypeStruct((rows, width), bf16),
            jax.ShapeDtypeStruct((rows, 128), f32),
        ),
        in_specs=[smem, smem] + [vmem] * (len(pieces) + 3),
        out_specs=(vmem,) * 4,
        scratch_shapes=[
            pltpu.VMEM((rows, width), bf16),
            pltpu.VMEM((heads, rows, width), bf16),
            pltpu.VMEM((heads, rows, width), bf16),
            pltpu.VMEM((tile_rows, width), f32),
        ],
        compiler_params=pltpu.CompilerParams(vmem_limit_bytes=VMEM_BYTES),
        cost_estimate=pl.CostEstimate(
            flops=flops, bytes_accessed=rows * (2 * D + 14 * width), transcendentals=rows * spans[0] * heads
        ),
    )(order, is_hi, *pieces, weight, bias, gains)


def backward_kernel(
    heads,
    spans,
    order_ref,
    hi_ref,
    raw_ref,
    val_ref,
    grad_ref,
    att_ref,
    lse_ref,
    gains_ref,
    out_ref,
    sums_ref,
    bias_ref,
    q_s,
    o_s,
    k_m,
    v_m,
    q_m,
    o_m,
    dq_s,
    dk_s,
    dv_s,
    lse_t,
    delta_t,
):
    width = heads * HD
    rows = val_ref.shape[0]
    blocks = rows // BLOCK
    grouping = _grouping(width)
    head_of = lax.broadcasted_iota(jnp.int32, (8, width), 1) // HD
    picks = jnp.where(head_of == lax.broadcasted_iota(jnp.int32, (8, width), 0), 1.0, 0.0).astype(bf16)

    def place(at, _):
        here = pl.ds(pl.multiple_of(order_ref[at] * BLOCK, BLOCK), BLOCK)
        there = pl.ds(pl.multiple_of(at * BLOCK, BLOCK), BLOCK)
        unit_q, _s = _unit(raw_ref[here, :width], grouping)
        unit_k, _s = _unit(raw_ref[here, width:], grouping)
        query = ((unit_q * gains_ref[0:1, :] + gains_ref[1:2, :]) * HD ** (-0.5)).astype(bf16)
        key = (unit_k * gains_ref[2:3, :] + gains_ref[3:4, :]).astype(bf16)
        value = val_ref[here, :]
        grad = grad_ref[here, :]
        q_s[there, :] = query
        o_s[there, :] = grad
        for head in range(heads):
            k_m[head, there, :] = _only(key, head)
            v_m[head, there, :] = _only(value, head)
            q_m[head, there, :] = _only(query, head)
            o_m[head, there, :] = _only(grad, head)
        both = grad.astype(f32) * att_ref[here, :].astype(f32)
        top = both.astype(bf16)
        rest = (both - top.astype(f32)).astype(bf16)
        delta_t[:, there] = lax.dot_general(picks, top, NT, preferred_element_type=f32) + lax.dot_general(
            picks, rest, NT, preferred_element_type=f32
        )
        lse_t[:, there] = jnp.transpose(lse_ref[there, :])[:8, :]
        dq_s[there, :] = jnp.zeros((BLOCK, width), f32)
        dk_s[there, :] = jnp.zeros((BLOCK, width), f32)
        dv_s[there, :] = jnp.zeros((BLOCK, width), f32)
        return 0

    lax.fori_loop(0, blocks, place, 0)
    span = jnp.where(hi_ref[0] == 1, spans[0], spans[1])

    def tile(at, _):
        here = pl.ds(pl.multiple_of(at * SPAN, SPAN), SPAN)
        first = at * SPAN // span * span // SPAN

        def chunk(key_at, _):
            there = pl.ds(pl.multiple_of(key_at * SPAN, SPAN), SPAN)
            for head in range(heads):
                scores = lax.dot_general(k_m[head, there, :], q_s[here, :], NT, preferred_element_type=f32)
                probs = jnp.exp2(scores * LOG2E - lse_t[head : head + 1, here])
                grad_probs = lax.dot_general(
                    v_m[head, there, :], o_s[here, :], NT, preferred_element_type=f32
                )
                grad_scores = (probs * (grad_probs - delta_t[head : head + 1, here])).astype(bf16)
                dv_s[there, :] += jnp.dot(probs.astype(bf16), o_m[head, here, :], preferred_element_type=f32)
                dk_s[there, :] += jnp.dot(grad_scores, q_m[head, here, :], preferred_element_type=f32)
                dq_s[here, :] += lax.dot_general(
                    grad_scores, k_m[head, there, :], TN, preferred_element_type=f32
                )
            return 0

        lax.fori_loop(first, first + span // SPAN, chunk, 0)
        return 0

    lax.fori_loop(0, rows // SPAN, tile, 0)
    sums_ref[...] = jnp.zeros_like(sums_ref)
    bias_ref[...] = jnp.zeros_like(bias_ref)

    def pull(grad, unit, scale, gain):
        grad_unit = grad * gain
        inner = _lane_mean(grad_unit, grouping)
        cross = _lane_mean(grad_unit * unit, grouping)
        return scale * (grad_unit - inner - unit * cross)

    def leave(at, _):
        here = pl.ds(pl.multiple_of(order_ref[at] * BLOCK, BLOCK), BLOCK)
        there = pl.ds(pl.multiple_of(at * BLOCK, BLOCK), BLOCK)
        unit_q, scale_q = _unit(raw_ref[here, :width], grouping)
        unit_k, scale_k = _unit(raw_ref[here, width:], grouping)
        grad_q = dq_s[there, :] * HD ** (-0.5)
        grad_k = dk_s[there, :]
        sums_ref[0:1, :] += jnp.sum(grad_q * unit_q, axis=0, keepdims=True)
        sums_ref[1:2, :] += jnp.sum(grad_q, axis=0, keepdims=True)
        sums_ref[2:3, :] += jnp.sum(grad_k * unit_k, axis=0, keepdims=True)
        sums_ref[3:4, :] += jnp.sum(grad_k, axis=0, keepdims=True)
        low_q = pull(grad_q, unit_q, scale_q, gains_ref[0:1, :]).astype(bf16)
        low_k = pull(grad_k, unit_k, scale_k, gains_ref[2:3, :]).astype(bf16)
        low_v = dv_s[there, :].astype(bf16)
        for part, low in enumerate((low_q, low_k, low_v)):
            lanes = slice(part * width, (part + 1) * width)
            out_ref[here, lanes] = low
            bias_ref[0:1, lanes] += jnp.sum(low.astype(f32), axis=0, keepdims=True)
        return 0

    lax.fori_loop(0, blocks, leave, 0)


def attention_backward(raw, values, grad, attended, lse, gains, order, is_hi, spans):
    rows, width = values.shape
    heads = width // HD
    smem = pl.BlockSpec(memory_space=pltpu.SMEM)
    vmem = pl.BlockSpec(memory_space=pltpu.VMEM)
    flops = 2 * rows * 20 * spans[0] * width
    masked = pltpu.VMEM((heads, rows, width), bf16)
    return pl.pallas_call(
        functools.partial(backward_kernel, heads, spans),
        out_shape=(
            jax.ShapeDtypeStruct((rows, 3 * width), bf16),
            jax.ShapeDtypeStruct((8, width), f32),
            jax.ShapeDtypeStruct((8, 3 * width), f32),
        ),
        in_specs=[smem, smem] + [vmem] * 6,
        out_specs=(vmem,) * 3,
        scratch_shapes=[
            pltpu.VMEM((rows, width), bf16),
            pltpu.VMEM((rows, width), bf16),
            masked,
            masked,
            masked,
            masked,
            pltpu.VMEM((rows, width), f32),
            pltpu.VMEM((rows, width), f32),
            pltpu.VMEM((rows, width), f32),
            pltpu.VMEM((8, rows), f32),
            pltpu.VMEM((8, rows), f32),
        ],
        compiler_params=pltpu.CompilerParams(vmem_limit_bytes=VMEM_BYTES),
        cost_estimate=pl.CostEstimate(
            flops=flops, bytes_accessed=rows * 24 * width, transcendentals=rows * spans[0] * heads
        ),
    )(order, is_hi, raw, values, grad, attended, lse, gains)


class Links:
    def __init__(self, mesh):
        self.n_tok = mesh.shape["tok"]
        self.n_head = mesh.shape["head"]
        self.paired = self.n_tok == 8 and self.n_head == 4

    def head(self, values, step):
        return lax.ppermute(values, "head", [(i, i ^ step) for i in range(self.n_head)])

    def tok(self, values, step):
        return lax.ppermute(values, "tok", [(i, i ^ step) for i in range(self.n_tok)])

    def rows_in(self, rows):
        if not self.paired:
            return [rows] + [self.head(rows, step) for step in range(1, self.n_head)]
        half = rows.shape[0] // 2
        one, two = self.head(rows, 1), self.head(rows, 2)
        far = jnp.concatenate([self.head(one[:half], 2), self.head(two[half:], 1)], axis=0)
        return [rows, one, two, far]

    def rows_out(self, parts):
        if not self.paired:
            moved = [self.head(parts[step], step).astype(f32) for step in range(1, self.n_head)]
            return parts[0].astype(f32) + sum(moved)
        half = parts[0].shape[0] // 2
        upper = [part[:half] for part in parts]
        lower = [part[half:] for part in parts]
        pass_up = (upper[2].astype(f32) + self.head(upper[3], 1).astype(f32)).astype(bf16)
        pass_low = (lower[1].astype(f32) + self.head(lower[3], 2).astype(f32)).astype(bf16)
        up = upper[0].astype(f32) + self.head(upper[1], 1).astype(f32) + self.head(pass_up, 2).astype(f32)
        low = lower[0].astype(f32) + self.head(lower[2], 2).astype(f32) + self.head(pass_low, 1).astype(f32)
        return jnp.concatenate([up, low], axis=0)

    def exchange(self, parts):
        return [parts[0]] + [self.head(parts[step], step) for step in range(1, self.n_head)]

    def by_index(self, pieces, own):
        return [
            lax.select_n((own ^ at).astype(jnp.int32), *pieces) if len(pieces) > 1 else pieces[0]
            for at in range(len(pieces))
        ]

    def zed(self):
        return lax.axis_index("tok") // 2

    def core(self):
        return lax.rem(lax.axis_index("tok"), 2)

    def planes(self, shard):
        pieces = [shard] + [self.tok(shard, 2 * step) for step in range(1, 4)]
        return jnp.stack(self.by_index(pieces, self.zed()))

    def gather_places(self):
        if not self.paired:
            return [None]
        spots = ((0, 4, 0), (0, 4, 1), (0, 4, 2), (0, 2, 3), (2, 2, 3))
        return [("head", first, count, core, to) for first, count, to in spots for core in range(2)]

    def gather_planes(self, shard):
        if not self.paired:
            whole = lax.all_gather(shard, BOTH, axis=0, tiled=True)
            return [whole.reshape(4, 2, 4, whole.shape[0] // 32, whole.shape[1])]
        return [self.planes(shard)]

    def gather_sides(self, own):
        if not self.paired:
            return own
        return [own[0], self.head(own[0], 1), self.head(own[0], 2)]

    def scatter_first(self, grads):
        if not self.paired:
            return grads
        low, top, keep = grads
        return [keep, self.head(low, 1), self.head(top, 2)]

    def scatter_add(self, grads):
        if not self.paired:
            return grads
        keep, low, top = grads
        plus = lambda one, two: (one.astype(f32) + two.astype(f32)).astype(bf16)
        own = [plus(keep[:2], low[:2]), plus(keep[4:6], top[:2])]
        return [own, [plus(keep[2:4], low[2:]), plus(keep[6:], top[2:])]]

    def scatter_second(self, halves):
        if not self.paired:
            return halves
        own, passed = halves
        low = own[0].astype(f32) + self.head(passed[0], 2).astype(f32)
        top = own[1].astype(f32) + self.head(passed[1], 1).astype(f32)
        return [jnp.concatenate([low, top], axis=0).astype(bf16)]

    def scatter_last(self, planes):
        if not self.paired:
            whole = planes[0].reshape(-1, planes[0].shape[-1])
            return lax.psum_scatter(whole, BOTH, scatter_dimension=0, tiled=True).astype(f32)
        return self.sum_planes(planes[0])

    def sum_planes(self, parts):
        zed = self.zed()
        pick = lambda step: lax.dynamic_slice_in_dim(parts, zed ^ step, 1, 0)[0]
        total = pick(0).astype(f32)
        for step in range(1, 4):
            total = total + self.tok(pick(step).astype(bf16), 2 * step).astype(f32)
        return total

    def fetch_heads(self, shards, own):
        own_rows = shards[0].shape[0]
        width = D // self.n_head
        cut = jnp.stack(shards).reshape(len(shards), own_rows, 3, D)
        parts = [
            lax.dynamic_slice_in_dim(cut, (own ^ step) * width, width, 3).reshape(
                len(shards), own_rows, 3 * width
            )
            for step in range(self.n_head)
        ]
        moved = jnp.stack(self.by_index(self.exchange(parts), own), axis=1)
        return [moved[at].reshape(self.n_head * own_rows, 3 * width) for at in range(len(shards))]

    def return_cores(self, grad):
        if not self.paired:
            return grad
        view = grad.reshape((4, 2, grad.shape[0] // 8, grad.shape[1]))
        core = self.core()
        cut = lambda at: lax.dynamic_slice_in_dim(view, at, 1, 1)[:, 0]
        return (cut(core).astype(f32) + self.tok(cut(core ^ 1), 1).astype(f32)).astype(bf16)

    def return_planes(self, grad):
        if not self.paired:
            return lax.psum_scatter(grad, "tok", scatter_dimension=0, tiled=True)
        return self.sum_planes(grad).astype(bf16)

    def return_heads(self, both, own):
        width = D // self.n_head
        stack = jnp.stack(both)
        own_rows = stack.shape[1] // self.n_head
        parts = [
            lax.dynamic_slice_in_dim(stack, (own ^ step) * own_rows, own_rows, 1)
            for step in range(self.n_head)
        ]
        back = jnp.stack(self.by_index(self.exchange(parts), own), axis=2)
        back = back.reshape(len(both), own_rows, self.n_head, 3, width)
        return jnp.swapaxes(back, 2, 3).reshape(len(both), own_rows, 3 * D).astype(f32)


def together(*values):
    return lax.optimization_barrier(values)


CHUNK = 512


def _paired(value, step, bits):
    total = 0
    for bit in range(bits):
        one = lax.rem(value // (1 << bit), 2)
        total = total + (1 - one if (step >> bit) % 2 else one) * (1 << bit)
    return total


def _slot(ref, place):
    if place is None:
        return ref
    tok = lax.axis_index("tok")
    side = _paired(lax.rem(tok, 2), place[-1] if place[0] == "plane" else place[3], 1)
    if place[0] == "plane":
        return ref.at[_paired(tok // 2, place[1], 2), side]
    return ref.at[pl.ds(place[1], place[2]), side, _paired(lax.axis_index("head"), place[4], 2)]


PROJ_AT, UP_AT, DOWN_AT, WIDE = 0, D, D + FF, D + 2 * FF


def _cols(ref, at, size):
    window = pl.ds(pl.multiple_of(at, 128), size)
    return ref.at[(slice(None),) * (len(ref.shape) - 1) + (window,)]


def _copies(pieces, places, whole, at, size, sems, inward):
    moves = []
    for index, (piece, place) in enumerate(zip(pieces, places)):
        outside = _cols(piece, at, size)
        inside = _slot(whole, place)
        pair = (outside, inside) if inward else (inside, outside)
        moves.append(pltpu.make_async_copy(pair[0], pair[1], sems.at[index]))
    return moves


def _start(moves):
    for move in moves:
        move.start()


def _wait(moves):
    for move in moves:
        move.wait()


def _flat(values):
    return values.reshape(D, values.shape[-1])


def _norm(values):
    centered = values - jnp.mean(values, axis=-1, keepdims=True)
    scale = lax.rsqrt(jnp.mean(centered * centered, axis=-1, keepdims=True) + norm_eps)
    return centered * scale, scale


def _own_column(step, n_head):
    at = _paired(lax.axis_index("head"), step, n_head.bit_length() - 1)
    return pl.multiple_of(at * (D // n_head), 128)


def _mate(step):
    return lax.axis_index("tok"), _paired(lax.axis_index("head"), step, 2)


def _sibling():
    return _paired(lax.axis_index("tok"), 1, 3), lax.axis_index("head")


def _greet(devices):
    barrier = pltpu.get_barrier_semaphore()
    for device in devices:
        pl.semaphore_signal(barrier, inc=1, device_id=device, device_id_type=MESH_ID)
    pl.semaphore_wait(barrier, len(devices))


def _send(source, target, send_sem, recv_sem, device):
    return pltpu.make_async_remote_copy(
        src_ref=source,
        dst_ref=target,
        send_sem=send_sem,
        recv_sem=recv_sem,
        device_id=device,
        device_id_type=MESH_ID,
    )


def enter_kernel(wide, *refs):
    x_ref, q_ref, refs = refs[0], refs[1], refs[2:]
    if wide:
        shard_ref, refs = refs[0], refs[1:]
    one_ref, two_ref, far_ref, full_ref, refs = *refs[:4], refs[4:]
    if wide:
        planes_ref, refs = refs[0], refs[1:]
    send_sem, recv_sem, z_send, z_recv, own_sem, core_sem = refs
    tok, head = lax.axis_index("tok"), lax.axis_index("head")
    zed, core = tok // 2, lax.rem(tok, 2)
    one_way, two_way = _mate(1), _mate(2)
    barrier = pltpu.get_barrier_semaphore()
    greet = lambda device: pl.semaphore_signal(barrier, inc=1, device_id=device, device_id_type=MESH_ID)
    for device in (one_way, two_way, _sibling()):
        greet(device)

    @pl.when(zed < 3)
    def _():
        greet((tok + 2, head))

    @pl.when(zed > 0)
    def _():
        greet((tok - 2, head))

    edge = (zed == 0) | (zed == 3)

    @pl.when(edge)
    def _():
        pl.semaphore_wait(barrier, 4)

    @pl.when(jnp.logical_not(edge))
    def _():
        pl.semaphore_wait(barrier, 5)

    rows = x_ref.shape[0]
    parts = 4
    size = rows // parts

    def move(lane, part, source, target, device):
        here = pl.ds(part * size, size)
        return _send(source.at[here], target.at[here], send_sem.at[lane, part], recv_sem.at[lane, part], device)

    to_one = lambda part: move(0, part, x_ref, one_ref, one_way)
    to_two = lambda part: move(1, part, x_ref, two_ref, two_way)
    on_two = lambda part: move(2, part, one_ref, far_ref, two_way)
    on_one = lambda part: move(2, part, two_ref, far_ref, one_way)
    homes = [(q_ref, lambda plane: full_ref.at[plane, core])]
    if wide:
        homes.append((shard_ref, lambda plane: planes_ref.at[plane]))

    def climb(up, step):
        plane = jnp.clip(zed - step if up else zed + step, 0, 3)
        device = (jnp.clip(tok + 2 if up else tok - 2, 0, 7), head)
        return [
            _send(
                home(plane) if step else source,
                home(plane),
                z_send.at[int(up), step, index],
                z_recv.at[int(up), step, index],
                device,
            )
            for index, (source, home) in enumerate(homes)
        ]

    def sends(up, step):
        return (zed >= step) & (zed < 3) if up else (zed <= 3 - step) & (zed > 0)

    def comes(up, step):
        return zed >= step + 1 if up else zed <= 2 - step

    def climb_start(up, step):
        @pl.when(sends(up, step))
        def _():
            _start(climb(up, step))

    def climb_come(up, step):
        @pl.when(comes(up, step))
        def _():
            for copy in climb(up, step):
                copy.wait_recv()

    for turn in range(parts):
        to_one(turn).start()
        to_two(parts - 1 - turn).start()
    for up in (True, False):
        climb_start(up, 0)
    stays = [
        pltpu.make_async_copy(source, home(zed), own_sem.at[index]) for index, (source, home) in enumerate(homes)
    ]
    _start(stays)
    for turn in range(parts // 2):
        to_one(turn).wait_recv()
        on_two(turn).start()
        to_two(parts - 1 - turn).wait_recv()
        on_one(parts - 1 - turn).start()
    for step in range(3):
        for up in (True, False):
            climb_come(up, step)
            if step < 2:
                climb_start(up, step + 1)
    _wait(stays)
    mine = full_ref.at[:, core]
    over = _send(mine, mine, core_sem.at[0], core_sem.at[1], _sibling())
    over.start()
    for turn in range(parts // 2, parts):
        to_one(turn).wait_recv()
        to_two(parts - 1 - turn).wait_recv()
    for turn in range(parts):
        to_one(turn).wait_send()
        to_two(turn).wait_send()
    for turn in range(parts // 2):
        on_two(turn).wait()
        on_one(parts - 1 - turn).wait()
    for step in range(3):
        for up in (True, False):

            @pl.when(sends(up, step))
            def _():
                for copy in climb(up, step):
                    copy.wait_send()

    over.wait()


def enter_rows(rows, mine, shard, collective_id):
    hbm = pl.BlockSpec(memory_space=pl.ANY)
    like = jax.ShapeDtypeStruct(rows.shape, rows.dtype)
    outs = [like, like, like, jax.ShapeDtypeStruct((4, 2) + mine.shape, mine.dtype)]
    given = [rows, mine]
    if shard is not None:
        outs.append(jax.ShapeDtypeStruct((4,) + shard.shape, shard.dtype))
        given.append(shard)
    sems = pltpu.SemaphoreType.DMA
    one, two, far, full, *planes = pl.pallas_call(
        functools.partial(enter_kernel, shard is not None),
        out_shape=tuple(outs),
        in_specs=[hbm] * len(given),
        out_specs=(hbm,) * len(outs),
        scratch_shapes=[sems((3, 4)), sems((3, 4)), sems((2, 3, 2)), sems((2, 3, 2)), sems((2,)), sems((2,))],
        compiler_params=pltpu.CompilerParams(collective_id=collective_id, has_side_effects=True),
        cost_estimate=pl.CostEstimate(flops=0, bytes_accessed=150 << 20, transcendentals=0),
    )(*given)
    return [rows, one, two, far], full.reshape(8 * mine.shape[0], mine.shape[1]), planes


def _norm_pull(grad_unit, unit, scale):
    inner = jnp.mean(grad_unit, axis=-1, keepdims=True)
    cross = jnp.mean(grad_unit * unit, axis=-1, keepdims=True)
    return scale * (grad_unit - inner - unit * cross)


def rows_out_kernel(grad_ref, weight_ref, hidden_ref, after_ref, gain_ref, out_ref, sums_ref, away, come, send_sem, recv_sem):
    one_way, two_way = _mate(1), _mate(2)
    _greet([one_way, two_way])
    rows = hidden_ref.shape[0]
    half = rows // 2

    def term(step, low):
        here = pl.ds(step * rows + (0 if low else half), half)
        return lax.dot_general(grad_ref[here, :], weight_ref[...], NT, preferred_element_type=f32)

    def move(slot, device):
        return _send(away.at[slot], come.at[slot], send_sem.at[slot], recv_sem.at[slot], device)

    ways = (one_way, two_way, one_way, two_way, two_way, one_way)
    for slot, (step, low) in enumerate(((3, True), (3, False), (1, True), (2, False))):
        away[slot] = term(step, low).astype(bf16)
        move(slot, ways[slot]).start()
    pass_low = term(2, True)
    pass_top = term(1, False)
    move(0, ways[0]).wait_recv()
    away[4] = (pass_low + come[0].astype(f32)).astype(bf16)
    move(4, ways[4]).start()
    move(1, ways[1]).wait_recv()
    away[5] = (pass_top + come[1].astype(f32)).astype(bf16)
    move(5, ways[5]).start()
    sums_ref[...] = jnp.zeros_like(sums_ref)
    for low in (True, False):
        here = pl.ds(0 if low else half, half)
        own = term(0, low)
        unit, scale = _norm(hidden_ref[here, :])
        near, far = (2, 4) if low else (3, 5)
        move(near, ways[near]).wait_recv()
        move(far, ways[far]).wait_recv()
        grad = own + come[near].astype(f32) + come[far].astype(f32)
        sums_ref[0:1, :] += jnp.sum(grad * unit, axis=0, keepdims=True)
        sums_ref[1:2, :] += jnp.sum(grad, axis=0, keepdims=True)
        out_ref[here, :] = after_ref[here, :] + _norm_pull(grad * gain_ref[0:1, :], unit, scale)
    for slot in range(6):
        move(slot, ways[slot]).wait_send()


def rows_out(grad, weight, hidden, after, gain, collective_id):
    rows = hidden.shape[0]
    vmem = pl.BlockSpec(memory_space=pltpu.VMEM)
    buffer = pltpu.VMEM((6, rows // 2, D), bf16)
    sems = pltpu.SemaphoreType.DMA((6,))
    return pl.pallas_call(
        rows_out_kernel,
        out_shape=(jax.ShapeDtypeStruct((rows, D), f32), jax.ShapeDtypeStruct((8, D), f32)),
        in_specs=[vmem] * 5,
        out_specs=(vmem, vmem),
        scratch_shapes=[buffer, buffer, sems, sems],
        compiler_params=pltpu.CompilerParams(
            collective_id=collective_id, has_side_effects=True, vmem_limit_bytes=VMEM_BYTES
        ),
        cost_estimate=pl.CostEstimate(flops=0, bytes_accessed=150 << 20, transcendentals=0),
    )(grad, weight, hidden, after, gain)


def post_forward_kernel(n_head, places, last, remote, *refs):
    count = len(places)
    att_ref, refs = refs[0], refs[1:]
    hidden_ref, rows_ref, up_bias_ref, refs = refs[0], refs[1], refs[2], refs[3:]
    given = 3 if remote else count
    weight_refs, refs = refs[:given], refs[given:]
    next_ref, normed_ref, down_ref, act_ref, slope_ref, branch_hbm, after_hbm, two_hbm, att_hbm, refs = *refs[:9], refs[9:]
    if remote:
        (own, one, two), (far_low, far_top), refs = weight_refs, refs[:2], refs[2:]
        side_own, side_one, side_two, side_low, side_top, refs = *refs[:5], refs[5:]
        weight_refs = (own, side_own, one, side_one, two, side_two, far_low, side_low, far_top, side_top)
    proj_s, up_s, down_s, att_s, branch_s, after_s, two_s, acc, proj_sem, up_sem, down_sem, out_sem, send_sem, recv_sem, refs = (
        *refs[:14],
        refs[14:],
    )
    at = pl.program_id(0)
    chunks = pl.num_programs(0)
    if remote:
        relay_send, relay_recv, side_send, side_recv = refs
        groups = WIDE // D
        order = [0] + [first for pair in zip(range(1, 1 + groups // 2), range(1 + groups // 2, groups)) for first in pair]

        def relay(group):
            part = lambda ref: _cols(ref, group * D, D)
            return [
                _send(
                    part(one.at[pl.ds(0, 2)]),
                    part(far_low),
                    relay_send.at[0, group],
                    relay_recv.at[0, group],
                    _mate(2),
                ),
                _send(
                    part(two.at[pl.ds(2, 2)]),
                    part(far_top),
                    relay_send.at[1, group],
                    relay_recv.at[1, group],
                    _mate(1),
                ),
            ]

        def across(group, pairs, first):
            return [
                _send(
                    _cols(source, group * D, D),
                    _cols(target, group * D, D),
                    side_send.at[first + index, group],
                    side_recv.at[first + index, group],
                    _sibling(),
                )
                for index, (source, target) in enumerate(pairs)
            ]

        near = lambda group: across(group, ((own, side_own), (one, side_one), (two, side_two)), 0)
        far = lambda group: across(group, ((far_low, side_low), (far_top, side_top)), 3)

        def advance(group):
            for copy in relay(group):
                copy.wait_recv()
            _start(far(group))

        def complete(group):
            for copy in near(group) + far(group):
                copy.wait_recv()

    def fetch(chunk, slot):
        up_at, down_at = UP_AT + chunk * CHUNK, DOWN_AT + chunk * CHUNK
        return _copies(weight_refs, places, up_s.at[slot], up_at, CHUNK, up_sem.at[slot], True) + _copies(
            weight_refs, places, down_s.at[slot], down_at, CHUNK, down_sem.at[slot], True
        )

    leaving = [
        pltpu.make_async_copy(branch_s, branch_hbm, out_sem.at[0]),
        pltpu.make_async_copy(after_s, after_hbm, out_sem.at[1]),
        pltpu.make_async_copy(two_s, two_hbm, out_sem.at[2]),
        pltpu.make_async_copy(att_s, att_hbm, out_sem.at[3]),
    ]

    @pl.when(at == 0)
    def _():
        proj = _copies(weight_refs, places, proj_s, PROJ_AT, D, proj_sem, True)
        if remote:
            width, rows = D // n_head, hidden_ref.shape[0]
            _greet([_mate(step) for step in range(1, n_head)] + [_sibling()])
            mine = att_s.at[:, pl.ds(_own_column(0, n_head), width)]
            moves = [
                _send(
                    att_ref.at[pl.ds(step * rows, rows)], mine, send_sem.at[step], recv_sem.at[step], _mate(step)
                )
                for step in range(1, n_head)
            ]
            moves.append(pltpu.make_async_copy(att_ref.at[pl.ds(0, rows)], mine, send_sem.at[0]))
            _start(moves)
            for group in order:
                _start(relay(group))
                _start(near(group))
            advance(order[0])
            _wait(moves)
            complete(order[0])
            _start(proj)
            for group in order[1:3]:
                advance(group)
        else:
            _start(proj)
            _start(fetch(0, 0))
            att_s[...] = att_ref[...]
        _wait(proj)
        branch = (
            lax.dot_general(att_s[...], _flat(proj_s[...]), NT, preferred_element_type=f32) + rows_ref[0:1, :]
        )
        branch_s[...] = branch
        after = hidden_ref[...] + rows_ref[1:2, :] * branch
        after_s[...] = after
        unit, _s = _norm(after)
        two_s[...] = (unit * rows_ref[2:3, :] + rows_ref[3:4, :]).astype(bf16)
        _start(leaving)
        if remote:
            for group in order[1:3]:
                complete(group)
            _start(fetch(0, 0))

    if remote:
        later = at // 2 + 2
        halves = groups // 2

        @pl.when((lax.rem(at, 2) == 0) & (later <= halves))
        def _():
            advance(later)
            advance(later + halves)

        @pl.when((lax.rem(at, 2) == 1) & (later <= halves))
        def _():
            complete(later)
            complete(later + halves)

    @pl.when(at + 1 < chunks)
    def _():
        _start(fetch(at + 1, lax.rem(at + 1, 2)))

    slot = lax.rem(at, 2)
    _wait(fetch(at, slot))
    expand = jnp.dot(two_s[...], _flat(up_s[slot]), preferred_element_type=f32) + up_bias_ref[...]
    cdf = 0.5 * (1.0 + lax.erf(expand * math.sqrt(0.5)))
    slope = cdf + expand * jnp.exp(-0.5 * expand * expand) * (1.0 / math.sqrt(2.0 * math.pi))
    act = (expand * cdf).astype(bf16)
    act_ref[...] = act
    slope_ref[...] = slope.astype(bf16)
    part = lax.dot_general(act, _flat(down_s[slot]), NT, preferred_element_type=f32)

    @pl.when(at == 0)
    def _():
        acc[...] = part

    @pl.when(at > 0)
    def _():
        acc[...] += part

    @pl.when(at == chunks - 1)
    def _():
        down = acc[...] + rows_ref[4:5, :]
        down_ref[...] = down
        hidden = after_s[...] + rows_ref[5:6, :] * down
        next_ref[...] = hidden
        if last:
            normed_ref[...] = jnp.zeros_like(normed_ref)
        else:
            unit, _s = _norm(hidden)
            normed_ref[...] = (unit * rows_ref[6:7, :] + rows_ref[7:8, :]).astype(bf16)
        _wait(leaving)
        if remote:
            for group in range(groups):
                for copy in relay(group) + near(group) + far(group):
                    copy.wait_send()


def _params(remote, collective_id):
    if not remote:
        return pltpu.CompilerParams(dimension_semantics=("arbitrary",), vmem_limit_bytes=VMEM_BYTES)
    return pltpu.CompilerParams(
        dimension_semantics=("arbitrary",),
        vmem_limit_bytes=VMEM_BYTES,
        collective_id=collective_id,
        has_side_effects=True,
    )


def post_forward(att, hidden, rows, up_bias, gathered, n_head, last, remote, collective_id):
    own_rows = hidden.shape[0]
    pieces, places = gathered
    count = len(places)
    unit_rows = D // 32
    vmem = pl.BlockSpec(memory_space=pltpu.VMEM)
    hbm = pl.BlockSpec(memory_space=pl.ANY)
    column = pl.BlockSpec((own_rows, CHUNK), lambda at: (0, at))
    fixed = lambda leaf_rows: pl.BlockSpec((leaf_rows, D), lambda at: (0, 0))
    whole = lambda dtype: jax.ShapeDtypeStruct((own_rows, D), dtype)
    wide = jax.ShapeDtypeStruct((own_rows, FF), bf16)
    weight = lambda *lead: pltpu.VMEM(lead + (4, 2, 4, unit_rows), bf16)
    normed_rows = 16 if last else own_rows
    landed, sems = [], []
    if remote:
        half, full = [
            jax.ShapeDtypeStruct((planes,) + pieces[0].shape[1:], bf16) for planes in (2, 4)
        ]
        landed = [half, half, full, full, full, half, half]
        for kinds in (2, 2, 5, 5):
            sems.append(pltpu.SemaphoreType.DMA((kinds, WIDE // D)))
    outs = pl.pallas_call(
        functools.partial(post_forward_kernel, n_head, places, last, remote),
        grid=(FF // CHUNK,),
        out_shape=(
            whole(f32),
            jax.ShapeDtypeStruct((normed_rows, D), bf16),
            whole(f32),
            wide,
            wide,
            whole(f32),
            whole(f32),
            whole(bf16),
            whole(bf16),
            *landed,
        ),
        in_specs=[hbm if remote else vmem, vmem, vmem, pl.BlockSpec((1, CHUNK), lambda at: (0, at))]
        + [hbm] * len(pieces),
        out_specs=(fixed(own_rows), fixed(normed_rows), fixed(own_rows), column, column)
        + (hbm,) * (4 + len(landed)),
        scratch_shapes=[
            pltpu.VMEM((4, 2, 4, unit_rows, D), bf16),
            pltpu.VMEM((2, 4, 2, 4, unit_rows, CHUNK), bf16),
            pltpu.VMEM((2, 4, 2, 4, unit_rows, CHUNK), bf16),
            pltpu.VMEM((own_rows, D), bf16),
            pltpu.VMEM((own_rows, D), f32),
            pltpu.VMEM((own_rows, D), f32),
            pltpu.VMEM((own_rows, D), bf16),
            pltpu.VMEM((own_rows, D), f32),
            pltpu.SemaphoreType.DMA((count,)),
            pltpu.SemaphoreType.DMA((2, count)),
            pltpu.SemaphoreType.DMA((2, count)),
            pltpu.SemaphoreType.DMA((4,)),
            pltpu.SemaphoreType.DMA((n_head,)),
            pltpu.SemaphoreType.DMA((n_head,)),
            *sems,
        ],
        compiler_params=_params(remote, collective_id),
        cost_estimate=pl.CostEstimate(
            flops=2 * own_rows * D * (D + 2 * FF),
            bytes_accessed=2 * D * (D + 2 * FF) + own_rows * (22 * D + 4 * FF),
            transcendentals=2 * own_rows * FF,
        ),
    )(att, hidden, rows, up_bias, *pieces)
    if remote:
        far_low, far_top, *sides = outs[9:]
        near = [*pieces, far_low, far_top]
        pieces = [piece for pair in zip(near, sides) for piece in pair]
    return list(outs[:9]), pieces


def post_backward_kernel(n_head, places, remote, *refs):
    count = len(places)
    far_places = [("head", 0, 4, 1, to) for to in range(4)] if remote else []
    out_count = 3 if remote else 1
    att_ref, grad_ref, down_ref, branch_ref, after_ref, two_ref, rows_ref, act_ref, slope_ref, refs = *refs[:9], refs[9:]
    weight_refs, refs = refs[:count], refs[count:]
    d_att_ref, d_after_ref, sums_ref, up_sum_ref, refs = *refs[:4], refs[4:]
    own_refs, refs = refs[:out_count], refs[out_count:]
    proj_s, up_s, down_s, d_proj_s, d_up_s, d_down_s, att_s, low_s, low_t, two_t, acc, refs = *refs[:11], refs[11:]
    proj_sem, up_sem, down_sem, own_sem, far_sem, got_sem, send_sem, recv_sem, refs = *refs[:8], refs[8:]
    if remote:
        stash, got = refs
        low_ref, top_ref, keep_ref = own_refs
    at = pl.program_id(0)
    chunks = pl.num_programs(0)
    width = D // n_head

    def fetch(chunk, slot):
        up_at, down_at = UP_AT + chunk * CHUNK, DOWN_AT + chunk * CHUNK
        return _copies(weight_refs, places, up_s.at[slot], up_at, CHUNK, up_sem.at[slot], True) + _copies(
            weight_refs, places, down_s.at[slot], down_at, CHUNK, down_sem.at[slot], True
        )

    def stay(whole, column, size, lane):
        return [] if remote else _copies(own_refs, [None], whole, column, size, own_sem.at[lane], False)

    def away(whole, column, size, lane, mark):
        return [
            _send(
                _slot(whole, place),
                _cols(got.at[to], column, size),
                far_sem.at[lane, to],
                got_sem.at[mark, to],
                _sibling(),
            )
            for to, place in enumerate(far_places)
        ]

    def over(chunk, slot):
        up_at, down_at = UP_AT + chunk * CHUNK, DOWN_AT + chunk * CHUNK
        return away(d_up_s.at[slot], up_at, CHUNK, slot, chunk) + away(
            d_down_s.at[slot], down_at, CHUNK, 2 + slot, chunks + chunk
        )

    def leave(chunk, slot):
        up_at, down_at = UP_AT + chunk * CHUNK, DOWN_AT + chunk * CHUNK
        local = stay(d_up_s.at[slot], up_at, CHUNK, slot) + stay(d_down_s.at[slot], down_at, CHUNK, 2 + slot)
        return local, over(chunk, slot)

    def left(pair):
        _wait(pair[0])
        for move in pair[1]:
            move.wait_send()

    def hold(staged, column, size):
        core, head = lax.rem(lax.axis_index("tok"), 2), lax.axis_index("head")
        for to in range(4):
            _cols(stash.at[to], column, size)[...] = staged[:, core, _paired(head, to, 2)]

    def add(column, size):
        mine, other = _cols(stash, column, size), _cols(got, column, size)
        for to in range(4):
            mine[to] = (mine[to].astype(f32) + other[to].astype(f32)).astype(bf16)

    def merge(chunk):
        for move in over(chunk, 0):
            move.wait_recv()
        add(UP_AT + chunk * CHUNK, CHUNK)
        add(DOWN_AT + chunk * CHUNK, CHUNK)

    def depart(column, size, lane):
        spots = (
            (low_ref, 0, 1, 0),
            (low_ref, 2, 3, 0),
            (top_ref, 0, 2, 2),
            (top_ref, 2, 3, 2),
            (keep_ref, 0, 0, 0),
            (keep_ref, 2, 2, 0),
            (keep_ref, 4, 0, 2),
            (keep_ref, 6, 1, 2),
        )
        return [
            pltpu.make_async_copy(
                _cols(stash.at[to, pl.ds(first, 2)], column, size),
                _cols(target.at[pl.ds(at_, 2)], column, size),
                own_sem.at[lane, index],
            )
            for index, (target, at_, to, first) in enumerate(spots)
        ]

    middle = FF // 2
    early = lambda: depart(UP_AT, middle, 0) + depart(DOWN_AT, middle, 1)

    proj = lambda: _copies(weight_refs, places, proj_s, PROJ_AT, D, proj_sem, True)

    @pl.when(at == 0)
    def _():
        if remote:
            _greet([_mate(step) for step in range(1, n_head)] + [_sibling()])
        _start(fetch(0, 0))
        _start(proj())
        grad = grad_ref[...]
        low = (rows_ref[2:3, :] * grad).astype(bf16)
        low_s[...] = low
        low_t[...] = jnp.transpose(low)
        two_t[...] = jnp.transpose(two_ref[...])
        sums_ref[...] = jnp.zeros_like(sums_ref)
        sums_ref[0:1, :] = jnp.sum(grad * down_ref[...], axis=0, keepdims=True)
        sums_ref[1:2, :] = jnp.sum(low.astype(f32), axis=0, keepdims=True)
        acc[...] = jnp.zeros_like(acc)

    @pl.when(at + 1 < chunks)
    def _():
        _start(fetch(at + 1, lax.rem(at + 1, 2)))

    slot = lax.rem(at, 2)
    _wait(fetch(at, slot))

    @pl.when(at >= 2)
    def _():
        left(leave(at - 2, slot))

    d_act = jnp.dot(low_s[...], _flat(down_s[slot]), preferred_element_type=f32)
    d_expand = (slope_ref[...].astype(f32) * d_act).astype(bf16)
    up_sum_ref[...] = jnp.sum(d_expand.astype(f32), axis=0, keepdims=True)
    acc[...] += lax.dot_general(d_expand, _flat(up_s[slot]), NT, preferred_element_type=f32)
    shape = d_up_s.shape[1:]
    d_up_s[slot] = jnp.dot(two_t[...], d_expand, preferred_element_type=f32).astype(bf16).reshape(shape)
    d_down_s[slot] = jnp.dot(low_t[...], act_ref[...], preferred_element_type=f32).astype(bf16).reshape(shape)
    for moves in leave(at, slot):
        _start(moves)
    if remote:
        hold(d_up_s.at[slot], UP_AT + at * CHUNK, CHUNK)
        hold(d_down_s.at[slot], DOWN_AT + at * CHUNK, CHUNK)

        @pl.when(at > 0)
        def _():
            merge(at - 1)

        @pl.when(at == chunks // 2)
        def _():
            _start(early())

    @pl.when(at == chunks - 1)
    def _():
        d_two = acc[...]
        unit, scale = _norm(after_ref[...])
        sums_ref[2:3, :] = jnp.sum(d_two * unit, axis=0, keepdims=True)
        sums_ref[3:4, :] = jnp.sum(d_two, axis=0, keepdims=True)
        d_unit = d_two * rows_ref[1:2, :]
        inner = jnp.mean(d_unit, axis=-1, keepdims=True)
        cross = jnp.mean(d_unit * unit, axis=-1, keepdims=True)
        d_after = grad_ref[...] + scale * (d_unit - inner - unit * cross)
        d_after_ref[...] = d_after
        sums_ref[4:5, :] = jnp.sum(d_after * branch_ref[...], axis=0, keepdims=True)
        d_branch = (rows_ref[0:1, :] * d_after).astype(bf16)
        sums_ref[5:6, :] = jnp.sum(d_branch.astype(f32), axis=0, keepdims=True)
        d_proj_s[...] = (
            lax.dot_general(d_branch, att_ref[...], TN, preferred_element_type=f32)
            .astype(bf16)
            .reshape(d_proj_s.shape)
        )
        gone = stay(d_proj_s, PROJ_AT, D, 4), away(d_proj_s, PROJ_AT, D, 4, 2 * chunks)
        for moves in gone:
            _start(moves)
        if remote:
            hold(d_proj_s, PROJ_AT, D)
        _wait(proj())
        d_att = jnp.dot(d_branch, _flat(proj_s[...]), preferred_element_type=f32).astype(bf16)
        if remote:
            rows = d_att.shape[0]
            att_s[...] = d_att
            moves = [
                _send(
                    att_s.at[:, pl.ds(_own_column(step, n_head), width)],
                    d_att_ref.at[pl.ds(step * rows, rows)],
                    send_sem.at[step],
                    recv_sem.at[step],
                    _mate(step),
                )
                for step in range(1, n_head)
            ]
            own = att_s.at[:, pl.ds(_own_column(0, n_head), width)]
            moves.append(pltpu.make_async_copy(own, d_att_ref.at[pl.ds(0, rows)], send_sem.at[0]))
            _start(moves)
        else:
            d_att_ref[...] = d_att
        left(leave(at - 1, 1 - slot))
        left(leave(at, slot))
        left(gone)
        if remote:
            merge(at)
            for move in gone[1]:
                move.wait_recv()
            add(PROJ_AT, D)
            late = (
                depart(UP_AT + middle, middle, 2) + depart(DOWN_AT + middle, middle, 3) + depart(PROJ_AT, D, 4)
            )
            _start(late)
            _wait(early())
            _wait(late)
            _wait(moves)


def post_backward(att, grad, down_out, branch, after, two, rows, act, slope, gathered, n_head, remote, collective_id):
    own_rows = grad.shape[0]
    pieces, places = gathered
    count = len(places)
    unit_rows = D // 32
    vmem = pl.BlockSpec(memory_space=pltpu.VMEM)
    hbm = pl.BlockSpec(memory_space=pl.ANY)
    column = pl.BlockSpec((own_rows, CHUNK), lambda at: (0, at))
    fixed = lambda *shape: pl.BlockSpec(shape, lambda at: (0, 0))
    width = D // n_head
    chunks = FF // CHUNK
    if remote:
        d_att_shape, d_att_spec = (n_head * own_rows, width), hbm
        grads = [jax.ShapeDtypeStruct((planes, unit_rows, WIDE), bf16) for planes in (4, 4, 8)]
        stashes = [pltpu.VMEM((4, 4, unit_rows, WIDE), bf16)] * 2
    else:
        d_att_shape, d_att_spec = (own_rows, D), fixed(own_rows, D)
        grads = [jax.ShapeDtypeStruct((4, 2, 4, unit_rows, WIDE), bf16)]
        stashes = []
    sems = pltpu.SemaphoreType.DMA
    outs = pl.pallas_call(
        functools.partial(post_backward_kernel, n_head, places, remote),
        grid=(chunks,),
        out_shape=tuple(
            [
                jax.ShapeDtypeStruct(d_att_shape, bf16),
                jax.ShapeDtypeStruct((own_rows, D), f32),
                jax.ShapeDtypeStruct((8, D), f32),
                jax.ShapeDtypeStruct((1, FF), f32),
            ]
            + grads
        ),
        in_specs=[vmem] * 7 + [column, column] + [hbm] * count,
        out_specs=tuple(
            [d_att_spec, fixed(own_rows, D), fixed(8, D), pl.BlockSpec((1, CHUNK), lambda at: (0, at))]
            + [hbm] * len(grads)
        ),
        scratch_shapes=[
            pltpu.VMEM((4, 2, 4, unit_rows, D), bf16),
            pltpu.VMEM((2, 4, 2, 4, unit_rows, CHUNK), bf16),
            pltpu.VMEM((2, 4, 2, 4, unit_rows, CHUNK), bf16),
            pltpu.VMEM((4, 2, 4, unit_rows, D), bf16),
            pltpu.VMEM((2, 4, 2, 4, unit_rows, CHUNK), bf16),
            pltpu.VMEM((2, 4, 2, 4, unit_rows, CHUNK), bf16),
            pltpu.VMEM((own_rows, D), bf16),
            pltpu.VMEM((own_rows, D), bf16),
            pltpu.VMEM((D, own_rows), bf16),
            pltpu.VMEM((D, own_rows), bf16),
            pltpu.VMEM((own_rows, D), f32),
            sems((count,)),
            sems((2, count)),
            sems((2, count)),
            sems((5, 8)),
            sems((5, 4)),
            sems((2 * chunks + 1, 4)),
            sems((n_head,)),
            sems((n_head,)),
            *stashes,
        ],
        compiler_params=_params(remote, collective_id),
        cost_estimate=pl.CostEstimate(
            flops=4 * own_rows * D * (D + 2 * FF),
            bytes_accessed=4 * D * (D + 2 * FF) + own_rows * (22 * D + 4 * FF),
            transcendentals=0,
        ),
    )(att, grad, down_out, branch, after, two, rows, act, slope, *pieces)
    d_att, d_after, sums, up_sum, grads = *outs[:4], list(outs[4:])
    return d_att, d_after, sums, up_sum[0], grads


FINISH_CUTS = 3


def finish_kernel(
    n_tok,
    n_head,
    grad_ref,
    weight_ref,
    hidden_ref,
    after_ref,
    gain_ref,
    x0_ref,
    x1_ref,
    x2_ref,
    x3_ref,
    keep_ref,
    low_ref,
    top_ref,
    tiles_ref,
    one_ref,
    square_ref,
    out_ref,
    sums_ref,
    rest_ref,
    qkv_ref,
    qkv_one_ref,
    vec_ref,
    all_ref,
    own_s,
    pass_s,
    tile_s,
    away,
    come,
    come_rest,
    away_z,
    come_z,
    q_acc,
    q_all,
    q_come,
    q_mine,
    q_z,
    q_sum,
    q_land,
    one_land,
    land,
    send_sem,
    recv_sem,
    rest_send,
    rest_recv,
    z_send,
    z_recv,
    q_send,
    q_recv,
    v_send,
    v_recv,
    n_send,
    n_recv,
):
    n = n_tok * n_head
    _enter(n_tok, n_head)
    tok = lax.axis_index("tok")
    head = lax.axis_index("head")
    me = tok * n_head + head
    zed, core = tok // 2, lax.rem(tok, 2)
    one_way, two_way = _mate(1), _mate(2)
    plane = lambda step: _paired(zed, step, 2)
    over = lambda step: (plane(step) * 2 + core, head)

    def tile(step):
        _, to, device = _peer(step, n_tok, n_head)
        return _send(tiles_ref.at[to], land.at[step], v_send.at[step], v_recv.at[step], device)

    def tile_start(step, _):
        tile(step).start()
        return 0

    def tile_wait(step, _):
        tile(step).wait()
        return 0

    lax.fori_loop(1, n, tile_start, 0)
    mate_at = lambda step: _paired(head, step, 2)

    def go_home(source, target, first):
        return [
            _send(
                source.at[mate_at(step)],
                target.at[head],
                q_send.at[first + step],
                q_recv.at[first + step],
                _mate(step),
            )
            for step in range(1, 4)
        ]

    one_home = go_home(one_ref, one_land, 6)
    _start(one_home)
    wide = keep_ref.shape[2] // FINISH_CUTS
    two_sum = lambda first, second: (first.astype(f32) + second.astype(f32)).astype(bf16)
    pass_s[0:2] = two_sum(keep_ref[2:4], low_ref[2:4])
    pass_s[2:4] = two_sum(keep_ref[6:8], top_ref[2:4])

    def rest(low, at):
        part = pl.ds(0 if low else 2, 2)
        lanes = pl.ds(at * wide, wide)
        side = 0 if low else 1
        return _send(
            pass_s.at[part, :, lanes],
            come_rest.at[part, :, lanes],
            rest_send.at[side, at],
            rest_recv.at[side, at],
            two_way if low else one_way,
        )

    for at in range(FINISH_CUTS):
        rest(True, at).start()
        rest(False, at).start()
    rows = hidden_ref.shape[0]
    half = rows // 2

    def term(step, low):
        here = pl.ds(step * rows + (0 if low else half), half)
        return lax.dot_general(grad_ref[here, :], weight_ref[...], NT, preferred_element_type=f32)

    def move(slot):
        return _send(away.at[slot], come.at[slot], send_sem.at[slot], recv_sem.at[slot], ways[slot])

    ways = (one_way, two_way, one_way, two_way, two_way, one_way)
    for slot, (step, low) in enumerate(((3, True), (3, False), (1, True), (2, False))):
        away[slot] = term(step, low).astype(bf16)
        move(slot).start()
    own_s[0:2] = two_sum(keep_ref[0:2], low_ref[0:2])
    own_s[2:4] = two_sum(keep_ref[4:6], top_ref[0:2])

    def cross(step, at):
        lanes = pl.ds(at * wide, wide)
        return _send(
            away_z.at[step - 1, :, lanes],
            come_z.at[step - 1, :, lanes],
            z_send.at[step - 1, at],
            z_recv.at[step - 1, at],
            over(step),
        )

    def rest_on(at):
        rest(True, at).wait_recv()
        rest(False, at).wait_recv()
        lanes = pl.ds(at * wide, wide)
        for step in range(4):
            total = own_s[plane(step), :, lanes].astype(f32) + come_rest[plane(step), :, lanes].astype(f32)
            if step:
                away_z[step - 1, :, lanes] = total.astype(bf16)
                cross(step, at).start()
            else:
                rest_ref[:, lanes] = total

    rest_on(0)
    q_acc[...] = lax.dot_general(x0_ref[...], grad_ref[0:rows, :], TN, preferred_element_type=f32)
    for step, x_ref in ((1, x1_ref), (2, x2_ref), (3, x3_ref)):
        here = slice(step * rows, (step + 1) * rows)
        q_acc[...] += lax.dot_general(x_ref[...], grad_ref[here, :], TN, preferred_element_type=f32)
    q_all[...] = q_acc[...].astype(bf16).reshape(q_all.shape)
    swap_core = _send(q_all.at[:, 1 - core], q_come, q_send.at[0], q_recv.at[0], _sibling())
    swap_core.start()
    rest_on(1)
    swap_core.wait_recv()
    q_mine[...] = (q_all[:, core].astype(f32) + q_come[...].astype(f32)).astype(bf16)
    q_cross = [
        _send(q_mine.at[plane(step)], q_z.at[step - 1], q_send.at[step], q_recv.at[step], over(step))
        for step in range(1, 4)
    ]
    _start(q_cross)
    rest_on(2)
    pass_low = term(2, True)
    pass_top = term(1, False)
    move(0).wait_recv()
    away[4] = (pass_low + come[0].astype(f32)).astype(bf16)
    move(4).start()
    move(1).wait_recv()
    away[5] = (pass_top + come[1].astype(f32)).astype(bf16)
    move(5).start()
    sums_ref[...] = jnp.zeros_like(sums_ref)
    for low in (True, False):
        here = pl.ds(0 if low else half, half)
        own = term(0, low)
        unit, scale = _norm(hidden_ref[here, :])
        near, far = (2, 4) if low else (3, 5)
        move(near).wait_recv()
        move(far).wait_recv()
        grad = own + come[near].astype(f32) + come[far].astype(f32)
        sums_ref[0:1, :] += jnp.sum(grad * unit, axis=0, keepdims=True)
        sums_ref[1:2, :] += jnp.sum(grad, axis=0, keepdims=True)
        out_ref[here, :] = after_ref[here, :] + _norm_pull(grad * gain_ref[0:1, :], unit, scale)
    for copy in q_cross:
        copy.wait_recv()
    total = q_mine[zed].astype(f32)
    for step in range(3):
        total = total + q_z[step].astype(f32)
    q_sum[...] = total.astype(bf16).reshape(q_sum.shape)
    q_home = go_home(q_sum, q_land, 3)
    _start(q_home)
    qkv_ref[head] = q_sum[head].astype(f32)
    qkv_one_ref[head] = one_ref[head].astype(f32)
    for step, copy in enumerate(one_home):
        copy.wait_recv()
        qkv_one_ref[mate_at(step + 1)] = one_land[mate_at(step + 1)].astype(f32)
    for at in range(FINISH_CUTS):
        lanes = pl.ds(at * wide, wide)
        for step in range(1, 4):
            cross(step, at).wait_recv()
            rest_ref[:, lanes] += come_z[step - 1, :, lanes].astype(f32)
    for step, copy in enumerate(q_home):
        copy.wait_recv()
        qkv_ref[mate_at(step + 1)] = q_land[mate_at(step + 1)].astype(f32)
    lax.fori_loop(1, n, tile_wait, 0)
    vec_ref[...] = tiles_ref[me] + jnp.sum(land[1:], axis=0)
    square = square_ref[0:1, 0:1]
    for ref in (rest_ref, vec_ref):
        square = square + jnp.sum(ref[...] * ref[...], keepdims=True)
    for ref in (qkv_ref, qkv_one_ref):
        for at in range(n_head):
            square = square + jnp.sum(ref[at] * ref[at], keepdims=True)
    tile_s[0:8, :] = jnp.broadcast_to(square, (8, 128))
    for at in range(16):
        first = at % 8 * 128
        tile_s[8 + at : 9 + at, :] = sums_ref[at // 8 : at // 8 + 1, first : first + 128]
    all_ref[me] = tile_s[...]

    def norm_tile(step):
        _, _, device = _peer(step, n_tok, n_head)
        return _send(tile_s, all_ref.at[me], n_send.at[step], n_recv.at[step], device)

    def norm_start(step, _):
        norm_tile(step).start()
        return 0

    def norm_wait(step, _):
        norm_tile(step).wait()
        return 0

    lax.fori_loop(1, n, norm_start, 0)
    lax.fori_loop(1, n, norm_wait, 0)
    for copy in [swap_core] + q_cross + q_home + one_home:
        copy.wait_send()
    for slot in range(6):
        move(slot).wait_send()
    for at in range(FINISH_CUTS):
        rest(True, at).wait_send()
        rest(False, at).wait_send()
        for step in range(1, 4):
            cross(step, at).wait_send()


def finish(grad, weight, hidden, after, gain, pieces, parts, tiles, mine_one, square, n_tok, n_head, collective_id):
    rows = hidden.shape[0]
    n = n_tok * n_head
    unit_rows, width = D // n, grad.shape[1]
    vmem = pl.BlockSpec(memory_space=pltpu.VMEM)
    hbm = pl.BlockSpec(memory_space=pl.ANY)
    sems = pltpu.SemaphoreType.DMA
    buffer = pltpu.VMEM((6, rows // 2, D), bf16)
    tok_rows = unit_rows * n_head
    low = lambda *shape: pltpu.VMEM(shape, bf16)
    return pl.pallas_call(
        functools.partial(finish_kernel, n_tok, n_head),
        out_shape=(
            jax.ShapeDtypeStruct((rows, D), f32),
            jax.ShapeDtypeStruct((8, D), f32),
            jax.ShapeDtypeStruct((unit_rows, WIDE), f32),
            jax.ShapeDtypeStruct((n_head, unit_rows, width), f32),
            jax.ShapeDtypeStruct((n_head, unit_rows, width), f32),
            jax.ShapeDtypeStruct(tiles.shape[1:], f32),
            jax.ShapeDtypeStruct((n, 24, 128), f32),
        ),
        in_specs=[vmem] * 15,
        out_specs=(vmem,) * 7,
        scratch_shapes=[
            low(4, unit_rows, WIDE),
            low(4, unit_rows, WIDE),
            pltpu.VMEM((24, 128), f32),
            buffer,
            buffer,
            low(4, unit_rows, WIDE),
            low(3, unit_rows, WIDE),
            low(3, unit_rows, WIDE),
            pltpu.VMEM((D, width), f32),
            low(4, 2, tok_rows, width),
            low(4, tok_rows, width),
            low(4, tok_rows, width),
            low(3, tok_rows, width),
            low(n_head, unit_rows, width),
            low(n_head, unit_rows, width),
            low(n_head, unit_rows, width),
            pltpu.VMEM(tiles.shape, f32),
            sems((6,)),
            sems((6,)),
            sems((2, FINISH_CUTS)),
            sems((2, FINISH_CUTS)),
            sems((3, FINISH_CUTS)),
            sems((3, FINISH_CUTS)),
            sems((10,)),
            sems((10,)),
            sems((n,)),
            sems((n,)),
            sems((n,)),
            sems((n,)),
        ],
        compiler_params=pltpu.CompilerParams(
            collective_id=collective_id, has_side_effects=True, vmem_limit_bytes=VMEM_BYTES
        ),
        cost_estimate=pl.CostEstimate(flops=0, bytes_accessed=250 << 20, transcendentals=0),
    )(grad, weight, hidden, after, gain, *pieces, *parts, tiles, mine_one.reshape(n_head, unit_rows, width), square)


def layer_norm(values, gain, shift):
    centered = values - jnp.mean(values, axis=-1, keepdims=True)
    spread_ = jnp.mean(centered * centered, axis=-1, keepdims=True)
    return centered * lax.rsqrt(spread_ + norm_eps) * gain + shift


def unpack(vector_row):
    lengths = (D, D, 3 * D, D, D, D, D, FF, D, D, HD, HD, HD, HD)
    pieces = []
    offset = 0
    for length in lengths:
        pieces.append(vector_row[offset : offset + length])
        offset = offset + length
    return pieces


def head_gains(vec, heads):
    rows = [jnp.tile(piece, heads) for piece in vec[10:14]]
    return jnp.concatenate([jnp.stack(rows), jnp.zeros((4, heads * HD), f32)], axis=0)


def adam_update(
    weight, gradient, moment_one, moment_two, average, step_rate, decay_rate, clip_scale, fix_one, fix_two
):
    clipped = gradient * clip_scale
    moment_one = beta_one * moment_one + (1.0 - beta_one) * clipped
    moment_two = beta_two * moment_two + (1.0 - beta_two) * clipped * clipped
    first_hat = moment_one / fix_one
    second_hat = moment_two / fix_two
    weight = weight - step_rate * (
        first_hat / (jnp.sqrt(second_hat) + adam_eps) + decay_rate * weight
    )
    average = ema_decay * average + (1.0 - ema_decay) * weight
    return (weight, moment_one, moment_two, average)


def body(
    links,
    tokens,
    cotangent,
    slot_frame,
    step_count,
    *params,
):
    n_tok, n_head = links.n_tok, links.n_head
    devices = n_tok * n_head
    own = lax.axis_index("head")
    flip = lambda leaf: jnp.swapaxes(leaf, 1, 2)
    groups = []
    for at in range(0, 20, 5):
        qkv, proj, fc1, fc2, vec = params[at : at + 5]
        groups.append([qkv, flip(proj), fc1, flip(fc2), vec])
    masters = groups[0]

    slots = slot_frame.shape[0]
    per_head = slots // n_head
    held = slot_frame.reshape(n_head, per_head)
    held = jnp.concatenate(
        [lax.dynamic_slice_in_dim(held, own ^ step, 1, 0)[0] for step in range(n_head)]
    )
    index = jnp.arange(slots, dtype=jnp.int32)
    ahead = (held[None, :] < held[:, None]) | (
        (held[None, :] == held[:, None]) & (index[None, :] < index[:, None])
    )
    rank = jnp.sum(ahead.astype(jnp.int32), axis=1)
    order = jnp.sum(jnp.where(rank[None, :] == index[:, None], index[None, :], 0), axis=1).astype(jnp.int32)
    is_hi = (jnp.sum((held == held[0]).astype(jnp.int32)) == HI_BLOCKS).astype(jnp.int32).reshape(1)
    spans = (
        (HI_BLOCKS * BLOCK, LO_BLOCKS * BLOCK),
        (FRAMES * HI_BLOCKS * BLOCK, FRAMES * LO_BLOCKS * BLOCK),
    )

    vec_here = masters[4].shape[1]
    tile = lax.reduce_precision(masters[4], 8, 7).reshape(-1)
    tile = jnp.pad(tile, (0, 1024 - tile.shape[0])).reshape(8, 128)
    tiles = spread(tile, n_tok, n_head, 0).reshape(devices, 1024)[:, : 2 * vec_here]
    vectors = jnp.swapaxes(tiles.reshape(devices, 2, vec_here), 0, 1).reshape(2, devices * vec_here)
    vecs = [unpack(vectors[block]) for block in range(2)]

    qkv_low = [masters[0][block].astype(bf16) for block in range(2)]
    low = [
        jnp.concatenate([masters[kind][block].astype(bf16) for kind in (1, 2, 3)], axis=1)
        for block in range(2)
    ]
    places = links.gather_places()
    paired = links.paired
    width = D // n_head
    heads = width // HD
    own_rows = tokens.shape[0]
    cut = lambda rows: [rows[step * own_rows : (step + 1) * own_rows] for step in range(n_head)]
    gains = [head_gains(vec, heads) for vec in vecs]

    def attend(block, pieces, qkv_cols):
        qkv_bias = lax.dynamic_slice_in_dim(vecs[block][2].reshape(3, D), own * width, width, 1)
        return attention_forward(
            pieces, qkv_cols, qkv_bias.reshape(1, 3 * width), gains[block], order, is_hi, spans[block]
        )

    def enter(rows, mine, shard, collective_id):
        if paired:
            return enter_rows(rows, mine, shard, collective_id)
        planes = None if shard is None else links.gather_planes(shard)
        return links.rows_in(rows), lax.all_gather(mine, "tok", axis=0, tiled=True), planes

    def post(block, attended, hidden, pieces):
        vec, tail = vecs[block], vecs[1]
        rows = jnp.stack([vec[3], vec[4], vec[5], vec[6], vec[8], vec[9], tail[0], tail[1]])
        if not paired:
            attended = jnp.concatenate(links.by_index(links.exchange(cut(attended)), own), axis=1)
        return post_forward(
            attended,
            hidden,
            rows,
            vec[7].reshape(1, FF),
            (pieces, places),
            n_head,
            block == 1,
            paired,
            3 + block,
        )

    hidden_in = [tokens.astype(f32), None]
    normed = layer_norm(hidden_in[0], vecs[0][0], vecs[0][1]).astype(bf16)
    group, qkv_cols, saved, att_owns, mids, weights = ([None, None] for _ in range(6))

    mine = links.fetch_heads(qkv_low, own)
    normed, mine, low[0] = together(normed, mine, low[0])
    group[0], qkv_cols[0], planes = enter(normed, mine[0], low[0], 5)
    group[0], planes, qkv_cols[0], low[1] = together(group[0], planes, qkv_cols[0], low[1])
    near = links.gather_sides(planes)
    planes = links.gather_planes(low[1])
    saved[0] = attend(0, group[0], qkv_cols[0])
    saved[0], near, planes = together(saved[0], near, planes)
    (hidden_in[1], normed, *mids[0]), weights[0] = post(0, saved[0][0], hidden_in[0], near)

    group[1], qkv_cols[1], _planes = enter(normed, mine[1], None, 6)
    group[1], planes = together(group[1], planes)
    near = links.gather_sides(planes)
    saved[1] = attend(1, group[1], qkv_cols[1])
    saved[1], near = together(saved[1], near)
    (hidden, _normed, *mids[1]), weights[1] = post(1, saved[1][0], hidden_in[1], near)

    def post_back(block, grad):
        vec = vecs[block]
        down, act, slope, branch, after, two, att_own = mids[block]
        rows = jnp.stack([vec[4], vec[5], vec[9]] + [vec[9]] * 5)
        d_att, *rest = post_backward(
            att_own,
            grad,
            down,
            branch,
            after,
            two,
            rows,
            act,
            slope,
            (weights[block], places),
            n_head,
            paired,
            7 + block,
        )
        if not paired:
            parts = [
                lax.dynamic_slice_in_dim(d_att, (own ^ step) * width, width, 1) for step in range(n_head)
            ]
            d_att = jnp.concatenate(links.exchange(parts), axis=0)
        return d_att, *rest

    def attend_back(block, grad_heads):
        attended, raw, values, lse = saved[block]
        return attention_backward(
            raw, values, grad_heads, attended, lse, gains[block], order, is_hi, spans[block]
        )

    def rows_back(block, d_qkv, d_after):
        gain, shift = vecs[block][0], vecs[block][1]
        if paired:
            grad, sums = rows_out(
                d_qkv, qkv_cols[block], hidden_in[block], d_after, gain.reshape(1, D), 9 + block
            )
            return grad, sums[0], sums[1]
        d_normed = jnp.einsum("rc,dc->rd", d_qkv, qkv_cols[block], preferred_element_type=f32)
        back = links.rows_out(cut(d_normed.astype(bf16)))
        d_hidden, d_gain, d_shift = jax.vjp(layer_norm, hidden_in[block], gain, shift)[1](back)
        return d_after + d_hidden, d_gain, d_shift

    def qkv_grad(block, d_qkv):
        rows = jnp.concatenate(group[block], axis=0)
        return jnp.einsum("rd,rc->dc", rows, d_qkv, preferred_element_type=f32).astype(bf16)

    def vector_grad(norm_sums, sums, d_up_bias, head_sums, bias_sums):
        d_qkv_bias = lax.dynamic_update_slice_in_dim(
            jnp.zeros((3, D), f32), bias_sums[0].reshape(3, width), own * width, 1
        ).reshape(3 * D)
        head_sums = jnp.sum(head_sums[:4].reshape(4, heads, HD), axis=1).reshape(4 * HD)
        parts = [*norm_sums, d_qkv_bias, sums[5], sums[4], sums[2], sums[3], d_up_bias, sums[1], sums[0], head_sums]
        return jnp.concatenate([part.reshape(-1, 128) for part in parts], axis=0)

    d_att, d_after, sums, d_up_bias, grads = post_back(1, cotangent.astype(f32))
    grads = links.scatter_first(grads)
    d_qkv, head_sums, bias_sums = attend_back(1, d_att)
    d_qkv, head_sums, bias_sums, grads = together(d_qkv, head_sums, bias_sums, grads)
    grads = links.scatter_add(grads)
    dw_qkv = links.return_cores(qkv_grad(1, d_qkv))
    grad_rows, *norm_sums = rows_back(1, d_qkv, d_after)
    d_vec_one = vector_grad(norm_sums, sums, d_up_bias, head_sums, bias_sums)
    grad_rows, grads, dw_qkv = together(grad_rows, grads, dw_qkv)
    grads_one = links.scatter_second(grads)
    mine_one = links.return_planes(dw_qkv)

    d_att, d_after, sums, d_up_bias, grads = post_back(0, grad_rows)
    d_att, grads_one, mine_one, grads = together(d_att, grads_one, mine_one, grads)
    sum_one = links.scatter_last(grads_one)
    grads = links.scatter_first(grads)
    d_qkv, head_sums, bias_sums = attend_back(0, d_att)
    d_qkv, head_sums, bias_sums, grads, sum_one = together(d_qkv, head_sums, bias_sums, grads, sum_one)
    vec_shape = (devices, 2 * vec_here)

    def tiles_of(row_zero, row_one):
        both = jnp.stack([row_zero, row_one]).reshape(2, devices, vec_here)
        flat = jnp.swapaxes(both, 0, 1).reshape(vec_shape)
        return jnp.pad(flat, ((0, 0), (0, 1024 - vec_shape[1]))).reshape(devices, 8, 128)

    if paired:
        none = jnp.zeros((D,), f32)
        tiles = tiles_of(vector_grad((none, none), sums, d_up_bias, head_sums, bias_sums), d_vec_one)
        gain = vecs[0][0].reshape(1, D)
        square = jnp.broadcast_to(jnp.sum(sum_one * sum_one), (8, 128))
        grad_rows, _sums, sum_zero, *qkv_grads, d_vec, squares = finish(
            d_qkv,
            qkv_cols[0],
            hidden_in[0],
            d_after,
            gain,
            group[0],
            grads,
            tiles,
            mine_one,
            square,
            n_tok,
            n_head,
            11,
        )
        qkv_zero, qkv_one = [
            jnp.transpose(part.reshape(n_head, -1, 3, width), (1, 2, 0, 3)).reshape(-1, 3 * D) for part in qkv_grads
        ]
    else:
        grad_rows, *norm_sums = rows_back(0, d_qkv, d_after)
        dw_qkv = links.return_cores(qkv_grad(0, d_qkv))
        tiles = tiles_of(vector_grad(norm_sums, sums, d_up_bias, head_sums, bias_sums), d_vec_one)
        d_vec = swap(tiles, n_tok, n_head, 1)
        sum_zero = links.scatter_last(links.scatter_second(links.scatter_add(grads)))
        qkv_zero, qkv_one = links.return_heads([links.return_planes(dw_qkv), mine_one], own)
    summed = []
    for qkv_part, rest in ((qkv_zero, sum_zero), (qkv_one, sum_one)):
        summed.append([qkv_part, rest[:, PROJ_AT:UP_AT], rest[:, UP_AT:DOWN_AT], rest[:, DOWN_AT:WIDE]])
    d_vec = d_vec.reshape(1024)[: 2 * vec_here].reshape(2, vec_here)
    gradients = [jnp.stack([summed[0][kind], summed[1][kind]]) for kind in range(4)]
    if not paired:
        local_square = sum((jnp.sum(gradient * gradient) for gradient in gradients)) + jnp.sum(d_vec * d_vec)
        tile = jnp.concatenate([jnp.broadcast_to(local_square, (8, 128)), jnp.zeros((16, 128), f32)], axis=0)
        squares = spread(tile, n_tok, n_head, 2)
    late = jnp.sum(squares[:, 8:], axis=0).reshape(2 * D)
    grad_norm = jnp.sqrt(jnp.sum(squares[:, 0, 0]) + jnp.sum(late * late))
    if paired:
        flat = jnp.concatenate([late, jnp.zeros((devices * vec_here - 2 * D,), f32)]).reshape(devices, vec_here)
        mine_late = lax.dynamic_slice_in_dim(flat, lax.axis_index("tok") * n_head + own, 1, 0)
        d_vec = d_vec + jnp.concatenate([mine_late, jnp.zeros((1, vec_here), f32)], axis=0)
    gradients.append(d_vec)
    clip_scale = clip_norm / jnp.maximum(grad_norm, clip_norm)
    step_float = step_count[0].astype(f32)
    fix_one = 1.0 - beta_one**step_float
    fix_two = 1.0 - beta_two**step_float
    updates = [
        adam_update(
            groups[0][kind],
            gradients[kind],
            groups[1][kind],
            groups[2][kind],
            groups[3][kind],
            step_rates[kind],
            decays[kind],
            clip_scale,
            fix_one,
            fix_two,
        )
        for kind in range(5)
    ]
    outs = [hidden, grad_rows, grad_norm]
    for part in range(4):
        for kind in range(5):
            leaf = updates[kind][part]
            outs.append(flip(leaf) if kind in (1, 3) else leaf)
    return tuple(outs)


def solution(mesh):
    rows = P(BOTH, None)
    kinds = (
        P(None, BOTH, None),
        P(None, None, BOTH),
        P(None, BOTH, None),
        P(None, None, BOTH),
        P(None, BOTH),
    )
    in_specs = (rows, rows, P("tok"), P()) + kinds * 4
    out_specs = (rows, rows, P()) + kinds * 4
    return jax.shard_map(
        functools.partial(body, Links(mesh)),
        mesh=mesh,
        in_specs=in_specs,
        out_specs=out_specs,
        check_vma=False,
    )
```

```python
import functools
import math

import jax
import jax.numpy as jnp
from jax import lax
from jax.experimental import pallas as pl
from jax.experimental.pallas import tpu as pltpu
from jax.sharding import PartitionSpec as P

D = 1024
HD = 64
FF = 4096
BLOCK = 128
HI_BLOCKS = 8
LO_BLOCKS = 4
FRAMES = 2

norm_eps = 1e-06
clip_norm = 1.0
beta_one = 0.9
beta_two = 0.999
adam_eps = 1e-08
ema_decay = 0.7
step_rates = (0.05, 0.4, 0.05, 0.025, 0.3)
decays = (0.05, 0.05, 0.05, 0.05, 0.0)

LOG2E = math.log2(math.e)
SPAN = 512
MESH_ID = pl.DeviceIdType.MESH
BOTH = ("tok", "head")
bf16 = jnp.bfloat16
f32 = jnp.float32
VMEM_BYTES = 60 << 20


def _peer(step, n_tok, n_head):
    n = n_tok * n_head
    me = lax.axis_index("tok") * n_head + lax.axis_index("head")
    to = lax.rem(me + step, n)
    return me, to, (to // n_head, lax.rem(to, n_head))


def _enter(n_tok, n_head):
    n = n_tok * n_head
    barrier = pltpu.get_barrier_semaphore()

    def greet(step, _):
        _, _, device = _peer(step, n_tok, n_head)
        pl.semaphore_signal(barrier, inc=1, device_id=device, device_id_type=MESH_ID)
        return 0

    lax.fori_loop(1, n, greet, 0)
    pl.semaphore_wait(barrier, n - 1)


def spread_kernel(n_tok, n_head, x_ref, o_ref, send_sem, recv_sem):
    n = n_tok * n_head
    _enter(n_tok, n_head)
    me = lax.axis_index("tok") * n_head + lax.axis_index("head")
    o_ref[me] = x_ref[...]

    def copy(step):
        me, _, device = _peer(step, n_tok, n_head)
        return pltpu.make_async_remote_copy(
            src_ref=x_ref,
            dst_ref=o_ref.at[me],
            send_sem=send_sem.at[step],
            recv_sem=recv_sem.at[step],
            device_id=device,
            device_id_type=MESH_ID,
        )

    def start(step, _):
        copy(step).start()
        return 0

    def finish(step, _):
        copy(step).wait()
        return 0

    lax.fori_loop(1, n, start, 0)
    lax.fori_loop(1, n, finish, 0)


def swap_kernel(n_tok, n_head, x_ref, o_ref, land, send_sem, recv_sem):
    n = n_tok * n_head
    _enter(n_tok, n_head)
    me = lax.axis_index("tok") * n_head + lax.axis_index("head")

    def copy(step):
        me, to, device = _peer(step, n_tok, n_head)
        return pltpu.make_async_remote_copy(
            src_ref=x_ref.at[to],
            dst_ref=land.at[step],
            send_sem=send_sem.at[step],
            recv_sem=recv_sem.at[step],
            device_id=device,
            device_id_type=MESH_ID,
        )

    def start(step, _):
        copy(step).start()
        return 0

    def finish(step, _):
        copy(step).wait()
        return 0

    lax.fori_loop(1, n, start, 0)
    lax.fori_loop(1, n, finish, 0)
    o_ref[...] = x_ref[me] + jnp.sum(land[1:], axis=0)


def spread(tile, n_tok, n_head, collective_id):
    n = n_tok * n_head
    return pl.pallas_call(
        functools.partial(spread_kernel, n_tok, n_head),
        out_shape=jax.ShapeDtypeStruct((n,) + tile.shape, tile.dtype),
        in_specs=[pl.BlockSpec(memory_space=pltpu.VMEM)],
        out_specs=pl.BlockSpec(memory_space=pltpu.VMEM),
        scratch_shapes=[pltpu.SemaphoreType.DMA((n,)), pltpu.SemaphoreType.DMA((n,))],
        compiler_params=pltpu.CompilerParams(collective_id=collective_id, has_side_effects=True),
    )(tile)


def swap(tiles, n_tok, n_head, collective_id):
    n = n_tok * n_head
    return pl.pallas_call(
        functools.partial(swap_kernel, n_tok, n_head),
        out_shape=jax.ShapeDtypeStruct(tiles.shape[1:], tiles.dtype),
        in_specs=[pl.BlockSpec(memory_space=pltpu.VMEM)],
        out_specs=pl.BlockSpec(memory_space=pltpu.VMEM),
        scratch_shapes=[
            pltpu.VMEM(tiles.shape, tiles.dtype),
            pltpu.SemaphoreType.DMA((n,)),
            pltpu.SemaphoreType.DMA((n,)),
        ],
        compiler_params=pltpu.CompilerParams(collective_id=collective_id, has_side_effects=True),
    )(tiles)


def _lane_mean(values, grouping):
    top = values.astype(bf16)
    rest = (values - top.astype(f32)).astype(bf16)
    return jnp.dot(top, grouping, preferred_element_type=f32) + jnp.dot(
        rest, grouping, preferred_element_type=f32
    )


def _grouping(width):
    row = lax.broadcasted_iota(jnp.int32, (width, width), 0) // HD
    col = lax.broadcasted_iota(jnp.int32, (width, width), 1) // HD
    return jnp.where(row == col, 1.0 / HD, 0.0).astype(bf16)


def _unit(values, grouping):
    centered = values - _lane_mean(values, grouping)
    spread_ = _lane_mean(centered * centered, grouping)
    scale = lax.rsqrt(spread_ + norm_eps)
    return centered * scale, scale


def _only(values, head):
    lane = lax.broadcasted_iota(jnp.int32, values.shape, 1)
    return jnp.where(lane // HD == head, values, jnp.zeros_like(values))


NT = (((1,), (1,)), ((), ()))
TN = (((0,), (0,)), ((), ()))


def forward_kernel(
    heads, pieces, spans, tile_rows, order_ref, hi_ref, *refs
):
    x_refs = refs[:pieces]
    w_ref, bias_ref, gains_ref, att_ref, raw_ref, val_ref, lse_ref, q_s, k_s, v_s, acc = refs[pieces:]
    width = heads * HD
    rows = att_ref.shape[0]
    blocks = rows // BLOCK
    piece_rows = rows // pieces
    for at in range(pieces):
        full = jnp.dot(x_refs[at][...], w_ref[...], preferred_element_type=f32) + bias_ref[...]
        here = pl.ds(at * piece_rows, piece_rows)
        raw_ref[here, :] = full[:, : 2 * width]
        val_ref[here, :] = full[:, 2 * width :].astype(bf16)
    grouping = _grouping(width)

    def place(at, _):
        here = pl.ds(pl.multiple_of(order_ref[at] * BLOCK, BLOCK), BLOCK)
        there = pl.ds(pl.multiple_of(at * BLOCK, BLOCK), BLOCK)
        unit_q, _s = _unit(raw_ref[here, :width], grouping)
        unit_k, _s = _unit(raw_ref[here, width:], grouping)
        q_s[there, :] = ((unit_q * gains_ref[0:1, :] + gains_ref[1:2, :]) * HD ** (-0.5)).astype(bf16)
        key = (unit_k * gains_ref[2:3, :] + gains_ref[3:4, :]).astype(bf16)
        value = val_ref[here, :]
        for head in range(heads):
            k_s[head, there, :] = _only(key, head)
            v_s[head, there, :] = _only(value, head)
        return 0

    lax.fori_loop(0, blocks, place, 0)
    per_tile = tile_rows // BLOCK

    def attend(span):
        def tile(at, _):
            here = pl.ds(pl.multiple_of(at * tile_rows, tile_rows), tile_rows)
            first = at * tile_rows // span * span
            there = pl.ds(pl.multiple_of(first, span), span)
            query = q_s[here, :]
            lane = lax.broadcasted_iota(jnp.int32, (tile_rows, 128), 1)
            logs = jnp.zeros((tile_rows, 128), f32)
            for head in range(heads):
                scores = lax.dot_general(query, k_s[head, there, :], NT, preferred_element_type=f32)
                top = jnp.max(scores, axis=1, keepdims=True) * LOG2E
                probs = jnp.exp2(scores * LOG2E - top)
                total = jnp.sum(probs, axis=1, keepdims=True)
                part = jnp.dot(
                    probs.astype(bf16), v_s[head, there, :], preferred_element_type=f32
                ) / total
                if head == 0:
                    acc[...] = part
                else:
                    acc[...] += part
                logs = jnp.where(lane == head, top + jnp.log2(total), logs)
            lse_ref[here, :] = logs
            for sub in range(per_tile):
                out = pl.ds(pl.multiple_of(order_ref[at * per_tile + sub] * BLOCK, BLOCK), BLOCK)
                att_ref[out, :] = acc[sub * BLOCK : (sub + 1) * BLOCK, :].astype(bf16)
            return 0

        lax.fori_loop(0, rows // tile_rows, tile, 0)

    @pl.when(hi_ref[0] == 1)
    def _():
        attend(spans[0])

    @pl.when(hi_ref[0] == 0)
    def _():
        attend(spans[1])


def attention_forward(pieces, weight, bias, gains, order, is_hi, spans):
    heads = weight.shape[1] // (3 * HD)
    width = heads * HD
    rows = sum(piece.shape[0] for piece in pieces)
    tile_rows = 256
    smem = pl.BlockSpec(memory_space=pltpu.SMEM)
    vmem = pl.BlockSpec(memory_space=pltpu.VMEM)
    flops = 2 * rows * (D * 3 * width + 8 * spans[0] * width)
    return pl.pallas_call(
        functools.partial(forward_kernel, heads, len(pieces), spans, tile_rows),
        out_shape=(
            jax.ShapeDtypeStruct((rows, width), bf16),
            jax.ShapeDtypeStruct((rows, 2 * width), f32),
            jax.ShapeDtypeStruct((rows, width), bf16),
            jax.ShapeDtypeStruct((rows, 128), f32),
        ),
        in_specs=[smem, smem] + [vmem] * (len(pieces) + 3),
        out_specs=(vmem,) * 4,
        scratch_shapes=[
            pltpu.VMEM((rows, width), bf16),
            pltpu.VMEM((heads, rows, width), bf16),
            pltpu.VMEM((heads, rows, width), bf16),
            pltpu.VMEM((tile_rows, width), f32),
        ],
        compiler_params=pltpu.CompilerParams(vmem_limit_bytes=VMEM_BYTES),
        cost_estimate=pl.CostEstimate(
            flops=flops, bytes_accessed=rows * (2 * D + 14 * width), transcendentals=rows * spans[0] * heads
        ),
    )(order, is_hi, *pieces, weight, bias, gains)


def backward_kernel(
    heads,
    spans,
    order_ref,
    hi_ref,
    raw_ref,
    val_ref,
    grad_ref,
    att_ref,
    lse_ref,
    gains_ref,
    out_ref,
    sums_ref,
    bias_ref,
    q_s,
    o_s,
    k_m,
    v_m,
    q_m,
    o_m,
    dq_s,
    dk_s,
    dv_s,
    lse_t,
    delta_t,
):
    width = heads * HD
    rows = val_ref.shape[0]
    blocks = rows // BLOCK
    grouping = _grouping(width)
    head_of = lax.broadcasted_iota(jnp.int32, (8, width), 1) // HD
    picks = jnp.where(head_of == lax.broadcasted_iota(jnp.int32, (8, width), 0), 1.0, 0.0).astype(bf16)

    def place(at, _):
        here = pl.ds(pl.multiple_of(order_ref[at] * BLOCK, BLOCK), BLOCK)
        there = pl.ds(pl.multiple_of(at * BLOCK, BLOCK), BLOCK)
        unit_q, _s = _unit(raw_ref[here, :width], grouping)
        unit_k, _s = _unit(raw_ref[here, width:], grouping)
        query = ((unit_q * gains_ref[0:1, :] + gains_ref[1:2, :]) * HD ** (-0.5)).astype(bf16)
        key = (unit_k * gains_ref[2:3, :] + gains_ref[3:4, :]).astype(bf16)
        value = val_ref[here, :]
        grad = grad_ref[here, :]
        q_s[there, :] = query
        o_s[there, :] = grad
        for head in range(heads):
            k_m[head, there, :] = _only(key, head)
            v_m[head, there, :] = _only(value, head)
            q_m[head, there, :] = _only(query, head)
            o_m[head, there, :] = _only(grad, head)
        both = grad.astype(f32) * att_ref[here, :].astype(f32)
        top = both.astype(bf16)
        rest = (both - top.astype(f32)).astype(bf16)
        delta_t[:, there] = lax.dot_general(picks, top, NT, preferred_element_type=f32) + lax.dot_general(
            picks, rest, NT, preferred_element_type=f32
        )
        lse_t[:, there] = jnp.transpose(lse_ref[there, :])[:8, :]
        dq_s[there, :] = jnp.zeros((BLOCK, width), f32)
        dk_s[there, :] = jnp.zeros((BLOCK, width), f32)
        dv_s[there, :] = jnp.zeros((BLOCK, width), f32)
        return 0

    lax.fori_loop(0, blocks, place, 0)
    span = jnp.where(hi_ref[0] == 1, spans[0], spans[1])

    def tile(at, _):
        here = pl.ds(pl.multiple_of(at * SPAN, SPAN), SPAN)
        first = at * SPAN // span * span // SPAN

        def chunk(key_at, _):
            there = pl.ds(pl.multiple_of(key_at * SPAN, SPAN), SPAN)
            for head in range(heads):
                scores = lax.dot_general(k_m[head, there, :], q_s[here, :], NT, preferred_element_type=f32)
                probs = jnp.exp2(scores * LOG2E - lse_t[head : head + 1, here])
                grad_probs = lax.dot_general(
                    v_m[head, there, :], o_s[here, :], NT, preferred_element_type=f32
                )
                grad_scores = (probs * (grad_probs - delta_t[head : head + 1, here])).astype(bf16)
                dv_s[there, :] += jnp.dot(probs.astype(bf16), o_m[head, here, :], preferred_element_type=f32)
                dk_s[there, :] += jnp.dot(grad_scores, q_m[head, here, :], preferred_element_type=f32)
                dq_s[here, :] += lax.dot_general(
                    grad_scores, k_m[head, there, :], TN, preferred_element_type=f32
                )
            return 0

        lax.fori_loop(first, first + span // SPAN, chunk, 0)
        return 0

    lax.fori_loop(0, rows // SPAN, tile, 0)
    sums_ref[...] = jnp.zeros_like(sums_ref)
    bias_ref[...] = jnp.zeros_like(bias_ref)

    def pull(grad, unit, scale, gain):
        grad_unit = grad * gain
        inner = _lane_mean(grad_unit, grouping)
        cross = _lane_mean(grad_unit * unit, grouping)
        return scale * (grad_unit - inner - unit * cross)

    def leave(at, _):
        here = pl.ds(pl.multiple_of(order_ref[at] * BLOCK, BLOCK), BLOCK)
        there = pl.ds(pl.multiple_of(at * BLOCK, BLOCK), BLOCK)
        unit_q, scale_q = _unit(raw_ref[here, :width], grouping)
        unit_k, scale_k = _unit(raw_ref[here, width:], grouping)
        grad_q = dq_s[there, :] * HD ** (-0.5)
        grad_k = dk_s[there, :]
        sums_ref[0:1, :] += jnp.sum(grad_q * unit_q, axis=0, keepdims=True)
        sums_ref[1:2, :] += jnp.sum(grad_q, axis=0, keepdims=True)
        sums_ref[2:3, :] += jnp.sum(grad_k * unit_k, axis=0, keepdims=True)
        sums_ref[3:4, :] += jnp.sum(grad_k, axis=0, keepdims=True)
        low_q = pull(grad_q, unit_q, scale_q, gains_ref[0:1, :]).astype(bf16)
        low_k = pull(grad_k, unit_k, scale_k, gains_ref[2:3, :]).astype(bf16)
        low_v = dv_s[there, :].astype(bf16)
        for part, low in enumerate((low_q, low_k, low_v)):
            lanes = slice(part * width, (part + 1) * width)
            out_ref[here, lanes] = low
            bias_ref[0:1, lanes] += jnp.sum(low.astype(f32), axis=0, keepdims=True)
        return 0

    lax.fori_loop(0, blocks, leave, 0)


def attention_backward(raw, values, grad, attended, lse, gains, order, is_hi, spans):
    rows, width = values.shape
    heads = width // HD
    smem = pl.BlockSpec(memory_space=pltpu.SMEM)
    vmem = pl.BlockSpec(memory_space=pltpu.VMEM)
    flops = 2 * rows * 20 * spans[0] * width
    masked = pltpu.VMEM((heads, rows, width), bf16)
    return pl.pallas_call(
        functools.partial(backward_kernel, heads, spans),
        out_shape=(
            jax.ShapeDtypeStruct((rows, 3 * width), bf16),
            jax.ShapeDtypeStruct((8, width), f32),
            jax.ShapeDtypeStruct((8, 3 * width), f32),
        ),
        in_specs=[smem, smem] + [vmem] * 6,
        out_specs=(vmem,) * 3,
        scratch_shapes=[
            pltpu.VMEM((rows, width), bf16),
            pltpu.VMEM((rows, width), bf16),
            masked,
            masked,
            masked,
            masked,
            pltpu.VMEM((rows, width), f32),
            pltpu.VMEM((rows, width), f32),
            pltpu.VMEM((rows, width), f32),
            pltpu.VMEM((8, rows), f32),
            pltpu.VMEM((8, rows), f32),
        ],
        compiler_params=pltpu.CompilerParams(vmem_limit_bytes=VMEM_BYTES),
        cost_estimate=pl.CostEstimate(
            flops=flops, bytes_accessed=rows * 24 * width, transcendentals=rows * spans[0] * heads
        ),
    )(order, is_hi, raw, values, grad, attended, lse, gains)


class Links:
    def __init__(self, mesh):
        self.n_tok = mesh.shape["tok"]
        self.n_head = mesh.shape["head"]
        self.paired = self.n_tok == 8 and self.n_head == 4

    def head(self, values, step):
        return lax.ppermute(values, "head", [(i, i ^ step) for i in range(self.n_head)])

    def tok(self, values, step):
        return lax.ppermute(values, "tok", [(i, i ^ step) for i in range(self.n_tok)])

    def rows_in(self, rows):
        if not self.paired:
            return [rows] + [self.head(rows, step) for step in range(1, self.n_head)]
        half = rows.shape[0] // 2
        one, two = self.head(rows, 1), self.head(rows, 2)
        far = jnp.concatenate([self.head(one[:half], 2), self.head(two[half:], 1)], axis=0)
        return [rows, one, two, far]

    def rows_out(self, parts):
        if not self.paired:
            moved = [self.head(parts[step], step).astype(f32) for step in range(1, self.n_head)]
            return parts[0].astype(f32) + sum(moved)
        half = parts[0].shape[0] // 2
        upper = [part[:half] for part in parts]
        lower = [part[half:] for part in parts]
        pass_up = (upper[2].astype(f32) + self.head(upper[3], 1).astype(f32)).astype(bf16)
        pass_low = (lower[1].astype(f32) + self.head(lower[3], 2).astype(f32)).astype(bf16)
        up = upper[0].astype(f32) + self.head(upper[1], 1).astype(f32) + self.head(pass_up, 2).astype(f32)
        low = lower[0].astype(f32) + self.head(lower[2], 2).astype(f32) + self.head(pass_low, 1).astype(f32)
        return jnp.concatenate([up, low], axis=0)

    def exchange(self, parts):
        return [parts[0]] + [self.head(parts[step], step) for step in range(1, self.n_head)]

    def by_index(self, pieces, own):
        return [
            lax.select_n((own ^ at).astype(jnp.int32), *pieces) if len(pieces) > 1 else pieces[0]
            for at in range(len(pieces))
        ]

    def zed(self):
        return lax.axis_index("tok") // 2

    def core(self):
        return lax.rem(lax.axis_index("tok"), 2)

    def planes(self, shard):
        pieces = [shard] + [self.tok(shard, 2 * step) for step in range(1, 4)]
        return jnp.stack(self.by_index(pieces, self.zed()))

    def gather_places(self):
        if not self.paired:
            return [None]
        spots = ((0, 4, 0), (0, 4, 1), (0, 4, 2), (0, 2, 3), (2, 2, 3))
        return [("head", first, count, core, to) for first, count, to in spots for core in range(2)]

    def gather_planes(self, shard):
        if not self.paired:
            whole = lax.all_gather(shard, BOTH, axis=0, tiled=True)
            return [whole.reshape(4, 2, 4, whole.shape[0] // 32, whole.shape[1])]
        return [self.planes(shard)]

    def gather_sides(self, own):
        if not self.paired:
            return own
        return [own[0], self.head(own[0], 1), self.head(own[0], 2)]

    def scatter_first(self, grads):
        if not self.paired:
            return grads
        low, top, keep = grads
        return [keep, self.head(low, 1), self.head(top, 2)]

    def scatter_add(self, grads):
        if not self.paired:
            return grads
        keep, low, top = grads
        plus = lambda one, two: (one.astype(f32) + two.astype(f32)).astype(bf16)
        own = [plus(keep[:2], low[:2]), plus(keep[4:6], top[:2])]
        return [own, [plus(keep[2:4], low[2:]), plus(keep[6:], top[2:])]]

    def scatter_second(self, halves):
        if not self.paired:
            return halves
        own, passed = halves
        low = own[0].astype(f32) + self.head(passed[0], 2).astype(f32)
        top = own[1].astype(f32) + self.head(passed[1], 1).astype(f32)
        return [jnp.concatenate([low, top], axis=0).astype(bf16)]

    def scatter_last(self, planes):
        if not self.paired:
            whole = planes[0].reshape(-1, planes[0].shape[-1])
            return lax.psum_scatter(whole, BOTH, scatter_dimension=0, tiled=True).astype(f32)
        return self.sum_planes(planes[0])

    def sum_planes(self, parts):
        zed = self.zed()
        pick = lambda step: lax.dynamic_slice_in_dim(parts, zed ^ step, 1, 0)[0]
        total = pick(0).astype(f32)
        for step in range(1, 4):
            total = total + self.tok(pick(step).astype(bf16), 2 * step).astype(f32)
        return total

    def fetch_heads(self, shards, own):
        own_rows = shards[0].shape[0]
        width = D // self.n_head
        cut = jnp.stack(shards).reshape(len(shards), own_rows, 3, D)
        parts = [
            lax.dynamic_slice_in_dim(cut, (own ^ step) * width, width, 3).reshape(
                len(shards), own_rows, 3 * width
            )
            for step in range(self.n_head)
        ]
        moved = jnp.stack(self.by_index(self.exchange(parts), own), axis=1)
        return [moved[at].reshape(self.n_head * own_rows, 3 * width) for at in range(len(shards))]

    def return_planes(self, grad):
        if not self.paired:
            return lax.psum_scatter(grad, "tok", scatter_dimension=0, tiled=True)
        return self.sum_planes(grad).astype(bf16)

    def return_heads(self, both, own):
        width = D // self.n_head
        stack = jnp.stack(both)
        own_rows = stack.shape[1] // self.n_head
        parts = [
            lax.dynamic_slice_in_dim(stack, (own ^ step) * own_rows, own_rows, 1)
            for step in range(self.n_head)
        ]
        back = jnp.stack(self.by_index(self.exchange(parts), own), axis=2)
        back = back.reshape(len(both), own_rows, self.n_head, 3, width)
        return jnp.swapaxes(back, 2, 3).reshape(len(both), own_rows, 3 * D).astype(f32)


def together(*values):
    return lax.optimization_barrier(values)


CHUNK = 512


def _paired(value, step, bits):
    total = 0
    for bit in range(bits):
        one = lax.rem(value // (1 << bit), 2)
        total = total + (1 - one if (step >> bit) % 2 else one) * (1 << bit)
    return total


def _slot(ref, place):
    if place is None:
        return ref
    tok = lax.axis_index("tok")
    side = _paired(lax.rem(tok, 2), place[-1] if place[0] == "plane" else place[3], 1)
    if place[0] == "plane":
        return ref.at[_paired(tok // 2, place[1], 2), side]
    return ref.at[pl.ds(place[1], place[2]), side, _paired(lax.axis_index("head"), place[4], 2)]


PROJ_AT, UP_AT, DOWN_AT, WIDE = 0, D, D + FF, D + 2 * FF


def _cols(ref, at, size):
    window = pl.ds(pl.multiple_of(at, 128), size)
    return ref.at[(slice(None),) * (len(ref.shape) - 1) + (window,)]


def _copies(pieces, places, whole, at, size, sems, inward):
    moves = []
    for index, (piece, place) in enumerate(zip(pieces, places)):
        outside = _cols(piece, at, size)
        inside = _slot(whole, place)
        pair = (outside, inside) if inward else (inside, outside)
        moves.append(pltpu.make_async_copy(pair[0], pair[1], sems.at[index]))
    return moves


def _start(moves):
    for move in moves:
        move.start()


def _wait(moves):
    for move in moves:
        move.wait()


def _flat(values):
    return values.reshape(D, values.shape[-1])


def _norm(values):
    centered = values - jnp.mean(values, axis=-1, keepdims=True)
    scale = lax.rsqrt(jnp.mean(centered * centered, axis=-1, keepdims=True) + norm_eps)
    return centered * scale, scale


def _own_column(step, n_head):
    at = _paired(lax.axis_index("head"), step, n_head.bit_length() - 1)
    return pl.multiple_of(at * (D // n_head), 128)


def _mate(step):
    return lax.axis_index("tok"), _paired(lax.axis_index("head"), step, 2)


def _sibling():
    return _paired(lax.axis_index("tok"), 1, 3), lax.axis_index("head")


def _greet(devices):
    barrier = pltpu.get_barrier_semaphore()
    for device in devices:
        pl.semaphore_signal(barrier, inc=1, device_id=device, device_id_type=MESH_ID)
    pl.semaphore_wait(barrier, len(devices))


def _send(source, target, send_sem, recv_sem, device):
    return pltpu.make_async_remote_copy(
        src_ref=source,
        dst_ref=target,
        send_sem=send_sem,
        recv_sem=recv_sem,
        device_id=device,
        device_id_type=MESH_ID,
    )


def enter_kernel(wide, *refs):
    x_ref, q_ref, refs = refs[0], refs[1], refs[2:]
    if wide:
        shard_ref, refs = refs[0], refs[1:]
    one_ref, two_ref, far_ref, full_ref, refs = *refs[:4], refs[4:]
    if wide:
        planes_ref, refs = refs[0], refs[1:]
    send_sem, recv_sem, z_send, z_recv, own_sem, core_sem = refs
    tok, head = lax.axis_index("tok"), lax.axis_index("head")
    zed, core = tok // 2, lax.rem(tok, 2)
    one_way, two_way = _mate(1), _mate(2)
    barrier = pltpu.get_barrier_semaphore()
    greet = lambda device: pl.semaphore_signal(barrier, inc=1, device_id=device, device_id_type=MESH_ID)
    for device in (one_way, two_way, _sibling()):
        greet(device)

    @pl.when(zed < 3)
    def _():
        greet((tok + 2, head))

    @pl.when(zed > 0)
    def _():
        greet((tok - 2, head))

    edge = (zed == 0) | (zed == 3)

    @pl.when(edge)
    def _():
        pl.semaphore_wait(barrier, 4)

    @pl.when(jnp.logical_not(edge))
    def _():
        pl.semaphore_wait(barrier, 5)

    rows = x_ref.shape[0]
    parts = 4
    size = rows // parts

    def move(lane, part, source, target, device):
        here = pl.ds(part * size, size)
        return _send(source.at[here], target.at[here], send_sem.at[lane, part], recv_sem.at[lane, part], device)

    to_one = lambda part: move(0, part, x_ref, one_ref, one_way)
    to_two = lambda part: move(1, part, x_ref, two_ref, two_way)
    on_two = lambda part: move(2, part, one_ref, far_ref, two_way)
    on_one = lambda part: move(2, part, two_ref, far_ref, one_way)
    homes = [(q_ref, lambda plane: full_ref.at[plane, core])]
    if wide:
        homes.append((shard_ref, lambda plane: planes_ref.at[plane]))

    def climb(up, step):
        plane = jnp.clip(zed - step if up else zed + step, 0, 3)
        device = (jnp.clip(tok + 2 if up else tok - 2, 0, 7), head)
        return [
            _send(
                home(plane) if step else source,
                home(plane),
                z_send.at[int(up), step, index],
                z_recv.at[int(up), step, index],
                device,
            )
            for index, (source, home) in enumerate(homes)
        ]

    def sends(up, step):
        return (zed >= step) & (zed < 3) if up else (zed <= 3 - step) & (zed > 0)

    def comes(up, step):
        return zed >= step + 1 if up else zed <= 2 - step

    def climb_start(up, step):
        @pl.when(sends(up, step))
        def _():
            _start(climb(up, step))

    def climb_come(up, step):
        @pl.when(comes(up, step))
        def _():
            for copy in climb(up, step):
                copy.wait_recv()

    for turn in range(parts):
        to_one(turn).start()
        to_two(parts - 1 - turn).start()
    for up in (True, False):
        climb_start(up, 0)
    stays = [
        pltpu.make_async_copy(source, home(zed), own_sem.at[index]) for index, (source, home) in enumerate(homes)
    ]
    _start(stays)
    for turn in range(parts // 2):
        to_one(turn).wait_recv()
        on_two(turn).start()
        to_two(parts - 1 - turn).wait_recv()
        on_one(parts - 1 - turn).start()
    for step in range(3):
        for up in (True, False):
            climb_come(up, step)
            if step < 2:
                climb_start(up, step + 1)
    _wait(stays)
    mine = full_ref.at[:, core]
    over = _send(mine, mine, core_sem.at[0], core_sem.at[1], _sibling())
    over.start()
    for turn in range(parts // 2, parts):
        to_one(turn).wait_recv()
        to_two(parts - 1 - turn).wait_recv()
    for turn in range(parts):
        to_one(turn).wait_send()
        to_two(turn).wait_send()
    for turn in range(parts // 2):
        on_two(turn).wait()
        on_one(parts - 1 - turn).wait()
    for step in range(3):
        for up in (True, False):

            @pl.when(sends(up, step))
            def _():
                for copy in climb(up, step):
                    copy.wait_send()

    over.wait()


def enter_rows(rows, mine, shard, collective_id):
    hbm = pl.BlockSpec(memory_space=pl.ANY)
    like = jax.ShapeDtypeStruct(rows.shape, rows.dtype)
    outs = [like, like, like, jax.ShapeDtypeStruct((4, 2) + mine.shape, mine.dtype)]
    given = [rows, mine]
    if shard is not None:
        outs.append(jax.ShapeDtypeStruct((4,) + shard.shape, shard.dtype))
        given.append(shard)
    sems = pltpu.SemaphoreType.DMA
    one, two, far, full, *planes = pl.pallas_call(
        functools.partial(enter_kernel, shard is not None),
        out_shape=tuple(outs),
        in_specs=[hbm] * len(given),
        out_specs=(hbm,) * len(outs),
        scratch_shapes=[sems((3, 4)), sems((3, 4)), sems((2, 3, 2)), sems((2, 3, 2)), sems((2,)), sems((2,))],
        compiler_params=pltpu.CompilerParams(collective_id=collective_id, has_side_effects=True),
        cost_estimate=pl.CostEstimate(flops=0, bytes_accessed=150 << 20, transcendentals=0),
    )(*given)
    return [rows, one, two, far], full.reshape(8 * mine.shape[0], mine.shape[1]), planes


def _norm_pull(grad_unit, unit, scale):
    inner = jnp.mean(grad_unit, axis=-1, keepdims=True)
    cross = jnp.mean(grad_unit * unit, axis=-1, keepdims=True)
    return scale * (grad_unit - inner - unit * cross)


def _qkv_grad(grad_ref, x_refs, total, low, come, send_sem, recv_sem):
    rows = x_refs[0].shape[0]
    for step, x_ref in enumerate(x_refs):
        part = lax.dot_general(
            x_ref[...], grad_ref[step * rows : (step + 1) * rows, :], TN, preferred_element_type=f32
        )
        if step:
            total[...] += part
        else:
            total[...] = part
    low[...] = total[...].astype(bf16).reshape(low.shape)
    core = lax.rem(lax.axis_index("tok"), 2)
    swap_core = _send(low.at[:, 1 - core], come, send_sem, recv_sem, _sibling())
    swap_core.start()
    return swap_core


def rows_out_kernel(
    grad_ref,
    weight_ref,
    hidden_ref,
    after_ref,
    gain_ref,
    x0_ref,
    x1_ref,
    x2_ref,
    x3_ref,
    out_ref,
    sums_ref,
    mine_ref,
    away,
    come,
    q_acc,
    q_all,
    q_come,
    send_sem,
    recv_sem,
    q_sem,
):
    one_way, two_way = _mate(1), _mate(2)
    _greet([one_way, two_way, _sibling()])
    rows = hidden_ref.shape[0]
    half = rows // 2

    def term(step, low):
        here = pl.ds(step * rows + (0 if low else half), half)
        return lax.dot_general(grad_ref[here, :], weight_ref[...], NT, preferred_element_type=f32)

    def move(slot, device):
        return _send(away.at[slot], come.at[slot], send_sem.at[slot], recv_sem.at[slot], device)

    ways = (one_way, two_way, one_way, two_way, two_way, one_way)
    for slot, (step, low) in enumerate(((3, True), (3, False), (1, True), (2, False))):
        away[slot] = term(step, low).astype(bf16)
        move(slot, ways[slot]).start()
    pass_low = term(2, True)
    pass_top = term(1, False)
    core = lax.rem(lax.axis_index("tok"), 2)
    swap_core = _qkv_grad(grad_ref, (x0_ref, x1_ref, x2_ref, x3_ref), q_acc, q_all, q_come, q_sem.at[0], q_sem.at[1])
    move(0, ways[0]).wait_recv()
    away[4] = (pass_low + come[0].astype(f32)).astype(bf16)
    move(4, ways[4]).start()
    move(1, ways[1]).wait_recv()
    away[5] = (pass_top + come[1].astype(f32)).astype(bf16)
    move(5, ways[5]).start()
    sums_ref[...] = jnp.zeros_like(sums_ref)
    for low in (True, False):
        here = pl.ds(0 if low else half, half)
        own = term(0, low)
        unit, scale = _norm(hidden_ref[here, :])
        near, far = (2, 4) if low else (3, 5)
        move(near, ways[near]).wait_recv()
        move(far, ways[far]).wait_recv()
        grad = own + come[near].astype(f32) + come[far].astype(f32)
        sums_ref[0:1, :] += jnp.sum(grad * unit, axis=0, keepdims=True)
        sums_ref[1:2, :] += jnp.sum(grad, axis=0, keepdims=True)
        out_ref[here, :] = after_ref[here, :] + _norm_pull(grad * gain_ref[0:1, :], unit, scale)
    swap_core.wait()
    mine_ref[...] = (q_all[:, core].astype(f32) + q_come[...].astype(f32)).astype(bf16)
    for slot in range(6):
        move(slot, ways[slot]).wait_send()


def rows_out(grad, weight, hidden, after, gain, pieces, collective_id):
    rows, width = hidden.shape[0], grad.shape[1]
    vmem = pl.BlockSpec(memory_space=pltpu.VMEM)
    buffer = pltpu.VMEM((6, rows // 2, D), bf16)
    sems = pltpu.SemaphoreType.DMA((6,))
    return pl.pallas_call(
        rows_out_kernel,
        out_shape=(
            jax.ShapeDtypeStruct((rows, D), f32),
            jax.ShapeDtypeStruct((8, D), f32),
            jax.ShapeDtypeStruct((4, D // 8, width), bf16),
        ),
        in_specs=[vmem] * 9,
        out_specs=(vmem, vmem, vmem),
        scratch_shapes=[
            buffer,
            buffer,
            pltpu.VMEM((D, width), f32),
            pltpu.VMEM((4, 2, D // 8, width), bf16),
            pltpu.VMEM((4, D // 8, width), bf16),
            sems,
            sems,
            pltpu.SemaphoreType.DMA((2,)),
        ],
        compiler_params=pltpu.CompilerParams(
            collective_id=collective_id, has_side_effects=True, vmem_limit_bytes=VMEM_BYTES
        ),
        cost_estimate=pl.CostEstimate(flops=0, bytes_accessed=150 << 20, transcendentals=0),
    )(grad, weight, hidden, after, gain, *pieces)


def post_forward_kernel(n_head, places, last, remote, *refs):
    count = len(places)
    att_ref, refs = refs[0], refs[1:]
    hidden_ref, rows_ref, up_bias_ref, refs = refs[0], refs[1], refs[2], refs[3:]
    given = 3 if remote else count
    weight_refs, refs = refs[:given], refs[given:]
    next_ref, normed_ref, down_ref, act_ref, slope_ref, branch_hbm, after_hbm, two_hbm, att_hbm, refs = *refs[:9], refs[9:]
    if remote:
        (own, one, two), (far_low, far_top), refs = weight_refs, refs[:2], refs[2:]
        side_own, side_one, side_two, side_low, side_top, refs = *refs[:5], refs[5:]
        weight_refs = (own, side_own, one, side_one, two, side_two, far_low, side_low, far_top, side_top)
    proj_s, up_s, down_s, att_s, branch_s, after_s, two_s, acc, proj_sem, up_sem, down_sem, out_sem, send_sem, recv_sem, refs = (
        *refs[:14],
        refs[14:],
    )
    at = pl.program_id(0)
    chunks = pl.num_programs(0)
    if remote:
        relay_send, relay_recv, side_send, side_recv = refs
        groups = WIDE // D
        order = [0] + [first for pair in zip(range(1, 1 + groups // 2), range(1 + groups // 2, groups)) for first in pair]

        def relay(group):
            part = lambda ref: _cols(ref, group * D, D)
            return [
                _send(
                    part(one.at[pl.ds(0, 2)]),
                    part(far_low),
                    relay_send.at[0, group],
                    relay_recv.at[0, group],
                    _mate(2),
                ),
                _send(
                    part(two.at[pl.ds(2, 2)]),
                    part(far_top),
                    relay_send.at[1, group],
                    relay_recv.at[1, group],
                    _mate(1),
                ),
            ]

        def across(group, pairs, first):
            return [
                _send(
                    _cols(source, group * D, D),
                    _cols(target, group * D, D),
                    side_send.at[first + index, group],
                    side_recv.at[first + index, group],
                    _sibling(),
                )
                for index, (source, target) in enumerate(pairs)
            ]

        near = lambda group: across(group, ((own, side_own), (one, side_one), (two, side_two)), 0)
        far = lambda group: across(group, ((far_low, side_low), (far_top, side_top)), 3)

        def advance(group):
            for copy in relay(group):
                copy.wait_recv()
            _start(far(group))

        def complete(group):
            for copy in near(group) + far(group):
                copy.wait_recv()

    def fetch(chunk, slot):
        up_at, down_at = UP_AT + chunk * CHUNK, DOWN_AT + chunk * CHUNK
        return _copies(weight_refs, places, up_s.at[slot], up_at, CHUNK, up_sem.at[slot], True) + _copies(
            weight_refs, places, down_s.at[slot], down_at, CHUNK, down_sem.at[slot], True
        )

    leaving = [
        pltpu.make_async_copy(branch_s, branch_hbm, out_sem.at[0]),
        pltpu.make_async_copy(after_s, after_hbm, out_sem.at[1]),
        pltpu.make_async_copy(two_s, two_hbm, out_sem.at[2]),
        pltpu.make_async_copy(att_s, att_hbm, out_sem.at[3]),
    ]

    @pl.when(at == 0)
    def _():
        proj = _copies(weight_refs, places, proj_s, PROJ_AT, D, proj_sem, True)
        if remote:
            width, rows = D // n_head, hidden_ref.shape[0]
            _greet([_mate(step) for step in range(1, n_head)] + [_sibling()])
            mine = att_s.at[:, pl.ds(_own_column(0, n_head), width)]
            moves = [
                _send(
                    att_ref.at[pl.ds(step * rows, rows)], mine, send_sem.at[step], recv_sem.at[step], _mate(step)
                )
                for step in range(1, n_head)
            ]
            moves.append(pltpu.make_async_copy(att_ref.at[pl.ds(0, rows)], mine, send_sem.at[0]))
            _start(moves)
            for group in order:
                _start(relay(group))
                _start(near(group))
            advance(order[0])
            _wait(moves)
            complete(order[0])
            _start(proj)
            for group in order[1:3]:
                advance(group)
        else:
            _start(proj)
            _start(fetch(0, 0))
            att_s[...] = att_ref[...]
        _wait(proj)
        branch = (
            lax.dot_general(att_s[...], _flat(proj_s[...]), NT, preferred_element_type=f32) + rows_ref[0:1, :]
        )
        branch_s[...] = branch
        after = hidden_ref[...] + rows_ref[1:2, :] * branch
        after_s[...] = after
        unit, _s = _norm(after)
        two_s[...] = (unit * rows_ref[2:3, :] + rows_ref[3:4, :]).astype(bf16)
        _start(leaving)
        if remote:
            for group in order[1:3]:
                complete(group)
            _start(fetch(0, 0))

    if remote:
        later = at // 2 + 2
        halves = groups // 2

        @pl.when((lax.rem(at, 2) == 0) & (later <= halves))
        def _():
            advance(later)
            advance(later + halves)

        @pl.when((lax.rem(at, 2) == 1) & (later <= halves))
        def _():
            complete(later)
            complete(later + halves)

    @pl.when(at + 1 < chunks)
    def _():
        _start(fetch(at + 1, lax.rem(at + 1, 2)))

    slot = lax.rem(at, 2)
    _wait(fetch(at, slot))
    expand = jnp.dot(two_s[...], _flat(up_s[slot]), preferred_element_type=f32) + up_bias_ref[...]
    cdf = 0.5 * (1.0 + lax.erf(expand * math.sqrt(0.5)))
    slope = cdf + expand * jnp.exp(-0.5 * expand * expand) * (1.0 / math.sqrt(2.0 * math.pi))
    act = (expand * cdf).astype(bf16)
    act_ref[...] = act
    slope_ref[...] = slope.astype(bf16)
    part = lax.dot_general(act, _flat(down_s[slot]), NT, preferred_element_type=f32)

    @pl.when(at == 0)
    def _():
        acc[...] = part

    @pl.when(at > 0)
    def _():
        acc[...] += part

    @pl.when(at == chunks - 1)
    def _():
        down = acc[...] + rows_ref[4:5, :]
        down_ref[...] = down
        hidden = after_s[...] + rows_ref[5:6, :] * down
        next_ref[...] = hidden
        if last:
            normed_ref[...] = jnp.zeros_like(normed_ref)
        else:
            unit, _s = _norm(hidden)
            normed_ref[...] = (unit * rows_ref[6:7, :] + rows_ref[7:8, :]).astype(bf16)
        _wait(leaving)
        if remote:
            for group in range(groups):
                for copy in relay(group) + near(group) + far(group):
                    copy.wait_send()


def _params(remote, collective_id):
    if not remote:
        return pltpu.CompilerParams(dimension_semantics=("arbitrary",), vmem_limit_bytes=VMEM_BYTES)
    return pltpu.CompilerParams(
        dimension_semantics=("arbitrary",),
        vmem_limit_bytes=VMEM_BYTES,
        collective_id=collective_id,
        has_side_effects=True,
    )


def post_forward(att, hidden, rows, up_bias, gathered, n_head, last, remote, collective_id):
    own_rows = hidden.shape[0]
    pieces, places = gathered
    count = len(places)
    unit_rows = D // 32
    vmem = pl.BlockSpec(memory_space=pltpu.VMEM)
    hbm = pl.BlockSpec(memory_space=pl.ANY)
    column = pl.BlockSpec((own_rows, CHUNK), lambda at: (0, at))
    fixed = lambda leaf_rows: pl.BlockSpec((leaf_rows, D), lambda at: (0, 0))
    whole = lambda dtype: jax.ShapeDtypeStruct((own_rows, D), dtype)
    wide = jax.ShapeDtypeStruct((own_rows, FF), bf16)
    weight = lambda *lead: pltpu.VMEM(lead + (4, 2, 4, unit_rows), bf16)
    normed_rows = 16 if last else own_rows
    landed, sems = [], []
    if remote:
        half, full = [
            jax.ShapeDtypeStruct((planes,) + pieces[0].shape[1:], bf16) for planes in (2, 4)
        ]
        landed = [half, half, full, full, full, half, half]
        for kinds in (2, 2, 5, 5):
            sems.append(pltpu.SemaphoreType.DMA((kinds, WIDE // D)))
    outs = pl.pallas_call(
        functools.partial(post_forward_kernel, n_head, places, last, remote),
        grid=(FF // CHUNK,),
        out_shape=(
            whole(f32),
            jax.ShapeDtypeStruct((normed_rows, D), bf16),
            whole(f32),
            wide,
            wide,
            whole(f32),
            whole(f32),
            whole(bf16),
            whole(bf16),
            *landed,
        ),
        in_specs=[hbm if remote else vmem, vmem, vmem, pl.BlockSpec((1, CHUNK), lambda at: (0, at))]
        + [hbm] * len(pieces),
        out_specs=(fixed(own_rows), fixed(normed_rows), fixed(own_rows), column, column)
        + (hbm,) * (4 + len(landed)),
        scratch_shapes=[
            pltpu.VMEM((4, 2, 4, unit_rows, D), bf16),
            pltpu.VMEM((2, 4, 2, 4, unit_rows, CHUNK), bf16),
            pltpu.VMEM((2, 4, 2, 4, unit_rows, CHUNK), bf16),
            pltpu.VMEM((own_rows, D), bf16),
            pltpu.VMEM((own_rows, D), f32),
            pltpu.VMEM((own_rows, D), f32),
            pltpu.VMEM((own_rows, D), bf16),
            pltpu.VMEM((own_rows, D), f32),
            pltpu.SemaphoreType.DMA((count,)),
            pltpu.SemaphoreType.DMA((2, count)),
            pltpu.SemaphoreType.DMA((2, count)),
            pltpu.SemaphoreType.DMA((4,)),
            pltpu.SemaphoreType.DMA((n_head,)),
            pltpu.SemaphoreType.DMA((n_head,)),
            *sems,
        ],
        compiler_params=_params(remote, collective_id),
        cost_estimate=pl.CostEstimate(
            flops=2 * own_rows * D * (D + 2 * FF),
            bytes_accessed=2 * D * (D + 2 * FF) + own_rows * (22 * D + 4 * FF),
            transcendentals=2 * own_rows * FF,
        ),
    )(att, hidden, rows, up_bias, *pieces)
    if remote:
        far_low, far_top, *sides = outs[9:]
        near = [*pieces, far_low, far_top]
        pieces = [piece for pair in zip(near, sides) for piece in pair]
    return list(outs[:9]), pieces


def post_backward_kernel(n_head, places, remote, *refs):
    count = len(places)
    far_places = [("head", 0, 4, 1, to) for to in range(4)] if remote else []
    out_count = 3 if remote else 1
    att_ref, grad_ref, down_ref, branch_ref, after_ref, two_ref, rows_ref, act_ref, slope_ref, refs = *refs[:9], refs[9:]
    weight_refs, refs = refs[:count], refs[count:]
    d_att_ref, d_after_ref, sums_ref, up_sum_ref, refs = *refs[:4], refs[4:]
    own_refs, refs = refs[:out_count], refs[out_count:]
    proj_s, up_s, down_s, d_proj_s, d_up_s, d_down_s, att_s, low_s, low_t, two_t, acc, refs = *refs[:11], refs[11:]
    proj_sem, up_sem, down_sem, own_sem, far_sem, got_sem, send_sem, recv_sem, refs = *refs[:8], refs[8:]
    if remote:
        stash, got = refs
        low_ref, top_ref, keep_ref = own_refs
    at = pl.program_id(0)
    chunks = pl.num_programs(0)
    width = D // n_head

    def fetch(chunk, slot):
        up_at, down_at = UP_AT + chunk * CHUNK, DOWN_AT + chunk * CHUNK
        return _copies(weight_refs, places, up_s.at[slot], up_at, CHUNK, up_sem.at[slot], True) + _copies(
            weight_refs, places, down_s.at[slot], down_at, CHUNK, down_sem.at[slot], True
        )

    def stay(whole, column, size, lane):
        return [] if remote else _copies(own_refs, [None], whole, column, size, own_sem.at[lane], False)

    def away(whole, column, size, lane, mark):
        return [
            _send(
                _slot(whole, place),
                _cols(got.at[to], column, size),
                far_sem.at[lane, to],
                got_sem.at[mark, to],
                _sibling(),
            )
            for to, place in enumerate(far_places)
        ]

    def over(chunk, slot):
        up_at, down_at = UP_AT + chunk * CHUNK, DOWN_AT + chunk * CHUNK
        return away(d_up_s.at[slot], up_at, CHUNK, slot, chunk) + away(
            d_down_s.at[slot], down_at, CHUNK, 2 + slot, chunks + chunk
        )

    def leave(chunk, slot):
        up_at, down_at = UP_AT + chunk * CHUNK, DOWN_AT + chunk * CHUNK
        local = stay(d_up_s.at[slot], up_at, CHUNK, slot) + stay(d_down_s.at[slot], down_at, CHUNK, 2 + slot)
        return local, over(chunk, slot)

    def left(pair):
        _wait(pair[0])
        for move in pair[1]:
            move.wait_send()

    def hold(staged, column, size):
        core, head = lax.rem(lax.axis_index("tok"), 2), lax.axis_index("head")
        for to in range(4):
            _cols(stash.at[to], column, size)[...] = staged[:, core, _paired(head, to, 2)]

    def add(column, size):
        mine, other = _cols(stash, column, size), _cols(got, column, size)
        for to in range(4):
            mine[to] = (mine[to].astype(f32) + other[to].astype(f32)).astype(bf16)

    def merge(chunk):
        for move in over(chunk, 0):
            move.wait_recv()
        add(UP_AT + chunk * CHUNK, CHUNK)
        add(DOWN_AT + chunk * CHUNK, CHUNK)

    def depart(column, size, lane):
        spots = (
            (low_ref, 0, 1, 0),
            (low_ref, 2, 3, 0),
            (top_ref, 0, 2, 2),
            (top_ref, 2, 3, 2),
            (keep_ref, 0, 0, 0),
            (keep_ref, 2, 2, 0),
            (keep_ref, 4, 0, 2),
            (keep_ref, 6, 1, 2),
        )
        return [
            pltpu.make_async_copy(
                _cols(stash.at[to, pl.ds(first, 2)], column, size),
                _cols(target.at[pl.ds(at_, 2)], column, size),
                own_sem.at[lane, index],
            )
            for index, (target, at_, to, first) in enumerate(spots)
        ]

    middle = FF // 2
    early = lambda: depart(UP_AT, middle, 0) + depart(DOWN_AT, middle, 1)

    proj = lambda: _copies(weight_refs, places, proj_s, PROJ_AT, D, proj_sem, True)

    @pl.when(at == 0)
    def _():
        if remote:
            _greet([_mate(step) for step in range(1, n_head)] + [_sibling()])
        _start(fetch(0, 0))
        _start(proj())
        grad = grad_ref[...]
        low = (rows_ref[2:3, :] * grad).astype(bf16)
        low_s[...] = low
        low_t[...] = jnp.transpose(low)
        two_t[...] = jnp.transpose(two_ref[...])
        sums_ref[...] = jnp.zeros_like(sums_ref)
        sums_ref[0:1, :] = jnp.sum(grad * down_ref[...], axis=0, keepdims=True)
        sums_ref[1:2, :] = jnp.sum(low.astype(f32), axis=0, keepdims=True)
        acc[...] = jnp.zeros_like(acc)

    @pl.when(at + 1 < chunks)
    def _():
        _start(fetch(at + 1, lax.rem(at + 1, 2)))

    slot = lax.rem(at, 2)
    _wait(fetch(at, slot))

    @pl.when(at >= 2)
    def _():
        left(leave(at - 2, slot))

    d_act = jnp.dot(low_s[...], _flat(down_s[slot]), preferred_element_type=f32)
    d_expand = (slope_ref[...].astype(f32) * d_act).astype(bf16)
    up_sum_ref[...] = jnp.sum(d_expand.astype(f32), axis=0, keepdims=True)
    acc[...] += lax.dot_general(d_expand, _flat(up_s[slot]), NT, preferred_element_type=f32)
    shape = d_up_s.shape[1:]
    d_up_s[slot] = jnp.dot(two_t[...], d_expand, preferred_element_type=f32).astype(bf16).reshape(shape)
    d_down_s[slot] = jnp.dot(low_t[...], act_ref[...], preferred_element_type=f32).astype(bf16).reshape(shape)
    for moves in leave(at, slot):
        _start(moves)
    if remote:
        hold(d_up_s.at[slot], UP_AT + at * CHUNK, CHUNK)
        hold(d_down_s.at[slot], DOWN_AT + at * CHUNK, CHUNK)

        @pl.when(at > 0)
        def _():
            merge(at - 1)

        @pl.when(at == chunks // 2)
        def _():
            _start(early())

    @pl.when(at == chunks - 1)
    def _():
        d_two = acc[...]
        unit, scale = _norm(after_ref[...])
        sums_ref[2:3, :] = jnp.sum(d_two * unit, axis=0, keepdims=True)
        sums_ref[3:4, :] = jnp.sum(d_two, axis=0, keepdims=True)
        d_unit = d_two * rows_ref[1:2, :]
        inner = jnp.mean(d_unit, axis=-1, keepdims=True)
        cross = jnp.mean(d_unit * unit, axis=-1, keepdims=True)
        d_after = grad_ref[...] + scale * (d_unit - inner - unit * cross)
        d_after_ref[...] = d_after
        sums_ref[4:5, :] = jnp.sum(d_after * branch_ref[...], axis=0, keepdims=True)
        d_branch = (rows_ref[0:1, :] * d_after).astype(bf16)
        sums_ref[5:6, :] = jnp.sum(d_branch.astype(f32), axis=0, keepdims=True)
        d_proj_s[...] = (
            lax.dot_general(d_branch, att_ref[...], TN, preferred_element_type=f32)
            .astype(bf16)
            .reshape(d_proj_s.shape)
        )
        gone = stay(d_proj_s, PROJ_AT, D, 4), away(d_proj_s, PROJ_AT, D, 4, 2 * chunks)
        for moves in gone:
            _start(moves)
        if remote:
            hold(d_proj_s, PROJ_AT, D)
        _wait(proj())
        d_att = jnp.dot(d_branch, _flat(proj_s[...]), preferred_element_type=f32).astype(bf16)
        if remote:
            rows = d_att.shape[0]
            att_s[...] = d_att
            moves = [
                _send(
                    att_s.at[:, pl.ds(_own_column(step, n_head), width)],
                    d_att_ref.at[pl.ds(step * rows, rows)],
                    send_sem.at[step],
                    recv_sem.at[step],
                    _mate(step),
                )
                for step in range(1, n_head)
            ]
            own = att_s.at[:, pl.ds(_own_column(0, n_head), width)]
            moves.append(pltpu.make_async_copy(own, d_att_ref.at[pl.ds(0, rows)], send_sem.at[0]))
            _start(moves)
        else:
            d_att_ref[...] = d_att
        left(leave(at - 1, 1 - slot))
        left(leave(at, slot))
        left(gone)
        if remote:
            merge(at)
            for move in gone[1]:
                move.wait_recv()
            add(PROJ_AT, D)
            late = (
                depart(UP_AT + middle, middle, 2) + depart(DOWN_AT + middle, middle, 3) + depart(PROJ_AT, D, 4)
            )
            _start(late)
            _wait(early())
            _wait(late)
            _wait(moves)


def post_backward(att, grad, down_out, branch, after, two, rows, act, slope, gathered, n_head, remote, collective_id):
    own_rows = grad.shape[0]
    pieces, places = gathered
    count = len(places)
    unit_rows = D // 32
    vmem = pl.BlockSpec(memory_space=pltpu.VMEM)
    hbm = pl.BlockSpec(memory_space=pl.ANY)
    column = pl.BlockSpec((own_rows, CHUNK), lambda at: (0, at))
    fixed = lambda *shape: pl.BlockSpec(shape, lambda at: (0, 0))
    width = D // n_head
    chunks = FF // CHUNK
    if remote:
        d_att_shape, d_att_spec = (n_head * own_rows, width), hbm
        grads = [jax.ShapeDtypeStruct((planes, unit_rows, WIDE), bf16) for planes in (4, 4, 8)]
        stashes = [pltpu.VMEM((4, 4, unit_rows, WIDE), bf16)] * 2
    else:
        d_att_shape, d_att_spec = (own_rows, D), fixed(own_rows, D)
        grads = [jax.ShapeDtypeStruct((4, 2, 4, unit_rows, WIDE), bf16)]
        stashes = []
    sems = pltpu.SemaphoreType.DMA
    outs = pl.pallas_call(
        functools.partial(post_backward_kernel, n_head, places, remote),
        grid=(chunks,),
        out_shape=tuple(
            [
                jax.ShapeDtypeStruct(d_att_shape, bf16),
                jax.ShapeDtypeStruct((own_rows, D), f32),
                jax.ShapeDtypeStruct((8, D), f32),
                jax.ShapeDtypeStruct((1, FF), f32),
            ]
            + grads
        ),
        in_specs=[vmem] * 7 + [column, column] + [hbm] * count,
        out_specs=tuple(
            [d_att_spec, fixed(own_rows, D), fixed(8, D), pl.BlockSpec((1, CHUNK), lambda at: (0, at))]
            + [hbm] * len(grads)
        ),
        scratch_shapes=[
            pltpu.VMEM((4, 2, 4, unit_rows, D), bf16),
            pltpu.VMEM((2, 4, 2, 4, unit_rows, CHUNK), bf16),
            pltpu.VMEM((2, 4, 2, 4, unit_rows, CHUNK), bf16),
            pltpu.VMEM((4, 2, 4, unit_rows, D), bf16),
            pltpu.VMEM((2, 4, 2, 4, unit_rows, CHUNK), bf16),
            pltpu.VMEM((2, 4, 2, 4, unit_rows, CHUNK), bf16),
            pltpu.VMEM((own_rows, D), bf16),
            pltpu.VMEM((own_rows, D), bf16),
            pltpu.VMEM((D, own_rows), bf16),
            pltpu.VMEM((D, own_rows), bf16),
            pltpu.VMEM((own_rows, D), f32),
            sems((count,)),
            sems((2, count)),
            sems((2, count)),
            sems((5, 8)),
            sems((5, 4)),
            sems((2 * chunks + 1, 4)),
            sems((n_head,)),
            sems((n_head,)),
            *stashes,
        ],
        compiler_params=_params(remote, collective_id),
        cost_estimate=pl.CostEstimate(
            flops=4 * own_rows * D * (D + 2 * FF),
            bytes_accessed=4 * D * (D + 2 * FF) + own_rows * (22 * D + 4 * FF),
            transcendentals=0,
        ),
    )(att, grad, down_out, branch, after, two, rows, act, slope, *pieces)
    d_att, d_after, sums, up_sum, grads = *outs[:4], list(outs[4:])
    return d_att, d_after, sums, up_sum, grads


FINISH_CUTS = 3


def finish_kernel(
    n_tok,
    n_head,
    grad_ref,
    weight_ref,
    hidden_ref,
    after_ref,
    gain_ref,
    x0_ref,
    x1_ref,
    x2_ref,
    x3_ref,
    keep_ref,
    low_ref,
    top_ref,
    tiles_ref,
    one_ref,
    square_ref,
    out_ref,
    sums_ref,
    rest_ref,
    qkv_ref,
    qkv_one_ref,
    vec_ref,
    all_ref,
    own_s,
    pass_s,
    tile_s,
    away,
    come,
    come_rest,
    away_z,
    come_z,
    q_acc,
    q_all,
    q_come,
    q_mine,
    q_z,
    q_sum,
    q_land,
    one_land,
    land,
    send_sem,
    recv_sem,
    rest_send,
    rest_recv,
    z_send,
    z_recv,
    q_send,
    q_recv,
    v_send,
    v_recv,
    n_send,
    n_recv,
):
    n = n_tok * n_head
    _enter(n_tok, n_head)
    tok = lax.axis_index("tok")
    head = lax.axis_index("head")
    me = tok * n_head + head
    zed, core = tok // 2, lax.rem(tok, 2)
    one_way, two_way = _mate(1), _mate(2)
    plane = lambda step: _paired(zed, step, 2)
    over = lambda step: (plane(step) * 2 + core, head)

    def tile(step):
        _, to, device = _peer(step, n_tok, n_head)
        return _send(tiles_ref.at[to], land.at[step], v_send.at[step], v_recv.at[step], device)

    def tile_start(step, _):
        tile(step).start()
        return 0

    def tile_wait(step, _):
        tile(step).wait()
        return 0

    lax.fori_loop(1, n, tile_start, 0)
    mate_at = lambda step: _paired(head, step, 2)

    def go_home(source, target, first):
        return [
            _send(
                source.at[mate_at(step)],
                target.at[head],
                q_send.at[first + step],
                q_recv.at[first + step],
                _mate(step),
            )
            for step in range(1, 4)
        ]

    one_home = go_home(one_ref, one_land, 6)
    _start(one_home)
    wide = keep_ref.shape[2] // FINISH_CUTS
    two_sum = lambda first, second: (first.astype(f32) + second.astype(f32)).astype(bf16)
    pass_s[0:2] = two_sum(keep_ref[2:4], low_ref[2:4])
    pass_s[2:4] = two_sum(keep_ref[6:8], top_ref[2:4])

    def rest(low, at):
        part = pl.ds(0 if low else 2, 2)
        lanes = pl.ds(at * wide, wide)
        side = 0 if low else 1
        return _send(
            pass_s.at[part, :, lanes],
            come_rest.at[part, :, lanes],
            rest_send.at[side, at],
            rest_recv.at[side, at],
            two_way if low else one_way,
        )

    for at in range(FINISH_CUTS):
        rest(True, at).start()
        rest(False, at).start()
    rows = hidden_ref.shape[0]
    half = rows // 2

    def term(step, low):
        here = pl.ds(step * rows + (0 if low else half), half)
        return lax.dot_general(grad_ref[here, :], weight_ref[...], NT, preferred_element_type=f32)

    def move(slot):
        return _send(away.at[slot], come.at[slot], send_sem.at[slot], recv_sem.at[slot], ways[slot])

    ways = (one_way, two_way, one_way, two_way, two_way, one_way)
    for slot, (step, low) in enumerate(((3, True), (3, False), (1, True), (2, False))):
        away[slot] = term(step, low).astype(bf16)
        move(slot).start()
    own_s[0:2] = two_sum(keep_ref[0:2], low_ref[0:2])
    own_s[2:4] = two_sum(keep_ref[4:6], top_ref[0:2])

    def cross(step, at):
        lanes = pl.ds(at * wide, wide)
        return _send(
            away_z.at[step - 1, :, lanes],
            come_z.at[step - 1, :, lanes],
            z_send.at[step - 1, at],
            z_recv.at[step - 1, at],
            over(step),
        )

    def rest_on(at):
        rest(True, at).wait_recv()
        rest(False, at).wait_recv()
        lanes = pl.ds(at * wide, wide)
        for step in range(4):
            total = own_s[plane(step), :, lanes].astype(f32) + come_rest[plane(step), :, lanes].astype(f32)
            if step:
                away_z[step - 1, :, lanes] = total.astype(bf16)
                cross(step, at).start()
            else:
                rest_ref[:, lanes] = total

    rest_on(0)
    swap_core = _qkv_grad(
        grad_ref, (x0_ref, x1_ref, x2_ref, x3_ref), q_acc, q_all, q_come, q_send.at[0], q_recv.at[0]
    )
    rest_on(1)
    swap_core.wait_recv()
    q_mine[...] = (q_all[:, core].astype(f32) + q_come[...].astype(f32)).astype(bf16)
    q_cross = [
        _send(q_mine.at[plane(step)], q_z.at[step - 1], q_send.at[step], q_recv.at[step], over(step))
        for step in range(1, 4)
    ]
    _start(q_cross)
    rest_on(2)
    pass_low = term(2, True)
    pass_top = term(1, False)
    move(0).wait_recv()
    away[4] = (pass_low + come[0].astype(f32)).astype(bf16)
    move(4).start()
    move(1).wait_recv()
    away[5] = (pass_top + come[1].astype(f32)).astype(bf16)
    move(5).start()
    sums_ref[...] = jnp.zeros_like(sums_ref)
    for low in (True, False):
        here = pl.ds(0 if low else half, half)
        own = term(0, low)
        unit, scale = _norm(hidden_ref[here, :])
        near, far = (2, 4) if low else (3, 5)
        move(near).wait_recv()
        move(far).wait_recv()
        grad = own + come[near].astype(f32) + come[far].astype(f32)
        sums_ref[0:1, :] += jnp.sum(grad * unit, axis=0, keepdims=True)
        sums_ref[1:2, :] += jnp.sum(grad, axis=0, keepdims=True)
        out_ref[here, :] = after_ref[here, :] + _norm_pull(grad * gain_ref[0:1, :], unit, scale)
    for copy in q_cross:
        copy.wait_recv()
    total = q_mine[zed].astype(f32)
    for step in range(3):
        total = total + q_z[step].astype(f32)
    q_sum[...] = total.astype(bf16).reshape(q_sum.shape)
    q_home = go_home(q_sum, q_land, 3)
    _start(q_home)

    def settle(target, at, values):
        width = values.shape[1] // 3
        for part in range(3):
            lanes = pl.ds(pl.multiple_of(part * D + at * width, 128), width)
            target[:, lanes] = values[:, part * width : (part + 1) * width].astype(f32)

    settle(qkv_ref, head, q_sum[head])
    settle(qkv_one_ref, head, one_ref[head])
    for step, copy in enumerate(one_home):
        copy.wait_recv()
        settle(qkv_one_ref, mate_at(step + 1), one_land[mate_at(step + 1)])
    for at in range(FINISH_CUTS):
        lanes = pl.ds(at * wide, wide)
        for step in range(1, 4):
            cross(step, at).wait_recv()
            rest_ref[:, lanes] += come_z[step - 1, :, lanes].astype(f32)
    for step, copy in enumerate(q_home):
        copy.wait_recv()
        settle(qkv_ref, mate_at(step + 1), q_land[mate_at(step + 1)])
    lax.fori_loop(1, n, tile_wait, 0)
    vec_ref[...] = tiles_ref[me] + jnp.sum(land[1:], axis=0)
    square = square_ref[0:1, 0:1]
    for ref in (rest_ref, vec_ref, qkv_ref, qkv_one_ref):
        square = square + jnp.sum(ref[...] * ref[...], keepdims=True)
    tile_s[0:8, :] = jnp.broadcast_to(square, (8, 128))
    for at in range(16):
        first = at % 8 * 128
        tile_s[8 + at : 9 + at, :] = sums_ref[at // 8 : at // 8 + 1, first : first + 128]
    all_ref[me] = tile_s[...]

    def norm_tile(step):
        _, _, device = _peer(step, n_tok, n_head)
        return _send(tile_s, all_ref.at[me], n_send.at[step], n_recv.at[step], device)

    def norm_start(step, _):
        norm_tile(step).start()
        return 0

    def norm_wait(step, _):
        norm_tile(step).wait()
        return 0

    lax.fori_loop(1, n, norm_start, 0)
    lax.fori_loop(1, n, norm_wait, 0)
    for copy in [swap_core] + q_cross + q_home + one_home:
        copy.wait_send()
    for slot in range(6):
        move(slot).wait_send()
    for at in range(FINISH_CUTS):
        rest(True, at).wait_send()
        rest(False, at).wait_send()
        for step in range(1, 4):
            cross(step, at).wait_send()


def finish(grad, weight, hidden, after, gain, pieces, parts, tiles, mine_one, square, n_tok, n_head, collective_id):
    rows = hidden.shape[0]
    n = n_tok * n_head
    unit_rows, width = D // n, grad.shape[1]
    vmem = pl.BlockSpec(memory_space=pltpu.VMEM)
    hbm = pl.BlockSpec(memory_space=pl.ANY)
    sems = pltpu.SemaphoreType.DMA
    buffer = pltpu.VMEM((6, rows // 2, D), bf16)
    tok_rows = unit_rows * n_head
    low = lambda *shape: pltpu.VMEM(shape, bf16)
    return pl.pallas_call(
        functools.partial(finish_kernel, n_tok, n_head),
        out_shape=(
            jax.ShapeDtypeStruct((rows, D), f32),
            jax.ShapeDtypeStruct((8, D), f32),
            jax.ShapeDtypeStruct((unit_rows, WIDE), f32),
            jax.ShapeDtypeStruct((unit_rows, 3 * D), f32),
            jax.ShapeDtypeStruct((unit_rows, 3 * D), f32),
            jax.ShapeDtypeStruct(tiles.shape[1:], f32),
            jax.ShapeDtypeStruct((n, 24, 128), f32),
        ),
        in_specs=[vmem] * 15,
        out_specs=(vmem,) * 7,
        scratch_shapes=[
            low(4, unit_rows, WIDE),
            low(4, unit_rows, WIDE),
            pltpu.VMEM((24, 128), f32),
            buffer,
            buffer,
            low(4, unit_rows, WIDE),
            low(3, unit_rows, WIDE),
            low(3, unit_rows, WIDE),
            pltpu.VMEM((D, width), f32),
            low(4, 2, tok_rows, width),
            low(4, tok_rows, width),
            low(4, tok_rows, width),
            low(3, tok_rows, width),
            low(n_head, unit_rows, width),
            low(n_head, unit_rows, width),
            low(n_head, unit_rows, width),
            pltpu.VMEM(tiles.shape, f32),
            sems((6,)),
            sems((6,)),
            sems((2, FINISH_CUTS)),
            sems((2, FINISH_CUTS)),
            sems((3, FINISH_CUTS)),
            sems((3, FINISH_CUTS)),
            sems((10,)),
            sems((10,)),
            sems((n,)),
            sems((n,)),
            sems((n,)),
            sems((n,)),
        ],
        compiler_params=pltpu.CompilerParams(
            collective_id=collective_id, has_side_effects=True, vmem_limit_bytes=VMEM_BYTES
        ),
        cost_estimate=pl.CostEstimate(flops=0, bytes_accessed=250 << 20, transcendentals=0),
    )(grad, weight, hidden, after, gain, *pieces, *parts, tiles, mine_one.reshape(n_head, unit_rows, width), square)


def pack_kernel(n_head, *refs):
    out_ref, refs = refs[-1], refs[:-1]
    own = lax.axis_index("head")
    out_ref[...] = jnp.zeros_like(out_ref)
    for block in range(2):
        norm_ref, sums_ref, up_ref, head_ref, bias_ref = refs[5 * block : 5 * block + 5]
        width = head_ref.shape[1]
        per = width // 128

        def lay(first, ref, row, count, start=0):
            for at in range(count):
                lanes = slice(start + at * 128, start + (at + 1) * 128)
                out_ref[block, pl.ds(first + at, 1), :] = ref[row : row + 1, lanes]

        count = D // 128
        lay(0, norm_ref, 0, count)
        lay(count, norm_ref, 1, count)
        for part in range(3):
            lay(2 * count + part * count + own * per, bias_ref, 0, per, part * width)
        for at, row in ((5, 5), (6, 4), (7, 2), (8, 3)):
            lay(at * count, sums_ref, row, count)
        lay(9 * count, up_ref, 0, FF // 128)
        tail = 9 * count + FF // 128
        lay(tail, sums_ref, 1, count)
        lay(tail + count, sums_ref, 0, count)
        folded = head_ref[0:4, 0:128]
        for at in range(1, per):
            folded = folded + head_ref[0:4, at * 128 : (at + 1) * 128]
        folded = folded + jnp.concatenate([folded[:, HD:], folded[:, :HD]], axis=1)
        lane = lax.broadcasted_iota(jnp.int32, (1, 128), 1)
        for at in range(2):
            pair = jnp.where(lane < HD, folded[2 * at : 2 * at + 1], folded[2 * at + 1 : 2 * at + 2])
            out_ref[block, pl.ds(tail + 2 * count + at, 1), :] = pair


def pack(parts, n_head):
    vmem = pl.BlockSpec(memory_space=pltpu.VMEM)
    return pl.pallas_call(
        functools.partial(pack_kernel, n_head),
        out_shape=jax.ShapeDtypeStruct((2, (11 * D + FF + 4 * HD) // 128, 128), f32),
        in_specs=[vmem] * 10,
        out_specs=vmem,
    )(*parts)


def layer_norm(values, gain, shift):
    centered = values - jnp.mean(values, axis=-1, keepdims=True)
    spread_ = jnp.mean(centered * centered, axis=-1, keepdims=True)
    return centered * lax.rsqrt(spread_ + norm_eps) * gain + shift


def unpack(vector_row):
    lengths = (D, D, 3 * D, D, D, D, D, FF, D, D, HD, HD, HD, HD)
    pieces = []
    offset = 0
    for length in lengths:
        pieces.append(vector_row[offset : offset + length])
        offset = offset + length
    return pieces


def head_gains(vec, heads):
    rows = [jnp.tile(piece, heads) for piece in vec[10:14]]
    return jnp.concatenate([jnp.stack(rows), jnp.zeros((4, heads * HD), f32)], axis=0)


def adam_update(
    weight, gradient, moment_one, moment_two, average, step_rate, decay_rate, clip_scale, fix_one, fix_two
):
    clipped = gradient * clip_scale
    moment_one = beta_one * moment_one + (1.0 - beta_one) * clipped
    moment_two = beta_two * moment_two + (1.0 - beta_two) * clipped * clipped
    first_hat = moment_one / fix_one
    second_hat = moment_two / fix_two
    weight = weight - step_rate * (
        first_hat / (jnp.sqrt(second_hat) + adam_eps) + decay_rate * weight
    )
    average = ema_decay * average + (1.0 - ema_decay) * weight
    return (weight, moment_one, moment_two, average)


def body(
    links,
    tokens,
    cotangent,
    slot_frame,
    step_count,
    *params,
):
    n_tok, n_head = links.n_tok, links.n_head
    devices = n_tok * n_head
    own = lax.axis_index("head")
    flip = lambda leaf: jnp.swapaxes(leaf, 1, 2)
    groups = []
    for at in range(0, 20, 5):
        qkv, proj, fc1, fc2, vec = params[at : at + 5]
        groups.append([qkv, flip(proj), fc1, flip(fc2), vec])
    masters = groups[0]

    slots = slot_frame.shape[0]
    per_head = slots // n_head
    held = slot_frame.reshape(n_head, per_head)
    held = jnp.concatenate(
        [lax.dynamic_slice_in_dim(held, own ^ step, 1, 0)[0] for step in range(n_head)]
    )
    index = jnp.arange(slots, dtype=jnp.int32)
    ahead = (held[None, :] < held[:, None]) | (
        (held[None, :] == held[:, None]) & (index[None, :] < index[:, None])
    )
    rank = jnp.sum(ahead.astype(jnp.int32), axis=1)
    order = jnp.sum(jnp.where(rank[None, :] == index[:, None], index[None, :], 0), axis=1).astype(jnp.int32)
    is_hi = (jnp.sum((held == held[0]).astype(jnp.int32)) == HI_BLOCKS).astype(jnp.int32).reshape(1)
    spans = (
        (HI_BLOCKS * BLOCK, LO_BLOCKS * BLOCK),
        (FRAMES * HI_BLOCKS * BLOCK, FRAMES * LO_BLOCKS * BLOCK),
    )

    vec_here = masters[4].shape[1]
    tile = lax.reduce_precision(masters[4], 8, 7).reshape(-1)
    tile = jnp.pad(tile, (0, 1024 - tile.shape[0])).reshape(8, 128)
    tiles = spread(tile, n_tok, n_head, 0).reshape(devices, 1024)[:, : 2 * vec_here]
    vectors = jnp.swapaxes(tiles.reshape(devices, 2, vec_here), 0, 1).reshape(2, devices * vec_here)
    vecs = [unpack(vectors[block]) for block in range(2)]

    qkv_low = [masters[0][block].astype(bf16) for block in range(2)]
    low = [
        jnp.concatenate([masters[kind][block].astype(bf16) for kind in (1, 2, 3)], axis=1)
        for block in range(2)
    ]
    places = links.gather_places()
    paired = links.paired
    width = D // n_head
    heads = width // HD
    own_rows = tokens.shape[0]
    cut = lambda rows: [rows[step * own_rows : (step + 1) * own_rows] for step in range(n_head)]
    gains = [head_gains(vec, heads) for vec in vecs]

    def attend(block, pieces, qkv_cols):
        qkv_bias = lax.dynamic_slice_in_dim(vecs[block][2].reshape(3, D), own * width, width, 1)
        return attention_forward(
            pieces, qkv_cols, qkv_bias.reshape(1, 3 * width), gains[block], order, is_hi, spans[block]
        )

    def enter(rows, mine, shard, collective_id):
        if paired:
            return enter_rows(rows, mine, shard, collective_id)
        planes = None if shard is None else links.gather_planes(shard)
        return links.rows_in(rows), lax.all_gather(mine, "tok", axis=0, tiled=True), planes

    def post(block, attended, hidden, pieces):
        vec, tail = vecs[block], vecs[1]
        rows = jnp.stack([vec[3], vec[4], vec[5], vec[6], vec[8], vec[9], tail[0], tail[1]])
        if not paired:
            attended = jnp.concatenate(links.by_index(links.exchange(cut(attended)), own), axis=1)
        return post_forward(
            attended,
            hidden,
            rows,
            vec[7].reshape(1, FF),
            (pieces, places),
            n_head,
            block == 1,
            paired,
            3 + block,
        )

    hidden_in = [tokens.astype(f32), None]
    normed = layer_norm(hidden_in[0], vecs[0][0], vecs[0][1]).astype(bf16)
    group, qkv_cols, saved, att_owns, mids, weights = ([None, None] for _ in range(6))

    mine = links.fetch_heads(qkv_low, own)
    normed, mine, low[0] = together(normed, mine, low[0])
    group[0], qkv_cols[0], planes = enter(normed, mine[0], low[0], 5)
    group[0], planes, qkv_cols[0], low[1] = together(group[0], planes, qkv_cols[0], low[1])
    near = links.gather_sides(planes)
    saved[0] = attend(0, group[0], qkv_cols[0])
    saved[0], near, low[1] = together(saved[0], near, low[1])
    planes = links.gather_planes(low[1])
    (hidden_in[1], normed, *mids[0]), weights[0] = post(0, saved[0][0], hidden_in[0], near)
    normed, planes = together(normed, planes)

    group[1], qkv_cols[1], _planes = enter(normed, mine[1], None, 6)
    group[1], planes = together(group[1], planes)
    near = links.gather_sides(planes)
    saved[1] = attend(1, group[1], qkv_cols[1])
    saved[1], near = together(saved[1], near)
    (hidden, _normed, *mids[1]), weights[1] = post(1, saved[1][0], hidden_in[1], near)

    def post_back(block, grad):
        vec = vecs[block]
        down, act, slope, branch, after, two, att_own = mids[block]
        rows = jnp.stack([vec[4], vec[5], vec[9]] + [vec[9]] * 5)
        d_att, *rest = post_backward(
            att_own,
            grad,
            down,
            branch,
            after,
            two,
            rows,
            act,
            slope,
            (weights[block], places),
            n_head,
            paired,
            7 + block,
        )
        if not paired:
            parts = [
                lax.dynamic_slice_in_dim(d_att, (own ^ step) * width, width, 1) for step in range(n_head)
            ]
            d_att = jnp.concatenate(links.exchange(parts), axis=0)
        return d_att, *rest

    def attend_back(block, grad_heads):
        attended, raw, values, lse = saved[block]
        return attention_backward(
            raw, values, grad_heads, attended, lse, gains[block], order, is_hi, spans[block]
        )

    def rows_back(block, d_qkv, d_after):
        gain, shift = vecs[block][0], vecs[block][1]
        if paired:
            grad, sums, mine = rows_out(
                d_qkv, qkv_cols[block], hidden_in[block], d_after, gain.reshape(1, D), group[block], 9 + block
            )
            return grad, mine, sums
        d_normed = jnp.einsum("rc,dc->rd", d_qkv, qkv_cols[block], preferred_element_type=f32)
        back = links.rows_out(cut(d_normed.astype(bf16)))
        d_hidden, d_gain, d_shift = jax.vjp(layer_norm, hidden_in[block], gain, shift)[1](back)
        sums = jnp.concatenate([jnp.stack([d_gain, d_shift]), jnp.zeros((6, D), f32)], axis=0)
        return d_after + d_hidden, qkv_grad(block, d_qkv), sums

    def qkv_grad(block, d_qkv):
        rows = jnp.concatenate(group[block], axis=0)
        return jnp.einsum("rd,rc->dc", rows, d_qkv, preferred_element_type=f32).astype(bf16)

    d_att, d_after, sums, d_up_bias, grads = post_back(1, cotangent.astype(f32))
    grads = links.scatter_first(grads)
    d_qkv, head_sums, bias_sums = attend_back(1, d_att)
    d_qkv, head_sums, bias_sums, grads = together(d_qkv, head_sums, bias_sums, grads)
    grads = links.scatter_add(grads)
    grad_rows, dw_qkv, norm_sums = rows_back(1, d_qkv, d_after)
    parts_one = [norm_sums, sums, d_up_bias, head_sums, bias_sums]
    grad_rows, grads, dw_qkv = together(grad_rows, grads, dw_qkv)
    grads_one = links.scatter_second(grads)
    mine_one = links.return_planes(dw_qkv)

    d_att, d_after, sums, d_up_bias, grads = post_back(0, grad_rows)
    d_att, grads_one, mine_one, grads = together(d_att, grads_one, mine_one, grads)
    sum_one = links.scatter_last(grads_one)
    grads = links.scatter_first(grads)
    d_qkv, head_sums, bias_sums = attend_back(0, d_att)
    d_qkv, head_sums, bias_sums, grads, sum_one = together(d_qkv, head_sums, bias_sums, grads, sum_one)
    vec_shape = (devices, 2 * vec_here)

    def tiles_of(norm_sums):
        both = pack([norm_sums, sums, d_up_bias, head_sums, bias_sums] + parts_one, n_head)
        flat = jnp.swapaxes(both.reshape(2, devices, vec_here), 0, 1).reshape(vec_shape)
        return jnp.pad(flat, ((0, 0), (0, 1024 - vec_shape[1]))).reshape(devices, 8, 128)

    if paired:
        tiles = tiles_of(jnp.zeros((8, D), f32))
        gain = vecs[0][0].reshape(1, D)
        square = jnp.broadcast_to(jnp.sum(sum_one * sum_one), (8, 128))
        grad_rows, _sums, sum_zero, qkv_zero, qkv_one, d_vec, squares = finish(
            d_qkv,
            qkv_cols[0],
            hidden_in[0],
            d_after,
            gain,
            group[0],
            grads,
            tiles,
            mine_one,
            square,
            n_tok,
            n_head,
            11,
        )
    else:
        grad_rows, dw_qkv, norm_sums = rows_back(0, d_qkv, d_after)
        tiles = tiles_of(norm_sums)
        d_vec = swap(tiles, n_tok, n_head, 1)
        sum_zero = links.scatter_last(links.scatter_second(links.scatter_add(grads)))
        qkv_zero, qkv_one = links.return_heads([links.return_planes(dw_qkv), mine_one], own)
    summed = []
    for qkv_part, rest in ((qkv_zero, sum_zero), (qkv_one, sum_one)):
        summed.append([qkv_part, rest[:, PROJ_AT:UP_AT], rest[:, UP_AT:DOWN_AT], rest[:, DOWN_AT:WIDE]])
    d_vec = d_vec.reshape(1024)[: 2 * vec_here].reshape(2, vec_here)
    gradients = [jnp.stack([summed[0][kind], summed[1][kind]]) for kind in range(4)]
    if not paired:
        local_square = sum((jnp.sum(gradient * gradient) for gradient in gradients)) + jnp.sum(d_vec * d_vec)
        tile = jnp.concatenate([jnp.broadcast_to(local_square, (8, 128)), jnp.zeros((16, 128), f32)], axis=0)
        squares = spread(tile, n_tok, n_head, 2)
    late = jnp.sum(squares[:, 8:], axis=0).reshape(2 * D)
    grad_norm = jnp.sqrt(jnp.sum(squares[:, 0, 0]) + jnp.sum(late * late))
    if paired:
        flat = jnp.concatenate([late, jnp.zeros((devices * vec_here - 2 * D,), f32)]).reshape(devices, vec_here)
        mine_late = lax.dynamic_slice_in_dim(flat, lax.axis_index("tok") * n_head + own, 1, 0)
        d_vec = d_vec + jnp.concatenate([mine_late, jnp.zeros((1, vec_here), f32)], axis=0)
    gradients.append(d_vec)
    clip_scale = clip_norm / jnp.maximum(grad_norm, clip_norm)
    step_float = step_count[0].astype(f32)
    fix_one = 1.0 - beta_one**step_float
    fix_two = 1.0 - beta_two**step_float
    updates = [
        adam_update(
            groups[0][kind],
            gradients[kind],
            groups[1][kind],
            groups[2][kind],
            groups[3][kind],
            step_rates[kind],
            decays[kind],
            clip_scale,
            fix_one,
            fix_two,
        )
        for kind in range(5)
    ]
    outs = [hidden, grad_rows, grad_norm]
    for part in range(4):
        for kind in range(5):
            leaf = updates[kind][part]
            outs.append(flip(leaf) if kind in (1, 3) else leaf)
    return tuple(outs)


def solution(mesh):
    rows = P(BOTH, None)
    kinds = (
        P(None, BOTH, None),
        P(None, None, BOTH),
        P(None, BOTH, None),
        P(None, None, BOTH),
        P(None, BOTH),
    )
    in_specs = (rows, rows, P("tok"), P()) + kinds * 4
    out_specs = (rows, rows, P()) + kinds * 4
    return jax.shard_map(
        functools.partial(body, Links(mesh)),
        mesh=mesh,
        in_specs=in_specs,
        out_specs=out_specs,
        check_vma=False,
    )
```

```python
import functools
import math

import jax
import jax.numpy as jnp
from jax import lax
from jax.experimental import pallas as pl
from jax.experimental.pallas import tpu as pltpu
from jax.sharding import PartitionSpec as P

D = 1024
HD = 64
FF = 4096
BLOCK = 128
HI_BLOCKS = 8
LO_BLOCKS = 4
FRAMES = 2

norm_eps = 1e-06
clip_norm = 1.0
beta_one = 0.9
beta_two = 0.999
adam_eps = 1e-08
ema_decay = 0.7
step_rates = (0.05, 0.4, 0.05, 0.025, 0.3)
decays = (0.05, 0.05, 0.05, 0.05, 0.0)

LOG2E = math.log2(math.e)
SPAN = 512
MESH_ID = pl.DeviceIdType.MESH
BOTH = ("tok", "head")
bf16 = jnp.bfloat16
f32 = jnp.float32
VMEM_BYTES = 60 << 20


def _peer(step, n_tok, n_head):
    n = n_tok * n_head
    me = lax.axis_index("tok") * n_head + lax.axis_index("head")
    to = lax.rem(me + step, n)
    return me, to, (to // n_head, lax.rem(to, n_head))


def _enter(n_tok, n_head):
    n = n_tok * n_head
    barrier = pltpu.get_barrier_semaphore()

    def greet(step, _):
        _, _, device = _peer(step, n_tok, n_head)
        pl.semaphore_signal(barrier, inc=1, device_id=device, device_id_type=MESH_ID)
        return 0

    lax.fori_loop(1, n, greet, 0)
    pl.semaphore_wait(barrier, n - 1)


def spread_kernel(n_tok, n_head, x_ref, o_ref, send_sem, recv_sem):
    n = n_tok * n_head
    _enter(n_tok, n_head)
    me = lax.axis_index("tok") * n_head + lax.axis_index("head")
    o_ref[me] = x_ref[...]

    def copy(step):
        me, _, device = _peer(step, n_tok, n_head)
        return pltpu.make_async_remote_copy(
            src_ref=x_ref,
            dst_ref=o_ref.at[me],
            send_sem=send_sem.at[step],
            recv_sem=recv_sem.at[step],
            device_id=device,
            device_id_type=MESH_ID,
        )

    def start(step, _):
        copy(step).start()
        return 0

    def finish(step, _):
        copy(step).wait()
        return 0

    lax.fori_loop(1, n, start, 0)
    lax.fori_loop(1, n, finish, 0)


def swap_kernel(n_tok, n_head, x_ref, o_ref, land, send_sem, recv_sem):
    n = n_tok * n_head
    _enter(n_tok, n_head)
    me = lax.axis_index("tok") * n_head + lax.axis_index("head")

    def copy(step):
        me, to, device = _peer(step, n_tok, n_head)
        return pltpu.make_async_remote_copy(
            src_ref=x_ref.at[to],
            dst_ref=land.at[step],
            send_sem=send_sem.at[step],
            recv_sem=recv_sem.at[step],
            device_id=device,
            device_id_type=MESH_ID,
        )

    def start(step, _):
        copy(step).start()
        return 0

    def finish(step, _):
        copy(step).wait()
        return 0

    lax.fori_loop(1, n, start, 0)
    lax.fori_loop(1, n, finish, 0)
    o_ref[...] = x_ref[me] + jnp.sum(land[1:], axis=0)


def spread(tile, n_tok, n_head, collective_id):
    n = n_tok * n_head
    return pl.pallas_call(
        functools.partial(spread_kernel, n_tok, n_head),
        out_shape=jax.ShapeDtypeStruct((n,) + tile.shape, tile.dtype),
        in_specs=[pl.BlockSpec(memory_space=pltpu.VMEM)],
        out_specs=pl.BlockSpec(memory_space=pltpu.VMEM),
        scratch_shapes=[pltpu.SemaphoreType.DMA((n,)), pltpu.SemaphoreType.DMA((n,))],
        compiler_params=pltpu.CompilerParams(collective_id=collective_id, has_side_effects=True),
    )(tile)


def swap(tiles, n_tok, n_head, collective_id):
    n = n_tok * n_head
    return pl.pallas_call(
        functools.partial(swap_kernel, n_tok, n_head),
        out_shape=jax.ShapeDtypeStruct(tiles.shape[1:], tiles.dtype),
        in_specs=[pl.BlockSpec(memory_space=pltpu.VMEM)],
        out_specs=pl.BlockSpec(memory_space=pltpu.VMEM),
        scratch_shapes=[
            pltpu.VMEM(tiles.shape, tiles.dtype),
            pltpu.SemaphoreType.DMA((n,)),
            pltpu.SemaphoreType.DMA((n,)),
        ],
        compiler_params=pltpu.CompilerParams(collective_id=collective_id, has_side_effects=True),
    )(tiles)


def _lane_mean(values, grouping):
    top = values.astype(bf16)
    rest = (values - top.astype(f32)).astype(bf16)
    return jnp.dot(top, grouping, preferred_element_type=f32) + jnp.dot(
        rest, grouping, preferred_element_type=f32
    )


def _grouping(width):
    row = lax.broadcasted_iota(jnp.int32, (width, width), 0) // HD
    col = lax.broadcasted_iota(jnp.int32, (width, width), 1) // HD
    return jnp.where(row == col, 1.0 / HD, 0.0).astype(bf16)


def _unit(values, grouping):
    centered = values - _lane_mean(values, grouping)
    spread_ = _lane_mean(centered * centered, grouping)
    scale = lax.rsqrt(spread_ + norm_eps)
    return centered * scale, scale


def _only(values, head):
    lane = lax.broadcasted_iota(jnp.int32, values.shape, 1)
    return jnp.where(lane // HD == head, values, jnp.zeros_like(values))


NT = (((1,), (1,)), ((), ()))
TN = (((0,), (0,)), ((), ()))


def forward_kernel(
    heads, pieces, spans, tile_rows, order_ref, hi_ref, *refs
):
    x_refs = refs[:pieces]
    w_ref, bias_ref, gains_ref, att_ref, raw_ref, val_ref, lse_ref, q_s, k_s, v_s, acc = refs[pieces:]
    width = heads * HD
    rows = att_ref.shape[0]
    blocks = rows // BLOCK
    piece_rows = rows // pieces
    for at in range(pieces):
        full = jnp.dot(x_refs[at][...], w_ref[...], preferred_element_type=f32) + bias_ref[...]
        here = pl.ds(at * piece_rows, piece_rows)
        raw_ref[here, :] = full[:, : 2 * width]
        val_ref[here, :] = full[:, 2 * width :].astype(bf16)
    grouping = _grouping(width)

    def place(at, _):
        here = pl.ds(pl.multiple_of(order_ref[at] * BLOCK, BLOCK), BLOCK)
        there = pl.ds(pl.multiple_of(at * BLOCK, BLOCK), BLOCK)
        unit_q, _s = _unit(raw_ref[here, :width], grouping)
        unit_k, _s = _unit(raw_ref[here, width:], grouping)
        q_s[there, :] = ((unit_q * gains_ref[0:1, :] + gains_ref[1:2, :]) * HD ** (-0.5)).astype(bf16)
        key = (unit_k * gains_ref[2:3, :] + gains_ref[3:4, :]).astype(bf16)
        value = val_ref[here, :]
        for head in range(heads):
            k_s[head, there, :] = _only(key, head)
            v_s[head, there, :] = _only(value, head)
        return 0

    lax.fori_loop(0, blocks, place, 0)
    per_tile = tile_rows // BLOCK

    def attend(span):
        def tile(at, _):
            here = pl.ds(pl.multiple_of(at * tile_rows, tile_rows), tile_rows)
            first = at * tile_rows // span * span
            there = pl.ds(pl.multiple_of(first, span), span)
            query = q_s[here, :]
            lane = lax.broadcasted_iota(jnp.int32, (tile_rows, 128), 1)
            logs = jnp.zeros((tile_rows, 128), f32)
            for head in range(heads):
                scores = lax.dot_general(query, k_s[head, there, :], NT, preferred_element_type=f32)
                top = jnp.max(scores, axis=1, keepdims=True) * LOG2E
                probs = jnp.exp2(scores * LOG2E - top)
                total = jnp.sum(probs, axis=1, keepdims=True)
                part = jnp.dot(
                    probs.astype(bf16), v_s[head, there, :], preferred_element_type=f32
                ) / total
                if head == 0:
                    acc[...] = part
                else:
                    acc[...] += part
                logs = jnp.where(lane == head, top + jnp.log2(total), logs)
            lse_ref[here, :] = logs
            for sub in range(per_tile):
                out = pl.ds(pl.multiple_of(order_ref[at * per_tile + sub] * BLOCK, BLOCK), BLOCK)
                att_ref[out, :] = acc[sub * BLOCK : (sub + 1) * BLOCK, :].astype(bf16)
            return 0

        lax.fori_loop(0, rows // tile_rows, tile, 0)

    @pl.when(hi_ref[0] == 1)
    def _():
        attend(spans[0])

    @pl.when(hi_ref[0] == 0)
    def _():
        attend(spans[1])


def attention_forward(pieces, weight, bias, gains, order, is_hi, spans):
    heads = weight.shape[1] // (3 * HD)
    width = heads * HD
    rows = sum(piece.shape[0] for piece in pieces)
    tile_rows = 512
    smem = pl.BlockSpec(memory_space=pltpu.SMEM)
    vmem = pl.BlockSpec(memory_space=pltpu.VMEM)
    flops = 2 * rows * (D * 3 * width + 8 * spans[0] * width)
    return pl.pallas_call(
        functools.partial(forward_kernel, heads, len(pieces), spans, tile_rows),
        out_shape=(
            jax.ShapeDtypeStruct((rows, width), bf16),
            jax.ShapeDtypeStruct((rows, 2 * width), f32),
            jax.ShapeDtypeStruct((rows, width), bf16),
            jax.ShapeDtypeStruct((rows, 128), f32),
        ),
        in_specs=[smem, smem] + [vmem] * (len(pieces) + 3),
        out_specs=(vmem,) * 4,
        scratch_shapes=[
            pltpu.VMEM((rows, width), bf16),
            pltpu.VMEM((heads, rows, width), bf16),
            pltpu.VMEM((heads, rows, width), bf16),
            pltpu.VMEM((tile_rows, width), f32),
        ],
        compiler_params=pltpu.CompilerParams(vmem_limit_bytes=VMEM_BYTES),
        cost_estimate=pl.CostEstimate(
            flops=flops, bytes_accessed=rows * (2 * D + 14 * width), transcendentals=rows * spans[0] * heads
        ),
    )(order, is_hi, *pieces, weight, bias, gains)


def backward_kernel(
    heads,
    spans,
    order_ref,
    hi_ref,
    raw_ref,
    val_ref,
    grad_ref,
    att_ref,
    lse_ref,
    gains_ref,
    out_ref,
    sums_ref,
    bias_ref,
    q_s,
    o_s,
    k_m,
    v_m,
    q_m,
    o_m,
    dq_s,
    dk_s,
    dv_s,
    lse_t,
    delta_t,
):
    width = heads * HD
    rows = val_ref.shape[0]
    blocks = rows // BLOCK
    grouping = _grouping(width)
    head_of = lax.broadcasted_iota(jnp.int32, (8, width), 1) // HD
    picks = jnp.where(head_of == lax.broadcasted_iota(jnp.int32, (8, width), 0), 1.0, 0.0).astype(bf16)

    def place(at, _):
        here = pl.ds(pl.multiple_of(order_ref[at] * BLOCK, BLOCK), BLOCK)
        there = pl.ds(pl.multiple_of(at * BLOCK, BLOCK), BLOCK)
        unit_q, _s = _unit(raw_ref[here, :width], grouping)
        unit_k, _s = _unit(raw_ref[here, width:], grouping)
        query = ((unit_q * gains_ref[0:1, :] + gains_ref[1:2, :]) * HD ** (-0.5)).astype(bf16)
        key = (unit_k * gains_ref[2:3, :] + gains_ref[3:4, :]).astype(bf16)
        value = val_ref[here, :]
        grad = grad_ref[here, :]
        q_s[there, :] = query
        o_s[there, :] = grad
        for head in range(heads):
            k_m[head, there, :] = _only(key, head)
            v_m[head, there, :] = _only(value, head)
            q_m[head, there, :] = _only(query, head)
            o_m[head, there, :] = _only(grad, head)
        both = grad.astype(f32) * att_ref[here, :].astype(f32)
        top = both.astype(bf16)
        rest = (both - top.astype(f32)).astype(bf16)
        delta_t[:, there] = lax.dot_general(picks, top, NT, preferred_element_type=f32) + lax.dot_general(
            picks, rest, NT, preferred_element_type=f32
        )
        lse_t[:, there] = jnp.transpose(lse_ref[there, :])[:8, :]
        dq_s[there, :] = jnp.zeros((BLOCK, width), f32)
        dk_s[there, :] = jnp.zeros((BLOCK, width), f32)
        dv_s[there, :] = jnp.zeros((BLOCK, width), f32)
        return 0

    lax.fori_loop(0, blocks, place, 0)
    span = jnp.where(hi_ref[0] == 1, spans[0], spans[1])

    def tile(at, _):
        here = pl.ds(pl.multiple_of(at * SPAN, SPAN), SPAN)
        first = at * SPAN // span * span // SPAN

        def chunk(key_at, _):
            there = pl.ds(pl.multiple_of(key_at * SPAN, SPAN), SPAN)
            for head in range(heads):
                scores = lax.dot_general(k_m[head, there, :], q_s[here, :], NT, preferred_element_type=f32)
                probs = jnp.exp2(scores * LOG2E - lse_t[head : head + 1, here])
                grad_probs = lax.dot_general(
                    v_m[head, there, :], o_s[here, :], NT, preferred_element_type=f32
                )
                grad_scores = (probs * (grad_probs - delta_t[head : head + 1, here])).astype(bf16)
                dv_s[there, :] += jnp.dot(probs.astype(bf16), o_m[head, here, :], preferred_element_type=f32)
                dk_s[there, :] += jnp.dot(grad_scores, q_m[head, here, :], preferred_element_type=f32)
                dq_s[here, :] += lax.dot_general(
                    grad_scores, k_m[head, there, :], TN, preferred_element_type=f32
                )
            return 0

        lax.fori_loop(first, first + span // SPAN, chunk, 0)
        return 0

    lax.fori_loop(0, rows // SPAN, tile, 0)
    sums_ref[...] = jnp.zeros_like(sums_ref)
    bias_ref[...] = jnp.zeros_like(bias_ref)

    def pull(grad, unit, scale, gain):
        grad_unit = grad * gain
        inner = _lane_mean(grad_unit, grouping)
        cross = _lane_mean(grad_unit * unit, grouping)
        return scale * (grad_unit - inner - unit * cross)

    def leave(at, _):
        here = pl.ds(pl.multiple_of(order_ref[at] * BLOCK, BLOCK), BLOCK)
        there = pl.ds(pl.multiple_of(at * BLOCK, BLOCK), BLOCK)
        unit_q, scale_q = _unit(raw_ref[here, :width], grouping)
        unit_k, scale_k = _unit(raw_ref[here, width:], grouping)
        grad_q = dq_s[there, :] * HD ** (-0.5)
        grad_k = dk_s[there, :]
        sums_ref[0:1, :] += jnp.sum(grad_q * unit_q, axis=0, keepdims=True)
        sums_ref[1:2, :] += jnp.sum(grad_q, axis=0, keepdims=True)
        sums_ref[2:3, :] += jnp.sum(grad_k * unit_k, axis=0, keepdims=True)
        sums_ref[3:4, :] += jnp.sum(grad_k, axis=0, keepdims=True)
        low_q = pull(grad_q, unit_q, scale_q, gains_ref[0:1, :]).astype(bf16)
        low_k = pull(grad_k, unit_k, scale_k, gains_ref[2:3, :]).astype(bf16)
        low_v = dv_s[there, :].astype(bf16)
        for part, low in enumerate((low_q, low_k, low_v)):
            lanes = slice(part * width, (part + 1) * width)
            out_ref[here, lanes] = low
            bias_ref[0:1, lanes] += jnp.sum(low.astype(f32), axis=0, keepdims=True)
        return 0

    lax.fori_loop(0, blocks, leave, 0)


def attention_backward(raw, values, grad, attended, lse, gains, order, is_hi, spans):
    rows, width = values.shape
    heads = width // HD
    smem = pl.BlockSpec(memory_space=pltpu.SMEM)
    vmem = pl.BlockSpec(memory_space=pltpu.VMEM)
    flops = 2 * rows * 20 * spans[0] * width
    masked = pltpu.VMEM((heads, rows, width), bf16)
    return pl.pallas_call(
        functools.partial(backward_kernel, heads, spans),
        out_shape=(
            jax.ShapeDtypeStruct((rows, 3 * width), bf16),
            jax.ShapeDtypeStruct((8, width), f32),
            jax.ShapeDtypeStruct((8, 3 * width), f32),
        ),
        in_specs=[smem, smem] + [vmem] * 6,
        out_specs=(vmem,) * 3,
        scratch_shapes=[
            pltpu.VMEM((rows, width), bf16),
            pltpu.VMEM((rows, width), bf16),
            masked,
            masked,
            masked,
            masked,
            pltpu.VMEM((rows, width), f32),
            pltpu.VMEM((rows, width), f32),
            pltpu.VMEM((rows, width), f32),
            pltpu.VMEM((8, rows), f32),
            pltpu.VMEM((8, rows), f32),
        ],
        compiler_params=pltpu.CompilerParams(vmem_limit_bytes=VMEM_BYTES),
        cost_estimate=pl.CostEstimate(
            flops=flops, bytes_accessed=rows * 24 * width, transcendentals=rows * spans[0] * heads
        ),
    )(order, is_hi, raw, values, grad, attended, lse, gains)


class Links:
    def __init__(self, mesh):
        self.n_tok = mesh.shape["tok"]
        self.n_head = mesh.shape["head"]
        self.paired = self.n_tok == 8 and self.n_head == 4

    def head(self, values, step):
        return lax.ppermute(values, "head", [(i, i ^ step) for i in range(self.n_head)])

    def tok(self, values, step):
        return lax.ppermute(values, "tok", [(i, i ^ step) for i in range(self.n_tok)])

    def rows_in(self, rows):
        if not self.paired:
            return [rows] + [self.head(rows, step) for step in range(1, self.n_head)]
        half = rows.shape[0] // 2
        one, two = self.head(rows, 1), self.head(rows, 2)
        far = jnp.concatenate([self.head(one[:half], 2), self.head(two[half:], 1)], axis=0)
        return [rows, one, two, far]

    def rows_out(self, parts):
        if not self.paired:
            moved = [self.head(parts[step], step).astype(f32) for step in range(1, self.n_head)]
            return parts[0].astype(f32) + sum(moved)
        half = parts[0].shape[0] // 2
        upper = [part[:half] for part in parts]
        lower = [part[half:] for part in parts]
        pass_up = (upper[2].astype(f32) + self.head(upper[3], 1).astype(f32)).astype(bf16)
        pass_low = (lower[1].astype(f32) + self.head(lower[3], 2).astype(f32)).astype(bf16)
        up = upper[0].astype(f32) + self.head(upper[1], 1).astype(f32) + self.head(pass_up, 2).astype(f32)
        low = lower[0].astype(f32) + self.head(lower[2], 2).astype(f32) + self.head(pass_low, 1).astype(f32)
        return jnp.concatenate([up, low], axis=0)

    def exchange(self, parts):
        return [parts[0]] + [self.head(parts[step], step) for step in range(1, self.n_head)]

    def by_index(self, pieces, own):
        return [
            lax.select_n((own ^ at).astype(jnp.int32), *pieces) if len(pieces) > 1 else pieces[0]
            for at in range(len(pieces))
        ]

    def zed(self):
        return lax.axis_index("tok") // 2

    def core(self):
        return lax.rem(lax.axis_index("tok"), 2)

    def planes(self, shard):
        pieces = [shard] + [self.tok(shard, 2 * step) for step in range(1, 4)]
        return jnp.stack(self.by_index(pieces, self.zed()))

    def gather_places(self):
        if not self.paired:
            return [None]
        spots = ((0, 4, 0), (0, 4, 1), (0, 4, 2), (0, 2, 3), (2, 2, 3))
        return [("head", first, count, core, to) for first, count, to in spots for core in range(2)]

    def gather_planes(self, shard):
        if not self.paired:
            whole = lax.all_gather(shard, BOTH, axis=0, tiled=True)
            return [whole.reshape(4, 2, 4, whole.shape[0] // 32, whole.shape[1])]
        return [self.planes(shard)]

    def gather_sides(self, own):
        if not self.paired:
            return own
        return [own[0], self.head(own[0], 1), self.head(own[0], 2)]

    def scatter_first(self, grads):
        if not self.paired:
            return grads
        low, top, keep = grads
        return [keep, self.head(low, 1), self.head(top, 2)]

    def scatter_add(self, grads):
        if not self.paired:
            return grads
        keep, low, top = grads
        plus = lambda one, two: (one.astype(f32) + two.astype(f32)).astype(bf16)
        own = [plus(keep[:2], low[:2]), plus(keep[4:6], top[:2])]
        return [own, [plus(keep[2:4], low[2:]), plus(keep[6:], top[2:])]]

    def scatter_second(self, halves):
        if not self.paired:
            return halves
        own, passed = halves
        low = own[0].astype(f32) + self.head(passed[0], 2).astype(f32)
        top = own[1].astype(f32) + self.head(passed[1], 1).astype(f32)
        return [jnp.concatenate([low, top], axis=0).astype(bf16)]

    def scatter_last(self, planes):
        if not self.paired:
            whole = planes[0].reshape(-1, planes[0].shape[-1])
            return lax.psum_scatter(whole, BOTH, scatter_dimension=0, tiled=True).astype(f32)
        return self.sum_planes(planes[0])

    def sum_planes(self, parts):
        zed = self.zed()
        pick = lambda step: lax.dynamic_slice_in_dim(parts, zed ^ step, 1, 0)[0]
        total = pick(0).astype(f32)
        for step in range(1, 4):
            total = total + self.tok(pick(step).astype(bf16), 2 * step).astype(f32)
        return total

    def fetch_heads(self, shards, own):
        own_rows = shards[0].shape[0]
        width = D // self.n_head
        cut = jnp.stack(shards).reshape(len(shards), own_rows, 3, D)
        parts = [
            lax.dynamic_slice_in_dim(cut, (own ^ step) * width, width, 3).reshape(
                len(shards), own_rows, 3 * width
            )
            for step in range(self.n_head)
        ]
        moved = jnp.stack(self.by_index(self.exchange(parts), own), axis=1)
        return [moved[at].reshape(self.n_head * own_rows, 3 * width) for at in range(len(shards))]

    def return_planes(self, grad):
        if not self.paired:
            return lax.psum_scatter(grad, "tok", scatter_dimension=0, tiled=True)
        return self.sum_planes(grad).astype(bf16)

    def return_heads(self, both, own):
        width = D // self.n_head
        stack = jnp.stack(both)
        own_rows = stack.shape[1] // self.n_head
        parts = [
            lax.dynamic_slice_in_dim(stack, (own ^ step) * own_rows, own_rows, 1)
            for step in range(self.n_head)
        ]
        back = jnp.stack(self.by_index(self.exchange(parts), own), axis=2)
        back = back.reshape(len(both), own_rows, self.n_head, 3, width)
        return jnp.swapaxes(back, 2, 3).reshape(len(both), own_rows, 3 * D).astype(f32)


def together(*values):
    return lax.optimization_barrier(values)


CHUNK = 512


def _paired(value, step, bits):
    total = 0
    for bit in range(bits):
        one = lax.rem(value // (1 << bit), 2)
        total = total + (1 - one if (step >> bit) % 2 else one) * (1 << bit)
    return total


def _slot(ref, place):
    if place is None:
        return ref
    tok = lax.axis_index("tok")
    side = _paired(lax.rem(tok, 2), place[-1] if place[0] == "plane" else place[3], 1)
    if place[0] == "plane":
        return ref.at[_paired(tok // 2, place[1], 2), side]
    return ref.at[pl.ds(place[1], place[2]), side, _paired(lax.axis_index("head"), place[4], 2)]


PROJ_AT, UP_AT, DOWN_AT, WIDE = 0, D, D + FF, D + 2 * FF


def _cols(ref, at, size):
    window = pl.ds(pl.multiple_of(at, 128), size)
    return ref.at[(slice(None),) * (len(ref.shape) - 1) + (window,)]


def _copies(pieces, places, whole, at, size, sems, inward):
    moves = []
    for index, (piece, place) in enumerate(zip(pieces, places)):
        outside = _cols(piece, at, size)
        inside = _slot(whole, place)
        pair = (outside, inside) if inward else (inside, outside)
        moves.append(pltpu.make_async_copy(pair[0], pair[1], sems.at[index]))
    return moves


def _start(moves):
    for move in moves:
        move.start()


def _wait(moves):
    for move in moves:
        move.wait()


def _flat(values):
    return values.reshape(D, values.shape[-1])


def _norm(values):
    centered = values - jnp.mean(values, axis=-1, keepdims=True)
    scale = lax.rsqrt(jnp.mean(centered * centered, axis=-1, keepdims=True) + norm_eps)
    return centered * scale, scale


def _own_column(step, n_head):
    at = _paired(lax.axis_index("head"), step, n_head.bit_length() - 1)
    return pl.multiple_of(at * (D // n_head), 128)


def _mate(step):
    return lax.axis_index("tok"), _paired(lax.axis_index("head"), step, 2)


def _sibling():
    return _paired(lax.axis_index("tok"), 1, 3), lax.axis_index("head")


def _greet(devices):
    barrier = pltpu.get_barrier_semaphore()
    for device in devices:
        pl.semaphore_signal(barrier, inc=1, device_id=device, device_id_type=MESH_ID)
    pl.semaphore_wait(barrier, len(devices))


def _send(source, target, send_sem, recv_sem, device):
    return pltpu.make_async_remote_copy(
        src_ref=source,
        dst_ref=target,
        send_sem=send_sem,
        recv_sem=recv_sem,
        device_id=device,
        device_id_type=MESH_ID,
    )


def enter_kernel(wide, *refs):
    x_ref, q_ref, refs = refs[0], refs[1], refs[2:]
    if wide:
        shard_ref, refs = refs[0], refs[1:]
    one_ref, two_ref, far_ref, full_ref, refs = *refs[:4], refs[4:]
    if wide:
        planes_ref, refs = refs[0], refs[1:]
    send_sem, recv_sem, z_send, z_recv, own_sem, core_sem = refs
    tok, head = lax.axis_index("tok"), lax.axis_index("head")
    zed, core = tok // 2, lax.rem(tok, 2)
    one_way, two_way = _mate(1), _mate(2)
    barrier = pltpu.get_barrier_semaphore()
    greet = lambda device: pl.semaphore_signal(barrier, inc=1, device_id=device, device_id_type=MESH_ID)
    for device in (one_way, two_way, _sibling()):
        greet(device)

    @pl.when(zed < 3)
    def _():
        greet((tok + 2, head))

    @pl.when(zed > 0)
    def _():
        greet((tok - 2, head))

    edge = (zed == 0) | (zed == 3)

    @pl.when(edge)
    def _():
        pl.semaphore_wait(barrier, 4)

    @pl.when(jnp.logical_not(edge))
    def _():
        pl.semaphore_wait(barrier, 5)

    rows = x_ref.shape[0]
    parts = 4
    size = rows // parts

    def move(lane, part, source, target, device):
        here = pl.ds(part * size, size)
        return _send(source.at[here], target.at[here], send_sem.at[lane, part], recv_sem.at[lane, part], device)

    to_one = lambda part: move(0, part, x_ref, one_ref, one_way)
    to_two = lambda part: move(1, part, x_ref, two_ref, two_way)
    on_two = lambda part: move(2, part, one_ref, far_ref, two_way)
    on_one = lambda part: move(2, part, two_ref, far_ref, one_way)
    homes = [(q_ref, lambda plane: full_ref.at[plane, core])]
    if wide:
        homes.append((shard_ref, lambda plane: planes_ref.at[plane]))

    def climb(up, step):
        plane = jnp.clip(zed - step if up else zed + step, 0, 3)
        device = (jnp.clip(tok + 2 if up else tok - 2, 0, 7), head)
        return [
            _send(
                home(plane) if step else source,
                home(plane),
                z_send.at[int(up), step, index],
                z_recv.at[int(up), step, index],
                device,
            )
            for index, (source, home) in enumerate(homes)
        ]

    def sends(up, step):
        return (zed >= step) & (zed < 3) if up else (zed <= 3 - step) & (zed > 0)

    def comes(up, step):
        return zed >= step + 1 if up else zed <= 2 - step

    def climb_start(up, step):
        @pl.when(sends(up, step))
        def _():
            _start(climb(up, step))

    def climb_come(up, step):
        @pl.when(comes(up, step))
        def _():
            for copy in climb(up, step):
                copy.wait_recv()

    for turn in range(parts):
        to_one(turn).start()
        to_two(parts - 1 - turn).start()
    for up in (True, False):
        climb_start(up, 0)
    stays = [
        pltpu.make_async_copy(source, home(zed), own_sem.at[index]) for index, (source, home) in enumerate(homes)
    ]
    _start(stays)
    for turn in range(parts // 2):
        to_one(turn).wait_recv()
        on_two(turn).start()
        to_two(parts - 1 - turn).wait_recv()
        on_one(parts - 1 - turn).start()
    for step in range(3):
        for up in (True, False):
            climb_come(up, step)
            if step < 2:
                climb_start(up, step + 1)
    _wait(stays)
    mine = full_ref.at[:, core]
    over = _send(mine, mine, core_sem.at[0], core_sem.at[1], _sibling())
    over.start()
    for turn in range(parts // 2, parts):
        to_one(turn).wait_recv()
        to_two(parts - 1 - turn).wait_recv()
    for turn in range(parts):
        to_one(turn).wait_send()
        to_two(turn).wait_send()
    for turn in range(parts // 2):
        on_two(turn).wait()
        on_one(parts - 1 - turn).wait()
    for step in range(3):
        for up in (True, False):

            @pl.when(sends(up, step))
            def _():
                for copy in climb(up, step):
                    copy.wait_send()

    over.wait()


def enter_rows(rows, mine, shard, collective_id):
    hbm = pl.BlockSpec(memory_space=pl.ANY)
    like = jax.ShapeDtypeStruct(rows.shape, rows.dtype)
    outs = [like, like, like, jax.ShapeDtypeStruct((4, 2) + mine.shape, mine.dtype)]
    given = [rows, mine]
    if shard is not None:
        outs.append(jax.ShapeDtypeStruct((4,) + shard.shape, shard.dtype))
        given.append(shard)
    sems = pltpu.SemaphoreType.DMA
    one, two, far, full, *planes = pl.pallas_call(
        functools.partial(enter_kernel, shard is not None),
        out_shape=tuple(outs),
        in_specs=[hbm] * len(given),
        out_specs=(hbm,) * len(outs),
        scratch_shapes=[sems((3, 4)), sems((3, 4)), sems((2, 3, 2)), sems((2, 3, 2)), sems((2,)), sems((2,))],
        compiler_params=pltpu.CompilerParams(collective_id=collective_id, has_side_effects=True),
        cost_estimate=pl.CostEstimate(flops=0, bytes_accessed=150 << 20, transcendentals=0),
    )(*given)
    return [rows, one, two, far], full.reshape(8 * mine.shape[0], mine.shape[1]), planes


def _norm_pull(grad_unit, unit, scale):
    inner = jnp.mean(grad_unit, axis=-1, keepdims=True)
    cross = jnp.mean(grad_unit * unit, axis=-1, keepdims=True)
    return scale * (grad_unit - inner - unit * cross)


def _qkv_grad(grad_ref, x_refs, total, low, come, send_sem, recv_sem):
    rows = x_refs[0].shape[0]
    for step, x_ref in enumerate(x_refs):
        part = lax.dot_general(
            x_ref[...], grad_ref[step * rows : (step + 1) * rows, :], TN, preferred_element_type=f32
        )
        if step:
            total[...] += part
        else:
            total[...] = part
    low[...] = total[...].astype(bf16).reshape(low.shape)
    core = lax.rem(lax.axis_index("tok"), 2)
    swap_core = _send(low.at[:, 1 - core], come, send_sem, recv_sem, _sibling())
    swap_core.start()
    return swap_core


def rows_out_kernel(
    grad_ref,
    weight_ref,
    hidden_ref,
    after_ref,
    gain_ref,
    x0_ref,
    x1_ref,
    x2_ref,
    x3_ref,
    out_ref,
    sums_ref,
    mine_ref,
    away,
    come,
    q_acc,
    q_all,
    q_come,
    send_sem,
    recv_sem,
    q_sem,
):
    one_way, two_way = _mate(1), _mate(2)
    _greet([one_way, two_way, _sibling()])
    rows = hidden_ref.shape[0]
    half = rows // 2

    def term(step, low):
        here = pl.ds(step * rows + (0 if low else half), half)
        return lax.dot_general(grad_ref[here, :], weight_ref[...], NT, preferred_element_type=f32)

    def move(slot, device):
        return _send(away.at[slot], come.at[slot], send_sem.at[slot], recv_sem.at[slot], device)

    ways = (one_way, two_way, one_way, two_way, two_way, one_way)
    for slot, (step, low) in enumerate(((3, True), (3, False), (1, True), (2, False))):
        away[slot] = term(step, low).astype(bf16)
        move(slot, ways[slot]).start()
    pass_low = term(2, True)
    pass_top = term(1, False)
    core = lax.rem(lax.axis_index("tok"), 2)
    swap_core = _qkv_grad(grad_ref, (x0_ref, x1_ref, x2_ref, x3_ref), q_acc, q_all, q_come, q_sem.at[0], q_sem.at[1])
    move(0, ways[0]).wait_recv()
    away[4] = (pass_low + come[0].astype(f32)).astype(bf16)
    move(4, ways[4]).start()
    move(1, ways[1]).wait_recv()
    away[5] = (pass_top + come[1].astype(f32)).astype(bf16)
    move(5, ways[5]).start()
    sums_ref[...] = jnp.zeros_like(sums_ref)
    for low in (True, False):
        here = pl.ds(0 if low else half, half)
        own = term(0, low)
        unit, scale = _norm(hidden_ref[here, :])
        near, far = (2, 4) if low else (3, 5)
        move(near, ways[near]).wait_recv()
        move(far, ways[far]).wait_recv()
        grad = own + come[near].astype(f32) + come[far].astype(f32)
        sums_ref[0:1, :] += jnp.sum(grad * unit, axis=0, keepdims=True)
        sums_ref[1:2, :] += jnp.sum(grad, axis=0, keepdims=True)
        out_ref[here, :] = after_ref[here, :] + _norm_pull(grad * gain_ref[0:1, :], unit, scale)
    swap_core.wait()
    mine_ref[...] = (q_all[:, core].astype(f32) + q_come[...].astype(f32)).astype(bf16)
    for slot in range(6):
        move(slot, ways[slot]).wait_send()


def rows_out(grad, weight, hidden, after, gain, pieces, collective_id):
    rows, width = hidden.shape[0], grad.shape[1]
    vmem = pl.BlockSpec(memory_space=pltpu.VMEM)
    buffer = pltpu.VMEM((6, rows // 2, D), bf16)
    sems = pltpu.SemaphoreType.DMA((6,))
    return pl.pallas_call(
        rows_out_kernel,
        out_shape=(
            jax.ShapeDtypeStruct((rows, D), f32),
            jax.ShapeDtypeStruct((8, D), f32),
            jax.ShapeDtypeStruct((4, D // 8, width), bf16),
        ),
        in_specs=[vmem] * 9,
        out_specs=(vmem, vmem, vmem),
        scratch_shapes=[
            buffer,
            buffer,
            pltpu.VMEM((D, width), f32),
            pltpu.VMEM((4, 2, D // 8, width), bf16),
            pltpu.VMEM((4, D // 8, width), bf16),
            sems,
            sems,
            pltpu.SemaphoreType.DMA((2,)),
        ],
        compiler_params=pltpu.CompilerParams(
            collective_id=collective_id, has_side_effects=True, vmem_limit_bytes=VMEM_BYTES
        ),
        cost_estimate=pl.CostEstimate(flops=0, bytes_accessed=150 << 20, transcendentals=0),
    )(grad, weight, hidden, after, gain, *pieces)


def post_forward_kernel(n_head, places, last, remote, *refs):
    count = len(places)
    att_ref, refs = refs[0], refs[1:]
    hidden_ref, rows_ref, up_bias_ref, refs = refs[0], refs[1], refs[2], refs[3:]
    given = 3 if remote else count
    weight_refs, refs = refs[:given], refs[given:]
    next_ref, normed_ref, down_ref, act_ref, slope_ref, branch_hbm, after_hbm, two_hbm, att_hbm, refs = *refs[:9], refs[9:]
    if remote:
        (own, one, two), (far_low, far_top), refs = weight_refs, refs[:2], refs[2:]
        side_own, side_one, side_two, side_low, side_top, refs = *refs[:5], refs[5:]
        weight_refs = (own, side_own, one, side_one, two, side_two, far_low, side_low, far_top, side_top)
    proj_s, up_s, down_s, att_s, branch_s, after_s, two_s, acc, proj_sem, up_sem, down_sem, out_sem, send_sem, recv_sem, refs = (
        *refs[:14],
        refs[14:],
    )
    at = pl.program_id(0)
    chunks = pl.num_programs(0)
    if remote:
        relay_send, relay_recv, side_send, side_recv = refs
        groups = WIDE // D
        order = [0] + [first for pair in zip(range(1, 1 + groups // 2), range(1 + groups // 2, groups)) for first in pair]

        def relay(group):
            part = lambda ref: _cols(ref, group * D, D)
            return [
                _send(
                    part(one.at[pl.ds(0, 2)]),
                    part(far_low),
                    relay_send.at[0, group],
                    relay_recv.at[0, group],
                    _mate(2),
                ),
                _send(
                    part(two.at[pl.ds(2, 2)]),
                    part(far_top),
                    relay_send.at[1, group],
                    relay_recv.at[1, group],
                    _mate(1),
                ),
            ]

        def across(group, pairs, first):
            return [
                _send(
                    _cols(source, group * D, D),
                    _cols(target, group * D, D),
                    side_send.at[first + index, group],
                    side_recv.at[first + index, group],
                    _sibling(),
                )
                for index, (source, target) in enumerate(pairs)
            ]

        near = lambda group: across(group, ((own, side_own), (one, side_one), (two, side_two)), 0)
        far = lambda group: across(group, ((far_low, side_low), (far_top, side_top)), 3)

        def advance(group):
            for copy in relay(group):
                copy.wait_recv()
            _start(far(group))

        def complete(group):
            for copy in near(group) + far(group):
                copy.wait_recv()

    def fetch(chunk, slot):
        up_at, down_at = UP_AT + chunk * CHUNK, DOWN_AT + chunk * CHUNK
        return _copies(weight_refs, places, up_s.at[slot], up_at, CHUNK, up_sem.at[slot], True) + _copies(
            weight_refs, places, down_s.at[slot], down_at, CHUNK, down_sem.at[slot], True
        )

    leaving = [
        pltpu.make_async_copy(branch_s, branch_hbm, out_sem.at[0]),
        pltpu.make_async_copy(after_s, after_hbm, out_sem.at[1]),
        pltpu.make_async_copy(two_s, two_hbm, out_sem.at[2]),
        pltpu.make_async_copy(att_s, att_hbm, out_sem.at[3]),
    ]

    @pl.when(at == 0)
    def _():
        proj = _copies(weight_refs, places, proj_s, PROJ_AT, D, proj_sem, True)
        if remote:
            width, rows = D // n_head, hidden_ref.shape[0]
            _greet([_mate(step) for step in range(1, n_head)] + [_sibling()])
            mine = att_s.at[:, pl.ds(_own_column(0, n_head), width)]
            moves = [
                _send(
                    att_ref.at[pl.ds(step * rows, rows)], mine, send_sem.at[step], recv_sem.at[step], _mate(step)
                )
                for step in range(1, n_head)
            ]
            moves.append(pltpu.make_async_copy(att_ref.at[pl.ds(0, rows)], mine, send_sem.at[0]))
            _start(moves)
            for group in order:
                _start(relay(group))
                _start(near(group))
            advance(order[0])
            _wait(moves)
            complete(order[0])
            _start(proj)
            for group in order[1:3]:
                advance(group)
        else:
            _start(proj)
            _start(fetch(0, 0))
            att_s[...] = att_ref[...]
        _wait(proj)
        branch = (
            lax.dot_general(att_s[...], _flat(proj_s[...]), NT, preferred_element_type=f32) + rows_ref[0:1, :]
        )
        branch_s[...] = branch
        after = hidden_ref[...] + rows_ref[1:2, :] * branch
        after_s[...] = after
        unit, _s = _norm(after)
        two_s[...] = (unit * rows_ref[2:3, :] + rows_ref[3:4, :]).astype(bf16)
        _start(leaving)
        if remote:
            for group in order[1:3]:
                complete(group)
            _start(fetch(0, 0))

    if remote:
        later = at // 2 + 2
        halves = groups // 2

        @pl.when((lax.rem(at, 2) == 0) & (later <= halves))
        def _():
            advance(later)
            advance(later + halves)

        @pl.when((lax.rem(at, 2) == 1) & (later <= halves))
        def _():
            complete(later)
            complete(later + halves)

    @pl.when(at + 1 < chunks)
    def _():
        _start(fetch(at + 1, lax.rem(at + 1, 2)))

    slot = lax.rem(at, 2)
    _wait(fetch(at, slot))
    expand = jnp.dot(two_s[...], _flat(up_s[slot]), preferred_element_type=f32) + up_bias_ref[...]
    cdf = 0.5 * (1.0 + lax.erf(expand * math.sqrt(0.5)))
    slope = cdf + expand * jnp.exp(-0.5 * expand * expand) * (1.0 / math.sqrt(2.0 * math.pi))
    act = (expand * cdf).astype(bf16)
    act_ref[...] = act
    slope_ref[...] = slope.astype(bf16)
    part = lax.dot_general(act, _flat(down_s[slot]), NT, preferred_element_type=f32)

    @pl.when(at == 0)
    def _():
        acc[...] = part

    @pl.when(at > 0)
    def _():
        acc[...] += part

    @pl.when(at == chunks - 1)
    def _():
        down = acc[...] + rows_ref[4:5, :]
        down_ref[...] = down
        hidden = after_s[...] + rows_ref[5:6, :] * down
        next_ref[...] = hidden
        if last:
            normed_ref[...] = jnp.zeros_like(normed_ref)
        else:
            unit, _s = _norm(hidden)
            normed_ref[...] = (unit * rows_ref[6:7, :] + rows_ref[7:8, :]).astype(bf16)
        _wait(leaving)
        if remote:
            for group in range(groups):
                for copy in relay(group) + near(group) + far(group):
                    copy.wait_send()


def _params(remote, collective_id):
    if not remote:
        return pltpu.CompilerParams(dimension_semantics=("arbitrary",), vmem_limit_bytes=VMEM_BYTES)
    return pltpu.CompilerParams(
        dimension_semantics=("arbitrary",),
        vmem_limit_bytes=VMEM_BYTES,
        collective_id=collective_id,
        has_side_effects=True,
    )


def post_forward(att, hidden, rows, up_bias, gathered, n_head, last, remote, collective_id):
    own_rows = hidden.shape[0]
    pieces, places = gathered
    count = len(places)
    unit_rows = D // 32
    vmem = pl.BlockSpec(memory_space=pltpu.VMEM)
    hbm = pl.BlockSpec(memory_space=pl.ANY)
    column = pl.BlockSpec((own_rows, CHUNK), lambda at: (0, at))
    fixed = lambda leaf_rows: pl.BlockSpec((leaf_rows, D), lambda at: (0, 0))
    whole = lambda dtype: jax.ShapeDtypeStruct((own_rows, D), dtype)
    wide = jax.ShapeDtypeStruct((own_rows, FF), bf16)
    weight = lambda *lead: pltpu.VMEM(lead + (4, 2, 4, unit_rows), bf16)
    normed_rows = 16 if last else own_rows
    landed, sems = [], []
    if remote:
        half, full = [
            jax.ShapeDtypeStruct((planes,) + pieces[0].shape[1:], bf16) for planes in (2, 4)
        ]
        landed = [half, half, full, full, full, half, half]
        for kinds in (2, 2, 5, 5):
            sems.append(pltpu.SemaphoreType.DMA((kinds, WIDE // D)))
    outs = pl.pallas_call(
        functools.partial(post_forward_kernel, n_head, places, last, remote),
        grid=(FF // CHUNK,),
        out_shape=(
            whole(f32),
            jax.ShapeDtypeStruct((normed_rows, D), bf16),
            whole(f32),
            wide,
            wide,
            whole(f32),
            whole(f32),
            whole(bf16),
            whole(bf16),
            *landed,
        ),
        in_specs=[hbm if remote else vmem, vmem, vmem, pl.BlockSpec((1, CHUNK), lambda at: (0, at))]
        + [hbm] * len(pieces),
        out_specs=(fixed(own_rows), fixed(normed_rows), fixed(own_rows), column, column)
        + (hbm,) * (4 + len(landed)),
        scratch_shapes=[
            pltpu.VMEM((4, 2, 4, unit_rows, D), bf16),
            pltpu.VMEM((2, 4, 2, 4, unit_rows, CHUNK), bf16),
            pltpu.VMEM((2, 4, 2, 4, unit_rows, CHUNK), bf16),
            pltpu.VMEM((own_rows, D), bf16),
            pltpu.VMEM((own_rows, D), f32),
            pltpu.VMEM((own_rows, D), f32),
            pltpu.VMEM((own_rows, D), bf16),
            pltpu.VMEM((own_rows, D), f32),
            pltpu.SemaphoreType.DMA((count,)),
            pltpu.SemaphoreType.DMA((2, count)),
            pltpu.SemaphoreType.DMA((2, count)),
            pltpu.SemaphoreType.DMA((4,)),
            pltpu.SemaphoreType.DMA((n_head,)),
            pltpu.SemaphoreType.DMA((n_head,)),
            *sems,
        ],
        compiler_params=_params(remote, collective_id),
        cost_estimate=pl.CostEstimate(
            flops=2 * own_rows * D * (D + 2 * FF),
            bytes_accessed=2 * D * (D + 2 * FF) + own_rows * (22 * D + 4 * FF),
            transcendentals=2 * own_rows * FF,
        ),
    )(att, hidden, rows, up_bias, *pieces)
    if remote:
        far_low, far_top, *sides = outs[9:]
        near = [*pieces, far_low, far_top]
        pieces = [piece for pair in zip(near, sides) for piece in pair]
    return list(outs[:9]), pieces


def post_backward_kernel(n_head, places, remote, *refs):
    count = len(places)
    far_places = [("head", 0, 4, 1, to) for to in range(4)] if remote else []
    out_count = 3 if remote else 1
    att_ref, grad_ref, down_ref, branch_ref, after_ref, two_ref, rows_ref, act_ref, slope_ref, refs = *refs[:9], refs[9:]
    weight_refs, refs = refs[:count], refs[count:]
    d_att_ref, d_after_ref, sums_ref, up_sum_ref, refs = *refs[:4], refs[4:]
    own_refs, refs = refs[:out_count], refs[out_count:]
    proj_s, up_s, down_s, d_proj_s, d_up_s, d_down_s, att_s, low_s, low_t, two_t, acc, refs = *refs[:11], refs[11:]
    proj_sem, up_sem, down_sem, own_sem, far_sem, got_sem, send_sem, recv_sem, refs = *refs[:8], refs[8:]
    if remote:
        stash, got = refs
        low_ref, top_ref, keep_ref = own_refs
    at = pl.program_id(0)
    chunks = pl.num_programs(0)
    width = D // n_head

    def fetch(chunk, slot):
        up_at, down_at = UP_AT + chunk * CHUNK, DOWN_AT + chunk * CHUNK
        return _copies(weight_refs, places, up_s.at[slot], up_at, CHUNK, up_sem.at[slot], True) + _copies(
            weight_refs, places, down_s.at[slot], down_at, CHUNK, down_sem.at[slot], True
        )

    def stay(whole, column, size, lane):
        return [] if remote else _copies(own_refs, [None], whole, column, size, own_sem.at[lane], False)

    def away(whole, column, size, lane, mark):
        return [
            _send(
                _slot(whole, place),
                _cols(got.at[to], column, size),
                far_sem.at[lane, to],
                got_sem.at[mark, to],
                _sibling(),
            )
            for to, place in enumerate(far_places)
        ]

    def over(chunk, slot):
        up_at, down_at = UP_AT + chunk * CHUNK, DOWN_AT + chunk * CHUNK
        return away(d_up_s.at[slot], up_at, CHUNK, slot, chunk) + away(
            d_down_s.at[slot], down_at, CHUNK, 2 + slot, chunks + chunk
        )

    def leave(chunk, slot):
        up_at, down_at = UP_AT + chunk * CHUNK, DOWN_AT + chunk * CHUNK
        local = stay(d_up_s.at[slot], up_at, CHUNK, slot) + stay(d_down_s.at[slot], down_at, CHUNK, 2 + slot)
        return local, over(chunk, slot)

    def left(pair):
        _wait(pair[0])
        for move in pair[1]:
            move.wait_send()

    def hold(staged, column, size):
        core, head = lax.rem(lax.axis_index("tok"), 2), lax.axis_index("head")
        for to in range(4):
            _cols(stash.at[to], column, size)[...] = staged[:, core, _paired(head, to, 2)]

    def add(column, size):
        mine, other = _cols(stash, column, size), _cols(got, column, size)
        for to in range(4):
            mine[to] = (mine[to].astype(f32) + other[to].astype(f32)).astype(bf16)

    def merge(chunk):
        for move in over(chunk, 0):
            move.wait_recv()
        add(UP_AT + chunk * CHUNK, CHUNK)
        add(DOWN_AT + chunk * CHUNK, CHUNK)

    def depart(column, size, lane):
        spots = (
            (low_ref, 0, 1, 0),
            (low_ref, 2, 3, 0),
            (top_ref, 0, 2, 2),
            (top_ref, 2, 3, 2),
            (keep_ref, 0, 0, 0),
            (keep_ref, 2, 2, 0),
            (keep_ref, 4, 0, 2),
            (keep_ref, 6, 1, 2),
        )
        return [
            pltpu.make_async_copy(
                _cols(stash.at[to, pl.ds(first, 2)], column, size),
                _cols(target.at[pl.ds(at_, 2)], column, size),
                own_sem.at[lane, index],
            )
            for index, (target, at_, to, first) in enumerate(spots)
        ]

    middle = FF // 2
    early = lambda: depart(UP_AT, middle, 0) + depart(DOWN_AT, middle, 1)

    proj = lambda: _copies(weight_refs, places, proj_s, PROJ_AT, D, proj_sem, True)

    @pl.when(at == 0)
    def _():
        if remote:
            _greet([_mate(step) for step in range(1, n_head)] + [_sibling()])
        _start(fetch(0, 0))
        _start(proj())
        grad = grad_ref[...]
        low = (rows_ref[2:3, :] * grad).astype(bf16)
        low_s[...] = low
        low_t[...] = jnp.transpose(low)
        two_t[...] = jnp.transpose(two_ref[...])
        sums_ref[...] = jnp.zeros_like(sums_ref)
        sums_ref[0:1, :] = jnp.sum(grad * down_ref[...], axis=0, keepdims=True)
        sums_ref[1:2, :] = jnp.sum(low.astype(f32), axis=0, keepdims=True)
        acc[...] = jnp.zeros_like(acc)

    @pl.when(at + 1 < chunks)
    def _():
        _start(fetch(at + 1, lax.rem(at + 1, 2)))

    slot = lax.rem(at, 2)
    _wait(fetch(at, slot))

    @pl.when(at >= 2)
    def _():
        left(leave(at - 2, slot))

    d_act = jnp.dot(low_s[...], _flat(down_s[slot]), preferred_element_type=f32)
    d_expand = (slope_ref[...].astype(f32) * d_act).astype(bf16)
    up_sum_ref[...] = jnp.sum(d_expand.astype(f32), axis=0, keepdims=True)
    acc[...] += lax.dot_general(d_expand, _flat(up_s[slot]), NT, preferred_element_type=f32)
    shape = d_up_s.shape[1:]
    d_up_s[slot] = jnp.dot(two_t[...], d_expand, preferred_element_type=f32).astype(bf16).reshape(shape)
    d_down_s[slot] = jnp.dot(low_t[...], act_ref[...], preferred_element_type=f32).astype(bf16).reshape(shape)
    for moves in leave(at, slot):
        _start(moves)
    if remote:
        hold(d_up_s.at[slot], UP_AT + at * CHUNK, CHUNK)
        hold(d_down_s.at[slot], DOWN_AT + at * CHUNK, CHUNK)

        @pl.when(at > 0)
        def _():
            merge(at - 1)

        @pl.when(at == chunks // 2)
        def _():
            _start(early())

    @pl.when(at == chunks - 1)
    def _():
        d_two = acc[...]
        unit, scale = _norm(after_ref[...])
        sums_ref[2:3, :] = jnp.sum(d_two * unit, axis=0, keepdims=True)
        sums_ref[3:4, :] = jnp.sum(d_two, axis=0, keepdims=True)
        d_unit = d_two * rows_ref[1:2, :]
        inner = jnp.mean(d_unit, axis=-1, keepdims=True)
        cross = jnp.mean(d_unit * unit, axis=-1, keepdims=True)
        d_after = grad_ref[...] + scale * (d_unit - inner - unit * cross)
        d_after_ref[...] = d_after
        sums_ref[4:5, :] = jnp.sum(d_after * branch_ref[...], axis=0, keepdims=True)
        d_branch = (rows_ref[0:1, :] * d_after).astype(bf16)
        sums_ref[5:6, :] = jnp.sum(d_branch.astype(f32), axis=0, keepdims=True)
        _wait(proj())
        d_att = jnp.dot(d_branch, _flat(proj_s[...]), preferred_element_type=f32).astype(bf16)
        if remote:
            rows = d_att.shape[0]
            att_s[...] = d_att
            moves = [
                _send(
                    att_s.at[:, pl.ds(_own_column(step, n_head), width)],
                    d_att_ref.at[pl.ds(step * rows, rows)],
                    send_sem.at[step],
                    recv_sem.at[step],
                    _mate(step),
                )
                for step in range(1, n_head)
            ]
            own = att_s.at[:, pl.ds(_own_column(0, n_head), width)]
            moves.append(pltpu.make_async_copy(own, d_att_ref.at[pl.ds(0, rows)], send_sem.at[0]))
            _start(moves)
        else:
            d_att_ref[...] = d_att
        d_proj_s[...] = (
            lax.dot_general(d_branch, att_ref[...], TN, preferred_element_type=f32)
            .astype(bf16)
            .reshape(d_proj_s.shape)
        )
        gone = stay(d_proj_s, PROJ_AT, D, 4), away(d_proj_s, PROJ_AT, D, 4, 2 * chunks)
        for group in gone:
            _start(group)
        if remote:
            hold(d_proj_s, PROJ_AT, D)
        left(leave(at - 1, 1 - slot))
        left(leave(at, slot))
        left(gone)
        if remote:
            merge(at)
            for move in gone[1]:
                move.wait_recv()
            add(PROJ_AT, D)
            late = (
                depart(UP_AT + middle, middle, 2) + depart(DOWN_AT + middle, middle, 3) + depart(PROJ_AT, D, 4)
            )
            _start(late)
            _wait(early())
            _wait(late)
            _wait(moves)


def post_backward(att, grad, down_out, branch, after, two, rows, act, slope, gathered, n_head, remote, collective_id):
    own_rows = grad.shape[0]
    pieces, places = gathered
    count = len(places)
    unit_rows = D // 32
    vmem = pl.BlockSpec(memory_space=pltpu.VMEM)
    hbm = pl.BlockSpec(memory_space=pl.ANY)
    column = pl.BlockSpec((own_rows, CHUNK), lambda at: (0, at))
    fixed = lambda *shape: pl.BlockSpec(shape, lambda at: (0, 0))
    width = D // n_head
    chunks = FF // CHUNK
    if remote:
        d_att_shape, d_att_spec = (n_head * own_rows, width), hbm
        grads = [jax.ShapeDtypeStruct((planes, unit_rows, WIDE), bf16) for planes in (4, 4, 8)]
        stashes = [pltpu.VMEM((4, 4, unit_rows, WIDE), bf16)] * 2
    else:
        d_att_shape, d_att_spec = (own_rows, D), fixed(own_rows, D)
        grads = [jax.ShapeDtypeStruct((4, 2, 4, unit_rows, WIDE), bf16)]
        stashes = []
    sems = pltpu.SemaphoreType.DMA
    outs = pl.pallas_call(
        functools.partial(post_backward_kernel, n_head, places, remote),
        grid=(chunks,),
        out_shape=tuple(
            [
                jax.ShapeDtypeStruct(d_att_shape, bf16),
                jax.ShapeDtypeStruct((own_rows, D), f32),
                jax.ShapeDtypeStruct((8, D), f32),
                jax.ShapeDtypeStruct((1, FF), f32),
            ]
            + grads
        ),
        in_specs=[vmem] * 7 + [column, column] + [hbm] * count,
        out_specs=tuple(
            [d_att_spec, fixed(own_rows, D), fixed(8, D), pl.BlockSpec((1, CHUNK), lambda at: (0, at))]
            + [hbm] * len(grads)
        ),
        scratch_shapes=[
            pltpu.VMEM((4, 2, 4, unit_rows, D), bf16),
            pltpu.VMEM((2, 4, 2, 4, unit_rows, CHUNK), bf16),
            pltpu.VMEM((2, 4, 2, 4, unit_rows, CHUNK), bf16),
            pltpu.VMEM((4, 2, 4, unit_rows, D), bf16),
            pltpu.VMEM((2, 4, 2, 4, unit_rows, CHUNK), bf16),
            pltpu.VMEM((2, 4, 2, 4, unit_rows, CHUNK), bf16),
            pltpu.VMEM((own_rows, D), bf16),
            pltpu.VMEM((own_rows, D), bf16),
            pltpu.VMEM((D, own_rows), bf16),
            pltpu.VMEM((D, own_rows), bf16),
            pltpu.VMEM((own_rows, D), f32),
            sems((count,)),
            sems((2, count)),
            sems((2, count)),
            sems((5, 8)),
            sems((5, 4)),
            sems((2 * chunks + 1, 4)),
            sems((n_head,)),
            sems((n_head,)),
            *stashes,
        ],
        compiler_params=_params(remote, collective_id),
        cost_estimate=pl.CostEstimate(
            flops=4 * own_rows * D * (D + 2 * FF),
            bytes_accessed=4 * D * (D + 2 * FF) + own_rows * (22 * D + 4 * FF),
            transcendentals=0,
        ),
    )(att, grad, down_out, branch, after, two, rows, act, slope, *pieces)
    d_att, d_after, sums, up_sum, grads = *outs[:4], list(outs[4:])
    return d_att, d_after, sums, up_sum, grads


FINISH_CUTS = 6


def finish_kernel(
    n_tok,
    n_head,
    grad_ref,
    weight_ref,
    hidden_ref,
    after_ref,
    gain_ref,
    x0_ref,
    x1_ref,
    x2_ref,
    x3_ref,
    keep_ref,
    low_ref,
    top_ref,
    tiles_ref,
    one_ref,
    square_ref,
    out_ref,
    sums_ref,
    rest_ref,
    qkv_ref,
    qkv_one_ref,
    vec_ref,
    all_ref,
    own_s,
    pass_s,
    tile_s,
    away,
    come,
    come_rest,
    away_z,
    come_z,
    q_acc,
    q_all,
    q_come,
    q_mine,
    q_z,
    q_sum,
    q_land,
    one_land,
    land,
    send_sem,
    recv_sem,
    rest_send,
    rest_recv,
    z_send,
    z_recv,
    q_send,
    q_recv,
    v_send,
    v_recv,
    n_send,
    n_recv,
):
    n = n_tok * n_head
    _enter(n_tok, n_head)
    tok = lax.axis_index("tok")
    head = lax.axis_index("head")
    me = tok * n_head + head
    zed, core = tok // 2, lax.rem(tok, 2)
    one_way, two_way = _mate(1), _mate(2)
    plane = lambda step: _paired(zed, step, 2)
    over = lambda step: (plane(step) * 2 + core, head)

    def tile(step):
        _, to, device = _peer(step, n_tok, n_head)
        return _send(tiles_ref.at[to], land.at[step], v_send.at[step], v_recv.at[step], device)

    def tile_start(step, _):
        tile(step).start()
        return 0

    def tile_wait(step, _):
        tile(step).wait()
        return 0

    lax.fori_loop(1, n, tile_start, 0)
    mate_at = lambda step: _paired(head, step, 2)

    def go_home(source, target, first):
        return [
            _send(
                source.at[mate_at(step)],
                target.at[head],
                q_send.at[first + step],
                q_recv.at[first + step],
                _mate(step),
            )
            for step in range(1, 4)
        ]

    one_home = go_home(one_ref, one_land, 6)
    _start(one_home)
    wide = keep_ref.shape[2] // FINISH_CUTS
    two_sum = lambda first, second: (first.astype(f32) + second.astype(f32)).astype(bf16)
    pass_s[0:2] = two_sum(keep_ref[2:4], low_ref[2:4])
    pass_s[2:4] = two_sum(keep_ref[6:8], top_ref[2:4])

    def rest(low, at):
        part = pl.ds(0 if low else 2, 2)
        lanes = pl.ds(at * wide, wide)
        side = 0 if low else 1
        return _send(
            pass_s.at[part, :, lanes],
            come_rest.at[part, :, lanes],
            rest_send.at[side, at],
            rest_recv.at[side, at],
            two_way if low else one_way,
        )

    for at in range(FINISH_CUTS):
        rest(True, at).start()
        rest(False, at).start()
    rows = hidden_ref.shape[0]
    half = rows // 2

    def term(step, low):
        here = pl.ds(step * rows + (0 if low else half), half)
        return lax.dot_general(grad_ref[here, :], weight_ref[...], NT, preferred_element_type=f32)

    def move(slot):
        return _send(away.at[slot], come.at[slot], send_sem.at[slot], recv_sem.at[slot], ways[slot])

    ways = (one_way, two_way, one_way, two_way, two_way, one_way)
    for slot, (step, low) in enumerate(((3, True), (3, False), (1, True), (2, False))):
        away[slot] = term(step, low).astype(bf16)
        move(slot).start()
    own_s[0:2] = two_sum(keep_ref[0:2], low_ref[0:2])
    own_s[2:4] = two_sum(keep_ref[4:6], top_ref[0:2])

    def cross(step, at):
        lanes = pl.ds(at * wide, wide)
        return _send(
            away_z.at[step - 1, :, lanes],
            come_z.at[step - 1, :, lanes],
            z_send.at[step - 1, at],
            z_recv.at[step - 1, at],
            over(step),
        )

    def rest_on(at):
        rest(True, at).wait_recv()
        rest(False, at).wait_recv()
        lanes = pl.ds(at * wide, wide)
        for step in range(4):
            total = own_s[plane(step), :, lanes].astype(f32) + come_rest[plane(step), :, lanes].astype(f32)
            if step:
                away_z[step - 1, :, lanes] = total.astype(bf16)
                cross(step, at).start()
            else:
                rest_ref[:, lanes] = total

    for at in range(FINISH_CUTS // 3):
        rest_on(at)
    swap_core = _qkv_grad(
        grad_ref, (x0_ref, x1_ref, x2_ref, x3_ref), q_acc, q_all, q_come, q_send.at[0], q_recv.at[0]
    )
    for at in range(FINISH_CUTS // 3, FINISH_CUTS // 3 * 2):
        rest_on(at)
    swap_core.wait_recv()
    q_mine[...] = (q_all[:, core].astype(f32) + q_come[...].astype(f32)).astype(bf16)
    q_cross = [
        _send(q_mine.at[plane(step)], q_z.at[step - 1], q_send.at[step], q_recv.at[step], over(step))
        for step in range(1, 4)
    ]
    _start(q_cross)
    for at in range(FINISH_CUTS // 3 * 2, FINISH_CUTS):
        rest_on(at)
    pass_low = term(2, True)
    pass_top = term(1, False)
    move(0).wait_recv()
    away[4] = (pass_low + come[0].astype(f32)).astype(bf16)
    move(4).start()
    move(1).wait_recv()
    away[5] = (pass_top + come[1].astype(f32)).astype(bf16)
    move(5).start()
    sums_ref[...] = jnp.zeros_like(sums_ref)
    for low in (True, False):
        here = pl.ds(0 if low else half, half)
        own = term(0, low)
        unit, scale = _norm(hidden_ref[here, :])
        near, far = (2, 4) if low else (3, 5)
        move(near).wait_recv()
        move(far).wait_recv()
        grad = own + come[near].astype(f32) + come[far].astype(f32)
        sums_ref[0:1, :] += jnp.sum(grad * unit, axis=0, keepdims=True)
        sums_ref[1:2, :] += jnp.sum(grad, axis=0, keepdims=True)
        out_ref[here, :] = after_ref[here, :] + _norm_pull(grad * gain_ref[0:1, :], unit, scale)
    for copy in q_cross:
        copy.wait_recv()
    total = q_mine[zed].astype(f32)
    for step in range(3):
        total = total + q_z[step].astype(f32)
    q_sum[...] = total.astype(bf16).reshape(q_sum.shape)
    q_home = go_home(q_sum, q_land, 3)
    _start(q_home)

    def settle(target, at, values):
        width = values.shape[1] // 3
        for part in range(3):
            lanes = pl.ds(pl.multiple_of(part * D + at * width, 128), width)
            target[:, lanes] = values[:, part * width : (part + 1) * width].astype(f32)

    settle(qkv_ref, head, q_sum[head])
    settle(qkv_one_ref, head, one_ref[head])
    for step, copy in enumerate(one_home):
        copy.wait_recv()
        settle(qkv_one_ref, mate_at(step + 1), one_land[mate_at(step + 1)])
    for at in range(FINISH_CUTS):
        lanes = pl.ds(at * wide, wide)
        for step in range(1, 4):
            cross(step, at).wait_recv()
            rest_ref[:, lanes] += come_z[step - 1, :, lanes].astype(f32)
    for step, copy in enumerate(q_home):
        copy.wait_recv()
        settle(qkv_ref, mate_at(step + 1), q_land[mate_at(step + 1)])
    lax.fori_loop(1, n, tile_wait, 0)
    vec_ref[...] = tiles_ref[me] + jnp.sum(land[1:], axis=0)
    square = square_ref[0:1, 0:1]
    for ref in (rest_ref, vec_ref, qkv_ref, qkv_one_ref):
        square = square + jnp.sum(ref[...] * ref[...], keepdims=True)
    tile_s[0:8, :] = jnp.broadcast_to(square, (8, 128))
    for at in range(16):
        first = at % 8 * 128
        tile_s[8 + at : 9 + at, :] = sums_ref[at // 8 : at // 8 + 1, first : first + 128]
    all_ref[me] = tile_s[...]

    def norm_tile(step):
        _, _, device = _peer(step, n_tok, n_head)
        return _send(tile_s, all_ref.at[me], n_send.at[step], n_recv.at[step], device)

    def norm_start(step, _):
        norm_tile(step).start()
        return 0

    def norm_wait(step, _):
        norm_tile(step).wait()
        return 0

    lax.fori_loop(1, n, norm_start, 0)
    lax.fori_loop(1, n, norm_wait, 0)
    for copy in [swap_core] + q_cross + q_home + one_home:
        copy.wait_send()
    for slot in range(6):
        move(slot).wait_send()
    for at in range(FINISH_CUTS):
        rest(True, at).wait_send()
        rest(False, at).wait_send()
        for step in range(1, 4):
            cross(step, at).wait_send()


def finish(grad, weight, hidden, after, gain, pieces, parts, tiles, mine_one, square, n_tok, n_head, collective_id):
    rows = hidden.shape[0]
    n = n_tok * n_head
    unit_rows, width = D // n, grad.shape[1]
    vmem = pl.BlockSpec(memory_space=pltpu.VMEM)
    hbm = pl.BlockSpec(memory_space=pl.ANY)
    sems = pltpu.SemaphoreType.DMA
    buffer = pltpu.VMEM((6, rows // 2, D), bf16)
    tok_rows = unit_rows * n_head
    low = lambda *shape: pltpu.VMEM(shape, bf16)
    return pl.pallas_call(
        functools.partial(finish_kernel, n_tok, n_head),
        out_shape=(
            jax.ShapeDtypeStruct((rows, D), f32),
            jax.ShapeDtypeStruct((8, D), f32),
            jax.ShapeDtypeStruct((unit_rows, WIDE), f32),
            jax.ShapeDtypeStruct((unit_rows, 3 * D), f32),
            jax.ShapeDtypeStruct((unit_rows, 3 * D), f32),
            jax.ShapeDtypeStruct(tiles.shape[1:], f32),
            jax.ShapeDtypeStruct((n, 24, 128), f32),
        ),
        in_specs=[vmem] * 15,
        out_specs=(vmem,) * 7,
        scratch_shapes=[
            low(4, unit_rows, WIDE),
            low(4, unit_rows, WIDE),
            pltpu.VMEM((24, 128), f32),
            buffer,
            buffer,
            low(4, unit_rows, WIDE),
            low(3, unit_rows, WIDE),
            low(3, unit_rows, WIDE),
            pltpu.VMEM((D, width), f32),
            low(4, 2, tok_rows, width),
            low(4, tok_rows, width),
            low(4, tok_rows, width),
            low(3, tok_rows, width),
            low(n_head, unit_rows, width),
            low(n_head, unit_rows, width),
            low(n_head, unit_rows, width),
            pltpu.VMEM(tiles.shape, f32),
            sems((6,)),
            sems((6,)),
            sems((2, FINISH_CUTS)),
            sems((2, FINISH_CUTS)),
            sems((3, FINISH_CUTS)),
            sems((3, FINISH_CUTS)),
            sems((10,)),
            sems((10,)),
            sems((n,)),
            sems((n,)),
            sems((n,)),
            sems((n,)),
        ],
        compiler_params=pltpu.CompilerParams(
            collective_id=collective_id, has_side_effects=True, vmem_limit_bytes=VMEM_BYTES
        ),
        cost_estimate=pl.CostEstimate(flops=0, bytes_accessed=250 << 20, transcendentals=0),
    )(grad, weight, hidden, after, gain, *pieces, *parts, tiles, mine_one.reshape(n_head, unit_rows, width), square)


def pack_kernel(n_head, *refs):
    out_ref, refs = refs[-1], refs[:-1]
    own = lax.axis_index("head")
    out_ref[...] = jnp.zeros_like(out_ref)
    for block in range(2):
        norm_ref, sums_ref, up_ref, head_ref, bias_ref = refs[5 * block : 5 * block + 5]
        width = head_ref.shape[1]
        per = width // 128

        def lay(first, ref, row, count, start=0):
            for at in range(count):
                lanes = slice(start + at * 128, start + (at + 1) * 128)
                out_ref[block, pl.ds(first + at, 1), :] = ref[row : row + 1, lanes]

        count = D // 128
        lay(0, norm_ref, 0, count)
        lay(count, norm_ref, 1, count)
        for part in range(3):
            lay(2 * count + part * count + own * per, bias_ref, 0, per, part * width)
        for at, row in ((5, 5), (6, 4), (7, 2), (8, 3)):
            lay(at * count, sums_ref, row, count)
        lay(9 * count, up_ref, 0, FF // 128)
        tail = 9 * count + FF // 128
        lay(tail, sums_ref, 1, count)
        lay(tail + count, sums_ref, 0, count)
        folded = head_ref[0:4, 0:128]
        for at in range(1, per):
            folded = folded + head_ref[0:4, at * 128 : (at + 1) * 128]
        folded = folded + jnp.concatenate([folded[:, HD:], folded[:, :HD]], axis=1)
        lane = lax.broadcasted_iota(jnp.int32, (1, 128), 1)
        for at in range(2):
            pair = jnp.where(lane < HD, folded[2 * at : 2 * at + 1], folded[2 * at + 1 : 2 * at + 2])
            out_ref[block, pl.ds(tail + 2 * count + at, 1), :] = pair


def pack(parts, n_head):
    vmem = pl.BlockSpec(memory_space=pltpu.VMEM)
    return pl.pallas_call(
        functools.partial(pack_kernel, n_head),
        out_shape=jax.ShapeDtypeStruct((2, (11 * D + FF + 4 * HD) // 128, 128), f32),
        in_specs=[vmem] * 10,
        out_specs=vmem,
    )(*parts)


def layer_norm(values, gain, shift):
    centered = values - jnp.mean(values, axis=-1, keepdims=True)
    spread_ = jnp.mean(centered * centered, axis=-1, keepdims=True)
    return centered * lax.rsqrt(spread_ + norm_eps) * gain + shift


def unpack(vector_row):
    lengths = (D, D, 3 * D, D, D, D, D, FF, D, D, HD, HD, HD, HD)
    pieces = []
    offset = 0
    for length in lengths:
        pieces.append(vector_row[offset : offset + length])
        offset = offset + length
    return pieces


def head_gains(vec, heads):
    rows = [jnp.tile(piece, heads) for piece in vec[10:14]]
    return jnp.concatenate([jnp.stack(rows), jnp.zeros((4, heads * HD), f32)], axis=0)


def adam_update(
    weight, gradient, moment_one, moment_two, average, step_rate, decay_rate, clip_scale, fix_one, fix_two
):
    clipped = gradient * clip_scale
    moment_one = beta_one * moment_one + (1.0 - beta_one) * clipped
    moment_two = beta_two * moment_two + (1.0 - beta_two) * clipped * clipped
    first_hat = moment_one / fix_one
    second_hat = moment_two / fix_two
    weight = weight - step_rate * (
        first_hat / (jnp.sqrt(second_hat) + adam_eps) + decay_rate * weight
    )
    average = ema_decay * average + (1.0 - ema_decay) * weight
    return (weight, moment_one, moment_two, average)


def body(
    links,
    tokens,
    cotangent,
    slot_frame,
    step_count,
    *params,
):
    n_tok, n_head = links.n_tok, links.n_head
    devices = n_tok * n_head
    own = lax.axis_index("head")
    flip = lambda leaf: jnp.swapaxes(leaf, 1, 2)
    groups = []
    for at in range(0, 20, 5):
        qkv, proj, fc1, fc2, vec = params[at : at + 5]
        groups.append([qkv, flip(proj), fc1, flip(fc2), vec])
    masters = groups[0]

    slots = slot_frame.shape[0]
    per_head = slots // n_head
    held = slot_frame.reshape(n_head, per_head)
    held = jnp.concatenate(
        [lax.dynamic_slice_in_dim(held, own ^ step, 1, 0)[0] for step in range(n_head)]
    )
    index = jnp.arange(slots, dtype=jnp.int32)
    ahead = (held[None, :] < held[:, None]) | (
        (held[None, :] == held[:, None]) & (index[None, :] < index[:, None])
    )
    rank = jnp.sum(ahead.astype(jnp.int32), axis=1)
    order = jnp.sum(jnp.where(rank[None, :] == index[:, None], index[None, :], 0), axis=1).astype(jnp.int32)
    is_hi = (jnp.sum((held == held[0]).astype(jnp.int32)) == HI_BLOCKS).astype(jnp.int32).reshape(1)
    spans = (
        (HI_BLOCKS * BLOCK, LO_BLOCKS * BLOCK),
        (FRAMES * HI_BLOCKS * BLOCK, FRAMES * LO_BLOCKS * BLOCK),
    )

    vec_here = masters[4].shape[1]
    tile = lax.reduce_precision(masters[4], 8, 7).reshape(-1)
    tile = jnp.pad(tile, (0, 1024 - tile.shape[0])).reshape(8, 128)
    tiles = spread(tile, n_tok, n_head, 0).reshape(devices, 1024)[:, : 2 * vec_here]
    vectors = jnp.swapaxes(tiles.reshape(devices, 2, vec_here), 0, 1).reshape(2, devices * vec_here)
    vecs = [unpack(vectors[block]) for block in range(2)]

    qkv_low = [masters[0][block].astype(bf16) for block in range(2)]
    low = [
        jnp.concatenate([masters[kind][block].astype(bf16) for kind in (1, 2, 3)], axis=1)
        for block in range(2)
    ]
    places = links.gather_places()
    paired = links.paired
    width = D // n_head
    heads = width // HD
    own_rows = tokens.shape[0]
    cut = lambda rows: [rows[step * own_rows : (step + 1) * own_rows] for step in range(n_head)]
    gains = [head_gains(vec, heads) for vec in vecs]

    def attend(block, pieces, qkv_cols):
        qkv_bias = lax.dynamic_slice_in_dim(vecs[block][2].reshape(3, D), own * width, width, 1)
        return attention_forward(
            pieces, qkv_cols, qkv_bias.reshape(1, 3 * width), gains[block], order, is_hi, spans[block]
        )

    def enter(rows, mine, shard, collective_id):
        if paired:
            return enter_rows(rows, mine, shard, collective_id)
        planes = None if shard is None else links.gather_planes(shard)
        return links.rows_in(rows), lax.all_gather(mine, "tok", axis=0, tiled=True), planes

    def post(block, attended, hidden, pieces):
        vec, tail = vecs[block], vecs[1]
        rows = jnp.stack([vec[3], vec[4], vec[5], vec[6], vec[8], vec[9], tail[0], tail[1]])
        if not paired:
            attended = jnp.concatenate(links.by_index(links.exchange(cut(attended)), own), axis=1)
        return post_forward(
            attended,
            hidden,
            rows,
            vec[7].reshape(1, FF),
            (pieces, places),
            n_head,
            block == 1,
            paired,
            3 + block,
        )

    hidden_in = [tokens.astype(f32), None]
    normed = layer_norm(hidden_in[0], vecs[0][0], vecs[0][1]).astype(bf16)
    group, qkv_cols, saved, att_owns, mids, weights = ([None, None] for _ in range(6))

    mine = links.fetch_heads(qkv_low, own)
    normed, mine, low[0] = together(normed, mine, low[0])
    group[0], qkv_cols[0], planes = enter(normed, mine[0], low[0], 5)
    group[0], planes, qkv_cols[0], low[1] = together(group[0], planes, qkv_cols[0], low[1])
    near = links.gather_sides(planes)
    saved[0] = attend(0, group[0], qkv_cols[0])
    saved[0], near, low[1] = together(saved[0], near, low[1])
    planes = links.gather_planes(low[1])
    (hidden_in[1], normed, *mids[0]), weights[0] = post(0, saved[0][0], hidden_in[0], near)
    normed, planes = together(normed, planes)

    group[1], qkv_cols[1], _planes = enter(normed, mine[1], None, 6)
    group[1], planes = together(group[1], planes)
    near = links.gather_sides(planes)
    saved[1] = attend(1, group[1], qkv_cols[1])
    saved[1], near = together(saved[1], near)
    (hidden, _normed, *mids[1]), weights[1] = post(1, saved[1][0], hidden_in[1], near)

    def post_back(block, grad):
        vec = vecs[block]
        down, act, slope, branch, after, two, att_own = mids[block]
        rows = jnp.stack([vec[4], vec[5], vec[9]] + [vec[9]] * 5)
        d_att, *rest = post_backward(
            att_own,
            grad,
            down,
            branch,
            after,
            two,
            rows,
            act,
            slope,
            (weights[block], places),
            n_head,
            paired,
            7 + block,
        )
        if not paired:
            parts = [
                lax.dynamic_slice_in_dim(d_att, (own ^ step) * width, width, 1) for step in range(n_head)
            ]
            d_att = jnp.concatenate(links.exchange(parts), axis=0)
        return d_att, *rest

    def attend_back(block, grad_heads):
        attended, raw, values, lse = saved[block]
        return attention_backward(
            raw, values, grad_heads, attended, lse, gains[block], order, is_hi, spans[block]
        )

    def rows_back(block, d_qkv, d_after):
        gain, shift = vecs[block][0], vecs[block][1]
        if paired:
            grad, sums, mine = rows_out(
                d_qkv, qkv_cols[block], hidden_in[block], d_after, gain.reshape(1, D), group[block], 9 + block
            )
            return grad, mine, sums
        d_normed = jnp.einsum("rc,dc->rd", d_qkv, qkv_cols[block], preferred_element_type=f32)
        back = links.rows_out(cut(d_normed.astype(bf16)))
        d_hidden, d_gain, d_shift = jax.vjp(layer_norm, hidden_in[block], gain, shift)[1](back)
        sums = jnp.concatenate([jnp.stack([d_gain, d_shift]), jnp.zeros((6, D), f32)], axis=0)
        return d_after + d_hidden, qkv_grad(block, d_qkv), sums

    def qkv_grad(block, d_qkv):
        rows = jnp.concatenate(group[block], axis=0)
        return jnp.einsum("rd,rc->dc", rows, d_qkv, preferred_element_type=f32).astype(bf16)

    d_att, d_after, sums, d_up_bias, grads = post_back(1, cotangent.astype(f32))
    grads = links.scatter_first(grads)
    d_qkv, head_sums, bias_sums = attend_back(1, d_att)
    d_qkv, head_sums, bias_sums, grads = together(d_qkv, head_sums, bias_sums, grads)
    grads = links.scatter_add(grads)
    grad_rows, dw_qkv, norm_sums = rows_back(1, d_qkv, d_after)
    parts_one = [norm_sums, sums, d_up_bias, head_sums, bias_sums]
    grad_rows, grads, dw_qkv = together(grad_rows, grads, dw_qkv)
    grads_one = links.scatter_second(grads)
    mine_one = links.return_planes(dw_qkv)

    d_att, d_after, sums, d_up_bias, grads = post_back(0, grad_rows)
    d_att, grads_one, mine_one, grads = together(d_att, grads_one, mine_one, grads)
    sum_one = links.scatter_last(grads_one)
    grads = links.scatter_first(grads)
    d_qkv, head_sums, bias_sums = attend_back(0, d_att)
    d_qkv, head_sums, bias_sums, grads, sum_one = together(d_qkv, head_sums, bias_sums, grads, sum_one)
    vec_shape = (devices, 2 * vec_here)

    def tiles_of(norm_sums):
        both = pack([norm_sums, sums, d_up_bias, head_sums, bias_sums] + parts_one, n_head)
        flat = jnp.swapaxes(both.reshape(2, devices, vec_here), 0, 1).reshape(vec_shape)
        return jnp.pad(flat, ((0, 0), (0, 1024 - vec_shape[1]))).reshape(devices, 8, 128)

    if paired:
        tiles = tiles_of(jnp.zeros((8, D), f32))
        gain = vecs[0][0].reshape(1, D)
        square = jnp.broadcast_to(jnp.sum(sum_one * sum_one), (8, 128))
        grad_rows, _sums, sum_zero, qkv_zero, qkv_one, d_vec, squares = finish(
            d_qkv,
            qkv_cols[0],
            hidden_in[0],
            d_after,
            gain,
            group[0],
            grads,
            tiles,
            mine_one,
            square,
            n_tok,
            n_head,
            11,
        )
    else:
        grad_rows, dw_qkv, norm_sums = rows_back(0, d_qkv, d_after)
        tiles = tiles_of(norm_sums)
        d_vec = swap(tiles, n_tok, n_head, 1)
        sum_zero = links.scatter_last(links.scatter_second(links.scatter_add(grads)))
        qkv_zero, qkv_one = links.return_heads([links.return_planes(dw_qkv), mine_one], own)
    summed = []
    for qkv_part, rest in ((qkv_zero, sum_zero), (qkv_one, sum_one)):
        summed.append([qkv_part, rest[:, PROJ_AT:UP_AT], rest[:, UP_AT:DOWN_AT], rest[:, DOWN_AT:WIDE]])
    d_vec = d_vec.reshape(1024)[: 2 * vec_here].reshape(2, vec_here)
    gradients = [jnp.stack([summed[0][kind], summed[1][kind]]) for kind in range(4)]
    if not paired:
        local_square = sum((jnp.sum(gradient * gradient) for gradient in gradients)) + jnp.sum(d_vec * d_vec)
        tile = jnp.concatenate([jnp.broadcast_to(local_square, (8, 128)), jnp.zeros((16, 128), f32)], axis=0)
        squares = spread(tile, n_tok, n_head, 2)
    late = jnp.sum(squares[:, 8:], axis=0).reshape(2 * D)
    grad_norm = jnp.sqrt(jnp.sum(squares[:, 0, 0]) + jnp.sum(late * late))
    if paired:
        flat = jnp.concatenate([late, jnp.zeros((devices * vec_here - 2 * D,), f32)]).reshape(devices, vec_here)
        mine_late = lax.dynamic_slice_in_dim(flat, lax.axis_index("tok") * n_head + own, 1, 0)
        d_vec = d_vec + jnp.concatenate([mine_late, jnp.zeros((1, vec_here), f32)], axis=0)
    gradients.append(d_vec)
    clip_scale = clip_norm / jnp.maximum(grad_norm, clip_norm)
    step_float = step_count[0].astype(f32)
    fix_one = 1.0 - beta_one**step_float
    fix_two = 1.0 - beta_two**step_float
    updates = [
        adam_update(
            groups[0][kind],
            gradients[kind],
            groups[1][kind],
            groups[2][kind],
            groups[3][kind],
            step_rates[kind],
            decays[kind],
            clip_scale,
            fix_one,
            fix_two,
        )
        for kind in range(5)
    ]
    outs = [hidden, grad_rows, grad_norm]
    for part in range(4):
        for kind in range(5):
            leaf = updates[kind][part]
            outs.append(flip(leaf) if kind in (1, 3) else leaf)
    return tuple(outs)


def solution(mesh):
    rows = P(BOTH, None)
    kinds = (
        P(None, BOTH, None),
        P(None, None, BOTH),
        P(None, BOTH, None),
        P(None, None, BOTH),
        P(None, BOTH),
    )
    in_specs = (rows, rows, P("tok"), P()) + kinds * 4
    out_specs = (rows, rows, P()) + kinds * 4
    return jax.shard_map(
        functools.partial(body, Links(mesh)),
        mesh=mesh,
        in_specs=in_specs,
        out_specs=out_specs,
        check_vma=False,
    )
```

```python
import functools
import math

import jax
import jax.numpy as jnp
from jax import lax
from jax.experimental import pallas as pl
from jax.experimental.pallas import tpu as pltpu
from jax.sharding import PartitionSpec as P

D = 1024
HD = 64
FF = 4096
BLOCK = 128
HI_BLOCKS = 8
LO_BLOCKS = 4
FRAMES = 2

norm_eps = 1e-06
clip_norm = 1.0
beta_one = 0.9
beta_two = 0.999
adam_eps = 1e-08
ema_decay = 0.7
step_rates = (0.05, 0.4, 0.05, 0.025, 0.3)
decays = (0.05, 0.05, 0.05, 0.05, 0.0)

LOG2E = math.log2(math.e)
SPAN = 512
MESH_ID = pl.DeviceIdType.MESH
BOTH = ("tok", "head")
bf16 = jnp.bfloat16
f32 = jnp.float32
VMEM_BYTES = 60 << 20


def _peer(step, n_tok, n_head):
    n = n_tok * n_head
    me = lax.axis_index("tok") * n_head + lax.axis_index("head")
    to = lax.rem(me + step, n)
    return me, to, (to // n_head, lax.rem(to, n_head))


def _enter(n_tok, n_head):
    n = n_tok * n_head
    barrier = pltpu.get_barrier_semaphore()

    def greet(step, _):
        _, _, device = _peer(step, n_tok, n_head)
        pl.semaphore_signal(barrier, inc=1, device_id=device, device_id_type=MESH_ID)
        return 0

    lax.fori_loop(1, n, greet, 0)
    pl.semaphore_wait(barrier, n - 1)


def spread_kernel(n_tok, n_head, x_ref, o_ref, send_sem, recv_sem):
    n = n_tok * n_head
    _enter(n_tok, n_head)
    me = lax.axis_index("tok") * n_head + lax.axis_index("head")
    o_ref[me] = x_ref[...]

    def copy(step):
        me, _, device = _peer(step, n_tok, n_head)
        return pltpu.make_async_remote_copy(
            src_ref=x_ref,
            dst_ref=o_ref.at[me],
            send_sem=send_sem.at[step],
            recv_sem=recv_sem.at[step],
            device_id=device,
            device_id_type=MESH_ID,
        )

    def start(step, _):
        copy(step).start()
        return 0

    def finish(step, _):
        copy(step).wait()
        return 0

    lax.fori_loop(1, n, start, 0)
    lax.fori_loop(1, n, finish, 0)


def swap_kernel(n_tok, n_head, x_ref, o_ref, land, send_sem, recv_sem):
    n = n_tok * n_head
    _enter(n_tok, n_head)
    me = lax.axis_index("tok") * n_head + lax.axis_index("head")

    def copy(step):
        me, to, device = _peer(step, n_tok, n_head)
        return pltpu.make_async_remote_copy(
            src_ref=x_ref.at[to],
            dst_ref=land.at[step],
            send_sem=send_sem.at[step],
            recv_sem=recv_sem.at[step],
            device_id=device,
            device_id_type=MESH_ID,
        )

    def start(step, _):
        copy(step).start()
        return 0

    def finish(step, _):
        copy(step).wait()
        return 0

    lax.fori_loop(1, n, start, 0)
    lax.fori_loop(1, n, finish, 0)
    o_ref[...] = x_ref[me] + jnp.sum(land[1:], axis=0)


def spread(tile, n_tok, n_head, collective_id):
    n = n_tok * n_head
    return pl.pallas_call(
        functools.partial(spread_kernel, n_tok, n_head),
        out_shape=jax.ShapeDtypeStruct((n,) + tile.shape, tile.dtype),
        in_specs=[pl.BlockSpec(memory_space=pltpu.VMEM)],
        out_specs=pl.BlockSpec(memory_space=pltpu.VMEM),
        scratch_shapes=[pltpu.SemaphoreType.DMA((n,)), pltpu.SemaphoreType.DMA((n,))],
        compiler_params=pltpu.CompilerParams(collective_id=collective_id, has_side_effects=True),
    )(tile)


def swap(tiles, n_tok, n_head, collective_id):
    n = n_tok * n_head
    return pl.pallas_call(
        functools.partial(swap_kernel, n_tok, n_head),
        out_shape=jax.ShapeDtypeStruct(tiles.shape[1:], tiles.dtype),
        in_specs=[pl.BlockSpec(memory_space=pltpu.VMEM)],
        out_specs=pl.BlockSpec(memory_space=pltpu.VMEM),
        scratch_shapes=[
            pltpu.VMEM(tiles.shape, tiles.dtype),
            pltpu.SemaphoreType.DMA((n,)),
            pltpu.SemaphoreType.DMA((n,)),
        ],
        compiler_params=pltpu.CompilerParams(collective_id=collective_id, has_side_effects=True),
    )(tiles)


def _lane_mean(values, grouping):
    top = values.astype(bf16)
    rest = (values - top.astype(f32)).astype(bf16)
    return jnp.dot(top, grouping, preferred_element_type=f32) + jnp.dot(
        rest, grouping, preferred_element_type=f32
    )


def _grouping(width):
    row = lax.broadcasted_iota(jnp.int32, (width, width), 0) // HD
    col = lax.broadcasted_iota(jnp.int32, (width, width), 1) // HD
    return jnp.where(row == col, 1.0 / HD, 0.0).astype(bf16)


def _unit(values, grouping):
    centered = values - _lane_mean(values, grouping)
    spread_ = _lane_mean(centered * centered, grouping)
    scale = lax.rsqrt(spread_ + norm_eps)
    return centered * scale, scale


def _only(values, head):
    lane = lax.broadcasted_iota(jnp.int32, values.shape, 1)
    return jnp.where(lane // HD == head, values, jnp.zeros_like(values))


NT = (((1,), (1,)), ((), ()))
TN = (((0,), (0,)), ((), ()))


def forward_kernel(
    heads, pieces, spans, tile_rows, order_ref, hi_ref, *refs
):
    x_refs = refs[:pieces]
    w_ref, bias_ref, gains_ref, att_ref, raw_ref, val_ref, lse_ref, q_s, k_s, v_s, acc = refs[pieces:]
    width = heads * HD
    rows = att_ref.shape[0]
    blocks = rows // BLOCK
    piece_rows = rows // pieces
    for at in range(pieces):
        full = jnp.dot(x_refs[at][...], w_ref[...], preferred_element_type=f32) + bias_ref[...]
        here = pl.ds(at * piece_rows, piece_rows)
        raw_ref[here, :] = full[:, : 2 * width]
        val_ref[here, :] = full[:, 2 * width :].astype(bf16)
    grouping = _grouping(width)

    def place(at, _):
        here = pl.ds(pl.multiple_of(order_ref[at] * BLOCK, BLOCK), BLOCK)
        there = pl.ds(pl.multiple_of(at * BLOCK, BLOCK), BLOCK)
        unit_q, _s = _unit(raw_ref[here, :width], grouping)
        unit_k, _s = _unit(raw_ref[here, width:], grouping)
        q_s[there, :] = ((unit_q * gains_ref[0:1, :] + gains_ref[1:2, :]) * HD ** (-0.5)).astype(bf16)
        key = (unit_k * gains_ref[2:3, :] + gains_ref[3:4, :]).astype(bf16)
        value = val_ref[here, :]
        for head in range(heads):
            k_s[head, there, :] = _only(key, head)
            v_s[head, there, :] = _only(value, head)
        return 0

    lax.fori_loop(0, blocks, place, 0)
    per_tile = tile_rows // BLOCK

    def attend(span):
        def tile(at, _):
            here = pl.ds(pl.multiple_of(at * tile_rows, tile_rows), tile_rows)
            first = at * tile_rows // span * span
            there = pl.ds(pl.multiple_of(first, span), span)
            query = q_s[here, :]
            lane = lax.broadcasted_iota(jnp.int32, (tile_rows, 128), 1)
            logs = jnp.zeros((tile_rows, 128), f32)
            for head in range(heads):
                scores = lax.dot_general(query, k_s[head, there, :], NT, preferred_element_type=f32)
                top = jnp.max(scores, axis=1, keepdims=True) * LOG2E
                probs = jnp.exp2(scores * LOG2E - top)
                total = jnp.sum(probs, axis=1, keepdims=True)
                part = jnp.dot(
                    probs.astype(bf16), v_s[head, there, :], preferred_element_type=f32
                ) / total
                if head == 0:
                    acc[...] = part
                else:
                    acc[...] += part
                logs = jnp.where(lane == head, top + jnp.log2(total), logs)
            lse_ref[here, :] = logs
            for sub in range(per_tile):
                out = pl.ds(pl.multiple_of(order_ref[at * per_tile + sub] * BLOCK, BLOCK), BLOCK)
                att_ref[out, :] = acc[sub * BLOCK : (sub + 1) * BLOCK, :].astype(bf16)
            return 0

        lax.fori_loop(0, rows // tile_rows, tile, 0)

    @pl.when(hi_ref[0] == 1)
    def _():
        attend(spans[0])

    @pl.when(hi_ref[0] == 0)
    def _():
        attend(spans[1])


def attention_forward(pieces, weight, bias, gains, order, is_hi, spans):
    heads = weight.shape[1] // (3 * HD)
    width = heads * HD
    rows = sum(piece.shape[0] for piece in pieces)
    tile_rows = 512
    smem = pl.BlockSpec(memory_space=pltpu.SMEM)
    vmem = pl.BlockSpec(memory_space=pltpu.VMEM)
    flops = 2 * rows * (D * 3 * width + 8 * spans[0] * width)
    return pl.pallas_call(
        functools.partial(forward_kernel, heads, len(pieces), spans, tile_rows),
        out_shape=(
            jax.ShapeDtypeStruct((rows, width), bf16),
            jax.ShapeDtypeStruct((rows, 2 * width), f32),
            jax.ShapeDtypeStruct((rows, width), bf16),
            jax.ShapeDtypeStruct((rows, 128), f32),
        ),
        in_specs=[smem, smem] + [vmem] * (len(pieces) + 3),
        out_specs=(vmem,) * 4,
        scratch_shapes=[
            pltpu.VMEM((rows, width), bf16),
            pltpu.VMEM((heads, rows, width), bf16),
            pltpu.VMEM((heads, rows, width), bf16),
            pltpu.VMEM((tile_rows, width), f32),
        ],
        compiler_params=pltpu.CompilerParams(vmem_limit_bytes=VMEM_BYTES),
        cost_estimate=pl.CostEstimate(
            flops=flops, bytes_accessed=rows * (2 * D + 14 * width), transcendentals=rows * spans[0] * heads
        ),
    )(order, is_hi, *pieces, weight, bias, gains)


def backward_kernel(
    heads,
    spans,
    order_ref,
    hi_ref,
    raw_ref,
    val_ref,
    grad_ref,
    att_ref,
    lse_ref,
    gains_ref,
    out_ref,
    sums_ref,
    bias_ref,
    q_s,
    o_s,
    k_m,
    v_m,
    q_m,
    o_m,
    dq_s,
    dk_s,
    dv_s,
    lse_t,
    delta_t,
):
    width = heads * HD
    rows = val_ref.shape[0]
    blocks = rows // BLOCK
    grouping = _grouping(width)
    head_of = lax.broadcasted_iota(jnp.int32, (8, width), 1) // HD
    picks = jnp.where(head_of == lax.broadcasted_iota(jnp.int32, (8, width), 0), 1.0, 0.0).astype(bf16)

    def place(at, _):
        here = pl.ds(pl.multiple_of(order_ref[at] * BLOCK, BLOCK), BLOCK)
        there = pl.ds(pl.multiple_of(at * BLOCK, BLOCK), BLOCK)
        unit_q, _s = _unit(raw_ref[here, :width], grouping)
        unit_k, _s = _unit(raw_ref[here, width:], grouping)
        query = ((unit_q * gains_ref[0:1, :] + gains_ref[1:2, :]) * HD ** (-0.5)).astype(bf16)
        key = (unit_k * gains_ref[2:3, :] + gains_ref[3:4, :]).astype(bf16)
        value = val_ref[here, :]
        grad = grad_ref[here, :]
        q_s[there, :] = query
        o_s[there, :] = grad
        for head in range(heads):
            k_m[head, there, :] = _only(key, head)
            v_m[head, there, :] = _only(value, head)
            q_m[head, there, :] = _only(query, head)
            o_m[head, there, :] = _only(grad, head)
        both = grad.astype(f32) * att_ref[here, :].astype(f32)
        top = both.astype(bf16)
        rest = (both - top.astype(f32)).astype(bf16)
        delta_t[:, there] = lax.dot_general(picks, top, NT, preferred_element_type=f32) + lax.dot_general(
            picks, rest, NT, preferred_element_type=f32
        )
        lse_t[:, there] = jnp.transpose(lse_ref[there, :])[:8, :]
        dq_s[there, :] = jnp.zeros((BLOCK, width), f32)
        dk_s[there, :] = jnp.zeros((BLOCK, width), f32)
        dv_s[there, :] = jnp.zeros((BLOCK, width), f32)
        return 0

    lax.fori_loop(0, blocks, place, 0)
    span = jnp.where(hi_ref[0] == 1, spans[0], spans[1])

    def tile(at, _):
        here = pl.ds(pl.multiple_of(at * SPAN, SPAN), SPAN)
        first = at * SPAN // span * span // SPAN

        def chunk(key_at, _):
            there = pl.ds(pl.multiple_of(key_at * SPAN, SPAN), SPAN)
            for head in range(heads):
                scores = lax.dot_general(k_m[head, there, :], q_s[here, :], NT, preferred_element_type=f32)
                probs = jnp.exp2(scores * LOG2E - lse_t[head : head + 1, here])
                grad_probs = lax.dot_general(
                    v_m[head, there, :], o_s[here, :], NT, preferred_element_type=f32
                )
                grad_scores = (probs * (grad_probs - delta_t[head : head + 1, here])).astype(bf16)
                dv_s[there, :] += jnp.dot(probs.astype(bf16), o_m[head, here, :], preferred_element_type=f32)
                dk_s[there, :] += jnp.dot(grad_scores, q_m[head, here, :], preferred_element_type=f32)
                dq_s[here, :] += lax.dot_general(
                    grad_scores, k_m[head, there, :], TN, preferred_element_type=f32
                )
            return 0

        lax.fori_loop(first, first + span // SPAN, chunk, 0)
        return 0

    lax.fori_loop(0, rows // SPAN, tile, 0)
    sums_ref[...] = jnp.zeros_like(sums_ref)
    bias_ref[...] = jnp.zeros_like(bias_ref)

    def pull(grad, unit, scale, gain):
        grad_unit = grad * gain
        inner = _lane_mean(grad_unit, grouping)
        cross = _lane_mean(grad_unit * unit, grouping)
        return scale * (grad_unit - inner - unit * cross)

    def leave(at, _):
        here = pl.ds(pl.multiple_of(order_ref[at] * BLOCK, BLOCK), BLOCK)
        there = pl.ds(pl.multiple_of(at * BLOCK, BLOCK), BLOCK)
        unit_q, scale_q = _unit(raw_ref[here, :width], grouping)
        unit_k, scale_k = _unit(raw_ref[here, width:], grouping)
        grad_q = dq_s[there, :] * HD ** (-0.5)
        grad_k = dk_s[there, :]
        sums_ref[0:1, :] += jnp.sum(grad_q * unit_q, axis=0, keepdims=True)
        sums_ref[1:2, :] += jnp.sum(grad_q, axis=0, keepdims=True)
        sums_ref[2:3, :] += jnp.sum(grad_k * unit_k, axis=0, keepdims=True)
        sums_ref[3:4, :] += jnp.sum(grad_k, axis=0, keepdims=True)
        low_q = pull(grad_q, unit_q, scale_q, gains_ref[0:1, :]).astype(bf16)
        low_k = pull(grad_k, unit_k, scale_k, gains_ref[2:3, :]).astype(bf16)
        low_v = dv_s[there, :].astype(bf16)
        for part, low in enumerate((low_q, low_k, low_v)):
            lanes = slice(part * width, (part + 1) * width)
            out_ref[here, lanes] = low
            bias_ref[0:1, lanes] += jnp.sum(low.astype(f32), axis=0, keepdims=True)
        return 0

    lax.fori_loop(0, blocks, leave, 0)


def attention_backward(raw, values, grad, attended, lse, gains, order, is_hi, spans):
    rows, width = values.shape
    heads = width // HD
    smem = pl.BlockSpec(memory_space=pltpu.SMEM)
    vmem = pl.BlockSpec(memory_space=pltpu.VMEM)
    flops = 2 * rows * 20 * spans[0] * width
    masked = pltpu.VMEM((heads, rows, width), bf16)
    return pl.pallas_call(
        functools.partial(backward_kernel, heads, spans),
        out_shape=(
            jax.ShapeDtypeStruct((rows, 3 * width), bf16),
            jax.ShapeDtypeStruct((8, width), f32),
            jax.ShapeDtypeStruct((8, 3 * width), f32),
        ),
        in_specs=[smem, smem] + [vmem] * 6,
        out_specs=(vmem,) * 3,
        scratch_shapes=[
            pltpu.VMEM((rows, width), bf16),
            pltpu.VMEM((rows, width), bf16),
            masked,
            masked,
            masked,
            masked,
            pltpu.VMEM((rows, width), f32),
            pltpu.VMEM((rows, width), f32),
            pltpu.VMEM((rows, width), f32),
            pltpu.VMEM((8, rows), f32),
            pltpu.VMEM((8, rows), f32),
        ],
        compiler_params=pltpu.CompilerParams(vmem_limit_bytes=VMEM_BYTES),
        cost_estimate=pl.CostEstimate(
            flops=flops, bytes_accessed=rows * 24 * width, transcendentals=rows * spans[0] * heads
        ),
    )(order, is_hi, raw, values, grad, attended, lse, gains)


class Links:
    def __init__(self, mesh):
        self.n_tok = mesh.shape["tok"]
        self.n_head = mesh.shape["head"]
        self.paired = self.n_tok == 8 and self.n_head == 4

    def head(self, values, step):
        return lax.ppermute(values, "head", [(i, i ^ step) for i in range(self.n_head)])

    def tok(self, values, step):
        return lax.ppermute(values, "tok", [(i, i ^ step) for i in range(self.n_tok)])

    def rows_in(self, rows):
        if not self.paired:
            return [rows] + [self.head(rows, step) for step in range(1, self.n_head)]
        half = rows.shape[0] // 2
        one, two = self.head(rows, 1), self.head(rows, 2)
        far = jnp.concatenate([self.head(one[:half], 2), self.head(two[half:], 1)], axis=0)
        return [rows, one, two, far]

    def rows_out(self, parts):
        if not self.paired:
            moved = [self.head(parts[step], step).astype(f32) for step in range(1, self.n_head)]
            return parts[0].astype(f32) + sum(moved)
        half = parts[0].shape[0] // 2
        upper = [part[:half] for part in parts]
        lower = [part[half:] for part in parts]
        pass_up = (upper[2].astype(f32) + self.head(upper[3], 1).astype(f32)).astype(bf16)
        pass_low = (lower[1].astype(f32) + self.head(lower[3], 2).astype(f32)).astype(bf16)
        up = upper[0].astype(f32) + self.head(upper[1], 1).astype(f32) + self.head(pass_up, 2).astype(f32)
        low = lower[0].astype(f32) + self.head(lower[2], 2).astype(f32) + self.head(pass_low, 1).astype(f32)
        return jnp.concatenate([up, low], axis=0)

    def exchange(self, parts):
        return [parts[0]] + [self.head(parts[step], step) for step in range(1, self.n_head)]

    def by_index(self, pieces, own):
        return [
            lax.select_n((own ^ at).astype(jnp.int32), *pieces) if len(pieces) > 1 else pieces[0]
            for at in range(len(pieces))
        ]

    def zed(self):
        return lax.axis_index("tok") // 2

    def core(self):
        return lax.rem(lax.axis_index("tok"), 2)

    def planes(self, shard):
        pieces = [shard] + [self.tok(shard, 2 * step) for step in range(1, 4)]
        return jnp.stack(self.by_index(pieces, self.zed()))

    def gather_places(self):
        if not self.paired:
            return [None]
        spots = ((0, 4, 0), (0, 4, 1), (0, 4, 2), (0, 2, 3), (2, 2, 3))
        return [("head", first, count, core, to) for first, count, to in spots for core in range(2)]

    def gather_planes(self, shard):
        if not self.paired:
            whole = lax.all_gather(shard, BOTH, axis=0, tiled=True)
            return [whole.reshape(4, 2, 4, whole.shape[0] // 32, whole.shape[1])]
        return [self.planes(shard)]

    def gather_sides(self, own):
        if not self.paired:
            return own
        return [own[0], self.head(own[0], 1), self.head(own[0], 2)]

    def scatter_first(self, grads):
        if not self.paired:
            return grads
        low, top, keep = grads
        return [keep, self.head(low, 1), self.head(top, 2)]

    def scatter_add(self, grads):
        if not self.paired:
            return grads
        keep, low, top = grads
        plus = lambda one, two: (one.astype(f32) + two.astype(f32)).astype(bf16)
        own = [plus(keep[:2], low[:2]), plus(keep[4:6], top[:2])]
        return [own, [plus(keep[2:4], low[2:]), plus(keep[6:], top[2:])]]

    def scatter_second(self, halves):
        if not self.paired:
            return halves
        own, passed = halves
        low = own[0].astype(f32) + self.head(passed[0], 2).astype(f32)
        top = own[1].astype(f32) + self.head(passed[1], 1).astype(f32)
        return [jnp.concatenate([low, top], axis=0).astype(bf16)]

    def scatter_last(self, planes):
        if not self.paired:
            whole = planes[0].reshape(-1, planes[0].shape[-1])
            return lax.psum_scatter(whole, BOTH, scatter_dimension=0, tiled=True).astype(f32)
        return self.sum_planes(planes[0])

    def sum_planes(self, parts):
        zed = self.zed()
        pick = lambda step: lax.dynamic_slice_in_dim(parts, zed ^ step, 1, 0)[0]
        total = pick(0).astype(f32)
        for step in range(1, 4):
            total = total + self.tok(pick(step).astype(bf16), 2 * step).astype(f32)
        return total

    def fetch_heads(self, shards, own):
        own_rows = shards[0].shape[0]
        width = D // self.n_head
        cut = jnp.stack(shards).reshape(len(shards), own_rows, 3, D)
        parts = [
            lax.dynamic_slice_in_dim(cut, (own ^ step) * width, width, 3).reshape(
                len(shards), own_rows, 3 * width
            )
            for step in range(self.n_head)
        ]
        moved = jnp.stack(self.by_index(self.exchange(parts), own), axis=1)
        return [moved[at].reshape(self.n_head * own_rows, 3 * width) for at in range(len(shards))]

    def return_planes(self, grad):
        if not self.paired:
            return lax.psum_scatter(grad, "tok", scatter_dimension=0, tiled=True)
        return self.sum_planes(grad).astype(bf16)

    def return_heads(self, both, own):
        width = D // self.n_head
        stack = jnp.stack(both)
        own_rows = stack.shape[1] // self.n_head
        parts = [
            lax.dynamic_slice_in_dim(stack, (own ^ step) * own_rows, own_rows, 1)
            for step in range(self.n_head)
        ]
        back = jnp.stack(self.by_index(self.exchange(parts), own), axis=2)
        back = back.reshape(len(both), own_rows, self.n_head, 3, width)
        return jnp.swapaxes(back, 2, 3).reshape(len(both), own_rows, 3 * D).astype(f32)


def together(*values):
    return lax.optimization_barrier(values)


CHUNK = 512


def _paired(value, step, bits):
    total = 0
    for bit in range(bits):
        one = lax.rem(value // (1 << bit), 2)
        total = total + (1 - one if (step >> bit) % 2 else one) * (1 << bit)
    return total


def _slot(ref, place):
    if place is None:
        return ref
    tok = lax.axis_index("tok")
    side = _paired(lax.rem(tok, 2), place[-1] if place[0] == "plane" else place[3], 1)
    if place[0] == "plane":
        return ref.at[_paired(tok // 2, place[1], 2), side]
    return ref.at[pl.ds(place[1], place[2]), side, _paired(lax.axis_index("head"), place[4], 2)]


PROJ_AT, UP_AT, DOWN_AT, WIDE = 0, D, D + FF, D + 2 * FF


def _cols(ref, at, size):
    window = pl.ds(pl.multiple_of(at, 128), size)
    return ref.at[(slice(None),) * (len(ref.shape) - 1) + (window,)]


def _copies(pieces, places, whole, at, size, sems, inward):
    moves = []
    for index, (piece, place) in enumerate(zip(pieces, places)):
        outside = _cols(piece, at, size)
        inside = _slot(whole, place)
        pair = (outside, inside) if inward else (inside, outside)
        moves.append(pltpu.make_async_copy(pair[0], pair[1], sems.at[index]))
    return moves


def _start(moves):
    for move in moves:
        move.start()


def _wait(moves):
    for move in moves:
        move.wait()


def _flat(values):
    return values.reshape(D, values.shape[-1])


def _norm(values):
    centered = values - jnp.mean(values, axis=-1, keepdims=True)
    scale = lax.rsqrt(jnp.mean(centered * centered, axis=-1, keepdims=True) + norm_eps)
    return centered * scale, scale


def _own_column(step, n_head):
    at = _paired(lax.axis_index("head"), step, n_head.bit_length() - 1)
    return pl.multiple_of(at * (D // n_head), 128)


def _mate(step):
    return lax.axis_index("tok"), _paired(lax.axis_index("head"), step, 2)


def _sibling():
    return _paired(lax.axis_index("tok"), 1, 3), lax.axis_index("head")


def _greet(devices):
    barrier = pltpu.get_barrier_semaphore()
    for device in devices:
        pl.semaphore_signal(barrier, inc=1, device_id=device, device_id_type=MESH_ID)
    pl.semaphore_wait(barrier, len(devices))


def _send(source, target, send_sem, recv_sem, device):
    return pltpu.make_async_remote_copy(
        src_ref=source,
        dst_ref=target,
        send_sem=send_sem,
        recv_sem=recv_sem,
        device_id=device,
        device_id_type=MESH_ID,
    )


def enter_kernel(wide, *refs):
    x_ref, q_ref, refs = refs[0], refs[1], refs[2:]
    if wide:
        shard_ref, refs = refs[0], refs[1:]
    one_ref, two_ref, far_ref, full_ref, refs = *refs[:4], refs[4:]
    if wide:
        planes_ref, refs = refs[0], refs[1:]
    send_sem, recv_sem, z_send, z_recv, own_sem, core_sem = refs
    tok, head = lax.axis_index("tok"), lax.axis_index("head")
    zed, core = tok // 2, lax.rem(tok, 2)
    one_way, two_way = _mate(1), _mate(2)
    barrier = pltpu.get_barrier_semaphore()
    greet = lambda device: pl.semaphore_signal(barrier, inc=1, device_id=device, device_id_type=MESH_ID)
    for device in (one_way, two_way, _sibling()):
        greet(device)

    @pl.when(zed < 3)
    def _():
        greet((tok + 2, head))

    @pl.when(zed > 0)
    def _():
        greet((tok - 2, head))

    edge = (zed == 0) | (zed == 3)

    @pl.when(edge)
    def _():
        pl.semaphore_wait(barrier, 4)

    @pl.when(jnp.logical_not(edge))
    def _():
        pl.semaphore_wait(barrier, 5)

    rows = x_ref.shape[0]
    parts = 4
    size = rows // parts

    def move(lane, part, source, target, device):
        here = pl.ds(part * size, size)
        return _send(source.at[here], target.at[here], send_sem.at[lane, part], recv_sem.at[lane, part], device)

    to_one = lambda part: move(0, part, x_ref, one_ref, one_way)
    to_two = lambda part: move(1, part, x_ref, two_ref, two_way)
    on_two = lambda part: move(2, part, one_ref, far_ref, two_way)
    on_one = lambda part: move(2, part, two_ref, far_ref, one_way)
    homes = [(q_ref, lambda plane: full_ref.at[plane, core])]
    if wide:
        homes.append((shard_ref, lambda plane: planes_ref.at[plane]))

    def climb(up, step):
        plane = jnp.clip(zed - step if up else zed + step, 0, 3)
        device = (jnp.clip(tok + 2 if up else tok - 2, 0, 7), head)
        return [
            _send(
                home(plane) if step else source,
                home(plane),
                z_send.at[int(up), step, index],
                z_recv.at[int(up), step, index],
                device,
            )
            for index, (source, home) in enumerate(homes)
        ]

    def sends(up, step):
        return (zed >= step) & (zed < 3) if up else (zed <= 3 - step) & (zed > 0)

    def comes(up, step):
        return zed >= step + 1 if up else zed <= 2 - step

    def climb_start(up, step):
        @pl.when(sends(up, step))
        def _():
            _start(climb(up, step))

    def climb_come(up, step):
        @pl.when(comes(up, step))
        def _():
            for copy in climb(up, step):
                copy.wait_recv()

    for turn in range(parts):
        to_one(turn).start()
        to_two(parts - 1 - turn).start()
    for up in (True, False):
        climb_start(up, 0)
    stays = [
        pltpu.make_async_copy(source, home(zed), own_sem.at[index]) for index, (source, home) in enumerate(homes)
    ]
    _start(stays)
    for turn in range(parts // 2):
        to_one(turn).wait_recv()
        on_two(turn).start()
        to_two(parts - 1 - turn).wait_recv()
        on_one(parts - 1 - turn).start()
    for step in range(3):
        for up in (True, False):
            climb_come(up, step)
            if step < 2:
                climb_start(up, step + 1)
    _wait(stays)
    mine = full_ref.at[:, core]
    over = _send(mine, mine, core_sem.at[0], core_sem.at[1], _sibling())
    over.start()
    for turn in range(parts // 2, parts):
        to_one(turn).wait_recv()
        to_two(parts - 1 - turn).wait_recv()
    for turn in range(parts):
        to_one(turn).wait_send()
        to_two(turn).wait_send()
    for turn in range(parts // 2):
        on_two(turn).wait()
        on_one(parts - 1 - turn).wait()
    for step in range(3):
        for up in (True, False):

            @pl.when(sends(up, step))
            def _():
                for copy in climb(up, step):
                    copy.wait_send()

    over.wait()


def enter_rows(rows, mine, shard, collective_id):
    hbm = pl.BlockSpec(memory_space=pl.ANY)
    like = jax.ShapeDtypeStruct(rows.shape, rows.dtype)
    outs = [like, like, like, jax.ShapeDtypeStruct((4, 2) + mine.shape, mine.dtype)]
    given = [rows, mine]
    if shard is not None:
        outs.append(jax.ShapeDtypeStruct((4,) + shard.shape, shard.dtype))
        given.append(shard)
    sems = pltpu.SemaphoreType.DMA
    one, two, far, full, *planes = pl.pallas_call(
        functools.partial(enter_kernel, shard is not None),
        out_shape=tuple(outs),
        in_specs=[hbm] * len(given),
        out_specs=(hbm,) * len(outs),
        scratch_shapes=[sems((3, 4)), sems((3, 4)), sems((2, 3, 2)), sems((2, 3, 2)), sems((2,)), sems((2,))],
        compiler_params=pltpu.CompilerParams(collective_id=collective_id, has_side_effects=True),
        cost_estimate=pl.CostEstimate(flops=0, bytes_accessed=150 << 20, transcendentals=0),
    )(*given)
    return [rows, one, two, far], full.reshape(8 * mine.shape[0], mine.shape[1]), planes


def _norm_pull(grad_unit, unit, scale):
    inner = jnp.mean(grad_unit, axis=-1, keepdims=True)
    cross = jnp.mean(grad_unit * unit, axis=-1, keepdims=True)
    return scale * (grad_unit - inner - unit * cross)


def _qkv_grad(grad_ref, x_refs, total, low, come, send_sem, recv_sem):
    rows = x_refs[0].shape[0]
    for step, x_ref in enumerate(x_refs):
        part = lax.dot_general(
            x_ref[...], grad_ref[step * rows : (step + 1) * rows, :], TN, preferred_element_type=f32
        )
        if step:
            total[...] += part
        else:
            total[...] = part
    low[...] = total[...].astype(bf16).reshape(low.shape)
    core = lax.rem(lax.axis_index("tok"), 2)
    swap_core = _send(low.at[:, 1 - core], come, send_sem, recv_sem, _sibling())
    swap_core.start()
    return swap_core


def rows_out_kernel(
    grad_ref,
    weight_ref,
    hidden_ref,
    after_ref,
    gain_ref,
    x0_ref,
    x1_ref,
    x2_ref,
    x3_ref,
    out_ref,
    sums_ref,
    mine_ref,
    away,
    come,
    q_acc,
    q_all,
    q_come,
    send_sem,
    recv_sem,
    q_sem,
):
    one_way, two_way = _mate(1), _mate(2)
    _greet([one_way, two_way, _sibling()])
    rows = hidden_ref.shape[0]
    half = rows // 2

    def term(step, low):
        here = pl.ds(step * rows + (0 if low else half), half)
        return lax.dot_general(grad_ref[here, :], weight_ref[...], NT, preferred_element_type=f32)

    def move(slot, device):
        return _send(away.at[slot], come.at[slot], send_sem.at[slot], recv_sem.at[slot], device)

    ways = (one_way, two_way, one_way, two_way, two_way, one_way)
    for slot, (step, low) in enumerate(((3, True), (3, False), (1, True), (2, False))):
        away[slot] = term(step, low).astype(bf16)
        move(slot, ways[slot]).start()
    pass_low = term(2, True)
    pass_top = term(1, False)
    core = lax.rem(lax.axis_index("tok"), 2)
    swap_core = _qkv_grad(grad_ref, (x0_ref, x1_ref, x2_ref, x3_ref), q_acc, q_all, q_come, q_sem.at[0], q_sem.at[1])
    move(0, ways[0]).wait_recv()
    away[4] = (pass_low + come[0].astype(f32)).astype(bf16)
    move(4, ways[4]).start()
    move(1, ways[1]).wait_recv()
    away[5] = (pass_top + come[1].astype(f32)).astype(bf16)
    move(5, ways[5]).start()
    sums_ref[...] = jnp.zeros_like(sums_ref)
    for low in (True, False):
        here = pl.ds(0 if low else half, half)
        own = term(0, low)
        unit, scale = _norm(hidden_ref[here, :].astype(f32))
        near, far = (2, 4) if low else (3, 5)
        move(near, ways[near]).wait_recv()
        move(far, ways[far]).wait_recv()
        grad = own + come[near].astype(f32) + come[far].astype(f32)
        sums_ref[0:1, :] += jnp.sum(grad * unit, axis=0, keepdims=True)
        sums_ref[1:2, :] += jnp.sum(grad, axis=0, keepdims=True)
        out_ref[here, :] = after_ref[here, :] + _norm_pull(grad * gain_ref[0:1, :], unit, scale)
    swap_core.wait()
    mine_ref[...] = (q_all[:, core].astype(f32) + q_come[...].astype(f32)).astype(bf16)
    for slot in range(6):
        move(slot, ways[slot]).wait_send()


def rows_out(grad, weight, hidden, after, gain, pieces, collective_id):
    rows, width = hidden.shape[0], grad.shape[1]
    vmem = pl.BlockSpec(memory_space=pltpu.VMEM)
    buffer = pltpu.VMEM((6, rows // 2, D), bf16)
    sems = pltpu.SemaphoreType.DMA((6,))
    return pl.pallas_call(
        rows_out_kernel,
        out_shape=(
            jax.ShapeDtypeStruct((rows, D), f32),
            jax.ShapeDtypeStruct((8, D), f32),
            jax.ShapeDtypeStruct((4, D // 8, width), bf16),
        ),
        in_specs=[vmem] * 9,
        out_specs=(vmem, vmem, vmem),
        scratch_shapes=[
            buffer,
            buffer,
            pltpu.VMEM((D, width), f32),
            pltpu.VMEM((4, 2, D // 8, width), bf16),
            pltpu.VMEM((4, D // 8, width), bf16),
            sems,
            sems,
            pltpu.SemaphoreType.DMA((2,)),
        ],
        compiler_params=pltpu.CompilerParams(
            collective_id=collective_id, has_side_effects=True, vmem_limit_bytes=VMEM_BYTES
        ),
        cost_estimate=pl.CostEstimate(flops=0, bytes_accessed=150 << 20, transcendentals=0),
    )(grad, weight, hidden, after, gain, *pieces)


def post_forward_kernel(n_head, places, last, remote, *refs):
    count = len(places)
    att_ref, refs = refs[0], refs[1:]
    hidden_ref, rows_ref, up_bias_ref, refs = refs[0], refs[1], refs[2], refs[3:]
    given = 3 if remote else count
    weight_refs, refs = refs[:given], refs[given:]
    next_ref, normed_ref, down_ref, act_ref, slope_ref, branch_hbm, after_hbm, two_hbm, att_hbm, refs = *refs[:9], refs[9:]
    if remote:
        (own, one, two), (far_low, far_top), refs = weight_refs, refs[:2], refs[2:]
        side_own, side_one, side_two, side_low, side_top, refs = *refs[:5], refs[5:]
        weight_refs = (own, side_own, one, side_one, two, side_two, far_low, side_low, far_top, side_top)
    proj_s, up_s, down_s, att_s, branch_s, after_s, two_s, acc, proj_sem, up_sem, down_sem, out_sem, send_sem, recv_sem, refs = (
        *refs[:14],
        refs[14:],
    )
    at = pl.program_id(0)
    chunks = pl.num_programs(0)
    if remote:
        relay_send, relay_recv, side_send, side_recv = refs
        groups = WIDE // D
        order = [0] + [first for pair in zip(range(1, 1 + groups // 2), range(1 + groups // 2, groups)) for first in pair]

        def relay(group):
            part = lambda ref: _cols(ref, group * D, D)
            return [
                _send(
                    part(one.at[pl.ds(0, 2)]),
                    part(far_low),
                    relay_send.at[0, group],
                    relay_recv.at[0, group],
                    _mate(2),
                ),
                _send(
                    part(two.at[pl.ds(2, 2)]),
                    part(far_top),
                    relay_send.at[1, group],
                    relay_recv.at[1, group],
                    _mate(1),
                ),
            ]

        def across(group, pairs, first):
            return [
                _send(
                    _cols(source, group * D, D),
                    _cols(target, group * D, D),
                    side_send.at[first + index, group],
                    side_recv.at[first + index, group],
                    _sibling(),
                )
                for index, (source, target) in enumerate(pairs)
            ]

        near = lambda group: across(group, ((own, side_own), (one, side_one), (two, side_two)), 0)
        far = lambda group: across(group, ((far_low, side_low), (far_top, side_top)), 3)

        def advance(group):
            for copy in relay(group):
                copy.wait_recv()
            _start(far(group))

        def complete(group):
            for copy in near(group) + far(group):
                copy.wait_recv()

    def fetch(chunk, slot):
        up_at, down_at = UP_AT + chunk * CHUNK, DOWN_AT + chunk * CHUNK
        return _copies(weight_refs, places, up_s.at[slot], up_at, CHUNK, up_sem.at[slot], True) + _copies(
            weight_refs, places, down_s.at[slot], down_at, CHUNK, down_sem.at[slot], True
        )

    leaving = [
        pltpu.make_async_copy(branch_s, branch_hbm, out_sem.at[0]),
        pltpu.make_async_copy(after_s, after_hbm, out_sem.at[1]),
        pltpu.make_async_copy(two_s, two_hbm, out_sem.at[2]),
        pltpu.make_async_copy(att_s, att_hbm, out_sem.at[3]),
    ]

    @pl.when(at == 0)
    def _():
        proj = _copies(weight_refs, places, proj_s, PROJ_AT, D, proj_sem, True)
        if remote:
            width, rows = D // n_head, hidden_ref.shape[0]
            _greet([_mate(step) for step in range(1, n_head)] + [_sibling()])
            mine = att_s.at[:, pl.ds(_own_column(0, n_head), width)]
            moves = [
                _send(
                    att_ref.at[pl.ds(step * rows, rows)], mine, send_sem.at[step], recv_sem.at[step], _mate(step)
                )
                for step in range(1, n_head)
            ]
            moves.append(pltpu.make_async_copy(att_ref.at[pl.ds(0, rows)], mine, send_sem.at[0]))
            _start(moves)
            for group in order:
                _start(relay(group))
                _start(near(group))
            advance(order[0])
            _wait(moves)
            complete(order[0])
            _start(proj)
            for group in order[1:3]:
                advance(group)
        else:
            _start(proj)
            _start(fetch(0, 0))
            att_s[...] = att_ref[...]
        _wait(proj)
        branch = (
            lax.dot_general(att_s[...], _flat(proj_s[...]), NT, preferred_element_type=f32) + rows_ref[0:1, :]
        )
        branch_s[...] = branch
        after = hidden_ref[...].astype(f32) + rows_ref[1:2, :] * branch
        after_s[...] = after
        unit, _s = _norm(after)
        two_s[...] = (unit * rows_ref[2:3, :] + rows_ref[3:4, :]).astype(bf16)
        _start(leaving)
        if remote:
            for group in order[1:3]:
                complete(group)
            _start(fetch(0, 0))

    if remote:
        later = at // 2 + 2
        halves = groups // 2

        @pl.when((lax.rem(at, 2) == 0) & (later <= halves))
        def _():
            advance(later)
            advance(later + halves)

        @pl.when((lax.rem(at, 2) == 1) & (later <= halves))
        def _():
            complete(later)
            complete(later + halves)

    @pl.when(at + 1 < chunks)
    def _():
        _start(fetch(at + 1, lax.rem(at + 1, 2)))

    slot = lax.rem(at, 2)
    _wait(fetch(at, slot))
    expand = jnp.dot(two_s[...], _flat(up_s[slot]), preferred_element_type=f32) + up_bias_ref[...]
    cdf = 0.5 * (1.0 + lax.erf(expand * math.sqrt(0.5)))
    slope = cdf + expand * jnp.exp(-0.5 * expand * expand) * (1.0 / math.sqrt(2.0 * math.pi))
    act = (expand * cdf).astype(bf16)
    act_ref[...] = act
    slope_ref[...] = slope.astype(bf16)
    part = lax.dot_general(act, _flat(down_s[slot]), NT, preferred_element_type=f32)

    @pl.when(at == 0)
    def _():
        acc[...] = part

    @pl.when(at > 0)
    def _():
        acc[...] += part

    @pl.when(at == chunks - 1)
    def _():
        down = acc[...] + rows_ref[4:5, :]
        down_ref[...] = down
        hidden = after_s[...] + rows_ref[5:6, :] * down
        next_ref[...] = hidden
        if last:
            normed_ref[...] = jnp.zeros_like(normed_ref)
        else:
            unit, _s = _norm(hidden)
            normed_ref[...] = (unit * rows_ref[6:7, :] + rows_ref[7:8, :]).astype(bf16)
        _wait(leaving)
        if remote:
            for group in range(groups):
                for copy in relay(group) + near(group) + far(group):
                    copy.wait_send()


def _params(remote, collective_id):
    if not remote:
        return pltpu.CompilerParams(dimension_semantics=("arbitrary",), vmem_limit_bytes=VMEM_BYTES)
    return pltpu.CompilerParams(
        dimension_semantics=("arbitrary",),
        vmem_limit_bytes=VMEM_BYTES,
        collective_id=collective_id,
        has_side_effects=True,
    )


def post_forward(att, hidden, rows, up_bias, gathered, n_head, last, remote, collective_id):
    own_rows = hidden.shape[0]
    pieces, places = gathered
    count = len(places)
    unit_rows = D // 32
    vmem = pl.BlockSpec(memory_space=pltpu.VMEM)
    hbm = pl.BlockSpec(memory_space=pl.ANY)
    column = pl.BlockSpec((own_rows, CHUNK), lambda at: (0, at))
    fixed = lambda leaf_rows: pl.BlockSpec((leaf_rows, D), lambda at: (0, 0))
    whole = lambda dtype: jax.ShapeDtypeStruct((own_rows, D), dtype)
    wide = jax.ShapeDtypeStruct((own_rows, FF), bf16)
    weight = lambda *lead: pltpu.VMEM(lead + (4, 2, 4, unit_rows), bf16)
    normed_rows = 16 if last else own_rows
    landed, sems = [], []
    if remote:
        half, full = [
            jax.ShapeDtypeStruct((planes,) + pieces[0].shape[1:], bf16) for planes in (2, 4)
        ]
        landed = [half, half, full, full, full, half, half]
        for kinds in (2, 2, 5, 5):
            sems.append(pltpu.SemaphoreType.DMA((kinds, WIDE // D)))
    outs = pl.pallas_call(
        functools.partial(post_forward_kernel, n_head, places, last, remote),
        grid=(FF // CHUNK,),
        out_shape=(
            whole(f32),
            jax.ShapeDtypeStruct((normed_rows, D), bf16),
            whole(f32),
            wide,
            wide,
            whole(f32),
            whole(f32),
            whole(bf16),
            whole(bf16),
            *landed,
        ),
        in_specs=[hbm if remote else vmem, vmem, vmem, pl.BlockSpec((1, CHUNK), lambda at: (0, at))]
        + [hbm] * len(pieces),
        out_specs=(fixed(own_rows), fixed(normed_rows), fixed(own_rows), column, column)
        + (hbm,) * (4 + len(landed)),
        scratch_shapes=[
            pltpu.VMEM((4, 2, 4, unit_rows, D), bf16),
            pltpu.VMEM((2, 4, 2, 4, unit_rows, CHUNK), bf16),
            pltpu.VMEM((2, 4, 2, 4, unit_rows, CHUNK), bf16),
            pltpu.VMEM((own_rows, D), bf16),
            pltpu.VMEM((own_rows, D), f32),
            pltpu.VMEM((own_rows, D), f32),
            pltpu.VMEM((own_rows, D), bf16),
            pltpu.VMEM((own_rows, D), f32),
            pltpu.SemaphoreType.DMA((count,)),
            pltpu.SemaphoreType.DMA((2, count)),
            pltpu.SemaphoreType.DMA((2, count)),
            pltpu.SemaphoreType.DMA((4,)),
            pltpu.SemaphoreType.DMA((n_head,)),
            pltpu.SemaphoreType.DMA((n_head,)),
            *sems,
        ],
        compiler_params=_params(remote, collective_id),
        cost_estimate=pl.CostEstimate(
            flops=2 * own_rows * D * (D + 2 * FF),
            bytes_accessed=2 * D * (D + 2 * FF) + own_rows * (22 * D + 4 * FF),
            transcendentals=2 * own_rows * FF,
        ),
    )(att, hidden, rows, up_bias, *pieces)
    if remote:
        far_low, far_top, *sides = outs[9:]
        near = [*pieces, far_low, far_top]
        pieces = [piece for pair in zip(near, sides) for piece in pair]
    return list(outs[:9]), pieces


def post_backward_kernel(n_head, places, remote, *refs):
    count = len(places)
    far_places = [("head", 0, 4, 1, to) for to in range(4)] if remote else []
    out_count = 3 if remote else 1
    att_ref, grad_ref, down_ref, branch_ref, after_ref, two_ref, rows_ref, act_ref, slope_ref, refs = *refs[:9], refs[9:]
    weight_refs, refs = refs[:count], refs[count:]
    d_att_ref, d_after_ref, sums_ref, up_sum_ref, refs = *refs[:4], refs[4:]
    own_refs, refs = refs[:out_count], refs[out_count:]
    proj_s, up_s, down_s, d_proj_s, d_up_s, d_down_s, att_s, low_s, low_t, two_t, acc, refs = *refs[:11], refs[11:]
    proj_sem, up_sem, down_sem, own_sem, far_sem, got_sem, send_sem, recv_sem, refs = *refs[:8], refs[8:]
    if remote:
        stash, got = refs
        low_ref, top_ref, keep_ref = own_refs
    at = pl.program_id(0)
    chunks = pl.num_programs(0)
    width = D // n_head

    def fetch(chunk, slot):
        up_at, down_at = UP_AT + chunk * CHUNK, DOWN_AT + chunk * CHUNK
        return _copies(weight_refs, places, up_s.at[slot], up_at, CHUNK, up_sem.at[slot], True) + _copies(
            weight_refs, places, down_s.at[slot], down_at, CHUNK, down_sem.at[slot], True
        )

    def stay(whole, column, size, lane):
        return [] if remote else _copies(own_refs, [None], whole, column, size, own_sem.at[lane], False)

    def away(whole, column, size, lane, mark):
        return [
            _send(
                _slot(whole, place),
                _cols(got.at[to], column, size),
                far_sem.at[lane, to],
                got_sem.at[mark, to],
                _sibling(),
            )
            for to, place in enumerate(far_places)
        ]

    def over(chunk, slot):
        up_at, down_at = UP_AT + chunk * CHUNK, DOWN_AT + chunk * CHUNK
        return away(d_up_s.at[slot], up_at, CHUNK, slot, chunk) + away(
            d_down_s.at[slot], down_at, CHUNK, 2 + slot, chunks + chunk
        )

    def leave(chunk, slot):
        up_at, down_at = UP_AT + chunk * CHUNK, DOWN_AT + chunk * CHUNK
        local = stay(d_up_s.at[slot], up_at, CHUNK, slot) + stay(d_down_s.at[slot], down_at, CHUNK, 2 + slot)
        return local, over(chunk, slot)

    def left(pair):
        _wait(pair[0])
        for move in pair[1]:
            move.wait_send()

    def hold(staged, column, size):
        core, head = lax.rem(lax.axis_index("tok"), 2), lax.axis_index("head")
        for to in range(4):
            _cols(stash.at[to], column, size)[...] = staged[:, core, _paired(head, to, 2)]

    def add(column, size):
        mine, other = _cols(stash, column, size), _cols(got, column, size)
        for to in range(4):
            mine[to] = (mine[to].astype(f32) + other[to].astype(f32)).astype(bf16)

    def merge(chunk):
        for move in over(chunk, 0):
            move.wait_recv()
        add(UP_AT + chunk * CHUNK, CHUNK)
        add(DOWN_AT + chunk * CHUNK, CHUNK)

    def depart(column, size, lane):
        spots = (
            (low_ref, 0, 1, 0),
            (low_ref, 2, 3, 0),
            (top_ref, 0, 2, 2),
            (top_ref, 2, 3, 2),
            (keep_ref, 0, 0, 0),
            (keep_ref, 2, 2, 0),
            (keep_ref, 4, 0, 2),
            (keep_ref, 6, 1, 2),
        )
        return [
            pltpu.make_async_copy(
                _cols(stash.at[to, pl.ds(first, 2)], column, size),
                _cols(target.at[pl.ds(at_, 2)], column, size),
                own_sem.at[lane, index],
            )
            for index, (target, at_, to, first) in enumerate(spots)
        ]

    middle = FF // 2
    early = lambda: depart(UP_AT, middle, 0) + depart(DOWN_AT, middle, 1)

    proj = lambda: _copies(weight_refs, places, proj_s, PROJ_AT, D, proj_sem, True)

    @pl.when(at == 0)
    def _():
        if remote:
            _greet([_mate(step) for step in range(1, n_head)] + [_sibling()])
        _start(fetch(0, 0))
        _start(proj())
        grad = grad_ref[...].astype(f32)
        low = (rows_ref[2:3, :] * grad).astype(bf16)
        low_s[...] = low
        low_t[...] = jnp.transpose(low)
        two_t[...] = jnp.transpose(two_ref[...])
        sums_ref[...] = jnp.zeros_like(sums_ref)
        sums_ref[0:1, :] = jnp.sum(grad * down_ref[...], axis=0, keepdims=True)
        sums_ref[1:2, :] = jnp.sum(low.astype(f32), axis=0, keepdims=True)
        acc[...] = jnp.zeros_like(acc)

    @pl.when(at + 1 < chunks)
    def _():
        _start(fetch(at + 1, lax.rem(at + 1, 2)))

    slot = lax.rem(at, 2)
    _wait(fetch(at, slot))

    @pl.when(at >= 2)
    def _():
        left(leave(at - 2, slot))

    d_act = jnp.dot(low_s[...], _flat(down_s[slot]), preferred_element_type=f32)
    d_expand = (slope_ref[...].astype(f32) * d_act).astype(bf16)
    up_sum_ref[...] = jnp.sum(d_expand.astype(f32), axis=0, keepdims=True)
    acc[...] += lax.dot_general(d_expand, _flat(up_s[slot]), NT, preferred_element_type=f32)
    shape = d_up_s.shape[1:]
    d_up_s[slot] = jnp.dot(two_t[...], d_expand, preferred_element_type=f32).astype(bf16).reshape(shape)
    d_down_s[slot] = jnp.dot(low_t[...], act_ref[...], preferred_element_type=f32).astype(bf16).reshape(shape)
    for moves in leave(at, slot):
        _start(moves)
    if remote:
        hold(d_up_s.at[slot], UP_AT + at * CHUNK, CHUNK)
        hold(d_down_s.at[slot], DOWN_AT + at * CHUNK, CHUNK)

        @pl.when(at > 0)
        def _():
            merge(at - 1)

        @pl.when(at == chunks // 2)
        def _():
            _start(early())

    @pl.when(at == chunks - 1)
    def _():
        d_two = acc[...]
        unit, scale = _norm(after_ref[...])
        sums_ref[2:3, :] = jnp.sum(d_two * unit, axis=0, keepdims=True)
        sums_ref[3:4, :] = jnp.sum(d_two, axis=0, keepdims=True)
        d_unit = d_two * rows_ref[1:2, :]
        inner = jnp.mean(d_unit, axis=-1, keepdims=True)
        cross = jnp.mean(d_unit * unit, axis=-1, keepdims=True)
        d_after = grad_ref[...].astype(f32) + scale * (d_unit - inner - unit * cross)
        d_after_ref[...] = d_after
        sums_ref[4:5, :] = jnp.sum(d_after * branch_ref[...], axis=0, keepdims=True)
        d_branch = (rows_ref[0:1, :] * d_after).astype(bf16)
        sums_ref[5:6, :] = jnp.sum(d_branch.astype(f32), axis=0, keepdims=True)
        _wait(proj())
        d_att = jnp.dot(d_branch, _flat(proj_s[...]), preferred_element_type=f32).astype(bf16)
        if remote:
            rows = d_att.shape[0]
            att_s[...] = d_att
            moves = [
                _send(
                    att_s.at[:, pl.ds(_own_column(step, n_head), width)],
                    d_att_ref.at[pl.ds(step * rows, rows)],
                    send_sem.at[step],
                    recv_sem.at[step],
                    _mate(step),
                )
                for step in range(1, n_head)
            ]
            own = att_s.at[:, pl.ds(_own_column(0, n_head), width)]
            moves.append(pltpu.make_async_copy(own, d_att_ref.at[pl.ds(0, rows)], send_sem.at[0]))
            _start(moves)
        else:
            d_att_ref[...] = d_att
        d_proj_s[...] = (
            lax.dot_general(d_branch, att_ref[...], TN, preferred_element_type=f32)
            .astype(bf16)
            .reshape(d_proj_s.shape)
        )
        gone = stay(d_proj_s, PROJ_AT, D, 4), away(d_proj_s, PROJ_AT, D, 4, 2 * chunks)
        for group in gone:
            _start(group)
        if remote:
            hold(d_proj_s, PROJ_AT, D)
        left(leave(at - 1, 1 - slot))
        left(leave(at, slot))
        left(gone)
        if remote:
            merge(at)
            for move in gone[1]:
                move.wait_recv()
            add(PROJ_AT, D)
            late = (
                depart(UP_AT + middle, middle, 2) + depart(DOWN_AT + middle, middle, 3) + depart(PROJ_AT, D, 4)
            )
            _start(late)
            _wait(early())
            _wait(late)
            _wait(moves)


def post_backward(att, grad, down_out, branch, after, two, rows, act, slope, gathered, n_head, remote, collective_id):
    own_rows = grad.shape[0]
    pieces, places = gathered
    count = len(places)
    unit_rows = D // 32
    vmem = pl.BlockSpec(memory_space=pltpu.VMEM)
    hbm = pl.BlockSpec(memory_space=pl.ANY)
    column = pl.BlockSpec((own_rows, CHUNK), lambda at: (0, at))
    fixed = lambda *shape: pl.BlockSpec(shape, lambda at: (0, 0))
    width = D // n_head
    chunks = FF // CHUNK
    if remote:
        d_att_shape, d_att_spec = (n_head * own_rows, width), hbm
        grads = [jax.ShapeDtypeStruct((planes, unit_rows, WIDE), bf16) for planes in (4, 4, 8)]
        stashes = [pltpu.VMEM((4, 4, unit_rows, WIDE), bf16)] * 2
    else:
        d_att_shape, d_att_spec = (own_rows, D), fixed(own_rows, D)
        grads = [jax.ShapeDtypeStruct((4, 2, 4, unit_rows, WIDE), bf16)]
        stashes = []
    sems = pltpu.SemaphoreType.DMA
    outs = pl.pallas_call(
        functools.partial(post_backward_kernel, n_head, places, remote),
        grid=(chunks,),
        out_shape=tuple(
            [
                jax.ShapeDtypeStruct(d_att_shape, bf16),
                jax.ShapeDtypeStruct((own_rows, D), f32),
                jax.ShapeDtypeStruct((8, D), f32),
                jax.ShapeDtypeStruct((1, FF), f32),
            ]
            + grads
        ),
        in_specs=[vmem] * 7 + [column, column] + [hbm] * count,
        out_specs=tuple(
            [d_att_spec, fixed(own_rows, D), fixed(8, D), pl.BlockSpec((1, CHUNK), lambda at: (0, at))]
            + [hbm] * len(grads)
        ),
        scratch_shapes=[
            pltpu.VMEM((4, 2, 4, unit_rows, D), bf16),
            pltpu.VMEM((2, 4, 2, 4, unit_rows, CHUNK), bf16),
            pltpu.VMEM((2, 4, 2, 4, unit_rows, CHUNK), bf16),
            pltpu.VMEM((4, 2, 4, unit_rows, D), bf16),
            pltpu.VMEM((2, 4, 2, 4, unit_rows, CHUNK), bf16),
            pltpu.VMEM((2, 4, 2, 4, unit_rows, CHUNK), bf16),
            pltpu.VMEM((own_rows, D), bf16),
            pltpu.VMEM((own_rows, D), bf16),
            pltpu.VMEM((D, own_rows), bf16),
            pltpu.VMEM((D, own_rows), bf16),
            pltpu.VMEM((own_rows, D), f32),
            sems((count,)),
            sems((2, count)),
            sems((2, count)),
            sems((5, 8)),
            sems((5, 4)),
            sems((2 * chunks + 1, 4)),
            sems((n_head,)),
            sems((n_head,)),
            *stashes,
        ],
        compiler_params=_params(remote, collective_id),
        cost_estimate=pl.CostEstimate(
            flops=4 * own_rows * D * (D + 2 * FF),
            bytes_accessed=4 * D * (D + 2 * FF) + own_rows * (22 * D + 4 * FF),
            transcendentals=0,
        ),
    )(att, grad, down_out, branch, after, two, rows, act, slope, *pieces)
    d_att, d_after, sums, up_sum, grads = *outs[:4], list(outs[4:])
    return d_att, d_after, sums, up_sum, grads


FINISH_CUTS = 9


def finish_kernel(
    n_tok,
    n_head,
    grad_ref,
    weight_ref,
    hidden_ref,
    after_ref,
    gain_ref,
    x0_ref,
    x1_ref,
    x2_ref,
    x3_ref,
    keep_ref,
    low_ref,
    top_ref,
    tiles_ref,
    one_ref,
    square_ref,
    out_ref,
    sums_ref,
    rest_ref,
    qkv_ref,
    qkv_one_ref,
    vec_ref,
    all_ref,
    own_s,
    pass_s,
    tile_s,
    away,
    come,
    come_rest,
    away_z,
    come_z,
    q_acc,
    q_all,
    q_come,
    q_mine,
    q_z,
    q_sum,
    q_land,
    one_land,
    land,
    send_sem,
    recv_sem,
    rest_send,
    rest_recv,
    z_send,
    z_recv,
    q_send,
    q_recv,
    v_send,
    v_recv,
    n_send,
    n_recv,
):
    n = n_tok * n_head
    _enter(n_tok, n_head)
    tok = lax.axis_index("tok")
    head = lax.axis_index("head")
    me = tok * n_head + head
    zed, core = tok // 2, lax.rem(tok, 2)
    one_way, two_way = _mate(1), _mate(2)
    plane = lambda step: _paired(zed, step, 2)
    over = lambda step: (plane(step) * 2 + core, head)

    def tile(step):
        _, to, device = _peer(step, n_tok, n_head)
        return _send(tiles_ref.at[to], land.at[step], v_send.at[step], v_recv.at[step], device)

    def tile_start(step, _):
        tile(step).start()
        return 0

    def tile_wait(step, _):
        tile(step).wait()
        return 0

    lax.fori_loop(1, n, tile_start, 0)
    mate_at = lambda step: _paired(head, step, 2)

    def go_home(source, target, first):
        return [
            _send(
                source.at[mate_at(step)],
                target.at[head],
                q_send.at[first + step],
                q_recv.at[first + step],
                _mate(step),
            )
            for step in range(1, 4)
        ]

    one_home = go_home(one_ref, one_land, 6)
    _start(one_home)
    wide = keep_ref.shape[2] // FINISH_CUTS
    two_sum = lambda first, second: (first.astype(f32) + second.astype(f32)).astype(bf16)
    pass_s[0:2] = two_sum(keep_ref[2:4], low_ref[2:4])
    pass_s[2:4] = two_sum(keep_ref[6:8], top_ref[2:4])

    def rest(low, at):
        part = pl.ds(0 if low else 2, 2)
        lanes = pl.ds(at * wide, wide)
        side = 0 if low else 1
        return _send(
            pass_s.at[part, :, lanes],
            come_rest.at[part, :, lanes],
            rest_send.at[side, at],
            rest_recv.at[side, at],
            two_way if low else one_way,
        )

    for at in range(FINISH_CUTS):
        rest(True, at).start()
        rest(False, at).start()
    rows = hidden_ref.shape[0]
    half = rows // 2

    def term(step, low):
        here = pl.ds(step * rows + (0 if low else half), half)
        return lax.dot_general(grad_ref[here, :], weight_ref[...], NT, preferred_element_type=f32)

    def move(slot):
        return _send(away.at[slot], come.at[slot], send_sem.at[slot], recv_sem.at[slot], ways[slot])

    ways = (one_way, two_way, one_way, two_way, two_way, one_way)
    for slot, (step, low) in enumerate(((3, True), (3, False), (1, True), (2, False))):
        away[slot] = term(step, low).astype(bf16)
        move(slot).start()
    own_s[0:2] = two_sum(keep_ref[0:2], low_ref[0:2])
    own_s[2:4] = two_sum(keep_ref[4:6], top_ref[0:2])

    def cross(step, at):
        lanes = pl.ds(at * wide, wide)
        return _send(
            away_z.at[step - 1, :, lanes],
            come_z.at[step - 1, :, lanes],
            z_send.at[step - 1, at],
            z_recv.at[step - 1, at],
            over(step),
        )

    def rest_on(at):
        rest(True, at).wait_recv()
        rest(False, at).wait_recv()
        lanes = pl.ds(at * wide, wide)
        for step in range(4):
            total = own_s[plane(step), :, lanes].astype(f32) + come_rest[plane(step), :, lanes].astype(f32)
            if step:
                away_z[step - 1, :, lanes] = total.astype(bf16)
                cross(step, at).start()
            else:
                rest_ref[:, lanes] = total

    for at in range(FINISH_CUTS // 3):
        rest_on(at)
    swap_core = _qkv_grad(
        grad_ref, (x0_ref, x1_ref, x2_ref, x3_ref), q_acc, q_all, q_come, q_send.at[0], q_recv.at[0]
    )
    for at in range(FINISH_CUTS // 3, FINISH_CUTS // 3 * 2):
        rest_on(at)
    swap_core.wait_recv()
    q_mine[...] = (q_all[:, core].astype(f32) + q_come[...].astype(f32)).astype(bf16)
    q_cross = [
        _send(q_mine.at[plane(step)], q_z.at[step - 1], q_send.at[step], q_recv.at[step], over(step))
        for step in range(1, 4)
    ]
    _start(q_cross)
    for at in range(FINISH_CUTS // 3 * 2, FINISH_CUTS):
        rest_on(at)
    pass_low = term(2, True)
    pass_top = term(1, False)
    move(0).wait_recv()
    away[4] = (pass_low + come[0].astype(f32)).astype(bf16)
    move(4).start()
    move(1).wait_recv()
    away[5] = (pass_top + come[1].astype(f32)).astype(bf16)
    move(5).start()
    sums_ref[...] = jnp.zeros_like(sums_ref)
    for low in (True, False):
        here = pl.ds(0 if low else half, half)
        own = term(0, low)
        unit, scale = _norm(hidden_ref[here, :].astype(f32))
        near, far = (2, 4) if low else (3, 5)
        move(near).wait_recv()
        move(far).wait_recv()
        grad = own + come[near].astype(f32) + come[far].astype(f32)
        sums_ref[0:1, :] += jnp.sum(grad * unit, axis=0, keepdims=True)
        sums_ref[1:2, :] += jnp.sum(grad, axis=0, keepdims=True)
        out_ref[here, :] = after_ref[here, :] + _norm_pull(grad * gain_ref[0:1, :], unit, scale)
    for copy in q_cross:
        copy.wait_recv()
    total = q_mine[zed].astype(f32)
    for step in range(3):
        total = total + q_z[step].astype(f32)
    q_sum[...] = total.astype(bf16).reshape(q_sum.shape)
    q_home = go_home(q_sum, q_land, 3)
    _start(q_home)

    def settle(target, at, values):
        width = values.shape[1] // 3
        for part in range(3):
            lanes = pl.ds(pl.multiple_of(part * D + at * width, 128), width)
            target[:, lanes] = values[:, part * width : (part + 1) * width].astype(f32)

    settle(qkv_ref, head, q_sum[head])
    settle(qkv_one_ref, head, one_ref[head])
    for step, copy in enumerate(one_home):
        copy.wait_recv()
        settle(qkv_one_ref, mate_at(step + 1), one_land[mate_at(step + 1)])
    for at in range(FINISH_CUTS):
        lanes = pl.ds(at * wide, wide)
        for step in range(1, 4):
            cross(step, at).wait_recv()
            rest_ref[:, lanes] += come_z[step - 1, :, lanes].astype(f32)
    for step, copy in enumerate(q_home):
        copy.wait_recv()
        settle(qkv_ref, mate_at(step + 1), q_land[mate_at(step + 1)])
    lax.fori_loop(1, n, tile_wait, 0)
    vec_ref[...] = tiles_ref[me] + jnp.sum(land[1:], axis=0)
    square = jnp.zeros((1, 1), f32)
    for ref in (square_ref, rest_ref, vec_ref, qkv_ref, qkv_one_ref):
        square = square + jnp.sum(ref[...] * ref[...], keepdims=True)
    tile_s[0:8, :] = jnp.broadcast_to(square, (8, 128))
    for at in range(16):
        first = at % 8 * 128
        tile_s[8 + at : 9 + at, :] = sums_ref[at // 8 : at // 8 + 1, first : first + 128]
    all_ref[me] = tile_s[...]

    def norm_tile(step):
        _, _, device = _peer(step, n_tok, n_head)
        return _send(tile_s, all_ref.at[me], n_send.at[step], n_recv.at[step], device)

    def norm_start(step, _):
        norm_tile(step).start()
        return 0

    def norm_wait(step, _):
        norm_tile(step).wait()
        return 0

    lax.fori_loop(1, n, norm_start, 0)
    lax.fori_loop(1, n, norm_wait, 0)
    for copy in [swap_core] + q_cross + q_home + one_home:
        copy.wait_send()
    for slot in range(6):
        move(slot).wait_send()
    for at in range(FINISH_CUTS):
        rest(True, at).wait_send()
        rest(False, at).wait_send()
        for step in range(1, 4):
            cross(step, at).wait_send()


def finish(grad, weight, hidden, after, gain, pieces, parts, tiles, mine_one, square, n_tok, n_head, collective_id):
    rows = hidden.shape[0]
    n = n_tok * n_head
    unit_rows, width = D // n, grad.shape[1]
    vmem = pl.BlockSpec(memory_space=pltpu.VMEM)
    hbm = pl.BlockSpec(memory_space=pl.ANY)
    sems = pltpu.SemaphoreType.DMA
    buffer = pltpu.VMEM((6, rows // 2, D), bf16)
    tok_rows = unit_rows * n_head
    low = lambda *shape: pltpu.VMEM(shape, bf16)
    return pl.pallas_call(
        functools.partial(finish_kernel, n_tok, n_head),
        out_shape=(
            jax.ShapeDtypeStruct((rows, D), f32),
            jax.ShapeDtypeStruct((8, D), f32),
            jax.ShapeDtypeStruct((unit_rows, WIDE), f32),
            jax.ShapeDtypeStruct((unit_rows, 3 * D), f32),
            jax.ShapeDtypeStruct((unit_rows, 3 * D), f32),
            jax.ShapeDtypeStruct(tiles.shape[1:], f32),
            jax.ShapeDtypeStruct((n, 24, 128), f32),
        ),
        in_specs=[vmem] * 15,
        out_specs=(vmem,) * 7,
        scratch_shapes=[
            low(4, unit_rows, WIDE),
            low(4, unit_rows, WIDE),
            pltpu.VMEM((24, 128), f32),
            buffer,
            buffer,
            low(4, unit_rows, WIDE),
            low(3, unit_rows, WIDE),
            low(3, unit_rows, WIDE),
            pltpu.VMEM((D, width), f32),
            low(4, 2, tok_rows, width),
            low(4, tok_rows, width),
            low(4, tok_rows, width),
            low(3, tok_rows, width),
            low(n_head, unit_rows, width),
            low(n_head, unit_rows, width),
            low(n_head, unit_rows, width),
            pltpu.VMEM(tiles.shape, f32),
            sems((6,)),
            sems((6,)),
            sems((2, FINISH_CUTS)),
            sems((2, FINISH_CUTS)),
            sems((3, FINISH_CUTS)),
            sems((3, FINISH_CUTS)),
            sems((10,)),
            sems((10,)),
            sems((n,)),
            sems((n,)),
            sems((n,)),
            sems((n,)),
        ],
        compiler_params=pltpu.CompilerParams(
            collective_id=collective_id, has_side_effects=True, vmem_limit_bytes=VMEM_BYTES
        ),
        cost_estimate=pl.CostEstimate(flops=0, bytes_accessed=250 << 20, transcendentals=0),
    )(grad, weight, hidden, after, gain, *pieces, *parts, tiles, mine_one.reshape(n_head, unit_rows, width), square)


def pack_kernel(n_head, *refs):
    out_ref, refs = refs[-1], refs[:-1]
    own = lax.axis_index("head")
    out_ref[...] = jnp.zeros_like(out_ref)
    for block in range(2):
        norm_ref, sums_ref, up_ref, head_ref, bias_ref = refs[5 * block : 5 * block + 5]
        width = head_ref.shape[1]
        per = width // 128

        def lay(first, ref, row, count, start=0):
            for at in range(count):
                lanes = slice(start + at * 128, start + (at + 1) * 128)
                out_ref[block, pl.ds(first + at, 1), :] = ref[row : row + 1, lanes]

        count = D // 128
        lay(0, norm_ref, 0, count)
        lay(count, norm_ref, 1, count)
        for part in range(3):
            lay(2 * count + part * count + own * per, bias_ref, 0, per, part * width)
        for at, row in ((5, 5), (6, 4), (7, 2), (8, 3)):
            lay(at * count, sums_ref, row, count)
        lay(9 * count, up_ref, 0, FF // 128)
        tail = 9 * count + FF // 128
        lay(tail, sums_ref, 1, count)
        lay(tail + count, sums_ref, 0, count)
        folded = head_ref[0:4, 0:128]
        for at in range(1, per):
            folded = folded + head_ref[0:4, at * 128 : (at + 1) * 128]
        folded = folded + jnp.concatenate([folded[:, HD:], folded[:, :HD]], axis=1)
        lane = lax.broadcasted_iota(jnp.int32, (1, 128), 1)
        for at in range(2):
            pair = jnp.where(lane < HD, folded[2 * at : 2 * at + 1], folded[2 * at + 1 : 2 * at + 2])
            out_ref[block, pl.ds(tail + 2 * count + at, 1), :] = pair


def pack(parts, n_head):
    vmem = pl.BlockSpec(memory_space=pltpu.VMEM)
    return pl.pallas_call(
        functools.partial(pack_kernel, n_head),
        out_shape=jax.ShapeDtypeStruct((2, (11 * D + FF + 4 * HD) // 128, 128), f32),
        in_specs=[vmem] * 10,
        out_specs=vmem,
    )(*parts)


def layer_norm(values, gain, shift):
    centered = values - jnp.mean(values, axis=-1, keepdims=True)
    spread_ = jnp.mean(centered * centered, axis=-1, keepdims=True)
    return centered * lax.rsqrt(spread_ + norm_eps) * gain + shift


def unpack(vector_row):
    lengths = (D, D, 3 * D, D, D, D, D, FF, D, D, HD, HD, HD, HD)
    pieces = []
    offset = 0
    for length in lengths:
        pieces.append(vector_row[offset : offset + length])
        offset = offset + length
    return pieces


def head_gains(vec, heads):
    rows = [jnp.tile(piece, heads) for piece in vec[10:14]]
    return jnp.concatenate([jnp.stack(rows), jnp.zeros((4, heads * HD), f32)], axis=0)


def adam_update(
    weight, gradient, moment_one, moment_two, average, step_rate, decay_rate, clip_scale, fix_one, fix_two
):
    clipped = gradient * clip_scale
    moment_one = beta_one * moment_one + (1.0 - beta_one) * clipped
    moment_two = beta_two * moment_two + (1.0 - beta_two) * clipped * clipped
    first_hat = moment_one / fix_one
    second_hat = moment_two / fix_two
    weight = weight - step_rate * (
        first_hat / (jnp.sqrt(second_hat) + adam_eps) + decay_rate * weight
    )
    average = ema_decay * average + (1.0 - ema_decay) * weight
    return (weight, moment_one, moment_two, average)


def body(
    links,
    tokens,
    cotangent,
    slot_frame,
    step_count,
    *params,
):
    n_tok, n_head = links.n_tok, links.n_head
    devices = n_tok * n_head
    own = lax.axis_index("head")
    flip = lambda leaf: jnp.swapaxes(leaf, 1, 2)
    groups = []
    for at in range(0, 20, 5):
        qkv, proj, fc1, fc2, vec = params[at : at + 5]
        groups.append([qkv, flip(proj), fc1, flip(fc2), vec])
    masters = groups[0]

    slots = slot_frame.shape[0]
    per_head = slots // n_head
    held = slot_frame.reshape(n_head, per_head)
    held = jnp.concatenate(
        [lax.dynamic_slice_in_dim(held, own ^ step, 1, 0)[0] for step in range(n_head)]
    )
    index = jnp.arange(slots, dtype=jnp.int32)
    ahead = (held[None, :] < held[:, None]) | (
        (held[None, :] == held[:, None]) & (index[None, :] < index[:, None])
    )
    rank = jnp.sum(ahead.astype(jnp.int32), axis=1)
    order = jnp.sum(jnp.where(rank[None, :] == index[:, None], index[None, :], 0), axis=1).astype(jnp.int32)
    is_hi = (jnp.sum((held == held[0]).astype(jnp.int32)) == HI_BLOCKS).astype(jnp.int32).reshape(1)
    spans = (
        (HI_BLOCKS * BLOCK, LO_BLOCKS * BLOCK),
        (FRAMES * HI_BLOCKS * BLOCK, FRAMES * LO_BLOCKS * BLOCK),
    )

    vec_here = masters[4].shape[1]
    tile = lax.reduce_precision(masters[4], 8, 7).reshape(-1)
    tile = jnp.pad(tile, (0, 1024 - tile.shape[0])).reshape(8, 128)
    tiles = spread(tile, n_tok, n_head, 0).reshape(devices, 1024)[:, : 2 * vec_here]
    vectors = jnp.swapaxes(tiles.reshape(devices, 2, vec_here), 0, 1).reshape(2, devices * vec_here)
    vecs = [unpack(vectors[block]) for block in range(2)]

    qkv_low = [masters[0][block].astype(bf16) for block in range(2)]
    low = [
        jnp.concatenate([masters[kind][block].astype(bf16) for kind in (1, 2, 3)], axis=1)
        for block in range(2)
    ]
    places = links.gather_places()
    paired = links.paired
    width = D // n_head
    heads = width // HD
    own_rows = tokens.shape[0]
    cut = lambda rows: [rows[step * own_rows : (step + 1) * own_rows] for step in range(n_head)]
    gains = [head_gains(vec, heads) for vec in vecs]

    def attend(block, pieces, qkv_cols):
        qkv_bias = lax.dynamic_slice_in_dim(vecs[block][2].reshape(3, D), own * width, width, 1)
        return attention_forward(
            pieces, qkv_cols, qkv_bias.reshape(1, 3 * width), gains[block], order, is_hi, spans[block]
        )

    def enter(rows, mine, shard, collective_id):
        if paired:
            return enter_rows(rows, mine, shard, collective_id)
        planes = None if shard is None else links.gather_planes(shard)
        return links.rows_in(rows), lax.all_gather(mine, "tok", axis=0, tiled=True), planes

    def post(block, attended, hidden, pieces):
        vec, tail = vecs[block], vecs[1]
        rows = jnp.stack([vec[3], vec[4], vec[5], vec[6], vec[8], vec[9], tail[0], tail[1]])
        if not paired:
            attended = jnp.concatenate(links.by_index(links.exchange(cut(attended)), own), axis=1)
        return post_forward(
            attended,
            hidden,
            rows,
            vec[7].reshape(1, FF),
            (pieces, places),
            n_head,
            block == 1,
            paired,
            3 + block,
        )

    hidden_in = [tokens, None]
    normed = layer_norm(tokens.astype(f32), vecs[0][0], vecs[0][1]).astype(bf16)
    group, qkv_cols, saved, att_owns, mids, weights = ([None, None] for _ in range(6))

    mine = links.fetch_heads(qkv_low, own)
    normed, mine, low[0] = together(normed, mine, low[0])
    group[0], qkv_cols[0], planes = enter(normed, mine[0], low[0], 5)
    group[0], planes, qkv_cols[0], low[1] = together(group[0], planes, qkv_cols[0], low[1])
    near = links.gather_sides(planes)
    saved[0] = attend(0, group[0], qkv_cols[0])
    saved[0], near, low[1] = together(saved[0], near, low[1])
    planes = links.gather_planes(low[1])
    (hidden_in[1], normed, *mids[0]), weights[0] = post(0, saved[0][0], hidden_in[0], near)
    normed, planes = together(normed, planes)

    group[1], qkv_cols[1], _planes = enter(normed, mine[1], None, 6)
    group[1], planes = together(group[1], planes)
    near = links.gather_sides(planes)
    saved[1] = attend(1, group[1], qkv_cols[1])
    saved[1], near = together(saved[1], near)
    (hidden, _normed, *mids[1]), weights[1] = post(1, saved[1][0], hidden_in[1], near)

    def post_back(block, grad):
        vec = vecs[block]
        down, act, slope, branch, after, two, att_own = mids[block]
        rows = jnp.stack([vec[4], vec[5], vec[9]] + [vec[9]] * 5)
        d_att, *rest = post_backward(
            att_own,
            grad,
            down,
            branch,
            after,
            two,
            rows,
            act,
            slope,
            (weights[block], places),
            n_head,
            paired,
            7 + block,
        )
        if not paired:
            parts = [
                lax.dynamic_slice_in_dim(d_att, (own ^ step) * width, width, 1) for step in range(n_head)
            ]
            d_att = jnp.concatenate(links.exchange(parts), axis=0)
        return d_att, *rest

    def attend_back(block, grad_heads):
        attended, raw, values, lse = saved[block]
        return attention_backward(
            raw, values, grad_heads, attended, lse, gains[block], order, is_hi, spans[block]
        )

    def rows_back(block, d_qkv, d_after):
        gain, shift = vecs[block][0], vecs[block][1]
        if paired:
            grad, sums, mine = rows_out(
                d_qkv, qkv_cols[block], hidden_in[block], d_after, gain.reshape(1, D), group[block], 9 + block
            )
            return grad, mine, sums
        d_normed = jnp.einsum("rc,dc->rd", d_qkv, qkv_cols[block], preferred_element_type=f32)
        back = links.rows_out(cut(d_normed.astype(bf16)))
        d_hidden, d_gain, d_shift = jax.vjp(layer_norm, hidden_in[block].astype(f32), gain, shift)[1](back)
        sums = jnp.concatenate([jnp.stack([d_gain, d_shift]), jnp.zeros((6, D), f32)], axis=0)
        return d_after + d_hidden, qkv_grad(block, d_qkv), sums

    def qkv_grad(block, d_qkv):
        rows = jnp.concatenate(group[block], axis=0)
        return jnp.einsum("rd,rc->dc", rows, d_qkv, preferred_element_type=f32).astype(bf16)

    d_att, d_after, sums, d_up_bias, grads = post_back(1, cotangent)
    grads = links.scatter_first(grads)
    d_qkv, head_sums, bias_sums = attend_back(1, d_att)
    d_qkv, head_sums, bias_sums, grads = together(d_qkv, head_sums, bias_sums, grads)
    grads = links.scatter_add(grads)
    grad_rows, dw_qkv, norm_sums = rows_back(1, d_qkv, d_after)
    parts_one = [norm_sums, sums, d_up_bias, head_sums, bias_sums]
    grad_rows, grads, dw_qkv = together(grad_rows, grads, dw_qkv)
    grads_one = links.scatter_second(grads)
    mine_one = links.return_planes(dw_qkv)

    d_att, d_after, sums, d_up_bias, grads = post_back(0, grad_rows)
    d_att, grads_one, mine_one, grads = together(d_att, grads_one, mine_one, grads)
    sum_one = links.scatter_last(grads_one)
    grads = links.scatter_first(grads)
    d_qkv, head_sums, bias_sums = attend_back(0, d_att)
    d_qkv, head_sums, bias_sums, grads, sum_one = together(d_qkv, head_sums, bias_sums, grads, sum_one)
    vec_shape = (devices, 2 * vec_here)

    def tiles_of(norm_sums):
        both = pack([norm_sums, sums, d_up_bias, head_sums, bias_sums] + parts_one, n_head)
        flat = jnp.swapaxes(both.reshape(2, devices, vec_here), 0, 1).reshape(vec_shape)
        return jnp.pad(flat, ((0, 0), (0, 1024 - vec_shape[1]))).reshape(devices, 8, 128)

    if paired:
        tiles = tiles_of(jnp.zeros((8, D), f32))
        gain = vecs[0][0].reshape(1, D)
        grad_rows, _sums, sum_zero, qkv_zero, qkv_one, d_vec, squares = finish(
            d_qkv,
            qkv_cols[0],
            hidden_in[0],
            d_after,
            gain,
            group[0],
            grads,
            tiles,
            mine_one,
            sum_one,
            n_tok,
            n_head,
            11,
        )
    else:
        grad_rows, dw_qkv, norm_sums = rows_back(0, d_qkv, d_after)
        tiles = tiles_of(norm_sums)
        d_vec = swap(tiles, n_tok, n_head, 1)
        sum_zero = links.scatter_last(links.scatter_second(links.scatter_add(grads)))
        qkv_zero, qkv_one = links.return_heads([links.return_planes(dw_qkv), mine_one], own)
    summed = []
    for qkv_part, rest in ((qkv_zero, sum_zero), (qkv_one, sum_one)):
        summed.append([qkv_part, rest[:, PROJ_AT:UP_AT], rest[:, UP_AT:DOWN_AT], rest[:, DOWN_AT:WIDE]])
    d_vec = d_vec.reshape(1024)[: 2 * vec_here].reshape(2, vec_here)
    gradients = [jnp.stack([summed[0][kind], summed[1][kind]]) for kind in range(4)]
    if not paired:
        local_square = sum((jnp.sum(gradient * gradient) for gradient in gradients)) + jnp.sum(d_vec * d_vec)
        tile = jnp.concatenate([jnp.broadcast_to(local_square, (8, 128)), jnp.zeros((16, 128), f32)], axis=0)
        squares = spread(tile, n_tok, n_head, 2)
    late = jnp.sum(squares[:, 8:], axis=0).reshape(2 * D)
    grad_norm = jnp.sqrt(jnp.sum(squares[:, 0, 0]) + jnp.sum(late * late))
    if paired:
        flat = jnp.concatenate([late, jnp.zeros((devices * vec_here - 2 * D,), f32)]).reshape(devices, vec_here)
        mine_late = lax.dynamic_slice_in_dim(flat, lax.axis_index("tok") * n_head + own, 1, 0)
        d_vec = d_vec + jnp.concatenate([mine_late, jnp.zeros((1, vec_here), f32)], axis=0)
    gradients.append(d_vec)
    clip_scale = clip_norm / jnp.maximum(grad_norm, clip_norm)
    step_float = step_count[0].astype(f32)
    fix_one = 1.0 - beta_one**step_float
    fix_two = 1.0 - beta_two**step_float
    updates = [
        adam_update(
            groups[0][kind],
            gradients[kind],
            groups[1][kind],
            groups[2][kind],
            groups[3][kind],
            step_rates[kind],
            decays[kind],
            clip_scale,
            fix_one,
            fix_two,
        )
        for kind in range(5)
    ]
    outs = [hidden, grad_rows, grad_norm]
    for part in range(4):
        for kind in range(5):
            leaf = updates[kind][part]
            outs.append(flip(leaf) if kind in (1, 3) else leaf)
    return tuple(outs)


def solution(mesh):
    rows = P(BOTH, None)
    kinds = (
        P(None, BOTH, None),
        P(None, None, BOTH),
        P(None, BOTH, None),
        P(None, None, BOTH),
        P(None, BOTH),
    )
    in_specs = (rows, rows, P("tok"), P()) + kinds * 4
    out_specs = (rows, rows, P()) + kinds * 4
    return jax.shard_map(
        functools.partial(body, Links(mesh)),
        mesh=mesh,
        in_specs=in_specs,
        out_specs=out_specs,
        check_vma=False,
    )
```
